32 devices in a mesh: dp: 4 (over z), fsdp: 8 (over y, x, core).
Axes of the slice: x: 2, y: 2, z: 4, core: 2. Of those that a mesh axis runs over, the one named last changes fastest.
Arguments:
- tokens: bfloat16 [4096, 2048], P(('dp', 'fsdp')), may hold values from -6 to 6
- ln_gain: float32 [2048], replicated, may hold values from 0.5 to 1.5
- ln_shift: float32 [2048], replicated, may hold values from -3 to 3
- w_qkv: bfloat16 [2048, 6144], P(('dp', 'fsdp')), may hold values from -0.125 to 0.125
- b_qkv: float32 [6144], replicated, may hold values from -3 to 3
- w_out: bfloat16 [2048, 2048], P(('dp', 'fsdp')), may hold values from -0.5 to 0.5
- w_gate: bfloat16 [2048, 5632], P(('dp', 'fsdp')), may hold values from -0.125 to 0.125
- w_up: bfloat16 [2048, 5632], P(('dp', 'fsdp')), may hold values from -0.125 to 0.125
- w_down: bfloat16 [5632, 2048], P(('dp', 'fsdp')), may hold values from -0.078125 to 0.078125
- grad_out: bfloat16 [4096, 2048], P(('dp', 'fsdp')), may hold values from -6 to 6
- seq_lengths: int32 [32, 4], P(('dp', 'fsdp')), may hold values from 0 to 128, as said below
Outputs:
- output: bfloat16 [4096, 2048], P(('dp', 'fsdp'))
- grad_tokens: bfloat16 [4096, 2048], P(('dp', 'fsdp'))
- grad_w_qkv: float32 [2048, 6144], P(('dp', 'fsdp'))
- grad_w_out: float32 [2048, 2048], P(('dp', 'fsdp'))
- grad_w_gate: float32 [2048, 5632], P(('dp', 'fsdp'))
- grad_w_up: float32 [2048, 5632], P(('dp', 'fsdp'))
- grad_w_down: float32 [5632, 2048], P(('dp', 'fsdp'))
- grad_gain: float32 [2048], P(('dp', 'fsdp'))
- grad_shift: float32 [2048], P(('dp', 'fsdp'))
- grad_bias: float32 [6144], P(('dp', 'fsdp'))
The draws below stay inside these ranges and needn't reach their ends.
Inputs may be any that keep to these rules, and one draw needn't show every extreme that they name: `seq_lengths`: each device's row of lengths sums to at most 128; some device holds a single sequence of exactly 128 tokens, and some slots are empty (length 0).
All inputs are finite; a program needn't handle non-finite values.
Results may differ from the reference program's by a relative error of at most 0.012.
Values may be sent and summed in bfloat16 or wider, within the bound.
No kernel may reach another device: no remote copies, remote signals or barrier semaphores. Data moves between devices by JAX's collectives and lax.ppermute only.
A program may use at most 256 MiB of HBM per device.

```python
import math
from functools import partial
import jax
import jax.numpy as jnp
from jax import lax

D = 2048
H = 32
HD = 64
ROT = 16
FF = 5632
TOK_DEV = 128
SLOTS = 4
SHARDS = 32
TOKENS = 4096


def draw_seq_lengths(key, part):
    keys = jax.random.split(jax.random.fold_in(key, 17), 4)
    devices = jnp.arange(SHARDS, dtype=jnp.int32)
    short = jax.random.randint(keys[0], (SHARDS, SLOTS), TOK_DEV // (2 * SLOTS), TOK_DEV // SLOTS + 1)
    longer = jax.random.randint(keys[1], (SHARDS,), TOK_DEV // 2, TOK_DEV + 1)
    kinds = jax.random.randint(keys[2], (SHARDS,), 0, 4)
    chosen = jax.random.randint(keys[3], (), 0, SHARDS)
    is_long = (kinds == 0) | (devices == chosen)
    longer = jnp.where(devices == chosen, TOK_DEV, longer)
    first = jnp.where(is_long, longer, short[:, 0])
    others = jnp.where(is_long[:, None], 0, short[:, 1:])
    return jnp.concatenate([first[:, None], others], axis=1).astype(jnp.int32)


def spiked(values, rng, source, target, blocks, factor):
    owner, partner = [(jnp.arange(values.shape[dim]) // (values.shape[dim] // blocks)).reshape([-1 if axis == dim else 1 for axis in range(values.ndim)]) for dim in (source, target)]
    chosen = jax.random.permutation(rng, blocks)[partner]
    strong = (owner == chosen) | (owner == (partner + blocks // 2) % blocks)
    return jnp.where(strong, factor * values, values)


def steps_of(rng, dims, cuts, smallest, top_value):
    loudness = 1.0
    for dim, shards_of in cuts:
        draws = jax.random.uniform(jax.random.fold_in(jax.random.fold_in(rng, 6), dim), (shards_of,), jnp.float32, smallest / len(cuts), top_value / len(cuts))
        loudness = loudness * jnp.repeat(jnp.exp(draws), dims[dim] // shards_of).reshape((-1,) + (1,) * (len(dims) - 1 - dim))
    return loudness


def scatter_about(key, extent, width, reach, shards=(), held_as=jnp.bfloat16):
    drawn = jax.random.normal(key, extent, jnp.float32) * width
    if len(shards) > 0:
        drawn = steps_of(key, extent, shards, -0.22, 0.18) * drawn
    return jnp.clip(drawn, min=-reach, max=reach).astype(held_as)


def gaussian_with(own_key, dims, width, bound, cuts, heavy, kind=jnp.bfloat16):
    entries = width * jax.random.normal(own_key, dims, jnp.float32)
    if cuts:
        entries = entries * steps_of(own_key, dims, cuts, -0.22, 0.18)
    return jnp.clip(spiked(entries, jax.random.fold_in(own_key, 3), *heavy), -bound, bound).astype(kind)


def setup_inputs(seed: int = 0) -> dict:
    streams_of = jax.random.split(jax.random.key(seed), 12)
    tokens = gaussian_with(streams_of[0], (TOKENS, D), 1.0, 6.0, ((0, 32),), (0, 1, 32, 2.75))
    ln_gain = jnp.clip(1.0 + 0.1 * jax.random.normal(streams_of[1], (D,), jnp.float32), 0.5, 1.5)
    ln_shift = scatter_about(streams_of[2], (D,), 0.3, 3.0, (), jnp.float32)
    w_qkv = scatter_about(streams_of[3], (D, 3 * D), D ** -0.5, 0.125, ((0, 32),))
    b_qkv = scatter_about(streams_of[4], (3 * D,), 0.5, 3.0, (), jnp.float32)
    w_out = scatter_about(streams_of[5], (D, D), (D // 16) ** -0.5, 0.5, ((0, 32),))
    w_gate = scatter_about(streams_of[6], (D, FF), D ** -0.5, 0.125, ((0, 32),))
    w_up = scatter_about(streams_of[7], (D, FF), D ** -0.5, 0.125, ((0, 32),))
    w_down = scatter_about(streams_of[8], (FF, D), FF ** -0.5, 0.078125, ((0, 32),))
    grad_out = scatter_about(streams_of[9], (TOKENS, D), 1.0, 6.0, ((0, 32),))
    seq_lengths = draw_seq_lengths(jax.random.fold_in(streams_of[11], 71), 0)
    return {"tokens": tokens, "ln_gain": ln_gain, "ln_shift": ln_shift, "w_qkv": w_qkv, "b_qkv": b_qkv, "w_out": w_out, "w_gate": w_gate, "w_up": w_up, "w_down": w_down, "grad_out": grad_out, "seq_lengths": seq_lengths}


EPS = 1e-05
NEG = -1e+30
HIGH = lax.Precision.HIGHEST

@jax.custom_vjp
def low(v):
    return lax.optimization_barrier(v.astype(jnp.bfloat16)).astype(jnp.float32)

@jax.custom_vjp
def low_back(v):
    return v

def low_keep(v):
    return (low(v), None)

def low_pass(kept, grad):
    return (grad,)

def back_keep(v):
    return (v, None)

def back_low(kept, grad):
    return (low(grad),)
low.defvjp(low_keep, low_pass)
low_back.defvjp(back_keep, back_low)

def block_terms(lengths_row, rows_tok):
    lengths_row = lengths_row.astype(jnp.int32)
    ends = jnp.cumsum(lengths_row).astype(jnp.int32)
    place = jnp.arange(rows_tok, dtype=jnp.int32)
    segment = lax.optimization_barrier(jnp.sum((place[:, None] >= ends[None, :]).astype(jnp.int32), axis=1)).astype(jnp.int32)
    starts = jnp.concatenate([ends - lengths_row, ends[-1:]]).astype(jnp.int32)
    labels = jnp.arange(starts.shape[0], dtype=jnp.int32)
    begin = lax.optimization_barrier(jnp.sum(jnp.where(segment[:, None] == labels[None, :], starts[None, :], 0), axis=1)).astype(jnp.int32)
    position = (place - begin).astype(jnp.float32)
    valid = segment < lengths_row.shape[0]
    label_tok = jnp.where(valid, segment, lengths_row.shape[0] + place)
    allowed = (label_tok[:, None] == label_tok[None, :]) & (place[None, :] <= place[:, None])
    return (position, valid, allowed)

def angles(position):
    half = ROT // 2
    freq = jnp.exp(jnp.arange(half, dtype=jnp.float32) * (-2.0 * math.log(10000.0) / ROT))
    turn = position[:, None] * freq[None, :]
    return (jnp.cos(turn), jnp.sin(turn))

def rotate(heads_in, cosine, sine):
    half = ROT // 2
    first = heads_in[..., :half]
    second = heads_in[..., half:ROT]
    cos_b = cosine[:, None, :]
    sin_b = sine[:, None, :]
    return jnp.concatenate([first * cos_b - second * sin_b, second * cos_b + first * sin_b, heads_in[..., ROT:]], axis=-1)

def forward(seq_lengths, widened, ln_gain, ln_shift, w_qkv, b_qkv, w_out, w_gate, w_up, w_down):
    centered = widened - lax.optimization_barrier(jnp.mean(widened, axis=1, keepdims=True))
    inv_std = lax.rsqrt(lax.optimization_barrier(jnp.mean(centered * centered, axis=1, keepdims=True)) + EPS)
    normed = low(centered * inv_std * ln_gain + ln_shift)
    proj_qkv = low_back(jnp.dot(normed, w_qkv, precision=HIGH) + b_qkv)
    proj_gate = low_back(jnp.dot(normed, w_gate, precision=HIGH))
    proj_up = low_back(jnp.dot(normed, w_up, precision=HIGH))
    hidden = low(jax.nn.silu(proj_gate) * proj_up)
    grouped = proj_qkv.reshape(SHARDS, TOK_DEV, 3, H, HD)

    def attend(operands):
        block, lengths_row = operands
        position, valid, allowed = block_terms(lengths_row, TOK_DEV)
        cosine, sine = angles(position)
        query = low(rotate(block[:, 0], cosine, sine))
        keys = low(rotate(block[:, 1], cosine, sine))
        values = low(block[:, 2])
        scores = low_back(jnp.einsum('qhd,khd->hqk', query, keys, precision=HIGH) * 0.125)
        scores = jnp.where(allowed[None], scores, NEG)
        probs = low(jax.nn.softmax(scores, axis=2))
        mixed = jnp.einsum('hqk,khd->qhd', probs, values, precision=HIGH)
        return low(low_back(mixed)).reshape(TOK_DEV, D)
    attended = lax.map(jax.checkpoint(attend), (grouped, seq_lengths)).reshape(TOKENS, D)

    def valid_of(lengths_row):
        return block_terms(lengths_row, TOK_DEV)[1]
    valid = jax.vmap(valid_of)(seq_lengths).reshape(TOKENS)
    branch = jnp.dot(attended, w_out, precision=HIGH) + jnp.dot(hidden, w_down, precision=HIGH)
    return widened + jnp.where(valid[:, None], branch, 0.0)

def widen(array):
    return array.astype(jnp.float32)

def reference(tokens, ln_gain, ln_shift, w_qkv, b_qkv, w_out, w_gate, w_up, w_down, grad_out, seq_lengths):
    operands = tuple((widen(array) for array in (tokens, ln_gain, ln_shift, w_qkv, b_qkv, w_out, w_gate, w_up, w_down)))
    result, pull = jax.vjp(partial(forward, seq_lengths), *operands)
    grads = pull(widen(grad_out))
    return (result.astype(jnp.bfloat16), grads[0].astype(jnp.bfloat16), grads[3], grads[5], grads[6], grads[7], grads[8], grads[1], grads[2], grads[4])
```

```python
import math

import jax
import jax.numpy as jnp
from jax import lax
from jax.sharding import PartitionSpec as P

HD = 64
ROT = 16
EPS = 1e-05
NEG = -1e30
AXES = ("dp", "fsdp")
BF = jnp.bfloat16
F32 = jnp.float32
CONTRACT_ROWS = (((0,), (0,)), ((), ()))
CONTRACT_COLS = (((1,), (1,)), ((), ()))


def block_terms(lengths_row, rows_tok):
    ends = jnp.cumsum(lengths_row)
    place = jnp.arange(rows_tok, dtype=jnp.int32)
    segment = jnp.sum((place[:, None] >= ends[None, :]).astype(jnp.int32), axis=1)
    starts = jnp.concatenate([ends - lengths_row, ends[-1:]])
    labels = jnp.arange(starts.shape[0], dtype=jnp.int32)
    begin = jnp.sum(jnp.where(segment[:, None] == labels[None, :], starts[None, :], 0), axis=1)
    position = (place - begin).astype(F32)
    valid = segment < lengths_row.shape[0]
    label_tok = jnp.where(valid, segment, lengths_row.shape[0] + place)
    allowed = (label_tok[:, None] == label_tok[None, :]) & (place[None, :] <= place[:, None])
    return (position, valid, allowed)


def angles(position):
    half = ROT // 2
    freq = jnp.exp(jnp.arange(half, dtype=F32) * (-2.0 * math.log(10000.0) / ROT))
    turn = position[..., None] * freq
    return (jnp.cos(turn), jnp.sin(turn))


def rotate(heads_in, cosine, sine):
    half = ROT // 2
    first = heads_in[..., :half]
    second = heads_in[..., half:ROT]
    cos_b = cosine[:, :, None, :]
    sin_b = sine[:, :, None, :]
    return jnp.concatenate(
        [first * cos_b - second * sin_b, second * cos_b + first * sin_b, heads_in[..., ROT:]],
        axis=-1,
    )


class Plain:
    def __init__(self, outer, inner):
        self.tp, self.wide, self.cores, self.outer = outer, inner, 1, outer
        self.member = lax.axis_index("dp")
        self.lane = lax.axis_index("fsdp")

    def group_ids(self):
        return jnp.arange(self.tp) * self.wide + self.lane

    def gather_tokens(self, block):
        return lax.all_gather(block, "dp", axis=0, tiled=True)

    def scatter_tokens(self, parts):
        sent = parts.astype(BF).reshape(-1, parts.shape[-1])
        return lax.psum_scatter(sent, "dp", scatter_dimension=0, tiled=True).astype(F32)

    def exchange(self, blocks):
        return lax.all_to_all(blocks, "dp", split_axis=0, concat_axis=0, tiled=True)

    def gather_weights(self, block):
        return lax.all_gather(block, "fsdp", axis=0)

    def scatter_weights(self, blocks):
        flat = blocks.reshape((-1,) + blocks.shape[2:])
        return lax.psum_scatter(flat, "fsdp", scatter_dimension=0, tiled=True)

    def relative(self, blocks, axis):
        return blocks


class Linked:
    def __init__(self, outer, inner):
        self.outer, self.cores, self.wide = outer, 2, inner // 2
        self.tp = outer * 2
        flat = lax.axis_index("fsdp")
        self.core = lax.rem(flat, 2)
        self.lane = flat // 2
        self.depth = lax.axis_index("dp")
        self.member = self.depth * 2 + self.core

    def pairs(self, dz, dk, dc):
        out = []
        for z in range(self.outer):
            for k in range(self.wide):
                for c in range(2):
                    here = (z * self.wide + k) * 2 + c
                    there = ((z ^ dz) * self.wide + (k ^ dk)) * 2 + (c ^ dc)
                    out.append((here, there))
        return out

    def send(self, value, dz=0, dk=0, dc=0):
        return lax.ppermute(value, AXES, self.pairs(dz, dk, dc))

    def group_ids(self):
        ids = []
        for dc in range(2):
            for dz in range(self.outer):
                row = lax.bitwise_xor(self.depth, dz) * self.wide + self.lane
                ids.append(row * 2 + lax.bitwise_xor(self.core, dc))
        return jnp.stack(ids)

    def gather_tokens(self, block):
        parts = [block] + [self.send(block, dz=dz) for dz in range(1, self.outer)]
        mine = jnp.concatenate(parts, axis=0)
        return jnp.concatenate([mine, self.send(mine, dc=1)], axis=0)

    def scatter_tokens(self, parts):
        half = self.outer
        got = self.send(parts[half:].astype(BF), dc=1)
        chip = parts[:half] + got.astype(F32)
        total = chip[0]
        for dz in range(1, self.outer):
            total = total + self.send(chip[dz].astype(BF), dz=dz).astype(F32)
        return total

    def exchange(self, blocks):
        out = blocks
        for step in range(1, self.tp):
            spot = lax.bitwise_xor(self.member, step)
            piece = lax.dynamic_index_in_dim(blocks, spot, 0, keepdims=False)
            got = self.send(piece, dz=step // 2, dc=step % 2)
            out = lax.dynamic_update_index_in_dim(out, got, spot, 0)
        return out

    def gather_weights(self, block):
        half = block.shape[0] // 2
        from_x = self.send(block, dk=1)
        from_y = self.send(block, dk=2)
        low = self.send(from_x[:half], dk=2)
        high = self.send(from_y[half:], dk=1)
        return jnp.stack([block, from_x, from_y, jnp.concatenate([low, high], axis=0)])

    def scatter_weights(self, blocks):
        half = blocks.shape[1] // 2
        low = self.send(blocks[3, :half], dk=1)
        high = self.send(blocks[3, half:], dk=2)
        x_low = self.send(blocks[1, :half], dk=1)
        y_high = self.send(blocks[2, half:], dk=2)
        x_high = self.send((blocks[1, half:].astype(F32) + high.astype(F32)).astype(BF), dk=1)
        y_low = self.send((blocks[2, :half].astype(F32) + low.astype(F32)).astype(BF), dk=2)
        wide = blocks[0].astype(F32)
        low_sum = wide[:half] + x_low.astype(F32) + y_low.astype(F32)
        high_sum = wide[half:] + x_high.astype(F32) + y_high.astype(F32)
        return jnp.concatenate([low_sum, high_sum], axis=0).astype(BF)

    def relative(self, blocks, axis):
        shape = blocks.shape
        split = blocks.reshape(shape[:axis] + (2, 2) + shape[axis + 1 :])
        split = jnp.where(self.lane >= 2, jnp.flip(split, axis), split)
        split = jnp.where(lax.rem(self.lane, 2) == 1, jnp.flip(split, axis + 1), split)
        return split.reshape(shape)


def on_device(
    tokens, ln_gain, ln_shift, w_qkv, b_qkv, w_out, w_gate, w_up, w_down, grad_out, seq_lengths
):
    outer, inner = lax.axis_size("dp"), lax.axis_size("fsdp")
    linked = outer == 4 and inner == 8
    net = Linked(outer, inner) if linked else Plain(outer, inner)
    tp, wide, cores = net.tp, net.wide, net.cores
    rows_tok, width = tokens.shape
    own = w_qkv.shape[0]
    own_ff = w_down.shape[0]
    ff = w_gate.shape[1]
    cols, cols_ff = wide * own, wide * own_ff
    heads = cols // HD
    all_tok = tp * rows_tok

    _, valid, _ = block_terms(seq_lengths[0], rows_tok)
    keep_row = valid.astype(F32)[:, None]
    widened = tokens.astype(F32)
    centered = widened - jnp.mean(widened, axis=1, keepdims=True)
    inv_std = lax.rsqrt(jnp.mean(centered * centered, axis=1, keepdims=True) + EPS)
    scaled = centered * inv_std
    normed = (scaled * ln_gain + ln_shift).astype(BF)
    masked = (grad_out.astype(F32) * keep_row).astype(BF)

    def lanes_first(x):
        split = x.reshape(rows_tok, outer, wide, cores * own)
        return net.relative(jnp.swapaxes(split, 1, 2), 1).reshape(rows_tok, width)

    def lanes_back(x):
        split = net.relative(x.reshape(rows_tok, wide, outer, cores * own), 1)
        return jnp.swapaxes(split, 1, 2).reshape(rows_tok, width)

    def pack(w, groups, piece):
        split = w.reshape(own, groups, outer, wide, cores, piece)
        return jnp.transpose(split, (2, 4, 0, 1, 3, 5)).reshape(tp, own, groups * wide * piece)

    packed = jnp.concatenate(
        [pack(w_qkv, 3, own), pack(w_gate, 1, own_ff), pack(w_up, 1, own_ff)], axis=2
    )
    entry = net.exchange(packed).reshape(tp * own, -1)
    mixer = net.gather_weights(jnp.concatenate([w_out, w_down], axis=0))
    mixer = net.relative(mixer, 0)
    mixer = jnp.concatenate(
        [mixer[:, :own].reshape(cols, width), mixer[:, own:].reshape(cols_ff, width)], axis=0
    )
    entry = net.gather_weights(entry).reshape(width, -1)

    normed_all = net.gather_tokens(lanes_first(normed))
    masked_all = net.gather_tokens(masked)
    lengths = jnp.take(lax.all_gather(seq_lengths, AXES, axis=0, tiled=True), net.group_ids(), 0)
    position, _, allowed = jax.vmap(lambda row: block_terms(row, rows_tok))(lengths)
    cosine, sine = angles(position)

    bias = lax.dynamic_index_in_dim(
        jnp.transpose(b_qkv.reshape(3, outer, wide, cores, own), (1, 3, 0, 2, 4)).reshape(tp, -1),
        net.member,
        0,
        keepdims=False,
    )
    proj = jnp.dot(normed_all, entry, preferred_element_type=F32)
    proj_gate = proj[:, 3 * cols : 3 * cols + cols_ff]
    proj_up = proj[:, 3 * cols + cols_ff :]
    split_qkv = (proj[:, : 3 * cols] + bias).reshape(tp, rows_tok, 3, heads, HD)
    query = rotate(split_qkv[:, :, 0], cosine, sine).astype(BF)
    keys = rotate(split_qkv[:, :, 1], cosine, sine).astype(BF)
    values = split_qkv[:, :, 2].astype(BF)
    scores = jnp.einsum("bqhd,bkhd->bhqk", query, keys, preferred_element_type=F32) * 0.125
    scores = jnp.where(allowed[:, None], scores, NEG)
    peak = jnp.max(scores, axis=3, keepdims=True)
    lifted = jnp.exp(scores - peak)
    probs = lifted / jnp.sum(lifted, axis=3, keepdims=True)
    probs_low = probs.astype(BF)
    attended = jnp.einsum("bhqk,bkhd->bqhd", probs_low, values, preferred_element_type=F32)
    attended = attended.reshape(all_tok, cols).astype(BF)
    sigma = jax.nn.sigmoid(proj_gate)
    activ = proj_gate * sigma
    hidden = (activ * proj_up).astype(BF)
    joined = jnp.concatenate([attended, hidden], axis=1)

    branch = jnp.dot(joined, mixer, preferred_element_type=F32)
    branch = net.scatter_tokens(branch.reshape(tp, rows_tok, width))
    output = (widened + keep_row * branch).astype(BF)

    back = lax.dot_general(masked_all, mixer, CONTRACT_COLS, preferred_element_type=F32)
    grad_mixed = back[:, :cols].astype(BF).reshape(tp, rows_tok, heads, HD)
    grad_hid = back[:, cols:]
    grad_probs = jnp.einsum("bqhd,bkhd->bhqk", grad_mixed, values, preferred_element_type=F32)
    inner_sum = jnp.sum(probs * grad_probs, axis=3, keepdims=True)
    grad_scores = (probs * (grad_probs - inner_sum)).astype(BF)
    grad_query = (
        jnp.einsum("bhqk,bkhd->bqhd", grad_scores, keys, preferred_element_type=F32) * 0.125
    )
    grad_keys = (
        jnp.einsum("bhqk,bqhd->bkhd", grad_scores, query, preferred_element_type=F32) * 0.125
    )
    grad_values = jnp.einsum("bhqk,bqhd->bkhd", probs_low, grad_mixed, preferred_element_type=F32)
    grad_proj = jnp.stack(
        [rotate(grad_query, cosine, -sine), rotate(grad_keys, cosine, -sine), grad_values], axis=2
    )
    grad_proj = grad_proj.reshape(all_tok, 3 * cols).astype(BF)
    slope = sigma * (1.0 + proj_gate * (1.0 - sigma))
    grad_gate = (grad_hid * proj_up * slope).astype(BF)
    grad_up = (grad_hid * activ).astype(BF)
    grad_entry = jnp.concatenate([grad_proj, grad_gate, grad_up], axis=1)

    mixer_part = lax.dot_general(
        joined, masked_all, CONTRACT_ROWS, preferred_element_type=F32
    ).astype(BF)
    mixer_part = jnp.concatenate(
        [
            mixer_part[:cols].reshape(wide, own, width),
            mixer_part[cols:].reshape(wide, own_ff, width),
        ],
        axis=1,
    )
    mixer_sum = net.scatter_weights(net.relative(mixer_part, 0)).astype(F32)
    entry_part = lax.dot_general(
        normed_all, grad_entry, CONTRACT_ROWS, preferred_element_type=F32
    ).astype(BF)
    entry_sum = net.scatter_weights(entry_part.reshape(wide, tp * own, -1))
    entry_sum = net.exchange(entry_sum.reshape(tp, own, -1)).astype(F32)

    def unpack(part, groups, piece):
        split = part.reshape(outer, cores, own, groups, wide, piece)
        return jnp.transpose(split, (2, 3, 0, 4, 1, 5)).reshape(own, -1)

    grad_w_qkv = unpack(entry_sum[:, :, : 3 * cols], 3, own)
    grad_w_gate = unpack(entry_sum[:, :, 3 * cols : 3 * cols + cols_ff], 1, own_ff)
    grad_w_up = unpack(entry_sum[:, :, 3 * cols + cols_ff :], 1, own_ff)

    grad_norm = lax.dot_general(grad_entry, entry, CONTRACT_COLS, preferred_element_type=F32)
    grad_norm = lanes_back(net.scatter_tokens(grad_norm.reshape(tp, rows_tok, width)))
    lifted_grad = grad_norm * ln_gain
    grad_in = inv_std * (
        lifted_grad
        - jnp.mean(lifted_grad, axis=1, keepdims=True)
        - scaled * jnp.mean(lifted_grad * scaled, axis=1, keepdims=True)
    )
    grad_tokens = (grad_out.astype(F32) + grad_in).astype(BF)

    shards = outer * inner
    gain_part = jnp.sum(grad_norm * scaled, axis=0)
    shift_part = jnp.sum(grad_norm, axis=0)
    bias_part = jnp.sum(grad_proj.astype(F32), axis=0)
    bias_full = lax.dynamic_update_index_in_dim(
        jnp.zeros((tp, 3 * cols), F32), bias_part, net.member, 0
    )
    bias_full = jnp.transpose(bias_full.reshape(outer, cores, 3, wide, own), (2, 0, 3, 1, 4))
    stats = jnp.concatenate(
        [
            gain_part.reshape(shards, own),
            shift_part.reshape(shards, own),
            bias_full.reshape(shards, 3 * own),
        ],
        axis=1,
    )
    stats = lax.psum_scatter(stats.reshape(-1), AXES, scatter_dimension=0, tiled=True)
    return (
        output,
        grad_tokens,
        grad_w_qkv,
        mixer_sum[:own],
        grad_w_gate,
        grad_w_up,
        mixer_sum[own:],
        stats[:own],
        stats[own : 2 * own],
        stats[2 * own :],
    )


def solution(mesh):
    rows = P(AXES, None)
    return jax.shard_map(
        on_device,
        mesh=mesh,
        in_specs=(rows, P(), P(), rows, P(), rows, rows, rows, rows, rows, rows),
        out_specs=(rows,) * 7 + (P(AXES),) * 3,
        check_vma=False,
    )
```

```python
import functools
import math

import jax
import jax.numpy as jnp
from jax import lax
from jax.experimental import pallas as pl
from jax.experimental.pallas import tpu as pltpu
from jax.sharding import PartitionSpec as P

HD = 64
ROT = 16
EPS = 1e-05
NEG = -1e30
TILE = 128
AXES = ("dp", "fsdp")
BF = jnp.bfloat16
F32 = jnp.float32
CONTRACT_ROWS = (((0,), (0,)), ((), ()))
CONTRACT_COLS = (((1,), (1,)), ((), ()))


def block_terms(lengths_row, rows_tok):
    ends = jnp.cumsum(lengths_row)
    place = jnp.arange(rows_tok, dtype=jnp.int32)
    segment = jnp.sum((place[:, None] >= ends[None, :]).astype(jnp.int32), axis=1)
    starts = jnp.concatenate([ends - lengths_row, ends[-1:]])
    labels = jnp.arange(starts.shape[0], dtype=jnp.int32)
    begin = jnp.sum(jnp.where(segment[:, None] == labels[None, :], starts[None, :], 0), axis=1)
    position = (place - begin).astype(F32)
    valid = segment < lengths_row.shape[0]
    label_tok = jnp.where(valid, segment, lengths_row.shape[0] + place)
    allowed = (label_tok[:, None] == label_tok[None, :]) & (place[None, :] <= place[:, None])
    return (position, valid, allowed)


def turn_tables(position):
    half = ROT // 2
    freq = jnp.exp(jnp.arange(half, dtype=F32) * (-2.0 * math.log(10000.0) / ROT))
    turn = position.reshape(-1)[:, None] * freq[None, :]
    cosine, sine = jnp.cos(turn), jnp.sin(turn)
    rest = (turn.shape[0], HD - ROT)
    cos_t = jnp.concatenate([cosine, cosine, jnp.ones(rest, F32)], axis=1)
    sin_t = jnp.concatenate([-sine, sine, jnp.zeros(rest, F32)], axis=1)
    return (jnp.tile(cos_t, (1, 2)), jnp.tile(sin_t, (1, 2)))


def turned(v, cos_t, sin_t, low_half):
    partner = jnp.where(low_half, pltpu.roll(v, TILE - ROT // 2, 1), pltpu.roll(v, ROT // 2, 1))
    return v * cos_t + partner * sin_t

def stacked(v, first):
    zero = jnp.zeros_like(v)
    return jnp.concatenate([jnp.where(first, v, zero), jnp.where(first, zero, v)], axis=0)

def softmax_of(query2, keys, bias2):
    scores = lax.dot_general(query2, keys, (((1,), (1,)), ((), ())), preferred_element_type=F32)
    scores = scores * 0.125 + bias2
    lifted = jnp.exp(scores - jnp.max(scores, axis=1, keepdims=True))
    return lifted / jnp.sum(lifted, axis=1, keepdims=True)

def forward_kernel(cols, main, rest, proj_ref, bqkv_ref, cos_ref, sin_ref, mask_ref, joined_ref, qkv_ref):
    rows = proj_ref.shape[0]
    lane = lax.broadcasted_iota(jnp.int32, (rows, TILE), 1)
    first = lane < HD
    low_half = lane % HD < ROT // 2
    cos_t, sin_t = cos_ref[...], sin_ref[...]
    bias2 = jnp.concatenate([mask_ref[0], mask_ref[0]], axis=0)
    for pair in range(cols // TILE):
        at = [g * cols + pair * TILE for g in range(3)]
        query, keys, values = (
            proj_ref[:, a : a + TILE] + bqkv_ref[0:1, a : a + TILE] for a in at
        )
        query = turned(query, cos_t, sin_t, low_half).astype(BF)
        keys = turned(keys, cos_t, sin_t, low_half).astype(BF)
        values = values.astype(BF)
        for a, v in zip(at, (query, keys, values)):
            qkv_ref[:, a : a + TILE] = v
        probs = softmax_of(stacked(query, first), keys, bias2).astype(BF)
        mixed = jnp.dot(probs, values, preferred_element_type=F32)
        joined_ref[:, pair * TILE : (pair + 1) * TILE] = jnp.where(
            first, mixed[:rows], mixed[rows:]
        ).astype(BF)
    base = 3 * cols
    for j in range(main // TILE):
        gate = proj_ref[:, base + j * TILE : base + (j + 1) * TILE]
        up = proj_ref[:, base + main + j * TILE : base + main + (j + 1) * TILE]
        hid = gate * jax.nn.sigmoid(gate) * up
        joined_ref[:, cols + j * TILE : cols + (j + 1) * TILE] = hid.astype(BF)
    if rest:
        tail = proj_ref[:, base + 2 * main :]
        up = pltpu.roll(tail, rest, 1)
        hid = tail * jax.nn.sigmoid(tail) * up
        joined_ref[:, cols + main :] = hid[:, :rest].astype(BF)

def backward_kernel(cols, main, rest, proj_ref, back_ref, qkv_ref, cos_ref, sin_ref, mask_ref, grad_ref, sum_ref):
    rows = proj_ref.shape[0]
    lane = lax.broadcasted_iota(jnp.int32, (rows, TILE), 1)
    first = lane < HD
    low_half = lane % HD < ROT // 2
    cos_t, sin_t = cos_ref[...], sin_ref[...]
    bias2 = jnp.concatenate([mask_ref[0], mask_ref[0]], axis=0)

    @pl.when(pl.program_id(0) == 0)
    def _():
        sum_ref[...] = jnp.zeros_like(sum_ref)

    across = (((0,), (0,)), ((), ()))
    for pair in range(cols // TILE):
        at = [g * cols + pair * TILE for g in range(3)]
        query, keys, values = (qkv_ref[:, a : a + TILE] for a in at)
        query2 = stacked(query, first)
        mixed2 = stacked(back_ref[:, pair * TILE : (pair + 1) * TILE].astype(BF), first)
        probs = softmax_of(query2, keys, bias2)
        grad_probs = lax.dot_general(
            mixed2, values, (((1,), (1,)), ((), ())), preferred_element_type=F32
        )
        inner = jnp.sum(probs * grad_probs, axis=1, keepdims=True)
        grad_scores = (probs * (grad_probs - inner)).astype(BF)
        gq = jnp.dot(grad_scores, keys, preferred_element_type=F32)
        gq = jnp.where(first, gq[:rows], gq[rows:]) * 0.125
        gk = lax.dot_general(grad_scores, query2, across, preferred_element_type=F32) * 0.125
        gv = lax.dot_general(probs.astype(BF), mixed2, across, preferred_element_type=F32)
        gq = turned(gq, cos_t, -sin_t, low_half)
        gk = turned(gk, cos_t, -sin_t, low_half)
        for a, v in zip(at, (gq, gk, gv)):
            low = v.astype(BF)
            grad_ref[:, a : a + TILE] = low
            sum_ref[0:1, a : a + TILE] += jnp.sum(low.astype(F32), axis=0, keepdims=True)
    base = 3 * cols

    def gates(gate, up, grad_hid):
        sigma = jax.nn.sigmoid(gate)
        slope = sigma * (1.0 + gate * (1.0 - sigma))
        return (grad_hid * up * slope, grad_hid * (gate * sigma))

    for j in range(main // TILE):
        a, b = base + j * TILE, base + main + j * TILE
        gate, up = proj_ref[:, a : a + TILE], proj_ref[:, b : b + TILE]
        grad_hid = back_ref[:, cols + j * TILE : cols + (j + 1) * TILE]
        gg, gu = gates(gate, up, grad_hid)
        grad_ref[:, a : a + TILE] = gg.astype(BF)
        grad_ref[:, b : b + TILE] = gu.astype(BF)
    if rest:
        tail = proj_ref[:, base + 2 * main :]
        short = back_ref[:, cols + main :]
        grad_hid = jnp.concatenate([short, jnp.zeros_like(short)], axis=1)
        gg, gu = gates(tail, pltpu.roll(tail, rest, 1), grad_hid)
        both = jnp.where(lane < rest, gg, pltpu.roll(gu, rest, 1))
        grad_ref[:, base + 2 * main :] = both.astype(BF)

def forward_call(proj, bqkv, cos_t, sin_t, mask, cols, main, rest, rows):
    n = proj.shape[0] // rows
    row = lambda w: pl.BlockSpec((rows, w), lambda i: (i, 0))
    return pl.pallas_call(
        functools.partial(forward_kernel, cols, main, rest),
        grid=(n,),
        in_specs=[row(proj.shape[1]), pl.BlockSpec((8, 3 * cols), lambda i: (0, 0)), row(TILE), row(TILE),
                  pl.BlockSpec((1, rows, rows), lambda i: (i, 0, 0))],
        out_specs=[row(cols + main + rest), row(3 * cols)],
        out_shape=[jax.ShapeDtypeStruct((proj.shape[0], cols + main + rest), BF), jax.ShapeDtypeStruct((proj.shape[0], 3 * cols), BF)],
        compiler_params=pltpu.CompilerParams(dimension_semantics=("arbitrary",), vmem_limit_bytes=32 << 20),
        name="attend",
    )(proj, bqkv, cos_t, sin_t, mask)

def backward_call(proj, back, qkv, cos_t, sin_t, mask, cols, main, rest, rows):
    n = proj.shape[0] // rows
    row = lambda w: pl.BlockSpec((rows, w), lambda i: (i, 0))
    return pl.pallas_call(
        functools.partial(backward_kernel, cols, main, rest),
        grid=(n,),
        in_specs=[row(proj.shape[1]), row(back.shape[1]), row(3 * cols), row(TILE), row(TILE),
                  pl.BlockSpec((1, rows, rows), lambda i: (i, 0, 0))],
        out_specs=[row(proj.shape[1]), pl.BlockSpec((8, 3 * cols), lambda i: (0, 0))],
        out_shape=[jax.ShapeDtypeStruct(proj.shape, BF), jax.ShapeDtypeStruct((8, 3 * cols), F32)],
        compiler_params=pltpu.CompilerParams(dimension_semantics=("arbitrary",), vmem_limit_bytes=32 << 20),
        name="attend_back",
    )(proj, back, qkv, cos_t, sin_t, mask)


def column_plan(member, outer, wide, cores, own, own_ff, cols, main, rest):
    z, c = member // cores, member % cores
    out = []
    for g in range(3):
        for k in range(wide):
            out.append((0, ((g * outer + z) * wide + k) * cores * own + c * own, g * cols + k * own, own))
    for which in range(2):
        for k in range(wide):
            src = ((z * wide + k) * cores + c) * own_ff
            lo, hi = k * own_ff, (k + 1) * own_ff
            cut = min(hi, main)
            if cut > lo:
                out.append((1 + which, src, 3 * cols + which * main + lo, cut - lo))
            low = max(lo, main)
            if hi > low:
                out.append((1 + which, src + low - lo, 3 * cols + 2 * main + which * rest + low - main, hi - low))
    return out

def pack_kernel(plan, tp, member_ref, qkv_ref, gate_ref, up_ref, *refs):
    outs, slots, sem = refs[:tp], refs[tp], refs[tp + 1]
    member = member_ref[0]
    arrays = (qkv_ref, gate_ref, up_ref)
    for t in range(tp):
        for which, src, dst, width in plan(t):
            slots[t, :, dst : dst + width] = arrays[which][:, src : src + width]
    copies = [
        pltpu.make_async_copy(slots.at[lax.bitwise_xor(member, r)], outs[r], sem.at[r]) for r in range(tp)
    ]
    for copy in copies:
        copy.start()
    for copy in copies:
        copy.wait()

def pack_call(member, w_qkv, w_gate, w_up, plan, tp, total):
    own = w_qkv.shape[0]
    return pl.pallas_call(
        functools.partial(pack_kernel, plan, tp),
        in_specs=[pl.BlockSpec(memory_space=pltpu.SMEM)] + [pl.BlockSpec(memory_space=pltpu.VMEM)] * 3,
        out_specs=[pl.BlockSpec(memory_space=pl.ANY)] * tp,
        out_shape=[jax.ShapeDtypeStruct((own, total), BF)] * tp,
        scratch_shapes=[pltpu.VMEM((tp, own, total), BF), pltpu.SemaphoreType.DMA((tp,))],
        compiler_params=pltpu.CompilerParams(vmem_limit_bytes=32 << 20),
        name="pack_columns",
    )(member, w_qkv, w_gate, w_up)

def unpack_kernel(plan, tp, member_ref, *refs):
    ins, outs, slots, sem = refs[:tp], refs[tp : tp + 3], refs[tp + 3], refs[tp + 4]
    member = member_ref[0]
    copies = [
        pltpu.make_async_copy(ins[r], slots.at[lax.bitwise_xor(member, r)], sem.at[r]) for r in range(tp)
    ]
    for copy in copies:
        copy.start()
    for copy in copies:
        copy.wait()
    for t in range(tp):
        for which, src, dst, width in plan(t):
            outs[which][:, src : src + width] = slots[t, :, dst : dst + width].astype(F32)

def unpack_call(member, parts, plan, widths):
    tp = len(parts)
    own, total = parts[0].shape
    return pl.pallas_call(
        functools.partial(unpack_kernel, plan, tp),
        in_specs=[pl.BlockSpec(memory_space=pltpu.SMEM)] + [pl.BlockSpec(memory_space=pl.ANY)] * tp,
        out_specs=[pl.BlockSpec(memory_space=pltpu.VMEM)] * 3,
        out_shape=[jax.ShapeDtypeStruct((own, w), F32) for w in widths],
        scratch_shapes=[pltpu.VMEM((tp, own, total), BF), pltpu.SemaphoreType.DMA((tp,))],
        compiler_params=pltpu.CompilerParams(vmem_limit_bytes=32 << 20),
        name="unpack_columns",
    )(member, *parts)


def move_all(pairs_of, *args):
    pairs = pairs_of(*args)
    for when, src, dst, sem in pairs:
        copy = pltpu.make_async_copy(src, dst, sem)
        if when is None:
            copy.start()
        else:
            pl.when(when)(copy.start)
    for when, src, dst, sem in pairs:
        copy = pltpu.make_async_copy(src, dst, sem)
        if when is None:
            copy.wait()
        else:
            pl.when(when)(copy.wait)


def mover(pairs_of, index, arrays, shapes, copies, name):
    count = len(arrays)

    def kernel(index_ref, *refs):
        move_all(pairs_of, index_ref[0], refs[:count], refs[count:-1], refs[-1])

    anywhere = pl.BlockSpec(memory_space=pl.ANY)
    return pl.pallas_call(
        kernel,
        in_specs=[pl.BlockSpec(memory_space=pltpu.SMEM)] + [anywhere] * count,
        out_specs=[anywhere] * len(shapes),
        out_shape=[jax.ShapeDtypeStruct(shape, BF) for shape in shapes],
        scratch_shapes=[pltpu.SemaphoreType.DMA((copies,))],
        name=name,
    )(index, *arrays)


def stack_call(member, parts):
    tp = len(parts)
    rows, width = parts[0].shape
    half = tp // 2

    def pairs(me, ins, outs, sem):
        out = []
        for r in range(tp):
            spot = lax.bitwise_xor(me, r)
            for h in range(2):
                at = pl.multiple_of((spot - h * half) * rows, rows)
                dst = outs[h].at[pl.ds(at, rows), :]
                out.append((spot // half == h, ins[r], dst, sem.at[r]))
        return out

    return mover(pairs, member, parts, [(half * rows, width)] * 2, tp, "stack_rows")


def cut_call(member, low, high, tp):
    half = tp // 2
    rows = low.shape[0] // half
    width = low.shape[1]

    def pairs(me, ins, outs, sem):
        out = []
        for r in range(tp):
            spot = lax.bitwise_xor(me, r)
            for h in range(2):
                at = pl.multiple_of((spot - h * half) * rows, rows)
                src = ins[h].at[pl.ds(at, rows), :]
                out.append((spot // half == h, src, outs[r], sem.at[r]))
        return out

    return mover(pairs, member, [low, high], [(rows, width)] * tp, tp, "cut_rows")


def row_pairs(me, wide, own, own_ff, cut, halves, whole, sem, inward):
    out = []
    for j in range(wide):
        spot = lax.bitwise_xor(me, j)
        base = wide * own
        spans = (
            (0, 0, pl.multiple_of(base + spot * own_ff, 16), cut),
            (1, 0, pl.multiple_of(spot * own, 16), own),
            (1, own, pl.multiple_of(base + spot * own_ff + cut, 16), own_ff - cut),
        )
        for i, (h, at, place, size) in enumerate(spans):
            here = halves[2 * j + h].at[pl.ds(at, size), :]
            there = whole.at[pl.ds(place, size), :]
            src, dst = (here, there) if inward else (there, here)
            out.append((None, src, dst, sem.at[3 * j + i]))
    return out


def place_call(lane, blocks, own, own_ff):
    wide = len(blocks)
    cut, width = blocks[0][0].shape
    arrays = [half for pair in blocks for half in pair]

    def pairs(me, ins, outs, sem):
        return row_pairs(me, wide, own, own_ff, cut, ins, outs[0], sem, True)

    shape = (wide * (own + own_ff), width)
    return mover(pairs, lane, arrays, [shape], 3 * wide, "place_rows")[0]


def pick_call(lane, part, wide, own, own_ff, cut):
    width = part.shape[1]

    def pairs(me, ins, outs, sem):
        return row_pairs(me, wide, own, own_ff, cut, outs, ins[0], sem, False)

    shapes = [(cut, width), (own + own_ff - cut, width)] * wide
    outs = mover(pairs, lane, [part], shapes, 3 * wide, "pick_rows")
    return [outs[2 * j : 2 * j + 2] for j in range(wide)]


class Plain:
    def __init__(self, outer, inner):
        self.tp, self.wide, self.cores, self.outer = outer, inner, 1, outer
        self.member = lax.axis_index("dp")
        self.lane = lax.axis_index("fsdp")

    def group_lengths(self, lengths):
        return lax.all_gather(lengths, "dp", axis=0, tiled=True)

    def gather_tokens(self, block):
        return lax.all_gather(block, "dp", axis=0, tiled=True)

    def scatter_tokens(self, lhs, rhs, dims):
        part = lax.dot_general(lhs, rhs, dims, preferred_element_type=F32).astype(BF)
        return lax.psum_scatter(part, "dp", scatter_dimension=0, tiled=True).astype(F32)

    def columns_in(self, arrays, plan, total):
        own = arrays[0].shape[0]
        packed = []
        for member in range(self.tp):
            pieces = sorted(plan(member), key=lambda item: item[2])
            packed.append(jnp.concatenate([arrays[i][:, s : s + w] for i, s, _, w in pieces], 1))
        got = lax.all_to_all(jnp.stack(packed), "dp", split_axis=0, concat_axis=0, tiled=True)
        got = got.reshape(self.tp * own, total)
        return lax.all_gather(got, "fsdp", axis=0, tiled=True)

    def columns_out(self, lhs, rhs, plan, widths):
        part = lax.dot_general(lhs, rhs, CONTRACT_ROWS, preferred_element_type=F32).astype(BF)
        part = lax.psum_scatter(part, "fsdp", scatter_dimension=0, tiled=True)
        part = part.reshape(self.tp, -1, part.shape[1])
        got = lax.all_to_all(part, "dp", split_axis=0, concat_axis=0, tiled=True)
        outs = []
        for which, width in enumerate(widths):
            pieces = [(s, m, d, w) for m in range(self.tp) for i, s, d, w in plan(m) if i == which]
            outs.append(jnp.concatenate([got[m][:, d : d + w] for s, m, d, w in sorted(pieces)], 1))
        return [out.astype(F32) for out in outs]

    def rows_in(self, w_out, w_down):
        return jnp.concatenate(
            [lax.all_gather(w, "fsdp", axis=0, tiled=True) for w in (w_out, w_down)], axis=0
        )

    def rows_out(self, part, own, own_ff):
        cols = self.wide * own
        return [
            lax.psum_scatter(p, "fsdp", scatter_dimension=0, tiled=True).astype(F32)
            for p in (part[:cols], part[cols:])
        ]

    def relative(self, blocks, axis):
        return blocks

    def scatter_stats(self, stats):
        return lax.psum_scatter(stats, AXES, scatter_dimension=0, tiled=True)[0]


class Linked:
    def __init__(self, outer, inner):
        self.outer, self.cores, self.wide = outer, 2, inner // 2
        self.tp = outer * 2
        flat = lax.axis_index("fsdp")
        self.core = lax.rem(flat, 2)
        self.lane = flat // 2
        self.depth = lax.axis_index("dp")
        self.member = self.depth * 2 + self.core

    def send(self, value, dz=0, dk=0, dc=0):
        pairs = []
        for z in range(self.outer):
            for k in range(self.wide):
                for c in range(2):
                    here = (z * self.wide + k) * 2 + c
                    pairs.append((here, ((z ^ dz) * self.wide + (k ^ dk)) * 2 + (c ^ dc)))
        return lax.ppermute(value, AXES, pairs)

    def group_lengths(self, lengths):
        return self.gather_tokens(lengths)

    def gather_tokens(self, block):
        parts = [block] + [self.send(block, dz=dz) for dz in range(1, self.outer)]
        mine = jnp.concatenate(parts, axis=0)
        return jnp.concatenate([mine, self.send(mine, dc=1)], axis=0)

    def scatter_tokens(self, lhs, rhs, dims):
        half = lhs.shape[0] // 2
        far = lax.dot_general(lhs[half:], rhs, dims, preferred_element_type=F32).astype(BF)
        got = self.send(far, dc=1)
        near = lax.dot_general(lhs[:half], rhs, dims, preferred_element_type=F32)
        rows = half // self.outer
        chip = near + got.astype(F32)
        total = chip[:rows]
        for dz in range(1, self.outer):
            piece = chip[dz * rows : (dz + 1) * rows].astype(BF)
            total = total + self.send(piece, dz=dz).astype(F32)
        return total

    def exchange(self, parts):
        return [parts[0]] + [
            self.send(parts[step], dz=step // 2, dc=step % 2) for step in range(1, self.tp)
        ]

    def index(self):
        return self.member.astype(jnp.int32).reshape(1)

    def columns_in(self, arrays, plan, total):
        parts = self.exchange(pack_call(self.index(), *arrays, plan, self.tp, total))
        halves = stack_call(self.index(), parts)
        from_x = [self.send(half, dk=1) for half in halves]
        from_y = [self.send(half, dk=2) for half in halves]
        last = [self.send(from_x[0], dk=2), self.send(from_y[1], dk=1)]
        return jnp.concatenate([*halves, *from_x, *from_y, *last], axis=0)

    def sum_halves(self, blocks):
        low = self.send(blocks[3][0], dk=1)
        high = self.send(blocks[3][1], dk=2)
        x_low = self.send(blocks[1][0], dk=1)
        y_high = self.send(blocks[2][1], dk=2)
        x_high = self.send((blocks[1][1].astype(F32) + high.astype(F32)).astype(BF), dk=1)
        y_low = self.send((blocks[2][0].astype(F32) + low.astype(F32)).astype(BF), dk=2)
        return [
            (blocks[0][0].astype(F32) + x_low.astype(F32) + y_low.astype(F32)),
            (blocks[0][1].astype(F32) + x_high.astype(F32) + y_high.astype(F32)),
        ]

    def columns_out(self, lhs, rhs, plan, widths):
        size = lhs.shape[1] // self.wide // 2
        blocks = [[None, None] for _ in range(self.wide)]
        for j, h in ((3, 0), (3, 1), (1, 0), (2, 1), (1, 1), (2, 0), (0, 0), (0, 1)):
            at = (2 * j + h) * size
            blocks[j][h] = lax.dot_general(
                lhs[:, at : at + size], rhs, CONTRACT_ROWS, preferred_element_type=F32
            ).astype(BF)
        low, high = self.sum_halves(blocks)
        parts = cut_call(self.index(), low.astype(BF), high.astype(BF), self.tp)
        return unpack_call(self.index(), self.exchange(parts), plan, widths)

    def rows_in(self, w_out, w_down):
        cut = w_down.shape[0] // 32 * 16 + 32
        halves = [w_down[:cut], jnp.concatenate([w_out, w_down[cut:]], axis=0)]
        from_x = [self.send(half, dk=1) for half in halves]
        from_y = [self.send(half, dk=2) for half in halves]
        last = [self.send(from_x[0], dk=2), self.send(from_y[1], dk=1)]
        lane = self.lane.astype(jnp.int32).reshape(1)
        return place_call(lane, [halves, from_x, from_y, last], w_out.shape[0], w_down.shape[0])

    def rows_out(self, part, own, own_ff):
        cut = own_ff // 32 * 16 + 32
        lane = self.lane.astype(jnp.int32).reshape(1)
        low, high = self.sum_halves(pick_call(lane, part, self.wide, own, own_ff, cut))
        return [high[:own], jnp.concatenate([low, high[own:]], axis=0)]

    def relative(self, blocks, axis):
        shape = blocks.shape
        split = blocks.reshape(shape[:axis] + (2, 2) + shape[axis + 1 :])
        split = jnp.where(self.lane >= 2, jnp.flip(split, axis), split)
        split = jnp.where(lax.rem(self.lane, 2) == 1, jnp.flip(split, axis + 1), split)
        return split.reshape(shape)

    def scatter_stats(self, stats):
        width = stats.shape[1]
        split = stats.reshape(self.outer, self.wide, 2, width)

        def keep(values, axis, place, count, name):
            total = lax.dynamic_index_in_dim(values, place, axis, keepdims=False)
            for step in range(1, count):
                spot = lax.bitwise_xor(place, step)
                piece = lax.dynamic_index_in_dim(values, spot, axis, keepdims=False)
                total = total + self.send(piece, **{name: step})
            return total

        split = keep(split, 2, self.core, 2, "dc")
        split = keep(split, 1, self.lane, self.wide, "dk")
        return keep(split, 0, self.depth, self.outer, "dz")


def on_device(
    tokens, ln_gain, ln_shift, w_qkv, b_qkv, w_out, w_gate, w_up, w_down, grad_out, seq_lengths
):
    outer, inner = lax.axis_size("dp"), lax.axis_size("fsdp")
    linked = outer == 4 and inner == 8
    net = Linked(outer, inner) if linked else Plain(outer, inner)
    tp, wide, cores = net.tp, net.wide, net.cores
    rows_tok, width = tokens.shape
    own = w_qkv.shape[0]
    own_ff = w_down.shape[0]
    cols, cols_ff = wide * own, wide * own_ff
    main = cols_ff // TILE * TILE
    rest = cols_ff - main
    total = 3 * cols + 2 * cols_ff
    plan = lambda member: column_plan(
        member, outer, wide, cores, own, own_ff, cols, main, rest
    )

    _, valid, _ = block_terms(seq_lengths[0], rows_tok)
    keep_row = valid.astype(F32)[:, None]
    widened = tokens.astype(F32)
    centered = widened - jnp.mean(widened, axis=1, keepdims=True)
    inv_std = lax.rsqrt(jnp.mean(centered * centered, axis=1, keepdims=True) + EPS)
    scaled = centered * inv_std
    normed = (scaled * ln_gain + ln_shift).astype(BF)
    masked = (grad_out.astype(F32) * keep_row).astype(BF)

    def lanes_first(x):
        split = x.reshape(rows_tok, outer, wide, cores * own)
        return net.relative(jnp.swapaxes(split, 1, 2), 1).reshape(rows_tok, width)

    def lanes_back(x):
        split = net.relative(x.reshape(rows_tok, wide, outer, cores * own), 1)
        return jnp.swapaxes(split, 1, 2).reshape(rows_tok, width)

    entry = net.columns_in([w_qkv, w_gate, w_up], plan, total)
    mixer = net.rows_in(w_out, w_down)
    lengths = net.group_lengths(seq_lengths)
    normed_all = net.gather_tokens(lanes_first(normed))
    masked_all = net.gather_tokens(masked)
    position, _, allowed = jax.vmap(lambda row: block_terms(row, rows_tok))(lengths)
    cos_t, sin_t = turn_tables(position)
    mask = jnp.where(allowed, 0.0, NEG)
    bias = lax.dynamic_index_in_dim(
        jnp.transpose(b_qkv.reshape(3, outer, wide, cores, own), (1, 3, 0, 2, 4)).reshape(tp, -1),
        net.member,
        0,
    )
    bias = jnp.broadcast_to(bias, (8, 3 * cols))

    proj = jnp.dot(normed_all, entry, preferred_element_type=F32)
    joined, qkv = forward_call(proj, bias, cos_t, sin_t, mask, cols, main, rest, rows_tok)
    branch = net.scatter_tokens(joined, mixer, (((1,), (0,)), ((), ())))
    output = (widened + keep_row * branch).astype(BF)

    back = lax.dot_general(masked_all, mixer, CONTRACT_COLS, preferred_element_type=F32)
    grad_entry, bias_part = backward_call(
        proj, back, qkv, cos_t, sin_t, mask, cols, main, rest, rows_tok
    )
    grad_w_qkv, grad_w_gate, grad_w_up = net.columns_out(
        normed_all, grad_entry, plan, (w_qkv.shape[1], w_gate.shape[1], w_up.shape[1])
    )
    mixer_part = lax.dot_general(
        joined, masked_all, CONTRACT_ROWS, preferred_element_type=F32
    ).astype(BF)
    grad_w_out, grad_w_down = net.rows_out(mixer_part, own, own_ff)

    grad_norm = lanes_back(net.scatter_tokens(grad_entry, entry, CONTRACT_COLS))
    lifted_grad = grad_norm * ln_gain
    grad_in = inv_std * (
        lifted_grad
        - jnp.mean(lifted_grad, axis=1, keepdims=True)
        - scaled * jnp.mean(lifted_grad * scaled, axis=1, keepdims=True)
    )
    grad_tokens = (grad_out.astype(F32) + grad_in).astype(BF)

    shards = outer * inner
    gain_part = jnp.sum(grad_norm * scaled, axis=0)
    shift_part = jnp.sum(grad_norm, axis=0)
    bias_full = lax.dynamic_update_index_in_dim(
        jnp.zeros((tp, 3 * cols), F32), bias_part[0], net.member, 0
    )
    bias_full = jnp.transpose(bias_full.reshape(outer, cores, 3, wide, own), (2, 0, 3, 1, 4))
    stats = jnp.concatenate(
        [
            gain_part.reshape(shards, own),
            shift_part.reshape(shards, own),
            bias_full.reshape(shards, 3 * own),
        ],
        axis=1,
    )
    stats = net.scatter_stats(stats)
    return (
        output,
        grad_tokens,
        grad_w_qkv,
        grad_w_out,
        grad_w_gate,
        grad_w_up,
        grad_w_down,
        stats[:own],
        stats[own : 2 * own],
        stats[2 * own :],
    )


def solution(mesh):
    rows = P(AXES, None)
    return jax.shard_map(
        on_device,
        mesh=mesh,
        in_specs=(rows, P(), P(), rows, P(), rows, rows, rows, rows, rows, rows),
        out_specs=(rows,) * 7 + (P(AXES),) * 3,
        check_vma=False,
    )
```

```python
import functools
import math

import jax
import jax.numpy as jnp
from jax import lax
from jax.experimental import pallas as pl
from jax.experimental.pallas import tpu as pltpu
from jax.sharding import PartitionSpec as P

HD = 64
ROT = 16
EPS = 1e-05
NEG = -1e30
TILE = 128
AXES = ("dp", "fsdp")
BF = jnp.bfloat16
F32 = jnp.float32
CONTRACT_ROWS = (((0,), (0,)), ((), ()))
CONTRACT_COLS = (((1,), (1,)), ((), ()))


def block_terms(lengths_row, rows_tok):
    ends = jnp.cumsum(lengths_row)
    place = jnp.arange(rows_tok, dtype=jnp.int32)
    segment = jnp.sum((place[:, None] >= ends[None, :]).astype(jnp.int32), axis=1)
    starts = jnp.concatenate([ends - lengths_row, ends[-1:]])
    labels = jnp.arange(starts.shape[0], dtype=jnp.int32)
    begin = jnp.sum(jnp.where(segment[:, None] == labels[None, :], starts[None, :], 0), axis=1)
    position = (place - begin).astype(F32)
    valid = segment < lengths_row.shape[0]
    label_tok = jnp.where(valid, segment, lengths_row.shape[0] + place)
    allowed = (label_tok[:, None] == label_tok[None, :]) & (place[None, :] <= place[:, None])
    return (position, valid, allowed)


def turn_tables(position):
    half = ROT // 2
    freq = jnp.exp(jnp.arange(half, dtype=F32) * (-2.0 * math.log(10000.0) / ROT))
    turn = position.reshape(-1)[:, None] * freq[None, :]
    cosine, sine = jnp.cos(turn), jnp.sin(turn)
    rest = (turn.shape[0], HD - ROT)
    cos_t = jnp.concatenate([cosine, cosine, jnp.ones(rest, F32)], axis=1)
    sin_t = jnp.concatenate([-sine, sine, jnp.zeros(rest, F32)], axis=1)
    return (jnp.tile(cos_t, (1, 2)), jnp.tile(sin_t, (1, 2)))


def turned(v, cos_t, sin_t, low_half):
    partner = jnp.where(low_half, pltpu.roll(v, TILE - ROT // 2, 1), pltpu.roll(v, ROT // 2, 1))
    return v * cos_t + partner * sin_t

def stacked(v, first):
    zero = jnp.zeros_like(v)
    return jnp.concatenate([jnp.where(first, v, zero), jnp.where(first, zero, v)], axis=0)

def softmax_of(query2, keys, bias2):
    scores = lax.dot_general(query2, keys, (((1,), (1,)), ((), ())), preferred_element_type=F32)
    scores = scores * 0.125 + bias2
    lifted = jnp.exp(scores - jnp.max(scores, axis=1, keepdims=True))
    return lifted / jnp.sum(lifted, axis=1, keepdims=True)

def forward_kernel(cols, main, rest, proj_ref, bqkv_ref, cos_ref, sin_ref, mask_ref, joined_ref, qkv_ref):
    rows = proj_ref.shape[0]
    lane = lax.broadcasted_iota(jnp.int32, (rows, TILE), 1)
    first = lane < HD
    low_half = lane % HD < ROT // 2
    cos_t, sin_t = cos_ref[...], sin_ref[...]
    bias2 = jnp.concatenate([mask_ref[0], mask_ref[0]], axis=0)
    for pair in range(cols // TILE):
        at = [g * cols + pair * TILE for g in range(3)]
        query, keys, values = (
            proj_ref[:, a : a + TILE] + bqkv_ref[0:1, a : a + TILE] for a in at
        )
        query = turned(query, cos_t, sin_t, low_half).astype(BF)
        keys = turned(keys, cos_t, sin_t, low_half).astype(BF)
        values = values.astype(BF)
        for a, v in zip(at, (query, keys, values)):
            qkv_ref[:, a : a + TILE] = v
        probs = softmax_of(stacked(query, first), keys, bias2).astype(BF)
        mixed = jnp.dot(probs, values, preferred_element_type=F32)
        joined_ref[:, pair * TILE : (pair + 1) * TILE] = jnp.where(
            first, mixed[:rows], mixed[rows:]
        ).astype(BF)
    base = 3 * cols
    for j in range(main // TILE):
        gate = proj_ref[:, base + j * TILE : base + (j + 1) * TILE]
        up = proj_ref[:, base + main + j * TILE : base + main + (j + 1) * TILE]
        hid = gate * jax.nn.sigmoid(gate) * up
        joined_ref[:, cols + j * TILE : cols + (j + 1) * TILE] = hid.astype(BF)
    if rest:
        tail = proj_ref[:, base + 2 * main :]
        up = pltpu.roll(tail, rest, 1)
        hid = tail * jax.nn.sigmoid(tail) * up
        joined_ref[:, cols + main :] = hid[:, :rest].astype(BF)

def backward_kernel(cols, main, rest, proj_ref, back_ref, qkv_ref, cos_ref, sin_ref, mask_ref, grad_ref, sum_ref):
    rows = proj_ref.shape[0]
    lane = lax.broadcasted_iota(jnp.int32, (rows, TILE), 1)
    first = lane < HD
    low_half = lane % HD < ROT // 2
    cos_t, sin_t = cos_ref[...], sin_ref[...]
    bias2 = jnp.concatenate([mask_ref[0], mask_ref[0]], axis=0)

    @pl.when(pl.program_id(0) == 0)
    def _():
        sum_ref[...] = jnp.zeros_like(sum_ref)

    across = (((0,), (0,)), ((), ()))
    for pair in range(cols // TILE):
        at = [g * cols + pair * TILE for g in range(3)]
        query, keys, values = (qkv_ref[:, a : a + TILE] for a in at)
        query2 = stacked(query, first)
        mixed2 = stacked(back_ref[:, pair * TILE : (pair + 1) * TILE].astype(BF), first)
        probs = softmax_of(query2, keys, bias2)
        grad_probs = lax.dot_general(
            mixed2, values, (((1,), (1,)), ((), ())), preferred_element_type=F32
        )
        inner = jnp.sum(probs * grad_probs, axis=1, keepdims=True)
        grad_scores = (probs * (grad_probs - inner)).astype(BF)
        gq = jnp.dot(grad_scores, keys, preferred_element_type=F32)
        gq = jnp.where(first, gq[:rows], gq[rows:]) * 0.125
        gk = lax.dot_general(grad_scores, query2, across, preferred_element_type=F32) * 0.125
        gv = lax.dot_general(probs.astype(BF), mixed2, across, preferred_element_type=F32)
        gq = turned(gq, cos_t, -sin_t, low_half)
        gk = turned(gk, cos_t, -sin_t, low_half)
        for a, v in zip(at, (gq, gk, gv)):
            low = v.astype(BF)
            grad_ref[:, a : a + TILE] = low
            sum_ref[0:1, a : a + TILE] += jnp.sum(low.astype(F32), axis=0, keepdims=True)
    base = 3 * cols

    def gates(gate, up, grad_hid):
        sigma = jax.nn.sigmoid(gate)
        slope = sigma * (1.0 + gate * (1.0 - sigma))
        return (grad_hid * up * slope, grad_hid * (gate * sigma))

    for j in range(main // TILE):
        a, b = base + j * TILE, base + main + j * TILE
        gate, up = proj_ref[:, a : a + TILE], proj_ref[:, b : b + TILE]
        grad_hid = back_ref[:, cols + j * TILE : cols + (j + 1) * TILE]
        gg, gu = gates(gate, up, grad_hid)
        grad_ref[:, a : a + TILE] = gg.astype(BF)
        grad_ref[:, b : b + TILE] = gu.astype(BF)
    if rest:
        tail = proj_ref[:, base + 2 * main :]
        short = back_ref[:, cols + main :]
        grad_hid = jnp.concatenate([short, jnp.zeros_like(short)], axis=1)
        gg, gu = gates(tail, pltpu.roll(tail, rest, 1), grad_hid)
        both = jnp.where(lane < rest, gg, pltpu.roll(gu, rest, 1))
        grad_ref[:, base + 2 * main :] = both.astype(BF)

def forward_call(proj, bqkv, cos_t, sin_t, mask, cols, main, rest, rows):
    n = proj.shape[0] // rows
    row = lambda w: pl.BlockSpec((rows, w), lambda i: (i, 0))
    return pl.pallas_call(
        functools.partial(forward_kernel, cols, main, rest),
        grid=(n,),
        in_specs=[row(proj.shape[1]), pl.BlockSpec((8, 3 * cols), lambda i: (0, 0)), row(TILE), row(TILE),
                  pl.BlockSpec((1, rows, rows), lambda i: (i, 0, 0))],
        out_specs=[row(cols + main + rest), row(3 * cols)],
        out_shape=[jax.ShapeDtypeStruct((proj.shape[0], cols + main + rest), BF), jax.ShapeDtypeStruct((proj.shape[0], 3 * cols), BF)],
        compiler_params=pltpu.CompilerParams(dimension_semantics=("arbitrary",), vmem_limit_bytes=32 << 20),
        name="attend",
    )(proj, bqkv, cos_t, sin_t, mask)

def backward_call(proj, back, qkv, cos_t, sin_t, mask, cols, main, rest, rows):
    n = proj.shape[0] // rows
    row = lambda w: pl.BlockSpec((rows, w), lambda i: (i, 0))
    return pl.pallas_call(
        functools.partial(backward_kernel, cols, main, rest),
        grid=(n,),
        in_specs=[row(proj.shape[1]), row(back.shape[1]), row(3 * cols), row(TILE), row(TILE),
                  pl.BlockSpec((1, rows, rows), lambda i: (i, 0, 0))],
        out_specs=[row(proj.shape[1]), pl.BlockSpec((8, 3 * cols), lambda i: (0, 0))],
        out_shape=[jax.ShapeDtypeStruct(proj.shape, BF), jax.ShapeDtypeStruct((8, 3 * cols), F32)],
        compiler_params=pltpu.CompilerParams(dimension_semantics=("arbitrary",), vmem_limit_bytes=32 << 20),
        name="attend_back",
    )(proj, back, qkv, cos_t, sin_t, mask)


def column_plan(member, outer, wide, cores, own, own_ff, cols, main, rest):
    z, c = member // cores, member % cores
    out = []
    for g in range(3):
        for k in range(wide):
            out.append((0, ((g * outer + z) * wide + k) * cores * own + c * own, g * cols + k * own, own))
    for which in range(2):
        for k in range(wide):
            src = ((z * wide + k) * cores + c) * own_ff
            lo, hi = k * own_ff, (k + 1) * own_ff
            cut = min(hi, main)
            if cut > lo:
                out.append((1 + which, src, 3 * cols + which * main + lo, cut - lo))
            low = max(lo, main)
            if hi > low:
                out.append((1 + which, src + low - lo, 3 * cols + 2 * main + which * rest + low - main, hi - low))
    return out

def pack_kernel(plan, tp, member_ref, qkv_ref, gate_ref, up_ref, *refs):
    outs, slots, sem = refs[:tp], refs[tp], refs[tp + 1]
    member = member_ref[0]
    arrays = (qkv_ref, gate_ref, up_ref)
    for t in range(tp):
        for which, src, dst, width in plan(t):
            slots[t, :, dst : dst + width] = arrays[which][:, src : src + width]
    copies = [
        pltpu.make_async_copy(slots.at[lax.bitwise_xor(member, r)], outs[r], sem.at[r]) for r in range(tp)
    ]
    for copy in copies:
        copy.start()
    for copy in copies:
        copy.wait()

def pack_call(member, w_qkv, w_gate, w_up, plan, tp, total):
    own = w_qkv.shape[0]
    return pl.pallas_call(
        functools.partial(pack_kernel, plan, tp),
        in_specs=[pl.BlockSpec(memory_space=pltpu.SMEM)] + [pl.BlockSpec(memory_space=pltpu.VMEM)] * 3,
        out_specs=[pl.BlockSpec(memory_space=pl.ANY)] * tp,
        out_shape=[jax.ShapeDtypeStruct((own, total), BF)] * tp,
        scratch_shapes=[pltpu.VMEM((tp, own, total), BF), pltpu.SemaphoreType.DMA((tp,))],
        compiler_params=pltpu.CompilerParams(vmem_limit_bytes=32 << 20),
        name="pack_columns",
    )(member, w_qkv, w_gate, w_up)

def unpack_kernel(plan, tp, member_ref, *refs):
    ins, outs, slots, sem = refs[:tp], refs[tp : tp + 3], refs[tp + 3], refs[tp + 4]
    member = member_ref[0]
    copies = [
        pltpu.make_async_copy(ins[r], slots.at[lax.bitwise_xor(member, r)], sem.at[r]) for r in range(tp)
    ]
    for copy in copies:
        copy.start()
    for copy in copies:
        copy.wait()
    for t in range(tp):
        for which, src, dst, width in plan(t):
            outs[which][:, src : src + width] = slots[t, :, dst : dst + width].astype(F32)

def unpack_call(member, parts, plan, widths):
    tp = len(parts)
    own, total = parts[0].shape
    return pl.pallas_call(
        functools.partial(unpack_kernel, plan, tp),
        in_specs=[pl.BlockSpec(memory_space=pltpu.SMEM)] + [pl.BlockSpec(memory_space=pl.ANY)] * tp,
        out_specs=[pl.BlockSpec(memory_space=pltpu.VMEM)] * 3,
        out_shape=[jax.ShapeDtypeStruct((own, w), F32) for w in widths],
        scratch_shapes=[pltpu.VMEM((tp, own, total), BF), pltpu.SemaphoreType.DMA((tp,))],
        compiler_params=pltpu.CompilerParams(vmem_limit_bytes=32 << 20),
        name="unpack_columns",
    )(member, *parts)


def move_all(pairs_of, *args):
    pairs = pairs_of(*args)
    for when, src, dst, sem in pairs:
        copy = pltpu.make_async_copy(src, dst, sem)
        if when is None:
            copy.start()
        else:
            pl.when(when)(copy.start)
    for when, src, dst, sem in pairs:
        copy = pltpu.make_async_copy(src, dst, sem)
        if when is None:
            copy.wait()
        else:
            pl.when(when)(copy.wait)


def mover(pairs_of, index, arrays, shapes, copies, name, inward):
    count = len(arrays)

    def kernel(index_ref, *refs):
        move_all(pairs_of, index_ref[0], refs[:count], refs[count:-1], refs[-1])

    anywhere = pl.BlockSpec(memory_space=pl.ANY)
    held = pl.BlockSpec(memory_space=pltpu.VMEM)
    return pl.pallas_call(
        kernel,
        in_specs=[pl.BlockSpec(memory_space=pltpu.SMEM)] + [anywhere if inward else held] * count,
        out_specs=[held if inward else anywhere] * len(shapes),
        out_shape=[jax.ShapeDtypeStruct(shape, BF) for shape in shapes],
        scratch_shapes=[pltpu.SemaphoreType.DMA((copies,))],
        compiler_params=pltpu.CompilerParams(vmem_limit_bytes=16 << 20),
        name=name,
    )(index, *arrays)


def stack_call(member, parts):
    tp = len(parts)
    rows, width = parts[0].shape
    half = tp // 2

    def pairs(me, ins, outs, sem):
        out = []
        for r in range(tp):
            spot = lax.bitwise_xor(me, r)
            for h in range(2):
                at = pl.multiple_of((spot - h * half) * rows, rows)
                dst = outs[h].at[pl.ds(at, rows), :]
                out.append((spot // half == h, ins[r], dst, sem.at[r]))
        return out

    return mover(pairs, member, parts, [(half * rows, width)] * 2, tp, "stack_rows", True)


def cut_call(member, low, high, tp):
    half = tp // 2
    rows = low.shape[0] // half
    width = low.shape[1]

    def pairs(me, ins, outs, sem):
        out = []
        for r in range(tp):
            spot = lax.bitwise_xor(me, r)
            for h in range(2):
                at = pl.multiple_of((spot - h * half) * rows, rows)
                src = ins[h].at[pl.ds(at, rows), :]
                out.append((spot // half == h, src, outs[r], sem.at[r]))
        return out

    return mover(pairs, member, [low, high], [(rows, width)] * tp, tp, "cut_rows", False)


def row_pairs(me, wide, own, own_ff, cut, halves, whole, sem, inward):
    out = []
    for j in range(wide):
        spot = lax.bitwise_xor(me, j)
        base = wide * own
        spans = (
            (0, 0, pl.multiple_of(base + spot * own_ff, 16), cut),
            (1, 0, pl.multiple_of(spot * own, 16), own),
            (1, own, pl.multiple_of(base + spot * own_ff + cut, 16), own_ff - cut),
        )
        for i, (h, at, place, size) in enumerate(spans):
            here = halves[2 * j + h].at[pl.ds(at, size), :]
            there = whole.at[pl.ds(place, size), :]
            src, dst = (here, there) if inward else (there, here)
            out.append((None, src, dst, sem.at[3 * j + i]))
    return out


def place_call(lane, blocks, own, own_ff):
    wide = len(blocks)
    cut, width = blocks[0][0].shape
    arrays = [half for pair in blocks for half in pair]

    def pairs(me, ins, outs, sem):
        return row_pairs(me, wide, own, own_ff, cut, ins, outs[0], sem, True)

    shape = (wide * (own + own_ff), width)
    return mover(pairs, lane, arrays, [shape], 3 * wide, "place_rows", True)[0]


def pick_call(lane, part, wide, own, own_ff, cut):
    width = part.shape[1]

    def pairs(me, ins, outs, sem):
        return row_pairs(me, wide, own, own_ff, cut, outs, ins[0], sem, False)

    shapes = [(cut, width), (own + own_ff - cut, width)] * wide
    outs = mover(pairs, lane, [part], shapes, 3 * wide, "pick_rows", False)
    return [outs[2 * j : 2 * j + 2] for j in range(wide)]


class Plain:
    def __init__(self, outer, inner):
        self.tp, self.wide, self.cores, self.outer = outer, inner, 1, outer
        self.member = lax.axis_index("dp")
        self.lane = lax.axis_index("fsdp")

    def group_lengths(self, lengths):
        return lax.all_gather(lengths, "dp", axis=0, tiled=True)

    def gather_tokens(self, block):
        return lax.all_gather(block, "dp", axis=0, tiled=True)

    def scatter_tokens(self, lhs, rhs, dims):
        part = lax.dot_general(lhs, rhs, dims, preferred_element_type=F32).astype(BF)
        return lax.psum_scatter(part, "dp", scatter_dimension=0, tiled=True).astype(F32)

    def columns_in(self, arrays, plan, total):
        own = arrays[0].shape[0]
        packed = []
        for member in range(self.tp):
            pieces = sorted(plan(member), key=lambda item: item[2])
            packed.append(jnp.concatenate([arrays[i][:, s : s + w] for i, s, _, w in pieces], 1))
        got = lax.all_to_all(jnp.stack(packed), "dp", split_axis=0, concat_axis=0, tiled=True)
        got = got.reshape(self.tp * own, total)
        return lax.all_gather(got, "fsdp", axis=0, tiled=True)

    def columns_out(self, lhs, rhs, plan, widths):
        part = lax.dot_general(lhs, rhs, CONTRACT_ROWS, preferred_element_type=F32).astype(BF)
        part = lax.psum_scatter(part, "fsdp", scatter_dimension=0, tiled=True)
        part = part.reshape(self.tp, -1, part.shape[1])
        got = lax.all_to_all(part, "dp", split_axis=0, concat_axis=0, tiled=True)
        outs = []
        for which, width in enumerate(widths):
            pieces = [(s, m, d, w) for m in range(self.tp) for i, s, d, w in plan(m) if i == which]
            outs.append(jnp.concatenate([got[m][:, d : d + w] for s, m, d, w in sorted(pieces)], 1))
        return [out.astype(F32) for out in outs]

    def rows_in(self, w_out, w_down):
        return jnp.concatenate(
            [lax.all_gather(w, "fsdp", axis=0, tiled=True) for w in (w_out, w_down)], axis=0
        )

    def rows_out(self, part, own, own_ff):
        cols = self.wide * own
        return [
            lax.psum_scatter(p, "fsdp", scatter_dimension=0, tiled=True).astype(F32)
            for p in (part[:cols], part[cols:])
        ]

    def relative(self, blocks, axis):
        return blocks

    def scatter_stats(self, stats):
        return lax.psum_scatter(stats, AXES, scatter_dimension=0, tiled=True)[0]


class Linked:
    def __init__(self, outer, inner):
        self.outer, self.cores, self.wide = outer, 2, inner // 2
        self.tp = outer * 2
        flat = lax.axis_index("fsdp")
        self.core = lax.rem(flat, 2)
        self.lane = flat // 2
        self.depth = lax.axis_index("dp")
        self.member = self.depth * 2 + self.core

    def send(self, value, dz=0, dk=0, dc=0):
        pairs = []
        for z in range(self.outer):
            for k in range(self.wide):
                for c in range(2):
                    here = (z * self.wide + k) * 2 + c
                    pairs.append((here, ((z ^ dz) * self.wide + (k ^ dk)) * 2 + (c ^ dc)))
        return lax.ppermute(value, AXES, pairs)

    def group_lengths(self, lengths):
        return self.gather_tokens(lengths)

    def gather_tokens(self, block):
        parts = [block] + [self.send(block, dz=dz) for dz in range(1, self.outer)]
        mine = jnp.concatenate(parts, axis=0)
        return jnp.concatenate([mine, self.send(mine, dc=1)], axis=0)

    def scatter_tokens(self, lhs, rhs, dims):
        half = lhs.shape[0] // 2
        far = lax.dot_general(lhs[half:], rhs, dims, preferred_element_type=F32).astype(BF)
        got = self.send(far, dc=1)
        near = lax.dot_general(lhs[:half], rhs, dims, preferred_element_type=F32)
        rows = half // self.outer
        chip = near + got.astype(F32)
        total = chip[:rows]
        for dz in range(1, self.outer):
            piece = chip[dz * rows : (dz + 1) * rows].astype(BF)
            total = total + self.send(piece, dz=dz).astype(F32)
        return total

    def exchange(self, parts):
        return [parts[0]] + [
            self.send(parts[step], dz=step // 2, dc=step % 2) for step in range(1, self.tp)
        ]

    def index(self):
        return self.member.astype(jnp.int32).reshape(1)

    def columns_in(self, arrays, plan, total):
        parts = self.exchange(pack_call(self.index(), *arrays, plan, self.tp, total))
        halves = stack_call(self.index(), parts)
        from_x = [self.send(half, dk=1) for half in halves]
        from_y = [self.send(half, dk=2) for half in halves]
        last = [self.send(from_x[0], dk=2), self.send(from_y[1], dk=1)]
        return jnp.concatenate([*halves, *from_x, *from_y, *last], axis=0)

    def sum_halves(self, blocks):
        low = self.send(blocks[3][0], dk=1)
        high = self.send(blocks[3][1], dk=2)
        x_low = self.send(blocks[1][0], dk=1)
        y_high = self.send(blocks[2][1], dk=2)
        x_high = self.send((blocks[1][1].astype(F32) + high.astype(F32)).astype(BF), dk=1)
        y_low = self.send((blocks[2][0].astype(F32) + low.astype(F32)).astype(BF), dk=2)
        return [
            (blocks[0][0].astype(F32) + x_low.astype(F32) + y_low.astype(F32)),
            (blocks[0][1].astype(F32) + x_high.astype(F32) + y_high.astype(F32)),
        ]

    def columns_out(self, lhs, rhs, plan, widths):
        size = lhs.shape[1] // self.wide // 2
        blocks = [[None, None] for _ in range(self.wide)]
        for j, h in ((3, 0), (3, 1), (1, 0), (2, 1), (1, 1), (2, 0), (0, 0), (0, 1)):
            at = (2 * j + h) * size
            blocks[j][h] = lax.dot_general(
                lhs[:, at : at + size], rhs, CONTRACT_ROWS, preferred_element_type=F32
            ).astype(BF)
        low, high = self.sum_halves(blocks)
        parts = cut_call(self.index(), low.astype(BF), high.astype(BF), self.tp)
        return unpack_call(self.index(), self.exchange(parts), plan, widths)

    def rows_in(self, w_out, w_down):
        cut = w_down.shape[0] // 32 * 16 + 32
        halves = [w_down[:cut], jnp.concatenate([w_out, w_down[cut:]], axis=0)]
        from_x = [self.send(half, dk=1) for half in halves]
        from_y = [self.send(half, dk=2) for half in halves]
        last = [self.send(from_x[0], dk=2), self.send(from_y[1], dk=1)]
        lane = self.lane.astype(jnp.int32).reshape(1)
        return place_call(lane, [halves, from_x, from_y, last], w_out.shape[0], w_down.shape[0])

    def rows_out(self, part, own, own_ff):
        cut = own_ff // 32 * 16 + 32
        lane = self.lane.astype(jnp.int32).reshape(1)
        low, high = self.sum_halves(pick_call(lane, part, self.wide, own, own_ff, cut))
        return [high[:own], jnp.concatenate([low, high[own:]], axis=0)]

    def relative(self, blocks, axis):
        shape = blocks.shape
        split = blocks.reshape(shape[:axis] + (2, 2) + shape[axis + 1 :])
        split = jnp.where(self.lane >= 2, jnp.flip(split, axis), split)
        split = jnp.where(lax.rem(self.lane, 2) == 1, jnp.flip(split, axis + 1), split)
        return split.reshape(shape)

    def scatter_stats(self, stats):
        width = stats.shape[1]
        split = stats.reshape(self.outer, self.wide, 2, width)

        def keep(values, axis, place, count, name):
            total = lax.dynamic_index_in_dim(values, place, axis, keepdims=False)
            for step in range(1, count):
                spot = lax.bitwise_xor(place, step)
                piece = lax.dynamic_index_in_dim(values, spot, axis, keepdims=False)
                total = total + self.send(piece, **{name: step})
            return total

        split = keep(split, 2, self.core, 2, "dc")
        split = keep(split, 1, self.lane, self.wide, "dk")
        return keep(split, 0, self.depth, self.outer, "dz")


def on_device(
    tokens, ln_gain, ln_shift, w_qkv, b_qkv, w_out, w_gate, w_up, w_down, grad_out, seq_lengths
):
    outer, inner = lax.axis_size("dp"), lax.axis_size("fsdp")
    linked = outer == 4 and inner == 8
    net = Linked(outer, inner) if linked else Plain(outer, inner)
    tp, wide, cores = net.tp, net.wide, net.cores
    rows_tok, width = tokens.shape
    own = w_qkv.shape[0]
    own_ff = w_down.shape[0]
    cols, cols_ff = wide * own, wide * own_ff
    main = cols_ff // TILE * TILE
    rest = cols_ff - main
    total = 3 * cols + 2 * cols_ff
    plan = lambda member: column_plan(
        member, outer, wide, cores, own, own_ff, cols, main, rest
    )

    _, valid, _ = block_terms(seq_lengths[0], rows_tok)
    keep_row = valid.astype(F32)[:, None]
    widened = tokens.astype(F32)
    centered = widened - jnp.mean(widened, axis=1, keepdims=True)
    inv_std = lax.rsqrt(jnp.mean(centered * centered, axis=1, keepdims=True) + EPS)
    scaled = centered * inv_std
    normed = (scaled * ln_gain + ln_shift).astype(BF)
    masked = (grad_out.astype(F32) * keep_row).astype(BF)

    def lanes_first(x):
        split = x.reshape(rows_tok, outer, wide, cores * own)
        return net.relative(jnp.swapaxes(split, 1, 2), 1).reshape(rows_tok, width)

    def lanes_back(x):
        split = net.relative(x.reshape(rows_tok, wide, outer, cores * own), 1)
        return jnp.swapaxes(split, 1, 2).reshape(rows_tok, width)

    entry = net.columns_in([w_qkv, w_gate, w_up], plan, total)
    mixer = net.rows_in(w_out, w_down)
    lengths = net.group_lengths(seq_lengths)
    normed_all = net.gather_tokens(lanes_first(normed))
    masked_all = net.gather_tokens(masked)
    position, _, allowed = jax.vmap(lambda row: block_terms(row, rows_tok))(lengths)
    cos_t, sin_t = turn_tables(position)
    mask = jnp.where(allowed, 0.0, NEG)
    bias = lax.dynamic_index_in_dim(
        jnp.transpose(b_qkv.reshape(3, outer, wide, cores, own), (1, 3, 0, 2, 4)).reshape(tp, -1),
        net.member,
        0,
    )
    bias = jnp.broadcast_to(bias, (8, 3 * cols))

    proj = jnp.dot(normed_all, entry, preferred_element_type=F32)
    joined, qkv = forward_call(proj, bias, cos_t, sin_t, mask, cols, main, rest, rows_tok)
    branch = net.scatter_tokens(joined, mixer, (((1,), (0,)), ((), ())))
    output = (widened + keep_row * branch).astype(BF)

    back = lax.dot_general(masked_all, mixer, CONTRACT_COLS, preferred_element_type=F32)
    grad_entry, bias_part = backward_call(
        proj, back, qkv, cos_t, sin_t, mask, cols, main, rest, rows_tok
    )
    grad_w_qkv, grad_w_gate, grad_w_up = net.columns_out(
        normed_all, grad_entry, plan, (w_qkv.shape[1], w_gate.shape[1], w_up.shape[1])
    )
    mixer_part = lax.dot_general(
        joined, masked_all, CONTRACT_ROWS, preferred_element_type=F32
    ).astype(BF)
    grad_w_out, grad_w_down = net.rows_out(mixer_part, own, own_ff)

    grad_norm = lanes_back(net.scatter_tokens(grad_entry, entry, CONTRACT_COLS))
    lifted_grad = grad_norm * ln_gain
    grad_in = inv_std * (
        lifted_grad
        - jnp.mean(lifted_grad, axis=1, keepdims=True)
        - scaled * jnp.mean(lifted_grad * scaled, axis=1, keepdims=True)
    )
    grad_tokens = (grad_out.astype(F32) + grad_in).astype(BF)

    shards = outer * inner
    gain_part = jnp.sum(grad_norm * scaled, axis=0)
    shift_part = jnp.sum(grad_norm, axis=0)
    bias_full = lax.dynamic_update_index_in_dim(
        jnp.zeros((tp, 3 * cols), F32), bias_part[0], net.member, 0
    )
    bias_full = jnp.transpose(bias_full.reshape(outer, cores, 3, wide, own), (2, 0, 3, 1, 4))
    stats = jnp.concatenate(
        [
            gain_part.reshape(shards, own),
            shift_part.reshape(shards, own),
            bias_full.reshape(shards, 3 * own),
        ],
        axis=1,
    )
    stats = net.scatter_stats(stats)
    return (
        output,
        grad_tokens,
        grad_w_qkv,
        grad_w_out,
        grad_w_gate,
        grad_w_up,
        grad_w_down,
        stats[:own],
        stats[own : 2 * own],
        stats[2 * own :],
    )


def solution(mesh):
    rows = P(AXES, None)
    return jax.shard_map(
        on_device,
        mesh=mesh,
        in_specs=(rows, P(), P(), rows, P(), rows, rows, rows, rows, rows, rows),
        out_specs=(rows,) * 7 + (P(AXES),) * 3,
        check_vma=False,
    )
```

```python
import functools
import math

import jax
import jax.numpy as jnp
from jax import lax
from jax.experimental import pallas as pl
from jax.experimental.pallas import tpu as pltpu
from jax.sharding import PartitionSpec as P

HD = 64
ROT = 16
EPS = 1e-05
NEG = -1e30
TILE = 128
AXES = ("dp", "fsdp")
BF = jnp.bfloat16
F32 = jnp.float32
CONTRACT_ROWS = (((0,), (0,)), ((), ()))
CONTRACT_COLS = (((1,), (1,)), ((), ()))


def block_terms(lengths_row, rows_tok):
    ends = jnp.cumsum(lengths_row)
    place = jnp.arange(rows_tok, dtype=jnp.int32)
    segment = jnp.sum((place[:, None] >= ends[None, :]).astype(jnp.int32), axis=1)
    starts = jnp.concatenate([ends - lengths_row, ends[-1:]])
    labels = jnp.arange(starts.shape[0], dtype=jnp.int32)
    begin = jnp.sum(jnp.where(segment[:, None] == labels[None, :], starts[None, :], 0), axis=1)
    position = (place - begin).astype(F32)
    valid = segment < lengths_row.shape[0]
    label_tok = jnp.where(valid, segment, lengths_row.shape[0] + place)
    allowed = (label_tok[:, None] == label_tok[None, :]) & (place[None, :] <= place[:, None])
    return (position, valid, allowed)


def turn_tables(position):
    half = ROT // 2
    freq = jnp.exp(jnp.arange(half, dtype=F32) * (-2.0 * math.log(10000.0) / ROT))
    turn = position.reshape(-1)[:, None] * freq[None, :]
    cosine, sine = jnp.cos(turn), jnp.sin(turn)
    rest = (turn.shape[0], HD - ROT)
    cos_t = jnp.concatenate([cosine, cosine, jnp.ones(rest, F32)], axis=1)
    sin_t = jnp.concatenate([-sine, sine, jnp.zeros(rest, F32)], axis=1)
    return (jnp.tile(cos_t, (1, 2)), jnp.tile(sin_t, (1, 2)))


def tie(*values):
    return lax.optimization_barrier(values)


def turned(v, cos_t, sin_t, low_half):
    partner = jnp.where(low_half, pltpu.roll(v, TILE - ROT // 2, 1), pltpu.roll(v, ROT // 2, 1))
    return v * cos_t + partner * sin_t

def stacked(v, first):
    zero = jnp.zeros_like(v)
    return jnp.concatenate([jnp.where(first, v, zero), jnp.where(first, zero, v)], axis=0)

def softmax_of(query2, keys, bias2):
    scores = lax.dot_general(query2, keys, (((1,), (1,)), ((), ())), preferred_element_type=F32)
    scores = scores * 0.125 + bias2
    lifted = jnp.exp(scores - jnp.max(scores, axis=1, keepdims=True))
    return lifted / jnp.sum(lifted, axis=1, keepdims=True)

def attend_rows(cols, main, rest, at, pq_ref, pf_ref, bias_ref, tables, joined_ref, qkv_ref):
    cos_t, sin_t, bias2, first, low_half = tables
    size = cos_t.shape[0]
    rows = slice(at, at + size)
    for pair in range(cols // TILE):
        places = [g * cols + pair * TILE for g in range(3)]
        query, keys, values = (
            pq_ref[rows, p : p + TILE] + bias_ref[0:1, p : p + TILE] for p in places
        )
        query = turned(query, cos_t, sin_t, low_half).astype(BF)
        keys = turned(keys, cos_t, sin_t, low_half).astype(BF)
        values = values.astype(BF)
        for p, v in zip(places, (query, keys, values)):
            qkv_ref[rows, p : p + TILE] = v
        probs = softmax_of(stacked(query, first), keys, bias2).astype(BF)
        mixed = jnp.dot(probs, values, preferred_element_type=F32)
        joined_ref[rows, pair * TILE : (pair + 1) * TILE] = jnp.where(
            first, mixed[:size], mixed[size:]
        ).astype(BF)
    for j in range(main // TILE):
        gate = pf_ref[rows, j * TILE : (j + 1) * TILE]
        up = pf_ref[rows, main + j * TILE : main + (j + 1) * TILE]
        hid = gate * jax.nn.sigmoid(gate) * up
        joined_ref[rows, cols + j * TILE : cols + (j + 1) * TILE] = hid.astype(BF)
    if rest:
        tail = pf_ref[rows, 2 * main :]
        up = pltpu.roll(tail, rest, 1)
        hid = tail * jax.nn.sigmoid(tail) * up
        joined_ref[rows, cols + main :] = hid[:, :rest].astype(BF)


def attend_back_rows(cols, main, rest, at, pf_ref, back_ref, qkv_ref, tables, gq_ref, gf_ref, sum_ref):
    cos_t, sin_t, bias2, first, low_half = tables
    size = cos_t.shape[0]
    rows = slice(at, at + size)
    across = (((0,), (0,)), ((), ()))
    for pair in range(cols // TILE):
        places = [g * cols + pair * TILE for g in range(3)]
        query, keys, values = (qkv_ref[rows, p : p + TILE] for p in places)
        query2 = stacked(query, first)
        mixed2 = stacked(back_ref[rows, pair * TILE : (pair + 1) * TILE].astype(BF), first)
        probs = softmax_of(query2, keys, bias2)
        grad_probs = lax.dot_general(
            mixed2, values, (((1,), (1,)), ((), ())), preferred_element_type=F32
        )
        inner = jnp.sum(probs * grad_probs, axis=1, keepdims=True)
        grad_scores = (probs * (grad_probs - inner)).astype(BF)
        gq = jnp.dot(grad_scores, keys, preferred_element_type=F32)
        gq = jnp.where(first, gq[:size], gq[size:]) * 0.125
        gk = lax.dot_general(grad_scores, query2, across, preferred_element_type=F32) * 0.125
        gv = lax.dot_general(probs.astype(BF), mixed2, across, preferred_element_type=F32)
        gq = turned(gq, cos_t, -sin_t, low_half)
        gk = turned(gk, cos_t, -sin_t, low_half)
        for p, v in zip(places, (gq, gk, gv)):
            low = v.astype(BF)
            gq_ref[rows, p : p + TILE] = low
            sum_ref[0:1, p : p + TILE] += jnp.sum(low.astype(F32), axis=0, keepdims=True)

    def gates(gate, up, grad_hid):
        sigma = jax.nn.sigmoid(gate)
        slope = sigma * (1.0 + gate * (1.0 - sigma))
        return (grad_hid * up * slope, grad_hid * (gate * sigma))

    for j in range(main // TILE):
        p, q = j * TILE, main + j * TILE
        grad_hid = back_ref[rows, cols + j * TILE : cols + (j + 1) * TILE]
        gg, gu = gates(pf_ref[rows, p : p + TILE], pf_ref[rows, q : q + TILE], grad_hid)
        gf_ref[rows, p : p + TILE] = gg.astype(BF)
        gf_ref[rows, q : q + TILE] = gu.astype(BF)
    if rest:
        tail = pf_ref[rows, 2 * main :]
        short = back_ref[rows, cols + main :]
        grad_hid = jnp.concatenate([short, jnp.zeros_like(short)], axis=1)
        gg, gu = gates(tail, pltpu.roll(tail, rest, 1), grad_hid)
        lane = lax.broadcasted_iota(jnp.int32, (size, TILE), 1)
        both = jnp.where(lane < rest, gg, pltpu.roll(gu, rest, 1))
        gf_ref[rows, 2 * main :] = both.astype(BF)


def block_tables(cos_ref, sin_ref, mask_ref, block, size):
    lane = lax.broadcasted_iota(jnp.int32, (size, TILE), 1)
    rows = slice(block * size, (block + 1) * size)
    mask = mask_ref[block]
    return (
        cos_ref[rows, :],
        sin_ref[rows, :],
        jnp.concatenate([mask, mask], axis=0),
        lane < HD,
        lane % HD < ROT // 2,
    )


def stack_copies(pieces, whole, sem, start):
    copies, at = [], 0
    for i, piece in enumerate(pieces):
        size = piece.shape[0]
        dst = whole.at[pl.ds(at, size), :]
        copies.append(pltpu.make_async_copy(piece, dst, sem.at[start + i]))
        at += size
    return copies


def forward_kernel(sizes, count, block, *refs):
    cols, main, rest = sizes
    normed_ref, bias_ref, cos_ref, sin_ref, mask_ref = refs[:5]
    pieces, mixer_any = refs[5 : 5 + count], refs[5 + count]
    joined_ref, qkv_ref, pf_ref, branch_ref = refs[6 + count : 10 + count]
    entry, wm, pq, sem = refs[10 + count :]
    groups = [
        stack_copies(pieces, entry, sem, 0),
        [pltpu.make_async_copy(mixer_any, wm, sem.at[count])],
    ]
    opening = pl.program_id(0) == 0

    @pl.when(opening)
    def _():
        for group in groups:
            for copy in group:
                copy.start()

    def arrive(group):
        @pl.when(opening)
        def _():
            for copy in groups[group]:
                copy.wait()

    normed = normed_ref[...]
    arrive(0)
    pq[...] = jnp.dot(normed, entry[:, : 3 * cols], preferred_element_type=F32)
    pf_ref[...] = jnp.dot(normed, entry[:, 3 * cols :], preferred_element_type=F32)
    for i in range(normed.shape[0] // block):
        tables = block_tables(cos_ref, sin_ref, mask_ref, i, block)
        attend_rows(
            cols, main, rest, i * block, pq, pf_ref, bias_ref, tables, joined_ref, qkv_ref
        )
    arrive(1)
    branch = jnp.dot(joined_ref[...], wm[...], preferred_element_type=F32)
    branch_ref[...] = branch.astype(BF)


def backward_kernel(sizes, block, *refs):
    cols, main, rest = sizes
    masked_ref, pf_ref, qkv_ref, cos_ref, sin_ref, mask_ref, mixer_any = refs[:7]
    gq_ref, gf_ref, sum_ref = refs[7:10]
    wm, back, sem = refs[10:]

    @pl.when(pl.program_id(0) == 0)
    def _():
        sum_ref[...] = jnp.zeros_like(sum_ref)
        copy = pltpu.make_async_copy(mixer_any, wm, sem.at[0])
        copy.start()
        copy.wait()

    back[...] = lax.dot_general(
        masked_ref[...], wm[...], CONTRACT_COLS, preferred_element_type=F32
    )
    for i in range(masked_ref.shape[0] // block):
        tables = block_tables(cos_ref, sin_ref, mask_ref, i, block)
        attend_back_rows(
            cols, main, rest, i * block, pf_ref, back, qkv_ref, tables, gq_ref, gf_ref, sum_ref
        )


def norm_kernel(count, *refs):
    gq_ref, gf_ref, pieces = refs[0], refs[1], refs[2 : 2 + count]
    out_ref, entry, sem = refs[2 + count :]
    copies = stack_copies(pieces, entry, sem, 0)

    @pl.when(pl.program_id(0) == 0)
    def _():
        for copy in copies:
            copy.start()
        for copy in copies:
            copy.wait()

    cut = gq_ref.shape[1]
    total = lax.dot_general(
        gq_ref[...], entry[:, :cut], CONTRACT_COLS, preferred_element_type=F32
    )
    total += lax.dot_general(
        gf_ref[...], entry[:, cut:], CONTRACT_COLS, preferred_element_type=F32
    )
    out_ref[...] = total.astype(BF)


STEP = 256
HIDDEN_COST = pl.CostEstimate(flops=1, bytes_accessed=1, transcendentals=0)


def row_spec(width, rows=STEP):
    return pl.BlockSpec((rows, width), lambda i: (i, 0))


ANYWHERE = pl.BlockSpec(memory_space=pl.ANY)
HELD = pl.BlockSpec(memory_space=pltpu.VMEM)


def stepping(limit):
    return pltpu.CompilerParams(
        dimension_semantics=("arbitrary",), vmem_limit_bytes=limit << 20
    )


def forward_call(normed, bias, cos_t, sin_t, mask, pieces, mixer, sizes):
    cols, main, rest = sizes
    everyone, width = normed.shape
    block = mask.shape[1]
    count = len(pieces)
    joint = cols + main + rest
    return pl.pallas_call(
        functools.partial(forward_kernel, sizes, count, block),
        grid=(everyone // STEP,),
        in_specs=[
            row_spec(width),
            pl.BlockSpec((8, 3 * cols), lambda i: (0, 0)),
            row_spec(TILE),
            row_spec(TILE),
            pl.BlockSpec((STEP // block, block, block), lambda i: (i, 0, 0)),
        ]
        + [ANYWHERE] * (count + 1),
        out_specs=[
            row_spec(joint),
            row_spec(3 * cols),
            row_spec(2 * (main + rest)),
            row_spec(width),
        ],
        out_shape=[
            jax.ShapeDtypeStruct((everyone, joint), BF),
            jax.ShapeDtypeStruct((everyone, 3 * cols), BF),
            jax.ShapeDtypeStruct((everyone, 2 * (main + rest)), F32),
            jax.ShapeDtypeStruct((everyone, width), BF),
        ],
        scratch_shapes=[
            pltpu.VMEM((width, 3 * cols + 2 * (main + rest)), BF),
            pltpu.VMEM((joint, width), BF),
            pltpu.VMEM((STEP, 3 * cols), F32),
            pltpu.SemaphoreType.DMA((count + 1,)),
        ],
        compiler_params=stepping(48),
        cost_estimate=HIDDEN_COST,
        name="forward",
    )(normed, bias, cos_t, sin_t, mask, *pieces, mixer)


def backward_call(masked, pf, qkv, cos_t, sin_t, mask, mixer, sizes):
    cols, main, rest = sizes
    everyone, width = masked.shape
    block = mask.shape[1]
    joint = cols + main + rest
    return pl.pallas_call(
        functools.partial(backward_kernel, sizes, block),
        grid=(everyone // STEP,),
        in_specs=[
            row_spec(width),
            row_spec(2 * (main + rest)),
            row_spec(3 * cols),
            row_spec(TILE),
            row_spec(TILE),
            pl.BlockSpec((STEP // block, block, block), lambda i: (i, 0, 0)),
            ANYWHERE,
        ],
        out_specs=[
            row_spec(3 * cols),
            row_spec(2 * (main + rest)),
            pl.BlockSpec((8, 3 * cols), lambda i: (0, 0)),
        ],
        out_shape=[
            jax.ShapeDtypeStruct((everyone, 3 * cols), BF),
            jax.ShapeDtypeStruct((everyone, 2 * (main + rest)), BF),
            jax.ShapeDtypeStruct((8, 3 * cols), F32),
        ],
        scratch_shapes=[
            pltpu.VMEM((joint, width), BF),
            pltpu.VMEM((STEP, joint), F32),
            pltpu.SemaphoreType.DMA((1,)),
        ],
        compiler_params=stepping(40),
        cost_estimate=HIDDEN_COST,
        name="backward",
    )(masked, pf, qkv, cos_t, sin_t, mask, mixer)


def norm_call(grad_qkv, grad_ff, pieces):
    everyone = grad_qkv.shape[0]
    count = len(pieces)
    width = sum(piece.shape[0] for piece in pieces)
    wide_q, wide_f = grad_qkv.shape[1], grad_ff.shape[1]
    return pl.pallas_call(
        functools.partial(norm_kernel, count),
        grid=(everyone // STEP,),
        in_specs=[row_spec(wide_q), row_spec(wide_f)] + [ANYWHERE] * count,
        out_specs=row_spec(width),
        out_shape=jax.ShapeDtypeStruct((everyone, width), BF),
        scratch_shapes=[
            pltpu.VMEM((width, wide_q + wide_f), BF),
            pltpu.SemaphoreType.DMA((count,)),
        ],
        compiler_params=stepping(40),
        cost_estimate=HIDDEN_COST,
        name="norm_grad",
    )(grad_qkv, grad_ff, *pieces)


def product_kernel(count, *refs):
    grad = refs[count][...]
    outs, held, sem = refs[count + 1 : 2 * count + 1], refs[2 * count + 1], refs[2 * count + 2]
    copies = []
    for i, (lhs, out) in enumerate(zip(refs[:count], outs)):
        held[i] = lax.dot_general(
            lhs[...], grad, CONTRACT_ROWS, preferred_element_type=F32
        ).astype(BF)
        copies.append(pltpu.make_async_copy(held.at[i], out, sem.at[i]))
        copies[-1].start()
    for copy in copies:
        copy.wait()


def product_call(normed, grad, slabs, size):
    everyone, width = normed.shape[0], grad.shape[1]
    count = len(slabs)
    spec = lambda slab: pl.BlockSpec((everyone, size), lambda i: (0, slab))
    return pl.pallas_call(
        functools.partial(product_kernel, count),
        grid=(1,),
        in_specs=[spec(slab) for slab in slabs]
        + [pl.BlockSpec((everyone, width), lambda i: (0, 0))],
        out_specs=[pl.BlockSpec(memory_space=pltpu.HBM)] * count,
        out_shape=[pltpu.HBM((size, width), BF)] * count,
        scratch_shapes=[
            pltpu.VMEM((count, size, width), BF),
            pltpu.SemaphoreType.DMA((count,)),
        ],
        compiler_params=stepping(40),
        cost_estimate=HIDDEN_COST,
        name="weight_grad",
    )(*[normed] * count, grad)


def mixer_grad_call(lane, joined, masked, wide, own, own_ff, cut):
    everyone, joint = joined.shape
    width = masked.shape[1]

    def kernel(lane_ref, joined_ref, masked_ref, *refs):
        outs, whole, sem = refs[:-2], refs[-2], refs[-1]
        masked = masked_ref[...]
        for at in range(0, joint, STEP):
            size = min(STEP, joint - at)
            whole[at : at + size, :] = lax.dot_general(
                joined_ref[:, at : at + size], masked, CONTRACT_ROWS, preferred_element_type=F32
            ).astype(BF)
        pairs = row_spans(wide, own, own_ff, cut, lane_ref[0], outs, whole)
        run_copies([(there, here) for here, there in pairs], sem)

    shapes = [(cut, width), (own + own_ff - cut, width)] * wide
    outs = pl.pallas_call(
        kernel,
        in_specs=[pl.BlockSpec(memory_space=pltpu.SMEM), HELD, HELD],
        out_specs=[pl.BlockSpec(memory_space=pltpu.HBM)] * len(shapes),
        out_shape=[pltpu.HBM(shape, BF) for shape in shapes],
        scratch_shapes=[
            pltpu.VMEM((joint, width), BF),
            pltpu.SemaphoreType.DMA((3 * wide,)),
        ],
        compiler_params=pltpu.CompilerParams(vmem_limit_bytes=40 << 20),
        cost_estimate=HIDDEN_COST,
        name="mixer_grad",
    )(lane, joined, masked)
    return outs


def column_plan(member, outer, wide, cores, own, own_ff, cols, main, rest):
    z, c = member // cores, member % cores
    out = []
    for g in range(3):
        for k in range(wide):
            src = (((g * outer + z) * wide + k) * cores + c) * own
            out.append((0, src, 0, g * cols + k * own, own))
    for which in range(2):
        for k in range(wide):
            src = ((z * wide + k) * cores + c) * own_ff
            lo, hi = k * own_ff, (k + 1) * own_ff
            cut = min(hi, main)
            if cut > lo:
                out.append((1 + which, src, 1, which * main + lo, cut - lo))
            low = max(lo, main)
            if hi > low:
                at = 2 * main + which * rest + low - main
                out.append((1 + which, src + low - lo, 1, at, hi - low))
    return out


def pack_kernel(plan, tp, bases, *refs):
    arrays, packed = refs[:3], refs[3]
    rows = arrays[0].shape[0]
    for member in range(tp):
        at = member * rows
        for which, src, part, dst, width in plan(member):
            dst += bases[part]
            packed[at : at + rows, dst : dst + width] = arrays[which][:, src : src + width]


def pack_call(arrays, plan, tp, widths):
    rows = arrays[0].shape[0]
    return pl.pallas_call(
        functools.partial(pack_kernel, plan, tp, (0, widths[0])),
        in_specs=[HELD] * 3,
        out_specs=HELD,
        out_shape=jax.ShapeDtypeStruct((tp * rows, sum(widths)), BF),
        compiler_params=pltpu.CompilerParams(vmem_limit_bytes=32 << 20),
        name="pack_columns",
    )(*arrays)


def unpack_kernel(plan, tp, count, *refs):
    parts, outs = refs[:count], refs[count:]
    rows = outs[0].shape[0]
    for member in range(tp):
        at = member * rows
        for which, src, part, dst, width in plan(member):
            piece = parts[part][at : at + rows, dst : dst + width]
            outs[which][:, src : src + width] = piece.astype(F32)


def unpack_call(parts, plan, tp, widths):
    rows = parts[0].shape[0] // tp
    held = pl.BlockSpec(memory_space=pltpu.VMEM)
    return pl.pallas_call(
        functools.partial(unpack_kernel, plan, tp, len(parts)),
        in_specs=[held] * len(parts),
        out_specs=[held] * 3,
        out_shape=[jax.ShapeDtypeStruct((rows, width), F32) for width in widths],
        compiler_params=pltpu.CompilerParams(vmem_limit_bytes=32 << 20),
        name="unpack_columns",
    )(*parts)


def join_kernel(count, *refs):
    ins, out, sem = refs[:count], refs[count], refs[count + 1]
    copies, at = [], 0
    for i, ref in enumerate(ins):
        size = ref.shape[0]
        copies.append(pltpu.make_async_copy(ref, out.at[pl.ds(at, size), :], sem.at[i]))
        at += size
    for copy in copies:
        copy.start()
    for copy in copies:
        copy.wait()


def join_call(arrays):
    count = len(arrays)
    rows, width = sum(array.shape[0] for array in arrays), arrays[0].shape[1]
    return pl.pallas_call(
        functools.partial(join_kernel, count),
        in_specs=[pl.BlockSpec(memory_space=pl.ANY)] * count,
        out_specs=pl.BlockSpec(memory_space=pltpu.VMEM),
        out_shape=jax.ShapeDtypeStruct((rows, width), BF),
        scratch_shapes=[pltpu.SemaphoreType.DMA((count,))],
        compiler_params=pltpu.CompilerParams(vmem_limit_bytes=16 << 20),
        name="join_rows",
    )(*arrays)


def row_spans(wide, own, own_ff, cut, lane, halves, whole):
    spans = []
    base = wide * own
    for j in range(wide):
        spot = lax.bitwise_xor(lane, j)
        down = pl.multiple_of(base + spot * own_ff, 16)
        down_low = pl.multiple_of(base + spot * own_ff + cut, 16)
        out = pl.multiple_of(spot * own, 16)
        low, high = halves[2 * j : 2 * j + 2]
        rest = own_ff - cut
        spans.append((low, whole.at[pl.ds(down, cut), :]))
        spans.append((high.at[pl.ds(0, rest), :], whole.at[pl.ds(down_low, rest), :]))
        spans.append((high.at[pl.ds(rest, own), :], whole.at[pl.ds(out, own), :]))
    return spans


def run_copies(pairs, sem):
    copies = [pltpu.make_async_copy(src, dst, sem.at[i]) for i, (src, dst) in enumerate(pairs)]
    for copy in copies:
        copy.start()
    for copy in copies:
        copy.wait()


def place_call(lane, halves, wide, own, own_ff, cut):
    width = halves[0].shape[1]

    def kernel(lane_ref, *refs):
        ins, out, sem = refs[:-2], refs[-2], refs[-1]
        run_copies(row_spans(wide, own, own_ff, cut, lane_ref[0], ins, out), sem)

    return pl.pallas_call(
        kernel,
        in_specs=[pl.BlockSpec(memory_space=pltpu.SMEM)]
        + [pl.BlockSpec(memory_space=pl.ANY)] * len(halves),
        out_specs=pl.BlockSpec(memory_space=pltpu.VMEM),
        out_shape=jax.ShapeDtypeStruct((wide * (own + own_ff), width), BF),
        scratch_shapes=[pltpu.SemaphoreType.DMA((3 * wide,))],
        compiler_params=pltpu.CompilerParams(vmem_limit_bytes=16 << 20),
        name="place_rows",
    )(lane, *halves)


def mixer_product(joined, masked):
    return lax.dot_general(joined, masked, CONTRACT_ROWS, preferred_element_type=F32).astype(BF)


class Plain:
    def __init__(self, outer, inner):
        self.tp, self.wide, self.cores, self.outer = outer, inner, 1, outer
        self.member = lax.axis_index("dp")
        self.token_axes, self.token_groups = "dp", None
        self.weight_axes, self.weight_groups = "fsdp", None

    def gather_tokens(self, block):
        return lax.all_gather(
            block, self.token_axes, axis=0, tiled=True, axis_index_groups=self.token_groups
        )

    def scatter_tokens(self, part):
        return lax.psum_scatter(
            part.astype(BF),
            self.token_axes,
            scatter_dimension=0,
            tiled=True,
            axis_index_groups=self.token_groups,
        ).astype(F32)

    def exchange(self, part):
        return lax.all_to_all(
            part,
            self.token_axes,
            split_axis=0,
            concat_axis=0,
            tiled=True,
            axis_index_groups=self.token_groups,
        )

    def gather_weights(self, block):
        return lax.all_gather(
            block, self.weight_axes, axis=0, tiled=True, axis_index_groups=self.weight_groups
        )

    def scatter_weights(self, part):
        return lax.psum_scatter(
            part,
            self.weight_axes,
            scatter_dimension=0,
            tiled=True,
            axis_index_groups=self.weight_groups,
        )

    def gather_lengths(self, lengths):
        return lax.all_gather(lengths, "dp", axis=0, tiled=True)

    def order_lengths(self, lengths):
        return lengths

    def inputs(self, packed, w_out, w_down, normed, masked):
        mixer = jnp.concatenate([self.gather_weights(w) for w in (w_out, w_down)], axis=0)
        entry = self.gather_weights(self.exchange(packed))
        return [entry], mixer, self.gather_tokens(normed), self.gather_tokens(masked)

    def outputs(self, joined, masked, branch, back_call, normed, entry, own, own_ff):
        cols = self.wide * own
        part = mixer_product(joined, masked)
        grads = [self.scatter_weights(p).astype(F32) for p in (part[:cols], part[cols:])]
        grad_qkv, grad_ff, bias_part = back_call(masked)
        parts = []
        for grad in (grad_qkv, grad_ff):
            part = lax.dot_general(normed, grad, CONTRACT_ROWS, preferred_element_type=F32)
            parts.append(self.scatter_weights(part.astype(BF)))
        norm_part = norm_call(grad_qkv, grad_ff, entry)
        return grads[0], grads[1], parts[0], self.exchange(parts[1]), norm_part, bias_part, branch

    def relative(self, blocks, axis):
        return blocks

    def scatter_stats(self, stats):
        parts = lax.all_to_all(stats, AXES, split_axis=0, concat_axis=0, tiled=True)
        return jnp.sum(parts, axis=0)


class Linked(Plain):
    def __init__(self, outer, inner):
        self.outer, self.cores, self.wide = outer, 2, inner // 2
        self.tp = outer * 2
        flat = lax.axis_index("fsdp")
        self.lane = flat // 2
        self.member = lax.axis_index("dp") * 2 + lax.rem(flat, 2)
        spots = [
            [[(z * self.wide + k) * 2 + c for c in range(2)] for k in range(self.wide)]
            for z in range(outer)
        ]
        self.token_axes = self.weight_axes = AXES
        self.token_groups = [
            [spots[z][k][c] for z in range(outer) for c in range(2)] for k in range(self.wide)
        ]
        self.weight_groups = [
            [spots[z][k][c] for k in range(self.wide)] for z in range(outer) for c in range(2)
        ]
        self.spots = spots
        self.lane_index = self.lane.astype(jnp.int32).reshape(1)

    def send(self, value, step=0, dz=0, dc=0):
        pairs = [
            (self.spots[z][k][c], self.spots[z ^ dz][k ^ step][c ^ dc])
            for z in range(self.outer)
            for k in range(self.wide)
            for c in range(2)
        ]
        return lax.ppermute(value, AXES, pairs)

    def gather_lengths(self, lengths):
        parts = [lengths] + [self.send(lengths, dz=dz) for dz in range(1, self.outer)]
        return jnp.concatenate(parts, axis=0)

    def order_lengths(self, mine):
        both = jnp.stack([mine, self.send(mine, dc=1)], axis=1).reshape(self.tp, -1)
        spot = lax.bitwise_xor(jnp.arange(self.tp, dtype=jnp.int32), self.member)
        pick = spot[:, None] == jnp.arange(self.tp, dtype=jnp.int32)[None, :]
        return jnp.sum(jnp.where(pick[:, :, None], both[None], 0), axis=1)

    def inputs(self, packed, w_out, w_down, normed, masked):
        own, own_ff = w_out.shape[0], w_down.shape[0]
        cut = own_ff // 32 * 16 + 32
        half = packed.shape[0] // 2
        rows, packed = tie(join_call([w_down, w_out]), packed)
        mix_x, mix_y = self.send(rows, 1), self.send(rows, 2)
        mix_low, mix_high = self.send(mix_x[:cut], 2), self.send(mix_y[cut:], 1)
        entry = self.exchange(packed)
        entry, normed, mix_low, mix_high = tie(entry, normed, mix_low, mix_high)
        normed_all = self.gather_tokens(normed)
        from_x, from_y = self.send(entry, 1), self.send(entry, 2)
        from_x, from_y, masked = tie(from_x, from_y, masked)
        masked_all = self.gather_tokens(masked)
        halves = [part for b in (rows, mix_x, mix_y) for part in (b[:cut], b[cut:])]
        halves += [mix_low, mix_high]
        mixer = place_call(self.lane_index, halves, self.wide, own, own_ff, cut)
        low, high = self.send(from_x[:half], 2), self.send(from_y[half:], 1)
        return [entry, from_x, from_y, low, high], mixer, normed_all, masked_all

    def first_sends(self, blocks):
        return [
            self.send(blocks[3][0], 1),
            self.send(blocks[3][1], 2),
            self.send(blocks[1][0], 1),
            self.send(blocks[2][1], 2),
        ]

    def last_sends(self, blocks, got):
        low, high, x_low, y_high = got
        x_high = self.send((blocks[1][1].astype(F32) + high.astype(F32)).astype(BF), 1)
        y_low = self.send((blocks[2][0].astype(F32) + low.astype(F32)).astype(BF), 2)
        return [
            blocks[0][0].astype(F32) + x_low.astype(F32) + y_low.astype(F32),
            blocks[0][1].astype(F32) + x_high.astype(F32) + y_high.astype(F32),
        ]

    def outputs(self, joined, masked, branch, back_call, normed, entry, own, own_ff):
        cut = own_ff // 32 * 16 + 32
        rest = own_ff - cut
        size = normed.shape[1] // self.wide // 2
        first, last = (6, 7, 2, 5), (3, 4, 0, 1)

        def halves(early, late):
            low, high, x_low, y_high = early
            x_high, y_low, own_low, own_high = late
            return [(own_low, own_high), (x_low, x_high), (y_low, y_high), (low, high)]

        mix = mixer_grad_call(self.lane_index, joined, masked, self.wide, own, own_ff, cut)
        *mix, masked = tie(*mix, masked)
        mix = [mix[2 * j : 2 * j + 2] for j in range(self.wide)]
        mix_got = self.first_sends(mix)
        grad_qkv, grad_ff, bias_part = back_call(masked)
        *mix_got, grad_ff, grad_qkv = tie(*mix_got, grad_ff, grad_qkv)
        low, high = self.last_sends(mix, mix_got)
        norm_part = norm_call(grad_qkv, grad_ff, entry)
        norm_part, grad_qkv, grad_ff, low, high = tie(norm_part, grad_qkv, grad_ff, low, high)
        grad_w_out = high[rest:]
        grad_w_down = jnp.concatenate([low, high[:rest]], axis=0)
        early = product_call(normed, grad_ff, first, size)
        *early, grad_ff = tie(*early, grad_ff)
        late = product_call(normed, grad_ff, last, size)
        ff_got = self.first_sends(halves(early, late))
        *late, grad_qkv = tie(*late, grad_qkv)
        ff = halves(early, late)
        early = product_call(normed, grad_qkv, first, size)
        *early, grad_qkv = tie(*early, grad_qkv)
        late = product_call(normed, grad_qkv, last, size)
        together = tie(branch, *early, *late, *ff_got)
        branch = together[0]
        early, late, ff_got = [together[1 + 4 * i :][:4] for i in range(3)]
        part_ff = jnp.concatenate(self.last_sends(ff, ff_got), axis=0).astype(BF)
        part_ff, *qkv = tie(part_ff, *early, *late)
        qkv = halves(qkv[:4], qkv[4:])
        qkv_got = self.first_sends(qkv)
        part_ff = self.exchange(part_ff)
        part_qkv = jnp.concatenate(self.last_sends(qkv, qkv_got), axis=0).astype(BF)
        part_ff, part_qkv = tie(part_ff, part_qkv)
        return grad_w_out, grad_w_down, part_qkv, part_ff, norm_part, bias_part, branch

    def relative(self, blocks, axis):
        shape = blocks.shape
        split = blocks.reshape(shape[:axis] + (2, 2) + shape[axis + 1 :])
        split = jnp.where(self.lane >= 2, jnp.flip(split, axis), split)
        split = jnp.where(lax.rem(self.lane, 2) == 1, jnp.flip(split, axis + 1), split)
        return split.reshape(shape)


def on_device(
    tokens, ln_gain, ln_shift, w_qkv, b_qkv, w_out, w_gate, w_up, w_down, grad_out, seq_lengths
):
    outer, inner = lax.axis_size("dp"), lax.axis_size("fsdp")
    linked = outer == 4 and inner == 8
    net = Linked(outer, inner) if linked else Plain(outer, inner)
    tp, wide, cores = net.tp, net.wide, net.cores
    rows_tok, width = tokens.shape
    own = w_qkv.shape[0]
    own_ff = w_down.shape[0]
    cols, cols_ff = wide * own, wide * own_ff
    main = cols_ff // TILE * TILE
    rest = cols_ff - main
    widths = (3 * cols, 2 * cols_ff)
    plan = lambda member: column_plan(
        member, outer, wide, cores, own, own_ff, cols, main, rest
    )

    _, valid, _ = block_terms(seq_lengths[0], rows_tok)
    keep_row = valid.astype(F32)[:, None]
    widened = tokens.astype(F32)
    centered = widened - jnp.mean(widened, axis=1, keepdims=True)
    inv_std = lax.rsqrt(jnp.mean(centered * centered, axis=1, keepdims=True) + EPS)
    scaled = centered * inv_std
    normed = (scaled * ln_gain + ln_shift).astype(BF)
    masked = (grad_out.astype(F32) * keep_row).astype(BF)

    def lanes_first(x):
        split = x.reshape(rows_tok, outer, wide, cores * own)
        return net.relative(jnp.swapaxes(split, 1, 2), 1).reshape(rows_tok, width)

    def lanes_back(x):
        split = net.relative(x.reshape(rows_tok, wide, outer, cores * own), 1)
        return jnp.swapaxes(split, 1, 2).reshape(rows_tok, width)

    lengths = net.gather_lengths(seq_lengths)
    arrays = [w_qkv, w_gate, w_up]
    packed, lengths = tie(pack_call(arrays, plan, tp, widths), lengths)
    entry, mixer, normed_all, masked_all = net.inputs(
        packed, w_out, w_down, lanes_first(normed), masked
    )
    lengths = net.order_lengths(lengths)
    position, _, allowed = jax.vmap(lambda row: block_terms(row, rows_tok))(lengths)
    cos_t, sin_t = turn_tables(position)
    mask = jnp.where(allowed, 0.0, NEG)
    bias = lax.dynamic_index_in_dim(
        jnp.transpose(b_qkv.reshape(3, outer, wide, cores, own), (1, 3, 0, 2, 4)).reshape(tp, -1),
        net.member,
        0,
    )
    bias = jnp.broadcast_to(bias, (8, 3 * cols))

    sizes = (cols, main, rest)
    joined, qkv, proj_ff, branch_part = forward_call(
        normed_all, bias, cos_t, sin_t, mask, entry, mixer, sizes
    )
    branch_part, masked_all = tie(branch_part, masked_all)
    branch = net.scatter_tokens(branch_part)
    back_call = lambda masked: backward_call(
        masked, proj_ff, qkv, cos_t, sin_t, mask, mixer, sizes
    )
    grad_w_out, grad_w_down, part_qkv, part_ff, norm_part, bias_part, branch = net.outputs(
        joined, masked_all, branch, back_call, normed_all, entry, own, own_ff
    )
    output = (widened + keep_row * branch).astype(BF)

    grad_norm, part_qkv = tie(net.scatter_tokens(norm_part), part_qkv)
    grad_norm = lanes_back(grad_norm)
    lifted_grad = grad_norm * ln_gain
    grad_in = inv_std * (
        lifted_grad
        - jnp.mean(lifted_grad, axis=1, keepdims=True)
        - scaled * jnp.mean(lifted_grad * scaled, axis=1, keepdims=True)
    )
    grad_tokens = (grad_out.astype(F32) + grad_in).astype(BF)

    shards = outer * inner
    gain_part = jnp.sum(grad_norm * scaled, axis=0)
    shift_part = jnp.sum(grad_norm, axis=0)
    bias_full = lax.dynamic_update_index_in_dim(
        jnp.zeros((tp, 3 * cols), F32), bias_part[0], net.member, 0
    )
    bias_full = jnp.transpose(bias_full.reshape(outer, cores, 3, wide, own), (2, 0, 3, 1, 4))
    stats = jnp.concatenate(
        [
            gain_part.reshape(shards, own),
            shift_part.reshape(shards, own),
            bias_full.reshape(shards, 3 * own),
        ],
        axis=1,
    )
    part_qkv, stats = tie(net.exchange(part_qkv), stats)
    grad_w_qkv, grad_w_gate, grad_w_up = unpack_call(
        [part_qkv, part_ff], plan, tp, [array.shape[1] for array in arrays]
    )
    stats = net.scatter_stats(stats)
    return (
        output,
        grad_tokens,
        grad_w_qkv,
        grad_w_out,
        grad_w_gate,
        grad_w_up,
        grad_w_down,
        stats[:own],
        stats[own : 2 * own],
        stats[2 * own :],
    )


def solution(mesh):
    rows = P(AXES, None)
    return jax.shard_map(
        on_device,
        mesh=mesh,
        in_specs=(rows, P(), P(), rows, P(), rows, rows, rows, rows, rows, rows),
        out_specs=(rows,) * 7 + (P(AXES),) * 3,
        check_vma=False,
    )
```

```python
import functools
import math

import jax
import jax.numpy as jnp
from jax import lax
from jax.experimental import pallas as pl
from jax.experimental.pallas import tpu as pltpu
from jax.sharding import PartitionSpec as P

HD = 64
ROT = 16
EPS = 1e-05
NEG = -1e30
TILE = 128
AXES = ("dp", "fsdp")
BF = jnp.bfloat16
F32 = jnp.float32
CONTRACT_ROWS = (((0,), (0,)), ((), ()))
CONTRACT_COLS = (((1,), (1,)), ((), ()))


def block_terms(lengths_row, rows_tok):
    ends = jnp.cumsum(lengths_row)
    place = jnp.arange(rows_tok, dtype=jnp.int32)
    segment = jnp.sum((place[:, None] >= ends[None, :]).astype(jnp.int32), axis=1)
    starts = jnp.concatenate([ends - lengths_row, ends[-1:]])
    labels = jnp.arange(starts.shape[0], dtype=jnp.int32)
    begin = jnp.sum(jnp.where(segment[:, None] == labels[None, :], starts[None, :], 0), axis=1)
    position = (place - begin).astype(F32)
    valid = segment < lengths_row.shape[0]
    label_tok = jnp.where(valid, segment, lengths_row.shape[0] + place)
    allowed = (label_tok[:, None] == label_tok[None, :]) & (place[None, :] <= place[:, None])
    return (position, valid, allowed)


def turn_tables(position):
    half = ROT // 2
    freq = jnp.exp(jnp.arange(half, dtype=F32) * (-2.0 * math.log(10000.0) / ROT))
    turn = position.reshape(-1)[:, None] * freq[None, :]
    cosine, sine = jnp.cos(turn), jnp.sin(turn)
    rest = (turn.shape[0], HD - ROT)
    cos_t = jnp.concatenate([cosine, cosine, jnp.ones(rest, F32)], axis=1)
    sin_t = jnp.concatenate([-sine, sine, jnp.zeros(rest, F32)], axis=1)
    return (jnp.tile(cos_t, (1, 2)), jnp.tile(sin_t, (1, 2)))


def tie(*values):
    return lax.optimization_barrier(values)


def turned(v, cos_t, sin_t, low_half):
    partner = jnp.where(low_half, pltpu.roll(v, TILE - ROT // 2, 1), pltpu.roll(v, ROT // 2, 1))
    return v * cos_t + partner * sin_t

def stacked(v, first):
    zero = jnp.zeros_like(v)
    return jnp.concatenate([jnp.where(first, v, zero), jnp.where(first, zero, v)], axis=0)

def softmax_of(query2, keys, bias2):
    scores = lax.dot_general(query2, keys, (((1,), (1,)), ((), ())), preferred_element_type=F32)
    scores = scores * 0.125 + bias2
    lifted = jnp.exp(scores - jnp.max(scores, axis=1, keepdims=True))
    return lifted / jnp.sum(lifted, axis=1, keepdims=True)

def attend_rows(cols, main, rest, at, pq_ref, pf_ref, bias_ref, tables, joined_ref, qkv_ref):
    cos_t, sin_t, bias2, first, low_half = tables
    size = cos_t.shape[0]
    rows = slice(at, at + size)
    for pair in range(cols // TILE):
        places = [g * cols + pair * TILE for g in range(3)]
        query, keys, values = (
            pq_ref[rows, p : p + TILE] + bias_ref[0:1, p : p + TILE] for p in places
        )
        query = turned(query, cos_t, sin_t, low_half).astype(BF)
        keys = turned(keys, cos_t, sin_t, low_half).astype(BF)
        values = values.astype(BF)
        for p, v in zip(places, (query, keys, values)):
            qkv_ref[rows, p : p + TILE] = v
        probs = softmax_of(stacked(query, first), keys, bias2).astype(BF)
        mixed = jnp.dot(probs, values, preferred_element_type=F32)
        joined_ref[rows, pair * TILE : (pair + 1) * TILE] = jnp.where(
            first, mixed[:size], mixed[size:]
        ).astype(BF)
    for j in range(main // TILE):
        gate = pf_ref[rows, j * TILE : (j + 1) * TILE]
        up = pf_ref[rows, main + j * TILE : main + (j + 1) * TILE]
        hid = gate * jax.nn.sigmoid(gate) * up
        joined_ref[rows, cols + j * TILE : cols + (j + 1) * TILE] = hid.astype(BF)
    if rest:
        tail = pf_ref[rows, 2 * main :]
        up = pltpu.roll(tail, rest, 1)
        hid = tail * jax.nn.sigmoid(tail) * up
        joined_ref[rows, cols + main :] = hid[:, :rest].astype(BF)


def attend_back_rows(cols, main, rest, at, pf_ref, back_ref, qkv_ref, tables, gq_ref, gf_ref, sum_ref):
    cos_t, sin_t, bias2, first, low_half = tables
    size = cos_t.shape[0]
    rows = slice(at, at + size)
    across = (((0,), (0,)), ((), ()))
    for pair in range(cols // TILE):
        places = [g * cols + pair * TILE for g in range(3)]
        query, keys, values = (qkv_ref[rows, p : p + TILE] for p in places)
        query2 = stacked(query, first)
        mixed2 = stacked(back_ref[rows, pair * TILE : (pair + 1) * TILE].astype(BF), first)
        probs = softmax_of(query2, keys, bias2)
        grad_probs = lax.dot_general(
            mixed2, values, (((1,), (1,)), ((), ())), preferred_element_type=F32
        )
        inner = jnp.sum(probs * grad_probs, axis=1, keepdims=True)
        grad_scores = (probs * (grad_probs - inner)).astype(BF)
        gq = jnp.dot(grad_scores, keys, preferred_element_type=F32)
        gq = jnp.where(first, gq[:size], gq[size:]) * 0.125
        gk = lax.dot_general(grad_scores, query2, across, preferred_element_type=F32) * 0.125
        gv = lax.dot_general(probs.astype(BF), mixed2, across, preferred_element_type=F32)
        gq = turned(gq, cos_t, -sin_t, low_half)
        gk = turned(gk, cos_t, -sin_t, low_half)
        for p, v in zip(places, (gq, gk, gv)):
            low = v.astype(BF)
            gq_ref[rows, p : p + TILE] = low
            sum_ref[0:1, p : p + TILE] += jnp.sum(low.astype(F32), axis=0, keepdims=True)

    def gates(gate, up, grad_hid):
        sigma = jax.nn.sigmoid(gate)
        slope = sigma * (1.0 + gate * (1.0 - sigma))
        return (grad_hid * up * slope, grad_hid * (gate * sigma))

    for j in range(main // TILE):
        p, q = j * TILE, main + j * TILE
        grad_hid = back_ref[rows, cols + j * TILE : cols + (j + 1) * TILE]
        gg, gu = gates(pf_ref[rows, p : p + TILE], pf_ref[rows, q : q + TILE], grad_hid)
        gf_ref[rows, p : p + TILE] = gg.astype(BF)
        gf_ref[rows, q : q + TILE] = gu.astype(BF)
    if rest:
        tail = pf_ref[rows, 2 * main :]
        short = back_ref[rows, cols + main :]
        grad_hid = jnp.concatenate([short, jnp.zeros_like(short)], axis=1)
        gg, gu = gates(tail, pltpu.roll(tail, rest, 1), grad_hid)
        lane = lax.broadcasted_iota(jnp.int32, (size, TILE), 1)
        both = jnp.where(lane < rest, gg, pltpu.roll(gu, rest, 1))
        gf_ref[rows, 2 * main :] = both.astype(BF)


def block_tables(cos_ref, sin_ref, mask_ref, block, size):
    lane = lax.broadcasted_iota(jnp.int32, (size, TILE), 1)
    rows = slice(block * size, (block + 1) * size)
    mask = mask_ref[block]
    return (
        cos_ref[rows, :],
        sin_ref[rows, :],
        jnp.concatenate([mask, mask], axis=0),
        lane < HD,
        lane % HD < ROT // 2,
    )


def stack_copies(pieces, whole, sem, start):
    copies, count = [], len(pieces) // 2
    edge = pieces[0].shape[1]
    for group, columns in enumerate((pl.ds(0, edge), pl.ds(edge, whole.shape[1] - edge))):
        at = 0
        for i in range(group * count, (group + 1) * count):
            size = pieces[i].shape[0]
            dst = whole.at[pl.ds(at, size), columns]
            copies.append(pltpu.make_async_copy(pieces[i], dst, sem.at[start + i]))
            at += size
    return copies


def forward_kernel(sizes, count, block, *refs):
    cols, main, rest = sizes
    normed_ref, bias_ref, cos_ref, sin_ref, mask_ref = refs[:5]
    pieces, mixer_any = refs[5 : 5 + count], refs[5 + count]
    joined_ref, qkv_ref, pf_ref, branch_ref = refs[6 + count : 10 + count]
    entry, wm, pq, sem = refs[10 + count :]
    groups = [
        stack_copies(pieces, entry, sem, 0),
        [pltpu.make_async_copy(mixer_any, wm, sem.at[count])],
    ]
    opening = pl.program_id(0) == 0

    @pl.when(opening)
    def _():
        for group in groups:
            for copy in group:
                copy.start()

    def arrive(group):
        @pl.when(opening)
        def _():
            for copy in groups[group]:
                copy.wait()

    normed = normed_ref[...]
    arrive(0)
    pq[...] = jnp.dot(normed, entry[:, : 3 * cols], preferred_element_type=F32)
    pf_ref[...] = jnp.dot(normed, entry[:, 3 * cols :], preferred_element_type=F32)
    for i in range(normed.shape[0] // block):
        tables = block_tables(cos_ref, sin_ref, mask_ref, i, block)
        attend_rows(
            cols, main, rest, i * block, pq, pf_ref, bias_ref, tables, joined_ref, qkv_ref
        )
    arrive(1)
    branch = jnp.dot(joined_ref[...], wm[...], preferred_element_type=F32)
    branch_ref[...] = branch.astype(BF)


def backward_kernel(sizes, count, block, *refs):
    cols, main, rest = sizes
    masked_ref, pf_ref, qkv_ref, cos_ref, sin_ref, mask_ref, mixer_any = refs[:7]
    pieces = refs[7 : 7 + count]
    gq_ref, gf_ref, norm_ref, sum_ref = refs[7 + count : 11 + count]
    wm, entry, back, sem = refs[11 + count :]
    mixer_copy = pltpu.make_async_copy(mixer_any, wm, sem.at[count])
    copies = stack_copies(pieces, entry, sem, 0)
    opening = pl.program_id(0) == 0

    @pl.when(opening)
    def _():
        mixer_copy.start()
        for copy in copies:
            copy.start()
        sum_ref[...] = jnp.zeros_like(sum_ref)
        mixer_copy.wait()

    back[...] = lax.dot_general(
        masked_ref[...], wm[...], CONTRACT_COLS, preferred_element_type=F32
    )
    for i in range(masked_ref.shape[0] // block):
        tables = block_tables(cos_ref, sin_ref, mask_ref, i, block)
        attend_back_rows(
            cols, main, rest, i * block, pf_ref, back, qkv_ref, tables, gq_ref, gf_ref, sum_ref
        )

    @pl.when(opening)
    def _():
        for copy in copies:
            copy.wait()

    cut = 3 * cols
    total = lax.dot_general(
        gq_ref[...], entry[:, :cut], CONTRACT_COLS, preferred_element_type=F32
    )
    total += lax.dot_general(
        gf_ref[...], entry[:, cut:], CONTRACT_COLS, preferred_element_type=F32
    )
    norm_ref[...] = total.astype(BF)


STEP = 256
HIDDEN_COST = pl.CostEstimate(flops=1, bytes_accessed=1, transcendentals=0)


def row_spec(width, rows=STEP):
    return pl.BlockSpec((rows, width), lambda i: (i, 0))


ANYWHERE = pl.BlockSpec(memory_space=pl.ANY)
HELD = pl.BlockSpec(memory_space=pltpu.VMEM)


def kept(*arrays):
    return [pltpu.with_memory_space_constraint(array, pltpu.HBM) for array in arrays]


def stepping(limit):
    return pltpu.CompilerParams(
        dimension_semantics=("arbitrary",), vmem_limit_bytes=limit << 20
    )


def forward_call(normed, bias, cos_t, sin_t, mask, pieces, mixer, sizes):
    cols, main, rest = sizes
    everyone, width = normed.shape
    block = mask.shape[1]
    count = len(pieces)
    joint = cols + main + rest
    return pl.pallas_call(
        functools.partial(forward_kernel, sizes, count, block),
        grid=(everyone // STEP,),
        in_specs=[
            row_spec(width),
            pl.BlockSpec((8, 3 * cols), lambda i: (0, 0)),
            row_spec(TILE),
            row_spec(TILE),
            pl.BlockSpec((STEP // block, block, block), lambda i: (i, 0, 0)),
        ]
        + [ANYWHERE] * (count + 1),
        out_specs=[
            row_spec(joint),
            row_spec(3 * cols),
            row_spec(2 * (main + rest)),
            row_spec(width),
        ],
        out_shape=[
            pltpu.HBM((everyone, joint), BF),
            pltpu.HBM((everyone, 3 * cols), BF),
            pltpu.HBM((everyone, 2 * (main + rest)), F32),
            pltpu.HBM((everyone, width), BF),
        ],
        scratch_shapes=[
            pltpu.VMEM((width, 3 * cols + 2 * (main + rest)), BF),
            pltpu.VMEM((joint, width), BF),
            pltpu.VMEM((STEP, 3 * cols), F32),
            pltpu.SemaphoreType.DMA((count + 1,)),
        ],
        compiler_params=stepping(36),
        cost_estimate=HIDDEN_COST,
        name="forward",
    )(*kept(normed, bias, cos_t, sin_t, mask, *pieces, mixer))


def backward_call(masked, pf, qkv, cos_t, sin_t, mask, mixer, pieces, sizes):
    cols, main, rest = sizes
    everyone, width = masked.shape
    block = mask.shape[1]
    count = len(pieces)
    joint = cols + main + rest
    total = 3 * cols + 2 * (main + rest)
    return pl.pallas_call(
        functools.partial(backward_kernel, sizes, count, block),
        grid=(everyone // STEP,),
        in_specs=[
            row_spec(width),
            row_spec(2 * (main + rest)),
            row_spec(3 * cols),
            row_spec(TILE),
            row_spec(TILE),
            pl.BlockSpec((STEP // block, block, block), lambda i: (i, 0, 0)),
        ]
        + [ANYWHERE] * (count + 1),
        out_specs=[
            row_spec(3 * cols),
            row_spec(2 * (main + rest)),
            row_spec(width),
            pl.BlockSpec((8, 3 * cols), lambda i: (0, 0)),
        ],
        out_shape=[
            pltpu.HBM((everyone, 3 * cols), BF),
            pltpu.HBM((everyone, 2 * (main + rest)), BF),
            pltpu.HBM((everyone, width), BF),
            pltpu.HBM((8, 3 * cols), F32),
        ],
        scratch_shapes=[
            pltpu.VMEM((joint, width), BF),
            pltpu.VMEM((width, total), BF),
            pltpu.VMEM((STEP, joint), F32),
            pltpu.SemaphoreType.DMA((count + 1,)),
        ],
        compiler_params=stepping(36),
        cost_estimate=HIDDEN_COST,
        name="backward",
    )(*kept(masked, pf, qkv, cos_t, sin_t, mask, mixer, *pieces))


def product_call(normed, grad, groups, size):
    low, width = 0, grad.shape[1]
    slabs = [slab for group in groups for slab in group]
    places = [(g, at) for g, group in enumerate(groups) for at in range(len(group))]
    count = len(slabs)

    def kernel(table_ref, lhs_any, grad_any, *refs):
        outs, (lhs, grad, held, sem) = refs[: len(groups)], refs[len(groups) :]
        loads = [pltpu.make_async_copy(grad_any.at[:, pl.ds(low, width)], grad, sem.at[2 * count])]
        copies = []
        for i, (g, at) in enumerate(places):
            slab = pl.multiple_of(table_ref[i] * size, size)
            src = lhs_any.at[:, pl.ds(slab, size)]
            loads.append(pltpu.make_async_copy(src, lhs.at[i], sem.at[count + i]))
            dst = outs[g].at[pl.ds(at * size, size), :]
            copies.append(pltpu.make_async_copy(held.at[i], dst, sem.at[i]))
        for load in loads:
            load.start()
        loads[0].wait()

        def step(i, _):
            for j in range(count):
                pl.when(i == j)(loads[1 + j].wait)
            held[i] = lax.dot_general(
                lhs[i], grad[...], CONTRACT_ROWS, preferred_element_type=F32
            ).astype(BF)
            for j, copy in enumerate(copies):
                pl.when(i == j)(copy.start)

        lax.fori_loop(0, count, step, None)
        for copy in copies:
            copy.wait()

    everyone = normed.shape[0]
    return pl.pallas_call(
        kernel,
        in_specs=[pl.BlockSpec(memory_space=pltpu.SMEM), ANYWHERE, ANYWHERE],
        out_specs=[pl.BlockSpec(memory_space=pltpu.HBM)] * len(groups),
        out_shape=[pltpu.HBM((len(group) * size, width), BF) for group in groups],
        scratch_shapes=[
            pltpu.VMEM((count, everyone, size), BF),
            pltpu.VMEM((everyone, width), BF),
            pltpu.VMEM((count, size, width), BF),
            pltpu.SemaphoreType.DMA((2 * count + 1,)),
        ],
        compiler_params=pltpu.CompilerParams(vmem_limit_bytes=24 << 20),
        cost_estimate=HIDDEN_COST,
        name="weight_grad",
    )(jnp.array(slabs, jnp.int32), *kept(normed, grad))


def mixer_grad_call(lane, joined, masked, wide, own, own_ff, cut):
    everyone, joint = joined.shape
    width = masked.shape[1]
    rest = own + own_ff - cut

    def kernel(lane_ref, joined_ref, masked_ref, *refs):
        to_x, to_y, x_high, y_low, own_low, own_high, whole, sem = refs
        masked = masked_ref[...]

        def product(at, size):
            whole[pl.ds(at, size), :] = lax.dot_general(
                joined_ref[:, pl.ds(at, size)],
                masked,
                CONTRACT_ROWS,
                preferred_element_type=F32,
            ).astype(BF)

        lax.fori_loop(
            0, joint // STEP, lambda i, _: product(pl.multiple_of(i * STEP, STEP), STEP), None
        )
        if joint % STEP:
            product(joint // STEP * STEP, joint % STEP)
        halves = [
            own_low,
            own_high,
            to_x.at[pl.ds(cut, cut), :],
            x_high,
            y_low,
            to_y.at[pl.ds(rest, rest), :],
            to_x.at[pl.ds(0, cut), :],
            to_y.at[pl.ds(0, rest), :],
        ]
        pairs = row_spans(wide, own, own_ff, cut, lane_ref[0], halves, whole)
        run_copies([(there, here) for here, there in pairs], sem)

    shapes = [(size, width) for size in (2 * cut, 2 * rest, rest, cut, cut, rest)]
    return pl.pallas_call(
        kernel,
        in_specs=[pl.BlockSpec(memory_space=pltpu.SMEM), HELD, HELD],
        out_specs=[pl.BlockSpec(memory_space=pltpu.HBM)] * len(shapes),
        out_shape=[pltpu.HBM(shape, BF) for shape in shapes],
        scratch_shapes=[
            pltpu.VMEM((joint, width), BF),
            pltpu.SemaphoreType.DMA((3 * wide,)),
        ],
        compiler_params=pltpu.CompilerParams(vmem_limit_bytes=40 << 20),
        cost_estimate=HIDDEN_COST,
        name="mixer_grad",
    )(lane, joined, masked)


def column_plan(member, outer, wide, cores, own, own_ff, cols, main, rest):
    z, c = member // cores, member % cores
    out = []
    for g in range(3):
        for k in range(wide):
            src = (((g * outer + z) * wide + k) * cores + c) * own
            out.append((0, src, 0, g * cols + k * own, own))
    for which in range(2):
        for k in range(wide):
            src = ((z * wide + k) * cores + c) * own_ff
            lo, hi = k * own_ff, (k + 1) * own_ff
            cut = min(hi, main)
            if cut > lo:
                out.append((1 + which, src, 1, which * main + lo, cut - lo))
            low = max(lo, main)
            if hi > low:
                at = 2 * main + which * rest + low - main
                out.append((1 + which, src + low - lo, 1, at, hi - low))
    return out


def pack_kernel(plan, tp, bases, *refs):
    arrays, packed = refs[:3], refs[3:]
    rows = arrays[0].shape[0]
    edge = packed[0].shape[1]
    for member in range(tp):
        at = slice(member * rows, (member + 1) * rows)
        for which, src, part, dst, width in plan(member):
            dst += bases[part]
            for ref, low, high in ((packed[0], 0, edge), (packed[1], edge, sum(bases))):
                start, stop = max(dst, low), min(dst + width, high)
                if start < stop:
                    there = slice(src + start - dst, src + stop - dst)
                    ref[at, start - low : stop - low] = arrays[which][:, there]


def pack_call(arrays, plan, tp, widths):
    rows = arrays[0].shape[0]
    total = sum(widths)
    edge = (total // 2 + TILE - 1) // TILE * TILE
    return pl.pallas_call(
        functools.partial(pack_kernel, plan, tp, (0, widths[0], total - widths[0])),
        in_specs=[HELD] * 3,
        out_specs=[HELD] * 2,
        out_shape=[jax.ShapeDtypeStruct((tp * rows, w), BF) for w in (edge, total - edge)],
        compiler_params=pltpu.CompilerParams(vmem_limit_bytes=32 << 20),
        name="pack_columns",
    )(*arrays)


def unpack_kernel(plan, tp, part, *refs):
    packed, outs = refs[0], refs[1:]
    rows = outs[0].shape[0]
    for member in range(tp):
        at = slice(member * rows, (member + 1) * rows)
        for which, src, source, dst, width in plan(member):
            if source == part:
                out = outs[which - part]
                out[:, src : src + width] = packed[at, dst : dst + width].astype(F32)


def unpack_call(packed, part, plan, tp, widths):
    rows = packed.shape[0] // tp
    return pl.pallas_call(
        functools.partial(unpack_kernel, plan, tp, part),
        in_specs=[HELD],
        out_specs=[HELD] * len(widths),
        out_shape=[jax.ShapeDtypeStruct((rows, width), F32) for width in widths],
        compiler_params=pltpu.CompilerParams(vmem_limit_bytes=32 << 20),
        cost_estimate=HIDDEN_COST,
        name="unpack_columns",
    )(packed)


def join_kernel(count, *refs):
    ins, out, sem = refs[:count], refs[count], refs[count + 1]
    copies, at = [], 0
    for i, ref in enumerate(ins):
        size = ref.shape[0]
        copies.append(pltpu.make_async_copy(ref, out.at[pl.ds(at, size), :], sem.at[i]))
        at += size
    for copy in copies:
        copy.start()
    for copy in copies:
        copy.wait()


def join_call(arrays):
    count = len(arrays)
    rows, width = sum(array.shape[0] for array in arrays), arrays[0].shape[1]
    return pl.pallas_call(
        functools.partial(join_kernel, count),
        in_specs=[pl.BlockSpec(memory_space=pl.ANY)] * count,
        out_specs=pl.BlockSpec(memory_space=pltpu.VMEM),
        out_shape=jax.ShapeDtypeStruct((rows, width), BF),
        scratch_shapes=[pltpu.SemaphoreType.DMA((count,))],
        compiler_params=pltpu.CompilerParams(vmem_limit_bytes=16 << 20),
        name="join_rows",
    )(*arrays)


def row_spans(wide, own, own_ff, cut, lane, halves, whole):
    spans = []
    base = wide * own
    for j in range(wide):
        spot = lax.bitwise_xor(lane, j)
        down = pl.multiple_of(base + spot * own_ff, 16)
        down_low = pl.multiple_of(base + spot * own_ff + cut, 16)
        out = pl.multiple_of(spot * own, 16)
        low, high = halves[2 * j : 2 * j + 2]
        rest = own_ff - cut
        spans.append((low, whole.at[pl.ds(down, cut), :]))
        spans.append((high.at[pl.ds(0, rest), :], whole.at[pl.ds(down_low, rest), :]))
        spans.append((high.at[pl.ds(rest, own), :], whole.at[pl.ds(out, own), :]))
    return spans


def run_copies(pairs, sem):
    copies = [pltpu.make_async_copy(src, dst, sem.at[i]) for i, (src, dst) in enumerate(pairs)]
    for copy in copies:
        copy.start()
    for copy in copies:
        copy.wait()


def place_call(lane, halves, wide, own, own_ff, cut):
    width = halves[0].shape[1]

    def kernel(lane_ref, *refs):
        ins, out, sem = refs[:-2], refs[-2], refs[-1]
        run_copies(row_spans(wide, own, own_ff, cut, lane_ref[0], ins, out), sem)

    return pl.pallas_call(
        kernel,
        in_specs=[pl.BlockSpec(memory_space=pltpu.SMEM)]
        + [pl.BlockSpec(memory_space=pl.ANY)] * len(halves),
        out_specs=pl.BlockSpec(memory_space=pltpu.VMEM),
        out_shape=jax.ShapeDtypeStruct((wide * (own + own_ff), width), BF),
        scratch_shapes=[pltpu.SemaphoreType.DMA((3 * wide,))],
        compiler_params=pltpu.CompilerParams(vmem_limit_bytes=16 << 20),
        name="place_rows",
    )(lane, *halves)


def mixer_product(joined, masked):
    return lax.dot_general(joined, masked, CONTRACT_ROWS, preferred_element_type=F32).astype(BF)


class Plain:
    def __init__(self, outer, inner):
        self.tp, self.wide, self.cores, self.outer = outer, inner, 1, outer
        self.member = lax.axis_index("dp")
        self.token_axes, self.token_groups = "dp", None
        self.weight_axes, self.weight_groups = "fsdp", None

    def gather_tokens(self, block):
        return lax.all_gather(
            block, self.token_axes, axis=0, tiled=True, axis_index_groups=self.token_groups
        )

    def scatter_tokens(self, part):
        return lax.psum_scatter(
            part.astype(BF),
            self.token_axes,
            scatter_dimension=0,
            tiled=True,
            axis_index_groups=self.token_groups,
        ).astype(F32)

    def exchange(self, part):
        return lax.all_to_all(
            part,
            self.token_axes,
            split_axis=0,
            concat_axis=0,
            tiled=True,
            axis_index_groups=self.token_groups,
        )

    def gather_weights(self, block):
        return lax.all_gather(
            block, self.weight_axes, axis=0, tiled=True, axis_index_groups=self.weight_groups
        )

    def scatter_weights(self, part):
        return lax.psum_scatter(
            part,
            self.weight_axes,
            scatter_dimension=0,
            tiled=True,
            axis_index_groups=self.weight_groups,
        )

    def inputs(self, packed, w_out, w_down, normed, masked, lengths, make_tables):
        mixer = jnp.concatenate([self.gather_weights(w) for w in (w_out, w_down)], axis=0)
        entry = [self.gather_weights(self.exchange(part)) for part in packed]
        tokens = [self.gather_tokens(block) for block in (normed, masked)]
        lengths = lax.all_gather(lengths, "dp", axis=0, tiled=True)
        return entry, mixer, tokens[0], tokens[1], make_tables(lengths)

    def outputs(self, joined, masked, branch, back_call, tail, normed, own, own_ff):
        cols = self.wide * own
        part = mixer_product(joined, masked)
        grads = [self.scatter_weights(p).astype(F32) for p in (part[:cols], part[cols:])]
        grad_qkv, grad_ff, norm, bias_part = back_call(masked)
        parts = []
        for grad in (grad_qkv, grad_ff):
            part = lax.dot_general(normed, grad, CONTRACT_ROWS, preferred_element_type=F32)
            parts.append(self.scatter_weights(part.astype(BF)))
        norm, branch = self.scatter_tokens(norm), self.scatter_tokens(branch)
        part_qkv, part_ff = [self.exchange(part) for part in parts]
        grad_tokens, stats = tail(norm, bias_part)
        stats = self.scatter_stats(stats)
        return grads[0], grads[1], part_qkv, part_ff, branch, grad_tokens, stats

    def relative(self, blocks, axis):
        return blocks

    def scatter_stats(self, stats):
        parts = lax.all_to_all(stats, AXES, split_axis=0, concat_axis=0, tiled=True)
        return jnp.sum(parts, axis=0)


class Linked(Plain):
    def __init__(self, outer, inner):
        self.outer, self.cores, self.wide = outer, 2, inner // 2
        self.tp = outer * 2
        flat = lax.axis_index("fsdp")
        self.lane = flat // 2
        self.member = lax.axis_index("dp") * 2 + lax.rem(flat, 2)
        spots = [
            [[(z * self.wide + k) * 2 + c for c in range(2)] for k in range(self.wide)]
            for z in range(outer)
        ]
        self.token_axes = self.weight_axes = AXES
        self.token_groups = [
            [spots[z][k][c] for z in range(outer) for c in range(2)] for k in range(self.wide)
        ]
        self.weight_groups = [
            [spots[z][k][c] for k in range(self.wide)] for z in range(outer) for c in range(2)
        ]
        self.spots = spots
        self.lane_index = self.lane.astype(jnp.int32).reshape(1)

    def send(self, value, step=0, dz=0, dc=0):
        pairs = [
            (self.spots[z][k][c], self.spots[z ^ dz][k ^ step][c ^ dc])
            for z in range(self.outer)
            for k in range(self.wide)
            for c in range(2)
        ]
        return lax.ppermute(value, AXES, pairs)

    def gather_lengths(self, lengths):
        parts = [lengths] + [self.send(lengths, dz=dz) for dz in range(1, self.outer)]
        return jnp.concatenate(parts, axis=0)

    def order_lengths(self, mine, other):
        both = jnp.stack([mine, other], axis=1).reshape(self.tp, -1)
        spot = lax.bitwise_xor(jnp.arange(self.tp, dtype=jnp.int32), self.member)
        pick = spot[:, None] == jnp.arange(self.tp, dtype=jnp.int32)[None, :]
        return jnp.sum(jnp.where(pick[:, :, None], both[None], 0), axis=1)

    def inputs(self, packed, w_out, w_down, normed, masked, lengths, make_tables):
        own, own_ff = w_out.shape[0], w_down.shape[0]
        cut = own_ff // 32 * 16 + 32
        half = packed[0].shape[0] // 2
        rows, left, right, lengths = tie(join_call([w_down, w_out]), *packed, lengths)
        mix_x, mix_y = self.send(rows, 1), self.send(rows, 2)
        lengths = self.gather_lengths(lengths)
        left = self.exchange(left)
        left, right, mix_x, mix_y = tie(left, right, mix_x, mix_y)
        left_x, left_y = self.send(left, 1), self.send(left, 2)
        right = self.exchange(right)
        right, left_x, left_y, normed, masked, lengths = tie(
            right, left_x, left_y, normed, masked, lengths
        )
        tables = make_tables(self.order_lengths(lengths, self.send(lengths, dc=1)))
        normed_all = self.gather_tokens(normed)
        right_x, right_y = self.send(right, 1), self.send(right, 2)
        left_low, left_high = self.send(left_x[:half], 2), self.send(left_y[half:], 1)
        mix_low, mix_high = self.send(mix_x[:cut], 2), self.send(mix_y[cut:], 1)
        halves = [part for b in (rows, mix_x, mix_y) for part in (b[:cut], b[cut:])]
        right_x, right_y, left_low, left_high, mix_low, mix_high, masked, *others = tie(
            right_x, right_y, left_low, left_high, mix_low, mix_high, masked, *halves, *tables
        )
        halves, tables = others[: len(halves)], others[len(halves) :]
        masked_all = self.gather_tokens(masked)
        right_low, right_high = self.send(right_x[:half], 2), self.send(right_y[half:], 1)
        halves += [mix_low, mix_high]
        mixer = place_call(self.lane_index, halves, self.wide, own, own_ff, cut)
        entry = [left, left_x, left_y, left_low, left_high]
        entry += [right, right_x, right_y, right_low, right_high]
        return entry, mixer, normed_all, masked_all, tables

    def first_sends(self, to_x, to_y):
        return self.send(to_x, 1), self.send(to_y, 2)

    def last_sends(self, got, x_high, y_low):
        from_x, from_y = got
        low, high = from_x[: y_low.shape[0]], from_y[: x_high.shape[0]]
        return (
            self.send((x_high.astype(F32) + high.astype(F32)).astype(BF), 1),
            self.send((y_low.astype(F32) + low.astype(F32)).astype(BF), 2),
        )

    def lane_sum(self, own_low, own_high, first, last):
        low = own_low.astype(F32) + first[0][own_low.shape[0] :].astype(F32)
        high = own_high.astype(F32) + first[1][own_high.shape[0] :].astype(F32)
        return low + last[1].astype(F32), high + last[0].astype(F32)

    def outputs(self, joined, masked, branch, back_call, tail, normed, own, own_ff):
        cut = own_ff // 32 * 16 + 32
        rest = own_ff - cut
        size = normed.shape[1] // self.wide // 2
        first, last = ((6, 2), (7, 5)), ((3,), (4,), (0,), (1,))

        branch = self.scatter_tokens(branch)
        mix = mixer_grad_call(self.lane_index, joined, masked, self.wide, own, own_ff, cut)
        *mix, masked = tie(*mix, masked)
        mix_first = self.first_sends(mix[0], mix[1])
        grad_qkv, grad_ff, norm, bias_part = back_call(masked)
        *mix_first, norm, grad_ff, grad_qkv = tie(*mix_first, norm, grad_ff, grad_qkv)
        norm = self.scatter_tokens(norm)
        to_x, to_y = product_call(normed, grad_ff, first, size)
        to_x, to_y, grad_ff = tie(to_x, to_y, grad_ff)
        ff_first = self.first_sends(to_x, to_y)
        x_high, y_low, ff_low, ff_high = product_call(normed, grad_ff, last, size)
        ff_low, grad_qkv = tie(ff_low, grad_qkv)
        to_x, to_y = product_call(normed, grad_qkv, first, size)
        to_x, grad_qkv = tie(to_x, grad_qkv)
        qkv_x, qkv_y, qkv_low, qkv_high = product_call(normed, grad_qkv, last, size)
        branch, to_x, to_y, x_high, y_low, qkv_low, *ff_first = tie(
            branch, to_x, to_y, x_high, y_low, qkv_low, *ff_first
        )
        ff_last = self.last_sends(ff_first, x_high, y_low)
        part_ff = self.joined_sum((x_high, y_low, ff_low, ff_high), ff_first, ff_last)
        part_ff, to_x, to_y = tie(part_ff, to_x, to_y)
        qkv_first = self.first_sends(to_x, to_y)
        part_ff = self.exchange(part_ff)
        results = tail(norm, bias_part)
        *qkv_first, grad_tokens, stats = tie(*qkv_first, *results)
        qkv_last = self.last_sends(qkv_first, qkv_x, qkv_y)
        part_qkv = self.joined_sum((qkv_x, qkv_y, qkv_low, qkv_high), qkv_first, qkv_last)
        part_ff, part_qkv, stats = tie(part_ff, part_qkv, stats)
        part_qkv = self.exchange(part_qkv)
        stats = self.chip_stats(stats)
        stats, *mix = tie(stats, *mix_first, *mix[2:])
        mix_first, mix = mix[:2], mix[2:]
        mix_last = self.last_sends(mix_first, mix[0], mix[1])
        stats = self.scatter_stats(stats)
        low, high = self.lane_sum(mix[2], mix[3], mix_first, mix_last)
        grad_w_out, grad_w_down = high[rest:], jnp.concatenate([low, high[:rest]], axis=0)
        return grad_w_out, grad_w_down, part_qkv, part_ff, branch, grad_tokens, stats

    def joined_sum(self, late, first, last):
        low, high = self.lane_sum(late[2], late[3], first, last)
        return jnp.concatenate([low, high], axis=0).astype(BF)

    def keep(self, values, axis, place, count, name):
        pick = lambda spot: lax.dynamic_index_in_dim(values, spot, axis, keepdims=False)
        got = [self.send(pick(lax.bitwise_xor(place, j)), **{name: j}) for j in range(1, count)]
        return pick(place) + sum(got)

    def chip_stats(self, stats):
        split = stats.reshape(self.outer, self.wide, 2, -1)
        return self.keep(split, 2, lax.rem(self.member, 2), 2, "dc")

    def scatter_stats(self, split):
        split = self.keep(split, 1, self.lane, self.wide, "step")
        return self.keep(split, 0, self.member // 2, self.outer, "dz")

    def relative(self, blocks, axis):
        shape = blocks.shape
        split = blocks.reshape(shape[:axis] + (2, 2) + shape[axis + 1 :])
        split = jnp.where(self.lane >= 2, jnp.flip(split, axis), split)
        split = jnp.where(lax.rem(self.lane, 2) == 1, jnp.flip(split, axis + 1), split)
        return split.reshape(shape)


def on_device(
    tokens, ln_gain, ln_shift, w_qkv, b_qkv, w_out, w_gate, w_up, w_down, grad_out, seq_lengths
):
    outer, inner = lax.axis_size("dp"), lax.axis_size("fsdp")
    linked = outer == 4 and inner == 8
    net = Linked(outer, inner) if linked else Plain(outer, inner)
    tp, wide, cores = net.tp, net.wide, net.cores
    rows_tok, width = tokens.shape
    own = w_qkv.shape[0]
    own_ff = w_down.shape[0]
    cols, cols_ff = wide * own, wide * own_ff
    main = cols_ff // TILE * TILE
    rest = cols_ff - main
    widths = (3 * cols, 2 * cols_ff)
    plan = lambda member: column_plan(
        member, outer, wide, cores, own, own_ff, cols, main, rest
    )

    _, valid, _ = block_terms(seq_lengths[0], rows_tok)
    keep_row = valid.astype(F32)[:, None]
    widened = tokens.astype(F32)
    centered = widened - jnp.mean(widened, axis=1, keepdims=True)
    inv_std = lax.rsqrt(jnp.mean(centered * centered, axis=1, keepdims=True) + EPS)
    scaled = centered * inv_std
    normed = (scaled * ln_gain + ln_shift).astype(BF)
    masked = (grad_out.astype(F32) * keep_row).astype(BF)

    def lanes_first(x):
        split = x.reshape(rows_tok, outer, wide, cores * own)
        return net.relative(jnp.swapaxes(split, 1, 2), 1).reshape(rows_tok, width)

    def lanes_back(x):
        split = net.relative(x.reshape(rows_tok, wide, outer, cores * own), 1)
        return jnp.swapaxes(split, 1, 2).reshape(rows_tok, width)

    lengths = seq_lengths
    arrays = [w_qkv, w_gate, w_up]

    def make_tables(lengths):
        position, _, allowed = jax.vmap(lambda row: block_terms(row, rows_tok))(lengths)
        return [*turn_tables(position), jnp.where(allowed, 0.0, NEG)]

    entry, mixer, normed_all, masked_all, (cos_t, sin_t, mask) = net.inputs(
        pack_call(arrays, plan, tp, widths),
        w_out,
        w_down,
        lanes_first(normed),
        masked,
        lengths,
        make_tables,
    )
    bias = lax.dynamic_index_in_dim(
        jnp.transpose(b_qkv.reshape(3, outer, wide, cores, own), (1, 3, 0, 2, 4)).reshape(tp, -1),
        net.member,
        0,
    )
    bias = jnp.broadcast_to(bias, (8, 3 * cols))

    sizes = (cols, main, rest)
    joined, qkv, proj_ff, branch = forward_call(
        normed_all, bias, cos_t, sin_t, mask, entry, mixer, sizes
    )
    back_call = lambda masked: backward_call(
        masked, proj_ff, qkv, cos_t, sin_t, mask, mixer, entry, sizes
    )

    def tail(grad_norm, bias_part):
        grad_norm = lanes_back(grad_norm)
        lifted_grad = grad_norm * ln_gain
        grad_in = inv_std * (
            lifted_grad
            - jnp.mean(lifted_grad, axis=1, keepdims=True)
            - scaled * jnp.mean(lifted_grad * scaled, axis=1, keepdims=True)
        )
        grad_tokens = (grad_out.astype(F32) + grad_in).astype(BF)
        shards = outer * inner
        gain_part = jnp.sum(grad_norm * scaled, axis=0)
        shift_part = jnp.sum(grad_norm, axis=0)
        bias_full = lax.dynamic_update_index_in_dim(
            jnp.zeros((tp, 3 * cols), F32), bias_part[0], net.member, 0
        )
        bias_full = jnp.transpose(bias_full.reshape(outer, cores, 3, wide, own), (2, 0, 3, 1, 4))
        stats = jnp.concatenate(
            [
                gain_part.reshape(shards, own),
                shift_part.reshape(shards, own),
                bias_full.reshape(shards, 3 * own),
            ],
            axis=1,
        )
        return grad_tokens, stats

    grad_w_out, grad_w_down, part_qkv, part_ff, branch, grad_tokens, stats = net.outputs(
        joined, masked_all, branch, back_call, tail, normed_all, own, own_ff
    )
    output = (widened + keep_row * branch).astype(BF)
    grad_w_gate, grad_w_up = unpack_call(
        part_ff, 1, plan, tp, [w_gate.shape[1], w_up.shape[1]]
    )
    part_qkv, stats, grad_w_gate, grad_w_up = tie(part_qkv, stats, grad_w_gate, grad_w_up)
    (grad_w_qkv,) = unpack_call(part_qkv, 0, plan, tp, [w_qkv.shape[1]])
    return (
        output,
        grad_tokens,
        grad_w_qkv,
        grad_w_out,
        grad_w_gate,
        grad_w_up,
        grad_w_down,
        stats[:own],
        stats[own : 2 * own],
        stats[2 * own :],
    )


def solution(mesh):
    rows = P(AXES, None)
    return jax.shard_map(
        on_device,
        mesh=mesh,
        in_specs=(rows, P(), P(), rows, P(), rows, rows, rows, rows, rows, rows),
        out_specs=(rows,) * 7 + (P(AXES),) * 3,
        check_vma=False,
    )
```

```python
import functools
import math

import jax
import jax.numpy as jnp
from jax import lax
from jax.experimental import pallas as pl
from jax.experimental.pallas import tpu as pltpu
from jax.sharding import PartitionSpec as P

HD = 64
ROT = 16
EPS = 1e-05
NEG = -1e30
TILE = 128
AXES = ("dp", "fsdp")
BF = jnp.bfloat16
F32 = jnp.float32
CONTRACT_ROWS = (((0,), (0,)), ((), ()))
CONTRACT_COLS = (((1,), (1,)), ((), ()))


def block_terms(lengths_row, rows_tok):
    ends = jnp.cumsum(lengths_row)
    place = jnp.arange(rows_tok, dtype=jnp.int32)
    segment = jnp.sum((place[:, None] >= ends[None, :]).astype(jnp.int32), axis=1)
    starts = jnp.concatenate([ends - lengths_row, ends[-1:]])
    labels = jnp.arange(starts.shape[0], dtype=jnp.int32)
    begin = jnp.sum(jnp.where(segment[:, None] == labels[None, :], starts[None, :], 0), axis=1)
    position = (place - begin).astype(F32)
    valid = segment < lengths_row.shape[0]
    label_tok = jnp.where(valid, segment, lengths_row.shape[0] + place)
    allowed = (label_tok[:, None] == label_tok[None, :]) & (place[None, :] <= place[:, None])
    return (position, valid, allowed)


def turn_tables(position):
    half = ROT // 2
    freq = jnp.exp(jnp.arange(half, dtype=F32) * (-2.0 * math.log(10000.0) / ROT))
    turn = position.reshape(-1)[:, None] * freq[None, :]
    cosine, sine = jnp.cos(turn), jnp.sin(turn)
    rest = (turn.shape[0], HD - ROT)
    cos_t = jnp.concatenate([cosine, cosine, jnp.ones(rest, F32)], axis=1)
    sin_t = jnp.concatenate([-sine, sine, jnp.zeros(rest, F32)], axis=1)
    return (jnp.tile(cos_t, (1, 2)), jnp.tile(sin_t, (1, 2)))


def tie(*values):
    return lax.optimization_barrier(values)


def turned(v, cos_t, sin_t, low_half):
    partner = jnp.where(low_half, pltpu.roll(v, TILE - ROT // 2, 1), pltpu.roll(v, ROT // 2, 1))
    return v * cos_t + partner * sin_t

def stacked(v, first):
    zero = jnp.zeros_like(v)
    return jnp.concatenate([jnp.where(first, v, zero), jnp.where(first, zero, v)], axis=0)

def softmax_of(query2, keys, bias2):
    scores = lax.dot_general(query2, keys, (((1,), (1,)), ((), ())), preferred_element_type=F32)
    scores = scores * 0.125 + bias2
    lifted = jnp.exp(scores - jnp.max(scores, axis=1, keepdims=True))
    return lifted / jnp.sum(lifted, axis=1, keepdims=True)

def attend_rows(cols, main, rest, at, pq_ref, pf_ref, bias_ref, tables, joined_ref, qkv_ref):
    cos_t, sin_t, bias2, first, low_half = tables
    size = cos_t.shape[0]
    rows = slice(at, at + size)
    for pair in range(cols // TILE):
        places = [g * cols + pair * TILE for g in range(3)]
        query, keys, values = (
            pq_ref[rows, p : p + TILE] + bias_ref[0:1, p : p + TILE] for p in places
        )
        query = turned(query, cos_t, sin_t, low_half).astype(BF)
        keys = turned(keys, cos_t, sin_t, low_half).astype(BF)
        values = values.astype(BF)
        for p, v in zip(places, (query, keys, values)):
            qkv_ref[rows, p : p + TILE] = v
        probs = softmax_of(stacked(query, first), keys, bias2).astype(BF)
        mixed = jnp.dot(probs, values, preferred_element_type=F32)
        joined_ref[rows, pair * TILE : (pair + 1) * TILE] = jnp.where(
            first, mixed[:size], mixed[size:]
        ).astype(BF)
    for j in range(main // TILE):
        gate = pf_ref[rows, j * TILE : (j + 1) * TILE]
        up = pf_ref[rows, main + j * TILE : main + (j + 1) * TILE]
        hid = gate * jax.nn.sigmoid(gate) * up
        joined_ref[rows, cols + j * TILE : cols + (j + 1) * TILE] = hid.astype(BF)
    if rest:
        tail = pf_ref[rows, 2 * main :]
        up = pltpu.roll(tail, rest, 1)
        hid = tail * jax.nn.sigmoid(tail) * up
        joined_ref[rows, cols + main :] = hid[:, :rest].astype(BF)


def attend_back_rows(cols, main, rest, at, pf_ref, back_ref, qkv_ref, tables, gq_ref, gf_ref, sum_ref):
    cos_t, sin_t, bias2, first, low_half = tables
    size = cos_t.shape[0]
    rows = slice(at, at + size)
    across = (((0,), (0,)), ((), ()))
    for pair in range(cols // TILE):
        places = [g * cols + pair * TILE for g in range(3)]
        query, keys, values = (qkv_ref[rows, p : p + TILE] for p in places)
        query2 = stacked(query, first)
        mixed2 = stacked(back_ref[rows, pair * TILE : (pair + 1) * TILE].astype(BF), first)
        probs = softmax_of(query2, keys, bias2)
        grad_probs = lax.dot_general(
            mixed2, values, (((1,), (1,)), ((), ())), preferred_element_type=F32
        )
        inner = jnp.sum(probs * grad_probs, axis=1, keepdims=True)
        grad_scores = (probs * (grad_probs - inner)).astype(BF)
        gq = jnp.dot(grad_scores, keys, preferred_element_type=F32)
        gq = jnp.where(first, gq[:size], gq[size:]) * 0.125
        gk = lax.dot_general(grad_scores, query2, across, preferred_element_type=F32) * 0.125
        gv = lax.dot_general(probs.astype(BF), mixed2, across, preferred_element_type=F32)
        gq = turned(gq, cos_t, -sin_t, low_half)
        gk = turned(gk, cos_t, -sin_t, low_half)
        for p, v in zip(places, (gq, gk, gv)):
            low = v.astype(BF)
            gq_ref[rows, p : p + TILE] = low
            sum_ref[0:1, p : p + TILE] += jnp.sum(low.astype(F32), axis=0, keepdims=True)

    def gates(gate, up, grad_hid):
        sigma = jax.nn.sigmoid(gate)
        slope = sigma * (1.0 + gate * (1.0 - sigma))
        return (grad_hid * up * slope, grad_hid * (gate * sigma))

    for j in range(main // TILE):
        p, q = j * TILE, main + j * TILE
        grad_hid = back_ref[rows, cols + j * TILE : cols + (j + 1) * TILE]
        gg, gu = gates(pf_ref[rows, p : p + TILE], pf_ref[rows, q : q + TILE], grad_hid)
        gf_ref[rows, p : p + TILE] = gg.astype(BF)
        gf_ref[rows, q : q + TILE] = gu.astype(BF)
    if rest:
        tail = pf_ref[rows, 2 * main :]
        short = back_ref[rows, cols + main :]
        grad_hid = jnp.concatenate([short, jnp.zeros_like(short)], axis=1)
        gg, gu = gates(tail, pltpu.roll(tail, rest, 1), grad_hid)
        lane = lax.broadcasted_iota(jnp.int32, (size, TILE), 1)
        both = jnp.where(lane < rest, gg, pltpu.roll(gu, rest, 1))
        gf_ref[rows, 2 * main :] = both.astype(BF)


def block_tables(cos_ref, sin_ref, mask_ref, block, size):
    lane = lax.broadcasted_iota(jnp.int32, (size, TILE), 1)
    rows = slice(block * size, (block + 1) * size)
    mask = mask_ref[block]
    return (
        cos_ref[rows, :],
        sin_ref[rows, :],
        jnp.concatenate([mask, mask], axis=0),
        lane < HD,
        lane % HD < ROT // 2,
    )


def stack_copies(pieces, whole, sem, start):
    copies, count = [], len(pieces) // 2
    edge = pieces[0].shape[1]
    for group, columns in enumerate((pl.ds(0, edge), pl.ds(edge, whole.shape[1] - edge))):
        at = 0
        for i in range(group * count, (group + 1) * count):
            size = pieces[i].shape[0]
            dst = whole.at[pl.ds(at, size), columns]
            copies.append(pltpu.make_async_copy(pieces[i], dst, sem.at[start + i]))
            at += size
    return copies


def forward_kernel(sizes, count, block, *refs):
    cols, main, rest = sizes
    normed_ref, bias_ref, cos_ref, sin_ref, mask_ref = refs[:5]
    pieces, mixer_any = refs[5 : 5 + count], refs[5 + count]
    joined_ref, qkv_ref, pf_ref, branch_ref = refs[6 + count : 10 + count]
    entry, wm, pq, sem = refs[10 + count :]
    groups = [
        stack_copies(pieces, entry, sem, 0),
        [pltpu.make_async_copy(mixer_any, wm, sem.at[count])],
    ]
    opening = pl.program_id(0) == 0

    @pl.when(opening)
    def _():
        for group in groups:
            for copy in group:
                copy.start()

    def arrive(group):
        @pl.when(opening)
        def _():
            for copy in groups[group]:
                copy.wait()

    normed = normed_ref[...]
    arrive(0)
    pq[...] = jnp.dot(normed, entry[:, : 3 * cols], preferred_element_type=F32)
    pf_ref[...] = jnp.dot(normed, entry[:, 3 * cols :], preferred_element_type=F32)
    for i in range(normed.shape[0] // block):
        tables = block_tables(cos_ref, sin_ref, mask_ref, i, block)
        attend_rows(
            cols, main, rest, i * block, pq, pf_ref, bias_ref, tables, joined_ref, qkv_ref
        )
    arrive(1)
    branch = jnp.dot(joined_ref[...], wm[...], preferred_element_type=F32)
    branch_ref[...] = branch.astype(BF)


def backward_kernel(sizes, count, block, *refs):
    cols, main, rest = sizes
    masked_ref, pf_ref, qkv_ref, cos_ref, sin_ref, mask_ref, mixer_any = refs[:7]
    pieces = refs[7 : 7 + count]
    gq_ref, gf_ref, norm_ref, sum_ref = refs[7 + count : 11 + count]
    wm, entry, back, sem = refs[11 + count :]
    mixer_copy = pltpu.make_async_copy(mixer_any, wm, sem.at[count])
    copies = stack_copies(pieces, entry, sem, 0)
    opening = pl.program_id(0) == 0

    @pl.when(opening)
    def _():
        mixer_copy.start()
        for copy in copies:
            copy.start()
        sum_ref[...] = jnp.zeros_like(sum_ref)
        mixer_copy.wait()

    back[...] = lax.dot_general(
        masked_ref[...], wm[...], CONTRACT_COLS, preferred_element_type=F32
    )
    for i in range(masked_ref.shape[0] // block):
        tables = block_tables(cos_ref, sin_ref, mask_ref, i, block)
        attend_back_rows(
            cols, main, rest, i * block, pf_ref, back, qkv_ref, tables, gq_ref, gf_ref, sum_ref
        )

    @pl.when(opening)
    def _():
        for copy in copies:
            copy.wait()

    cut = 3 * cols
    total = lax.dot_general(
        gq_ref[...], entry[:, :cut], CONTRACT_COLS, preferred_element_type=F32
    )
    total += lax.dot_general(
        gf_ref[...], entry[:, cut:], CONTRACT_COLS, preferred_element_type=F32
    )
    norm_ref[...] = total.astype(BF)


STEP = 256
HIDDEN_COST = pl.CostEstimate(flops=1, bytes_accessed=1, transcendentals=0)


def row_spec(width, rows=STEP):
    return pl.BlockSpec((rows, width), lambda i: (i, 0))


ANYWHERE = pl.BlockSpec(memory_space=pl.ANY)
HELD = pl.BlockSpec(memory_space=pltpu.VMEM)


def kept(*arrays):
    return [pltpu.with_memory_space_constraint(array, pltpu.HBM) for array in arrays]


def stepping(limit):
    return pltpu.CompilerParams(
        dimension_semantics=("arbitrary",), vmem_limit_bytes=limit << 20
    )


def forward_call(normed, bias, cos_t, sin_t, mask, pieces, mixer, sizes):
    cols, main, rest = sizes
    everyone, width = normed.shape
    block = mask.shape[1]
    count = len(pieces)
    joint = cols + main + rest
    return pl.pallas_call(
        functools.partial(forward_kernel, sizes, count, block),
        grid=(everyone // STEP,),
        in_specs=[
            row_spec(width),
            pl.BlockSpec((8, 3 * cols), lambda i: (0, 0)),
            row_spec(TILE),
            row_spec(TILE),
            pl.BlockSpec((STEP // block, block, block), lambda i: (i, 0, 0)),
        ]
        + [ANYWHERE] * (count + 1),
        out_specs=[
            row_spec(joint),
            row_spec(3 * cols),
            row_spec(2 * (main + rest)),
            row_spec(width),
        ],
        out_shape=[
            pltpu.HBM((everyone, joint), BF),
            pltpu.HBM((everyone, 3 * cols), BF),
            pltpu.HBM((everyone, 2 * (main + rest)), F32),
            pltpu.HBM((everyone, width), BF),
        ],
        scratch_shapes=[
            pltpu.VMEM((width, 3 * cols + 2 * (main + rest)), BF),
            pltpu.VMEM((joint, width), BF),
            pltpu.VMEM((STEP, 3 * cols), F32),
            pltpu.SemaphoreType.DMA((count + 1,)),
        ],
        compiler_params=stepping(36),
        cost_estimate=HIDDEN_COST,
        name="forward",
    )(*kept(normed, bias, cos_t, sin_t, mask, *pieces, mixer))


def backward_call(masked, pf, qkv, cos_t, sin_t, mask, mixer, pieces, sizes):
    cols, main, rest = sizes
    everyone, width = masked.shape
    block = mask.shape[1]
    count = len(pieces)
    joint = cols + main + rest
    total = 3 * cols + 2 * (main + rest)
    return pl.pallas_call(
        functools.partial(backward_kernel, sizes, count, block),
        grid=(everyone // STEP,),
        in_specs=[
            row_spec(width),
            row_spec(2 * (main + rest)),
            row_spec(3 * cols),
            row_spec(TILE),
            row_spec(TILE),
            pl.BlockSpec((STEP // block, block, block), lambda i: (i, 0, 0)),
        ]
        + [ANYWHERE] * (count + 1),
        out_specs=[
            row_spec(3 * cols),
            row_spec(2 * (main + rest)),
            row_spec(width),
            pl.BlockSpec((8, 3 * cols), lambda i: (0, 0)),
        ],
        out_shape=[
            pltpu.HBM((everyone, 3 * cols), BF),
            pltpu.HBM((everyone, 2 * (main + rest)), BF),
            pltpu.HBM((everyone, width), BF),
            pltpu.HBM((8, 3 * cols), F32),
        ],
        scratch_shapes=[
            pltpu.VMEM((joint, width), BF),
            pltpu.VMEM((width, total), BF),
            pltpu.VMEM((STEP, joint), F32),
            pltpu.SemaphoreType.DMA((count + 1,)),
        ],
        compiler_params=stepping(36),
        cost_estimate=HIDDEN_COST,
        name="backward",
    )(*kept(masked, pf, qkv, cos_t, sin_t, mask, mixer, *pieces))


def product_call(normed, grad, groups, size):
    low, width = 0, grad.shape[1]
    slabs = [slab for group in groups for slab in group]
    places = [(g, at) for g, group in enumerate(groups) for at in range(len(group))]
    count = len(slabs)

    def kernel(table_ref, lhs_any, grad_any, *refs):
        outs, (lhs, grad, held, sem) = refs[: len(groups)], refs[len(groups) :]
        loads = [pltpu.make_async_copy(grad_any.at[:, pl.ds(low, width)], grad, sem.at[2 * count])]
        copies = []
        for i, (g, at) in enumerate(places):
            slab = pl.multiple_of(table_ref[i] * size, size)
            src = lhs_any.at[:, pl.ds(slab, size)]
            loads.append(pltpu.make_async_copy(src, lhs.at[i], sem.at[count + i]))
            dst = outs[g].at[pl.ds(at * size, size), :]
            copies.append(pltpu.make_async_copy(held.at[i], dst, sem.at[i]))
        for load in loads:
            load.start()
        loads[0].wait()

        def step(i, _):
            for j in range(count):
                pl.when(i == j)(loads[1 + j].wait)
            held[i] = lax.dot_general(
                lhs[i], grad[...], CONTRACT_ROWS, preferred_element_type=F32
            ).astype(BF)
            for j, copy in enumerate(copies):
                pl.when(i == j)(copy.start)

        lax.fori_loop(0, count, step, None)
        for copy in copies:
            copy.wait()

    everyone = normed.shape[0]
    return pl.pallas_call(
        kernel,
        in_specs=[pl.BlockSpec(memory_space=pltpu.SMEM), ANYWHERE, ANYWHERE],
        out_specs=[pl.BlockSpec(memory_space=pltpu.HBM)] * len(groups),
        out_shape=[pltpu.HBM((len(group) * size, width), BF) for group in groups],
        scratch_shapes=[
            pltpu.VMEM((count, everyone, size), BF),
            pltpu.VMEM((everyone, width), BF),
            pltpu.VMEM((count, size, width), BF),
            pltpu.SemaphoreType.DMA((2 * count + 1,)),
        ],
        compiler_params=pltpu.CompilerParams(vmem_limit_bytes=24 << 20),
        cost_estimate=HIDDEN_COST,
        name="weight_grad",
    )(jnp.array(slabs, jnp.int32), *kept(normed, grad))


def mixer_grad_call(lane, joined, masked, wide, own, own_ff, cut):
    everyone, joint = joined.shape
    width = masked.shape[1]
    rest = own + own_ff - cut

    def kernel(lane_ref, joined_ref, masked_ref, *refs):
        to_x, to_y, x_high, y_low, own_low, own_high, whole, sem = refs
        masked = masked_ref[...]

        def product(at, size):
            whole[pl.ds(at, size), :] = lax.dot_general(
                joined_ref[:, pl.ds(at, size)],
                masked,
                CONTRACT_ROWS,
                preferred_element_type=F32,
            ).astype(BF)

        lax.fori_loop(
            0, joint // STEP, lambda i, _: product(pl.multiple_of(i * STEP, STEP), STEP), None
        )
        if joint % STEP:
            product(joint // STEP * STEP, joint % STEP)
        halves = [
            own_low,
            own_high,
            to_x.at[pl.ds(cut, cut), :],
            x_high,
            y_low,
            to_y.at[pl.ds(rest, rest), :],
            to_x.at[pl.ds(0, cut), :],
            to_y.at[pl.ds(0, rest), :],
        ]
        pairs = row_spans(wide, own, own_ff, cut, lane_ref[0], halves, whole)
        run_copies([(there, here) for here, there in pairs], sem)

    shapes = [(size, width) for size in (2 * cut, 2 * rest, rest, cut, cut, rest)]
    return pl.pallas_call(
        kernel,
        in_specs=[pl.BlockSpec(memory_space=pltpu.SMEM), HELD, HELD],
        out_specs=[pl.BlockSpec(memory_space=pltpu.HBM)] * len(shapes),
        out_shape=[pltpu.HBM(shape, BF) for shape in shapes],
        scratch_shapes=[
            pltpu.VMEM((joint, width), BF),
            pltpu.SemaphoreType.DMA((3 * wide,)),
        ],
        compiler_params=pltpu.CompilerParams(vmem_limit_bytes=40 << 20),
        cost_estimate=HIDDEN_COST,
        name="mixer_grad",
    )(lane, joined, masked)


def column_plan(member, outer, wide, cores, own, own_ff, cols, main, rest):
    z, c = member // cores, member % cores
    out = []
    for g in range(3):
        for k in range(wide):
            src = (((g * outer + z) * wide + k) * cores + c) * own
            out.append((0, src, 0, g * cols + k * own, own))
    for which in range(2):
        for k in range(wide):
            src = ((z * wide + k) * cores + c) * own_ff
            lo, hi = k * own_ff, (k + 1) * own_ff
            cut = min(hi, main)
            if cut > lo:
                out.append((1 + which, src, 1, which * main + lo, cut - lo))
            low = max(lo, main)
            if hi > low:
                at = 2 * main + which * rest + low - main
                out.append((1 + which, src + low - lo, 1, at, hi - low))
    return out


def pack_kernel(plan, tp, bases, *refs):
    arrays, packed = refs[:3], refs[3:]
    rows = arrays[0].shape[0]
    edge = packed[0].shape[1]
    for member in range(tp):
        at = slice(member * rows, (member + 1) * rows)
        for which, src, part, dst, width in plan(member):
            dst += bases[part]
            for ref, low, high in ((packed[0], 0, edge), (packed[1], edge, sum(bases))):
                start, stop = max(dst, low), min(dst + width, high)
                if start < stop:
                    there = slice(src + start - dst, src + stop - dst)
                    ref[at, start - low : stop - low] = arrays[which][:, there]


def pack_call(arrays, plan, tp, widths):
    rows = arrays[0].shape[0]
    total = sum(widths)
    edge = total // 2 // TILE * TILE
    return pl.pallas_call(
        functools.partial(pack_kernel, plan, tp, (0, widths[0], total - widths[0])),
        in_specs=[HELD] * 3,
        out_specs=[HELD] * 2,
        out_shape=[jax.ShapeDtypeStruct((tp * rows, w), BF) for w in (edge, total - edge)],
        compiler_params=pltpu.CompilerParams(vmem_limit_bytes=32 << 20),
        name="pack_columns",
    )(*arrays)


def unpack_kernel(plan, tp, part, *refs):
    packed, outs = refs[0], refs[1:]
    rows = outs[0].shape[0]
    for member in range(tp):
        at = slice(member * rows, (member + 1) * rows)
        for which, src, source, dst, width in plan(member):
            if source == part:
                out = outs[which - part]
                out[:, src : src + width] = packed[at, dst : dst + width].astype(F32)


def unpack_call(packed, part, plan, tp, widths):
    rows = packed.shape[0] // tp
    return pl.pallas_call(
        functools.partial(unpack_kernel, plan, tp, part),
        in_specs=[HELD],
        out_specs=[HELD] * len(widths),
        out_shape=[jax.ShapeDtypeStruct((rows, width), F32) for width in widths],
        compiler_params=pltpu.CompilerParams(vmem_limit_bytes=32 << 20),
        cost_estimate=HIDDEN_COST,
        name="unpack_columns",
    )(packed)


def join_kernel(count, *refs):
    ins, out, sem = refs[:count], refs[count], refs[count + 1]
    copies, at = [], 0
    for i, ref in enumerate(ins):
        size = ref.shape[0]
        copies.append(pltpu.make_async_copy(ref, out.at[pl.ds(at, size), :], sem.at[i]))
        at += size
    for copy in copies:
        copy.start()
    for copy in copies:
        copy.wait()


def join_call(arrays):
    count = len(arrays)
    rows, width = sum(array.shape[0] for array in arrays), arrays[0].shape[1]
    return pl.pallas_call(
        functools.partial(join_kernel, count),
        in_specs=[pl.BlockSpec(memory_space=pl.ANY)] * count,
        out_specs=pl.BlockSpec(memory_space=pltpu.VMEM),
        out_shape=jax.ShapeDtypeStruct((rows, width), BF),
        scratch_shapes=[pltpu.SemaphoreType.DMA((count,))],
        compiler_params=pltpu.CompilerParams(vmem_limit_bytes=16 << 20),
        name="join_rows",
    )(*arrays)


def row_spans(wide, own, own_ff, cut, lane, halves, whole):
    spans = []
    base = wide * own
    for j in range(wide):
        spot = lax.bitwise_xor(lane, j)
        down = pl.multiple_of(base + spot * own_ff, 16)
        down_low = pl.multiple_of(base + spot * own_ff + cut, 16)
        out = pl.multiple_of(spot * own, 16)
        low, high = halves[2 * j : 2 * j + 2]
        rest = own_ff - cut
        spans.append((low, whole.at[pl.ds(down, cut), :]))
        spans.append((high.at[pl.ds(0, rest), :], whole.at[pl.ds(down_low, rest), :]))
        spans.append((high.at[pl.ds(rest, own), :], whole.at[pl.ds(out, own), :]))
    return spans


def run_copies(pairs, sem):
    copies = [pltpu.make_async_copy(src, dst, sem.at[i]) for i, (src, dst) in enumerate(pairs)]
    for copy in copies:
        copy.start()
    for copy in copies:
        copy.wait()


def place_call(lane, halves, wide, own, own_ff, cut):
    width = halves[0].shape[1]

    def kernel(lane_ref, *refs):
        ins, out, sem = refs[:-2], refs[-2], refs[-1]
        run_copies(row_spans(wide, own, own_ff, cut, lane_ref[0], ins, out), sem)

    return pl.pallas_call(
        kernel,
        in_specs=[pl.BlockSpec(memory_space=pltpu.SMEM)]
        + [pl.BlockSpec(memory_space=pl.ANY)] * len(halves),
        out_specs=pl.BlockSpec(memory_space=pltpu.VMEM),
        out_shape=jax.ShapeDtypeStruct((wide * (own + own_ff), width), BF),
        scratch_shapes=[pltpu.SemaphoreType.DMA((3 * wide,))],
        compiler_params=pltpu.CompilerParams(vmem_limit_bytes=16 << 20),
        name="place_rows",
    )(lane, *halves)


def mixer_product(joined, masked):
    return lax.dot_general(joined, masked, CONTRACT_ROWS, preferred_element_type=F32).astype(BF)


class Plain:
    def __init__(self, outer, inner):
        self.tp, self.wide, self.cores, self.outer = outer, inner, 1, outer
        self.member = lax.axis_index("dp")
        self.token_axes, self.token_groups = "dp", None
        self.weight_axes, self.weight_groups = "fsdp", None

    def gather_tokens(self, block):
        return lax.all_gather(
            block, self.token_axes, axis=0, tiled=True, axis_index_groups=self.token_groups
        )

    def scatter_tokens(self, part):
        return lax.psum_scatter(
            part.astype(BF),
            self.token_axes,
            scatter_dimension=0,
            tiled=True,
            axis_index_groups=self.token_groups,
        ).astype(F32)

    def exchange(self, part):
        return lax.all_to_all(
            part,
            self.token_axes,
            split_axis=0,
            concat_axis=0,
            tiled=True,
            axis_index_groups=self.token_groups,
        )

    def gather_weights(self, block):
        return lax.all_gather(
            block, self.weight_axes, axis=0, tiled=True, axis_index_groups=self.weight_groups
        )

    def scatter_weights(self, part):
        return lax.psum_scatter(
            part,
            self.weight_axes,
            scatter_dimension=0,
            tiled=True,
            axis_index_groups=self.weight_groups,
        )

    def inputs(self, packed, w_out, w_down, normed, masked, lengths, make_tables):
        mixer = jnp.concatenate([self.gather_weights(w) for w in (w_out, w_down)], axis=0)
        entry = [self.gather_weights(self.exchange(part)) for part in packed]
        tokens = [self.gather_tokens(block) for block in (normed, masked)]
        lengths = lax.all_gather(lengths, "dp", axis=0, tiled=True)
        return entry, mixer, tokens[0], tokens[1], make_tables(lengths)

    def outputs(self, joined, masked, branch, back_call, tail, normed, own, own_ff):
        cols = self.wide * own
        part = mixer_product(joined, masked)
        grads = [self.scatter_weights(p).astype(F32) for p in (part[:cols], part[cols:])]
        grad_qkv, grad_ff, norm, bias_part = back_call(masked)
        parts = []
        for grad in (grad_qkv, grad_ff):
            part = lax.dot_general(normed, grad, CONTRACT_ROWS, preferred_element_type=F32)
            parts.append(self.scatter_weights(part.astype(BF)))
        norm, branch = self.scatter_tokens(norm), self.scatter_tokens(branch)
        part_qkv, part_ff = [self.exchange(part) for part in parts]
        grad_tokens, stats = tail(norm, bias_part)
        stats = self.scatter_stats(stats)
        return grads[0], grads[1], part_qkv, part_ff, branch, grad_tokens, stats

    def relative(self, blocks, axis):
        return blocks

    def scatter_stats(self, stats):
        parts = lax.all_to_all(stats, AXES, split_axis=0, concat_axis=0, tiled=True)
        return jnp.sum(parts, axis=0)


class Linked(Plain):
    def __init__(self, outer, inner):
        self.outer, self.cores, self.wide = outer, 2, inner // 2
        self.tp = outer * 2
        flat = lax.axis_index("fsdp")
        self.lane = flat // 2
        self.member = lax.axis_index("dp") * 2 + lax.rem(flat, 2)
        spots = [
            [[(z * self.wide + k) * 2 + c for c in range(2)] for k in range(self.wide)]
            for z in range(outer)
        ]
        self.token_axes = self.weight_axes = AXES
        self.token_groups = [
            [spots[z][k][c] for z in range(outer) for c in range(2)] for k in range(self.wide)
        ]
        self.weight_groups = [
            [spots[z][k][c] for k in range(self.wide)] for z in range(outer) for c in range(2)
        ]
        self.spots = spots
        self.lane_index = self.lane.astype(jnp.int32).reshape(1)

    def send(self, value, step=0, dz=0, dc=0):
        pairs = [
            (self.spots[z][k][c], self.spots[z ^ dz][k ^ step][c ^ dc])
            for z in range(self.outer)
            for k in range(self.wide)
            for c in range(2)
        ]
        return lax.ppermute(value, AXES, pairs)

    def gather_lengths(self, lengths):
        parts = [lengths] + [self.send(lengths, dz=dz) for dz in range(1, self.outer)]
        return jnp.concatenate(parts, axis=0)

    def order_lengths(self, mine, other):
        both = jnp.stack([mine, other], axis=1).reshape(self.tp, -1)
        spot = lax.bitwise_xor(jnp.arange(self.tp, dtype=jnp.int32), self.member)
        pick = spot[:, None] == jnp.arange(self.tp, dtype=jnp.int32)[None, :]
        return jnp.sum(jnp.where(pick[:, :, None], both[None], 0), axis=1)

    def inputs(self, packed, w_out, w_down, normed, masked, lengths, make_tables):
        own, own_ff = w_out.shape[0], w_down.shape[0]
        cut = own_ff // 32 * 16 + 32
        half = packed[0].shape[0] // 2
        rows, left, right, lengths = tie(join_call([w_down, w_out]), *packed, lengths)
        mix_x, mix_y = self.send(rows, 1), self.send(rows, 2)
        lengths = self.gather_lengths(lengths)
        left = self.exchange(left)
        left, right, mix_x, mix_y = tie(left, right, mix_x, mix_y)
        left_x, left_y = self.send(left, 1), self.send(left, 2)
        right = self.exchange(right)
        halves = [part for b in (rows, mix_x, mix_y) for part in (b[:cut], b[cut:])]
        right, left_x, left_y, normed, masked, lengths, *halves = tie(
            right, left_x, left_y, normed, masked, lengths, *halves
        )
        normed_all, masked_all = self.gather_tokens(normed), self.gather_tokens(masked)
        right_x, right_y = self.send(right, 1), self.send(right, 2)
        mix_low, mix_high = self.send(halves[2], 2), self.send(halves[5], 1)
        left_low, left_high = self.send(left_x[:half], 2), self.send(left_y[half:], 1)
        tables = make_tables(self.order_lengths(lengths, self.send(lengths, dc=1)))
        halves += [mix_low, mix_high]
        mixer = place_call(self.lane_index, halves, self.wide, own, own_ff, cut)
        right_x, right_y, left_low, left_high, mixer, *tables = tie(
            right_x, right_y, left_low, left_high, *kept(mixer, *tables)
        )
        right_low, right_high = self.send(right_x[:half], 2), self.send(right_y[half:], 1)
        entry = [left, left_x, left_y, left_low, left_high]
        entry += [right, right_x, right_y, right_low, right_high]
        return entry, mixer, normed_all, masked_all, tables

    def first_sends(self, to_x, to_y):
        return self.send(to_x, 1), self.send(to_y, 2)

    def last_sends(self, got, x_high, y_low):
        from_x, from_y = got
        low, high = from_x[: y_low.shape[0]], from_y[: x_high.shape[0]]
        return (
            self.send((x_high.astype(F32) + high.astype(F32)).astype(BF), 1),
            self.send((y_low.astype(F32) + low.astype(F32)).astype(BF), 2),
        )

    def lane_sum(self, own_low, own_high, first, last):
        low = own_low.astype(F32) + first[0][own_low.shape[0] :].astype(F32)
        high = own_high.astype(F32) + first[1][own_high.shape[0] :].astype(F32)
        return low + last[1].astype(F32), high + last[0].astype(F32)

    def outputs(self, joined, masked, branch, back_call, tail, normed, own, own_ff):
        cut = own_ff // 32 * 16 + 32
        rest = own_ff - cut
        size = normed.shape[1] // self.wide // 2
        first, last = ((6, 2), (7, 5)), ((3,), (4,), (0,), (1,))

        branch = self.scatter_tokens(branch)
        mix = mixer_grad_call(self.lane_index, joined, masked, self.wide, own, own_ff, cut)
        *mix, masked = tie(*mix, masked)
        mix_first = self.first_sends(mix[0], mix[1])
        grad_qkv, grad_ff, norm, bias_part = back_call(masked)
        *mix_first, norm, grad_ff, grad_qkv = tie(*mix_first, norm, grad_ff, grad_qkv)
        norm = self.scatter_tokens(norm)
        to_x, to_y = product_call(normed, grad_ff, first, size)
        to_x, to_y, grad_ff = tie(to_x, to_y, grad_ff)
        ff_first = self.first_sends(to_x, to_y)
        x_high, y_low, ff_low, ff_high = product_call(normed, grad_ff, last, size)
        ff_low, grad_qkv = tie(ff_low, grad_qkv)
        to_x, to_y = product_call(normed, grad_qkv, first, size)
        to_x, grad_qkv = tie(to_x, grad_qkv)
        qkv_x, qkv_y, qkv_low, qkv_high = product_call(normed, grad_qkv, last, size)
        branch, to_x, to_y, x_high, y_low, qkv_low, *ff_first = tie(
            branch, to_x, to_y, x_high, y_low, qkv_low, *ff_first
        )
        ff_last = self.last_sends(ff_first, x_high, y_low)
        part_ff = self.joined_sum((x_high, y_low, ff_low, ff_high), ff_first, ff_last)
        part_ff, to_x, to_y = tie(part_ff, to_x, to_y)
        qkv_first = self.first_sends(to_x, to_y)
        part_ff = self.exchange(part_ff)
        results = tail(norm, bias_part)
        *qkv_first, grad_tokens, stats = tie(*qkv_first, *results)
        qkv_last = self.last_sends(qkv_first, qkv_x, qkv_y)
        part_qkv = self.joined_sum((qkv_x, qkv_y, qkv_low, qkv_high), qkv_first, qkv_last)
        part_ff, part_qkv, stats, *mix = tie(part_ff, part_qkv, stats, *mix_first, *mix[2:])
        part_qkv = self.exchange(part_qkv)
        stats = self.chip_stats(stats)
        mix_first, mix = mix[:2], mix[2:]
        mix_last = self.last_sends(mix_first, mix[0], mix[1])
        stats = self.scatter_stats(stats)
        low, high = self.lane_sum(mix[2], mix[3], mix_first, mix_last)
        grad_w_out, grad_w_down = high[rest:], jnp.concatenate([low, high[:rest]], axis=0)
        return grad_w_out, grad_w_down, part_qkv, part_ff, branch, grad_tokens, stats

    def joined_sum(self, late, first, last):
        low, high = self.lane_sum(late[2], late[3], first, last)
        return jnp.concatenate([low, high], axis=0).astype(BF)

    def keep(self, values, axis, place, count, name):
        pick = lambda spot: lax.dynamic_index_in_dim(values, spot, axis, keepdims=False)
        got = [self.send(pick(lax.bitwise_xor(place, j)), **{name: j}) for j in range(1, count)]
        return pick(place) + sum(got)

    def chip_stats(self, stats):
        split = stats.reshape(self.outer, self.wide, 2, -1)
        return self.keep(split, 2, lax.rem(self.member, 2), 2, "dc")

    def scatter_stats(self, split):
        split = self.keep(split, 1, self.lane, self.wide, "step")
        return self.keep(split, 0, self.member // 2, self.outer, "dz")

    def relative(self, blocks, axis):
        shape = blocks.shape
        split = blocks.reshape(shape[:axis] + (2, 2) + shape[axis + 1 :])
        split = jnp.where(self.lane >= 2, jnp.flip(split, axis), split)
        split = jnp.where(lax.rem(self.lane, 2) == 1, jnp.flip(split, axis + 1), split)
        return split.reshape(shape)


def on_device(
    tokens, ln_gain, ln_shift, w_qkv, b_qkv, w_out, w_gate, w_up, w_down, grad_out, seq_lengths
):
    outer, inner = lax.axis_size("dp"), lax.axis_size("fsdp")
    linked = outer == 4 and inner == 8
    net = Linked(outer, inner) if linked else Plain(outer, inner)
    tp, wide, cores = net.tp, net.wide, net.cores
    rows_tok, width = tokens.shape
    own = w_qkv.shape[0]
    own_ff = w_down.shape[0]
    cols, cols_ff = wide * own, wide * own_ff
    main = cols_ff // TILE * TILE
    rest = cols_ff - main
    widths = (3 * cols, 2 * cols_ff)
    plan = lambda member: column_plan(
        member, outer, wide, cores, own, own_ff, cols, main, rest
    )

    _, valid, _ = block_terms(seq_lengths[0], rows_tok)
    keep_row = valid.astype(F32)[:, None]
    widened = tokens.astype(F32)
    centered = widened - jnp.mean(widened, axis=1, keepdims=True)
    inv_std = lax.rsqrt(jnp.mean(centered * centered, axis=1, keepdims=True) + EPS)
    scaled = centered * inv_std
    normed = (scaled * ln_gain + ln_shift).astype(BF)
    masked = (grad_out.astype(F32) * keep_row).astype(BF)

    def lanes_first(x):
        split = x.reshape(rows_tok, outer, wide, cores * own)
        return net.relative(jnp.swapaxes(split, 1, 2), 1).reshape(rows_tok, width)

    def lanes_back(x):
        split = net.relative(x.reshape(rows_tok, wide, outer, cores * own), 1)
        return jnp.swapaxes(split, 1, 2).reshape(rows_tok, width)

    lengths = seq_lengths
    arrays = [w_qkv, w_gate, w_up]

    bias = lax.dynamic_index_in_dim(
        jnp.transpose(b_qkv.reshape(3, outer, wide, cores, own), (1, 3, 0, 2, 4)).reshape(tp, -1),
        net.member,
        0,
    )
    bias = jnp.broadcast_to(bias, (8, 3 * cols))

    def make_tables(lengths):
        position, _, allowed = jax.vmap(lambda row: block_terms(row, rows_tok))(lengths)
        return [*turn_tables(position), jnp.where(allowed, 0.0, NEG), bias]

    entry, mixer, normed_all, masked_all, (cos_t, sin_t, mask, bias) = net.inputs(
        pack_call(arrays, plan, tp, widths),
        w_out,
        w_down,
        lanes_first(normed),
        masked,
        lengths,
        make_tables,
    )
    sizes = (cols, main, rest)
    joined, qkv, proj_ff, branch = forward_call(
        normed_all, bias, cos_t, sin_t, mask, entry, mixer, sizes
    )
    back_call = lambda masked: backward_call(
        masked, proj_ff, qkv, cos_t, sin_t, mask, mixer, entry, sizes
    )

    def tail(grad_norm, bias_part):
        grad_norm = lanes_back(grad_norm)
        lifted_grad = grad_norm * ln_gain
        grad_in = inv_std * (
            lifted_grad
            - jnp.mean(lifted_grad, axis=1, keepdims=True)
            - scaled * jnp.mean(lifted_grad * scaled, axis=1, keepdims=True)
        )
        grad_tokens = (grad_out.astype(F32) + grad_in).astype(BF)
        shards = outer * inner
        gain_part = jnp.sum(grad_norm * scaled, axis=0)
        shift_part = jnp.sum(grad_norm, axis=0)
        bias_full = lax.dynamic_update_index_in_dim(
            jnp.zeros((tp, 3 * cols), F32), bias_part[0], net.member, 0
        )
        bias_full = jnp.transpose(bias_full.reshape(outer, cores, 3, wide, own), (2, 0, 3, 1, 4))
        stats = jnp.concatenate(
            [
                gain_part.reshape(shards, own),
                shift_part.reshape(shards, own),
                bias_full.reshape(shards, 3 * own),
            ],
            axis=1,
        )
        return grad_tokens, stats

    grad_w_out, grad_w_down, part_qkv, part_ff, branch, grad_tokens, stats = net.outputs(
        joined, masked_all, branch, back_call, tail, normed_all, own, own_ff
    )
    output = (widened + keep_row * branch).astype(BF)
    grad_w_gate, grad_w_up = unpack_call(
        part_ff, 1, plan, tp, [w_gate.shape[1], w_up.shape[1]]
    )
    part_qkv, stats, grad_w_gate, grad_w_up = tie(part_qkv, stats, grad_w_gate, grad_w_up)
    (grad_w_qkv,) = unpack_call(part_qkv, 0, plan, tp, [w_qkv.shape[1]])
    return (
        output,
        grad_tokens,
        grad_w_qkv,
        grad_w_out,
        grad_w_gate,
        grad_w_up,
        grad_w_down,
        stats[:own],
        stats[own : 2 * own],
        stats[2 * own :],
    )


def solution(mesh):
    rows = P(AXES, None)
    return jax.shard_map(
        on_device,
        mesh=mesh,
        in_specs=(rows, P(), P(), rows, P(), rows, rows, rows, rows, rows, rows),
        out_specs=(rows,) * 7 + (P(AXES),) * 3,
        check_vma=False,
    )
```

```python
import functools
import math

import jax
import jax.numpy as jnp
from jax import lax
from jax.experimental import pallas as pl
from jax.experimental.pallas import tpu as pltpu
from jax.sharding import PartitionSpec as P

HD = 64
ROT = 16
EPS = 1e-05
NEG = -1e30
TILE = 128
AXES = ("dp", "fsdp")
BF = jnp.bfloat16
F32 = jnp.float32
CONTRACT_ROWS = (((0,), (0,)), ((), ()))
CONTRACT_COLS = (((1,), (1,)), ((), ()))


def block_terms(lengths_row, rows_tok):
    ends = jnp.cumsum(lengths_row)
    place = jnp.arange(rows_tok, dtype=jnp.int32)
    segment = jnp.sum((place[:, None] >= ends[None, :]).astype(jnp.int32), axis=1)
    starts = jnp.concatenate([ends - lengths_row, ends[-1:]])
    labels = jnp.arange(starts.shape[0], dtype=jnp.int32)
    begin = jnp.sum(jnp.where(segment[:, None] == labels[None, :], starts[None, :], 0), axis=1)
    position = (place - begin).astype(F32)
    valid = segment < lengths_row.shape[0]
    label_tok = jnp.where(valid, segment, lengths_row.shape[0] + place)
    allowed = (label_tok[:, None] == label_tok[None, :]) & (place[None, :] <= place[:, None])
    return (position, valid, allowed)


def turn_tables(position):
    half = ROT // 2
    freq = jnp.exp(jnp.arange(half, dtype=F32) * (-2.0 * math.log(10000.0) / ROT))
    turn = position.reshape(-1)[:, None] * freq[None, :]
    cosine, sine = jnp.cos(turn), jnp.sin(turn)
    rest = (turn.shape[0], HD - ROT)
    cos_t = jnp.concatenate([cosine, cosine, jnp.ones(rest, F32)], axis=1)
    sin_t = jnp.concatenate([-sine, sine, jnp.zeros(rest, F32)], axis=1)
    return (jnp.tile(cos_t, (1, 2)), jnp.tile(sin_t, (1, 2)))


def tie(*values):
    return lax.optimization_barrier(values)


def turned(v, cos_t, sin_t, low_half):
    partner = jnp.where(low_half, pltpu.roll(v, TILE - ROT // 2, 1), pltpu.roll(v, ROT // 2, 1))
    return v * cos_t + partner * sin_t

def stacked(v, first):
    zero = jnp.zeros_like(v)
    return jnp.concatenate([jnp.where(first, v, zero), jnp.where(first, zero, v)], axis=0)

def softmax_of(query2, keys, bias2):
    scores = lax.dot_general(query2, keys, (((1,), (1,)), ((), ())), preferred_element_type=F32)
    scores = scores * 0.125 + bias2
    lifted = jnp.exp(scores - jnp.max(scores, axis=1, keepdims=True))
    return lifted / jnp.sum(lifted, axis=1, keepdims=True)

def attend_rows(cols, main, rest, at, pq_ref, pf_ref, bias_ref, tables, joined_ref, qkv_ref):
    cos_t, sin_t, bias2, first, low_half = tables
    size = cos_t.shape[0]
    rows = slice(at, at + size)
    for pair in range(cols // TILE):
        places = [g * cols + pair * TILE for g in range(3)]
        query, keys, values = (
            pq_ref[rows, p : p + TILE] + bias_ref[0:1, p : p + TILE] for p in places
        )
        query = turned(query, cos_t, sin_t, low_half).astype(BF)
        keys = turned(keys, cos_t, sin_t, low_half).astype(BF)
        values = values.astype(BF)
        for p, v in zip(places, (query, keys, values)):
            qkv_ref[rows, p : p + TILE] = v
        probs = softmax_of(stacked(query, first), keys, bias2).astype(BF)
        mixed = jnp.dot(probs, values, preferred_element_type=F32)
        joined_ref[rows, pair * TILE : (pair + 1) * TILE] = jnp.where(
            first, mixed[:size], mixed[size:]
        ).astype(BF)
    for j in range(main // TILE):
        gate = pf_ref[rows, j * TILE : (j + 1) * TILE]
        up = pf_ref[rows, main + j * TILE : main + (j + 1) * TILE]
        hid = gate * jax.nn.sigmoid(gate) * up
        joined_ref[rows, cols + j * TILE : cols + (j + 1) * TILE] = hid.astype(BF)
    if rest:
        tail = pf_ref[rows, 2 * main :]
        up = pltpu.roll(tail, rest, 1)
        hid = tail * jax.nn.sigmoid(tail) * up
        joined_ref[rows, cols + main :] = hid[:, :rest].astype(BF)


def attend_back_rows(cols, main, rest, at, pf_ref, back_ref, qkv_ref, tables, gq_ref, gf_ref, sum_ref):
    cos_t, sin_t, bias2, first, low_half = tables
    size = cos_t.shape[0]
    rows = slice(at, at + size)
    across = (((0,), (0,)), ((), ()))
    for pair in range(cols // TILE):
        places = [g * cols + pair * TILE for g in range(3)]
        query, keys, values = (qkv_ref[rows, p : p + TILE] for p in places)
        query2 = stacked(query, first)
        mixed2 = stacked(back_ref[rows, pair * TILE : (pair + 1) * TILE].astype(BF), first)
        probs = softmax_of(query2, keys, bias2)
        grad_probs = lax.dot_general(
            mixed2, values, (((1,), (1,)), ((), ())), preferred_element_type=F32
        )
        inner = jnp.sum(probs * grad_probs, axis=1, keepdims=True)
        grad_scores = (probs * (grad_probs - inner)).astype(BF)
        gq = jnp.dot(grad_scores, keys, preferred_element_type=F32)
        gq = jnp.where(first, gq[:size], gq[size:]) * 0.125
        gk = lax.dot_general(grad_scores, query2, across, preferred_element_type=F32) * 0.125
        gv = lax.dot_general(probs.astype(BF), mixed2, across, preferred_element_type=F32)
        gq = turned(gq, cos_t, -sin_t, low_half)
        gk = turned(gk, cos_t, -sin_t, low_half)
        for p, v in zip(places, (gq, gk, gv)):
            low = v.astype(BF)
            gq_ref[rows, p : p + TILE] = low
            sum_ref[0:1, p : p + TILE] += jnp.sum(low.astype(F32), axis=0, keepdims=True)

    def gates(gate, up, grad_hid):
        sigma = jax.nn.sigmoid(gate)
        slope = sigma * (1.0 + gate * (1.0 - sigma))
        return (grad_hid * up * slope, grad_hid * (gate * sigma))

    for j in range(main // TILE):
        p, q = j * TILE, main + j * TILE
        grad_hid = back_ref[rows, cols + j * TILE : cols + (j + 1) * TILE]
        gg, gu = gates(pf_ref[rows, p : p + TILE], pf_ref[rows, q : q + TILE], grad_hid)
        gf_ref[rows, p : p + TILE] = gg.astype(BF)
        gf_ref[rows, q : q + TILE] = gu.astype(BF)
    if rest:
        tail = pf_ref[rows, 2 * main :]
        short = back_ref[rows, cols + main :]
        grad_hid = jnp.concatenate([short, jnp.zeros_like(short)], axis=1)
        gg, gu = gates(tail, pltpu.roll(tail, rest, 1), grad_hid)
        lane = lax.broadcasted_iota(jnp.int32, (size, TILE), 1)
        both = jnp.where(lane < rest, gg, pltpu.roll(gu, rest, 1))
        gf_ref[rows, 2 * main :] = both.astype(BF)


def block_tables(cos_ref, sin_ref, mask_ref, block, size):
    lane = lax.broadcasted_iota(jnp.int32, (size, TILE), 1)
    rows = slice(block * size, (block + 1) * size)
    mask = mask_ref[block]
    return (
        cos_ref[rows, :],
        sin_ref[rows, :],
        jnp.concatenate([mask, mask], axis=0),
        lane < HD,
        lane % HD < ROT // 2,
    )


def stack_copies(pieces, whole, sem, start):
    copies, count = [], len(pieces) // 2
    edge = pieces[0].shape[1]
    for group, columns in enumerate((pl.ds(0, edge), pl.ds(edge, whole.shape[1] - edge))):
        at = 0
        for i in range(group * count, (group + 1) * count):
            size = pieces[i].shape[0]
            dst = whole.at[pl.ds(at, size), columns]
            copies.append(pltpu.make_async_copy(pieces[i], dst, sem.at[start + i]))
            at += size
    return copies


def forward_kernel(sizes, count, block, *refs):
    cols, main, rest = sizes
    normed_ref, bias_ref, cos_ref, sin_ref, mask_ref = refs[:5]
    pieces, mixer_any = refs[5 : 5 + count], refs[5 + count]
    joined_ref, qkv_ref, pf_ref, branch_ref = refs[6 + count : 10 + count]
    entry, wm, pq, sem = refs[10 + count :]
    groups = [
        stack_copies(pieces, entry, sem, 0),
        [pltpu.make_async_copy(mixer_any, wm, sem.at[count])],
    ]
    opening = pl.program_id(0) == 0

    @pl.when(opening)
    def _():
        for group in groups:
            for copy in group:
                copy.start()

    def arrive(group):
        @pl.when(opening)
        def _():
            for copy in groups[group]:
                copy.wait()

    normed = normed_ref[...]
    arrive(0)
    pq[...] = jnp.dot(normed, entry[:, : 3 * cols], preferred_element_type=F32)
    pf_ref[...] = jnp.dot(normed, entry[:, 3 * cols :], preferred_element_type=F32)
    for i in range(normed.shape[0] // block):
        tables = block_tables(cos_ref, sin_ref, mask_ref, i, block)
        attend_rows(
            cols, main, rest, i * block, pq, pf_ref, bias_ref, tables, joined_ref, qkv_ref
        )
    arrive(1)
    branch = jnp.dot(joined_ref[...], wm[...], preferred_element_type=F32)
    branch_ref[...] = branch.astype(BF)


def backward_kernel(sizes, count, block, *refs):
    cols, main, rest = sizes
    masked_ref, pf_ref, qkv_ref, cos_ref, sin_ref, mask_ref, mixer_any = refs[:7]
    pieces = refs[7 : 7 + count]
    gq_ref, gf_ref, norm_ref, sum_ref = refs[7 + count : 11 + count]
    wm, entry, back, sem = refs[11 + count :]
    mixer_copy = pltpu.make_async_copy(mixer_any, wm, sem.at[count])
    copies = stack_copies(pieces, entry, sem, 0)
    opening = pl.program_id(0) == 0

    @pl.when(opening)
    def _():
        mixer_copy.start()
        for copy in copies:
            copy.start()
        sum_ref[...] = jnp.zeros_like(sum_ref)
        mixer_copy.wait()

    back[...] = lax.dot_general(
        masked_ref[...], wm[...], CONTRACT_COLS, preferred_element_type=F32
    )
    for i in range(masked_ref.shape[0] // block):
        tables = block_tables(cos_ref, sin_ref, mask_ref, i, block)
        attend_back_rows(
            cols, main, rest, i * block, pf_ref, back, qkv_ref, tables, gq_ref, gf_ref, sum_ref
        )

    @pl.when(opening)
    def _():
        for copy in copies:
            copy.wait()

    cut = 3 * cols
    total = lax.dot_general(
        gq_ref[...], entry[:, :cut], CONTRACT_COLS, preferred_element_type=F32
    )
    total += lax.dot_general(
        gf_ref[...], entry[:, cut:], CONTRACT_COLS, preferred_element_type=F32
    )
    norm_ref[...] = total.astype(BF)


STEP = 256
HIDDEN_COST = pl.CostEstimate(flops=1, bytes_accessed=1, transcendentals=0)


def row_spec(width, rows=STEP):
    return pl.BlockSpec((rows, width), lambda i: (i, 0))


ANYWHERE = pl.BlockSpec(memory_space=pl.ANY)
HELD = pl.BlockSpec(memory_space=pltpu.VMEM)


def kept(*arrays):
    return [pltpu.with_memory_space_constraint(array, pltpu.HBM) for array in arrays]


def stepping(limit):
    return pltpu.CompilerParams(
        dimension_semantics=("arbitrary",), vmem_limit_bytes=limit << 20
    )


def forward_call(normed, bias, cos_t, sin_t, mask, pieces, mixer, sizes):
    cols, main, rest = sizes
    everyone, width = normed.shape
    block = mask.shape[1]
    count = len(pieces)
    joint = cols + main + rest
    return pl.pallas_call(
        functools.partial(forward_kernel, sizes, count, block),
        grid=(everyone // STEP,),
        in_specs=[
            row_spec(width),
            pl.BlockSpec((8, 3 * cols), lambda i: (0, 0)),
            row_spec(TILE),
            row_spec(TILE),
            pl.BlockSpec((STEP // block, block, block), lambda i: (i, 0, 0)),
        ]
        + [ANYWHERE] * (count + 1),
        out_specs=[
            row_spec(joint),
            row_spec(3 * cols),
            row_spec(2 * (main + rest)),
            row_spec(width),
        ],
        out_shape=[
            pltpu.HBM((everyone, joint), BF),
            pltpu.HBM((everyone, 3 * cols), BF),
            pltpu.HBM((everyone, 2 * (main + rest)), F32),
            pltpu.HBM((everyone, width), BF),
        ],
        scratch_shapes=[
            pltpu.VMEM((width, 3 * cols + 2 * (main + rest)), BF),
            pltpu.VMEM((joint, width), BF),
            pltpu.VMEM((STEP, 3 * cols), F32),
            pltpu.SemaphoreType.DMA((count + 1,)),
        ],
        compiler_params=stepping(36),
        cost_estimate=HIDDEN_COST,
        name="forward",
    )(*kept(normed, bias, cos_t, sin_t, mask, *pieces, mixer))


def backward_call(masked, pf, qkv, cos_t, sin_t, mask, mixer, pieces, sizes):
    cols, main, rest = sizes
    everyone, width = masked.shape
    block = mask.shape[1]
    count = len(pieces)
    joint = cols + main + rest
    total = 3 * cols + 2 * (main + rest)
    return pl.pallas_call(
        functools.partial(backward_kernel, sizes, count, block),
        grid=(everyone // STEP,),
        in_specs=[
            row_spec(width),
            row_spec(2 * (main + rest)),
            row_spec(3 * cols),
            row_spec(TILE),
            row_spec(TILE),
            pl.BlockSpec((STEP // block, block, block), lambda i: (i, 0, 0)),
        ]
        + [ANYWHERE] * (count + 1),
        out_specs=[
            row_spec(3 * cols),
            row_spec(2 * (main + rest)),
            row_spec(width),
            pl.BlockSpec((8, 3 * cols), lambda i: (0, 0)),
        ],
        out_shape=[
            pltpu.HBM((everyone, 3 * cols), BF),
            pltpu.HBM((everyone, 2 * (main + rest)), BF),
            pltpu.HBM((everyone, width), BF),
            pltpu.HBM((8, 3 * cols), F32),
        ],
        scratch_shapes=[
            pltpu.VMEM((joint, width), BF),
            pltpu.VMEM((width, total), BF),
            pltpu.VMEM((STEP, joint), F32),
            pltpu.SemaphoreType.DMA((count + 1,)),
        ],
        compiler_params=stepping(36),
        cost_estimate=HIDDEN_COST,
        name="backward",
    )(*kept(masked, pf, qkv, cos_t, sin_t, mask, mixer, *pieces))


def product_call(normed, grad, groups, size):
    low, width = 0, grad.shape[1]
    slabs = [slab for group in groups for slab in group]
    places = [(g, at) for g, group in enumerate(groups) for at in range(len(group))]
    count = len(slabs)

    def kernel(table_ref, lhs_any, grad_any, *refs):
        outs, (lhs, grad, held, sem) = refs[: len(groups)], refs[len(groups) :]
        loads = [pltpu.make_async_copy(grad_any.at[:, pl.ds(low, width)], grad, sem.at[2 * count])]
        copies = []
        for i, (g, at) in enumerate(places):
            slab = pl.multiple_of(table_ref[i] * size, size)
            src = lhs_any.at[:, pl.ds(slab, size)]
            loads.append(pltpu.make_async_copy(src, lhs.at[i], sem.at[count + i]))
            dst = outs[g].at[pl.ds(at * size, size), :]
            copies.append(pltpu.make_async_copy(held.at[i], dst, sem.at[i]))
        for load in loads:
            load.start()
        loads[0].wait()

        def step(i, _):
            for j in range(count):
                pl.when(i == j)(loads[1 + j].wait)
            held[i] = lax.dot_general(
                lhs[i], grad[...], CONTRACT_ROWS, preferred_element_type=F32
            ).astype(BF)
            for j, copy in enumerate(copies):
                pl.when(i == j)(copy.start)

        lax.fori_loop(0, count, step, None)
        for copy in copies:
            copy.wait()

    everyone = normed.shape[0]
    return pl.pallas_call(
        kernel,
        in_specs=[pl.BlockSpec(memory_space=pltpu.SMEM), ANYWHERE, ANYWHERE],
        out_specs=[pl.BlockSpec(memory_space=pltpu.HBM)] * len(groups),
        out_shape=[pltpu.HBM((len(group) * size, width), BF) for group in groups],
        scratch_shapes=[
            pltpu.VMEM((count, everyone, size), BF),
            pltpu.VMEM((everyone, width), BF),
            pltpu.VMEM((count, size, width), BF),
            pltpu.SemaphoreType.DMA((2 * count + 1,)),
        ],
        compiler_params=pltpu.CompilerParams(vmem_limit_bytes=24 << 20),
        cost_estimate=HIDDEN_COST,
        name="weight_grad",
    )(jnp.array(slabs, jnp.int32), *kept(normed, grad))


def sum_kernel(own_low, own_high, from_x, from_y, last_x, last_y, out_ref):
    def total(*refs):
        return sum(ref[...].astype(F32) for ref in refs).astype(BF)

    out_ref[0] = total(own_low, from_x, last_y)
    out_ref[1] = total(own_high, from_y, last_x)


def sum_call(own_low, own_high, first, last):
    half, width = own_low.shape
    rows = half // 2
    near = pl.BlockSpec((rows, width), lambda i: (i, 0))
    second = pl.BlockSpec((rows, width), lambda i: (i + 2, 0))
    out = pl.pallas_call(
        sum_kernel,
        grid=(2,),
        in_specs=[near, near, second, second, near, near],
        out_specs=pl.BlockSpec((2, rows, width), lambda i: (0, i, 0)),
        out_shape=pltpu.HBM((2, half, width), BF),
        compiler_params=stepping(24),
        cost_estimate=HIDDEN_COST,
        name="sum_lanes",
    )(*kept(own_low, own_high, *first, *last))
    return out.reshape(2 * half, width)


def add_kernel(from_x, from_y, x_high, y_low, to_x, to_y):
    to_x[...] = (x_high[...].astype(F32) + from_y[...].astype(F32)).astype(BF)
    to_y[...] = (y_low[...].astype(F32) + from_x[...].astype(F32)).astype(BF)


def add_call(got, x_high, y_low):
    high, low = x_high.shape, y_low.shape
    block = lambda shape: pl.BlockSpec(shape, lambda i: (0, 0))
    return pl.pallas_call(
        add_kernel,
        grid=(1,),
        in_specs=[block(low), block(high), block(high), block(low)],
        out_specs=[block(high), block(low)],
        out_shape=[pltpu.HBM(high, BF), pltpu.HBM(low, BF)],
        compiler_params=stepping(24),
        cost_estimate=HIDDEN_COST,
        name="add_halves",
    )(*kept(*got, x_high, y_low))


def mixer_sum_call(own_low, own_high, first, last, own):
    (low, width), high = own_low.shape, own_high.shape[0]
    rest = high - own

    def kernel(low_ref, high_ref, x_ref, y_ref, last_x, last_y, out_ref, down_ref):
        low_sum = low_ref[...].astype(F32) + x_ref[...].astype(F32) + last_y[...].astype(F32)
        high_sum = high_ref[...].astype(F32) + y_ref[...].astype(F32) + last_x[...].astype(F32)
        down_ref[:low, :] = low_sum
        down_ref[low:, :] = high_sum[:rest]
        out_ref[...] = high_sum[rest:]

    block = lambda rows, at=0: pl.BlockSpec((rows, width), lambda i: (at, 0))
    return pl.pallas_call(
        kernel,
        grid=(1,),
        in_specs=[block(low), block(high), block(low, 1), block(high, 1), block(high), block(low)],
        out_specs=[block(own), block(low + rest)],
        out_shape=[pltpu.HBM((own, width), F32), pltpu.HBM((low + rest, width), F32)],
        compiler_params=stepping(24),
        cost_estimate=HIDDEN_COST,
        name="sum_mixer",
    )(*kept(own_low, own_high, *first, *last))


def mixer_grad_call(lane, joined, masked, wide, own, own_ff, cut):
    everyone, joint = joined.shape
    width = masked.shape[1]
    rest = own + own_ff - cut

    def kernel(lane_ref, joined_any, masked_any, *refs):
        to_x, to_y, x_high, y_low, own_low, own_high, joined_ref, masked_ref, whole, sem = refs
        run_copies([(joined_any, joined_ref), (masked_any, masked_ref)], sem)
        masked = masked_ref[...]

        def product(at, size):
            whole[pl.ds(at, size), :] = lax.dot_general(
                joined_ref[:, pl.ds(at, size)],
                masked,
                CONTRACT_ROWS,
                preferred_element_type=F32,
            ).astype(BF)

        lax.fori_loop(
            0, joint // STEP, lambda i, _: product(pl.multiple_of(i * STEP, STEP), STEP), None
        )
        if joint % STEP:
            product(joint // STEP * STEP, joint % STEP)
        halves = [
            own_low,
            own_high,
            to_x.at[pl.ds(cut, cut), :],
            x_high,
            y_low,
            to_y.at[pl.ds(rest, rest), :],
            to_x.at[pl.ds(0, cut), :],
            to_y.at[pl.ds(0, rest), :],
        ]
        pairs = row_spans(wide, own, own_ff, cut, lane_ref[0], halves, whole)
        run_copies([(there, here) for here, there in pairs], sem)

    shapes = [(size, width) for size in (2 * cut, 2 * rest, rest, cut, cut, rest)]
    return pl.pallas_call(
        kernel,
        in_specs=[pl.BlockSpec(memory_space=pltpu.SMEM), ANYWHERE, ANYWHERE],
        out_specs=[pl.BlockSpec(memory_space=pltpu.HBM)] * len(shapes),
        out_shape=[pltpu.HBM(shape, BF) for shape in shapes],
        scratch_shapes=[
            pltpu.VMEM((everyone, joint), BF),
            pltpu.VMEM((everyone, width), BF),
            pltpu.VMEM((joint, width), BF),
            pltpu.SemaphoreType.DMA((3 * wide,)),
        ],
        compiler_params=pltpu.CompilerParams(vmem_limit_bytes=40 << 20),
        cost_estimate=HIDDEN_COST,
        name="mixer_grad",
    )(lane, *kept(joined, masked))


def column_plan(member, outer, wide, cores, own, own_ff, cols, main, rest):
    z, c = member // cores, member % cores
    out = []
    for g in range(3):
        for k in range(wide):
            src = (((g * outer + z) * wide + k) * cores + c) * own
            out.append((0, src, 0, g * cols + k * own, own))
    for which in range(2):
        for k in range(wide):
            src = ((z * wide + k) * cores + c) * own_ff
            lo, hi = k * own_ff, (k + 1) * own_ff
            cut = min(hi, main)
            if cut > lo:
                out.append((1 + which, src, 1, which * main + lo, cut - lo))
            low = max(lo, main)
            if hi > low:
                at = 2 * main + which * rest + low - main
                out.append((1 + which, src + low - lo, 1, at, hi - low))
    return out


def pack_kernel(plan, tp, bases, *refs):
    arrays, packed = refs[:3], refs[3:]
    rows = arrays[0].shape[0]
    edge = packed[0].shape[1]
    for member in range(tp):
        at = slice(member * rows, (member + 1) * rows)
        for which, src, part, dst, width in plan(member):
            dst += bases[part]
            for ref, low, high in ((packed[0], 0, edge), (packed[1], edge, sum(bases))):
                start, stop = max(dst, low), min(dst + width, high)
                if start < stop:
                    there = slice(src + start - dst, src + stop - dst)
                    ref[at, start - low : stop - low] = arrays[which][:, there]


def pack_call(arrays, plan, tp, widths):
    rows = arrays[0].shape[0]
    total = sum(widths)
    edge = total // 2 // TILE * TILE
    return pl.pallas_call(
        functools.partial(pack_kernel, plan, tp, (0, widths[0], total - widths[0])),
        in_specs=[HELD] * 3,
        out_specs=[HELD] * 2,
        out_shape=[jax.ShapeDtypeStruct((tp * rows, w), BF) for w in (edge, total - edge)],
        compiler_params=pltpu.CompilerParams(vmem_limit_bytes=32 << 20),
        name="pack_columns",
    )(*arrays)


def unpack_kernel(plan, tp, part, *refs):
    packed, outs = refs[0], refs[1:]
    rows = outs[0].shape[0]
    for member in range(tp):
        at = slice(member * rows, (member + 1) * rows)
        for which, src, source, dst, width in plan(member):
            if source == part:
                out = outs[which - part]
                out[:, src : src + width] = packed[at, dst : dst + width].astype(F32)


def unpack_call(packed, part, plan, tp, widths):
    rows = packed.shape[0] // tp
    return pl.pallas_call(
        functools.partial(unpack_kernel, plan, tp, part),
        in_specs=[HELD],
        out_specs=[HELD] * len(widths),
        out_shape=[jax.ShapeDtypeStruct((rows, width), F32) for width in widths],
        compiler_params=pltpu.CompilerParams(vmem_limit_bytes=32 << 20),
        cost_estimate=HIDDEN_COST,
        name="unpack_columns",
    )(packed)


def join_kernel(count, *refs):
    ins, out, sem = refs[:count], refs[count], refs[count + 1]
    copies, at = [], 0
    for i, ref in enumerate(ins):
        size = ref.shape[0]
        copies.append(pltpu.make_async_copy(ref, out.at[pl.ds(at, size), :], sem.at[i]))
        at += size
    for copy in copies:
        copy.start()
    for copy in copies:
        copy.wait()


def join_call(arrays):
    count = len(arrays)
    rows, width = sum(array.shape[0] for array in arrays), arrays[0].shape[1]
    return pl.pallas_call(
        functools.partial(join_kernel, count),
        in_specs=[pl.BlockSpec(memory_space=pl.ANY)] * count,
        out_specs=pl.BlockSpec(memory_space=pltpu.VMEM),
        out_shape=jax.ShapeDtypeStruct((rows, width), BF),
        scratch_shapes=[pltpu.SemaphoreType.DMA((count,))],
        compiler_params=pltpu.CompilerParams(vmem_limit_bytes=16 << 20),
        name="join_rows",
    )(*arrays)


def row_spans(wide, own, own_ff, cut, lane, halves, whole):
    spans = []
    base = wide * own
    for j in range(wide):
        spot = lax.bitwise_xor(lane, j)
        down = pl.multiple_of(base + spot * own_ff, 16)
        down_low = pl.multiple_of(base + spot * own_ff + cut, 16)
        out = pl.multiple_of(spot * own, 16)
        low, high = halves[2 * j : 2 * j + 2]
        rest = own_ff - cut
        spans.append((low, whole.at[pl.ds(down, cut), :]))
        spans.append((high.at[pl.ds(0, rest), :], whole.at[pl.ds(down_low, rest), :]))
        spans.append((high.at[pl.ds(rest, own), :], whole.at[pl.ds(out, own), :]))
    return spans


def run_copies(pairs, sem):
    copies = [pltpu.make_async_copy(src, dst, sem.at[i]) for i, (src, dst) in enumerate(pairs)]
    for copy in copies:
        copy.start()
    for copy in copies:
        copy.wait()


def place_call(lane, halves, wide, own, own_ff, cut):
    width = halves[0].shape[1]

    def kernel(lane_ref, *refs):
        ins, out, sem = refs[:-2], refs[-2], refs[-1]
        run_copies(row_spans(wide, own, own_ff, cut, lane_ref[0], ins, out), sem)

    return pl.pallas_call(
        kernel,
        in_specs=[pl.BlockSpec(memory_space=pltpu.SMEM)]
        + [pl.BlockSpec(memory_space=pl.ANY)] * len(halves),
        out_specs=pl.BlockSpec(memory_space=pltpu.VMEM),
        out_shape=jax.ShapeDtypeStruct((wide * (own + own_ff), width), BF),
        scratch_shapes=[pltpu.SemaphoreType.DMA((3 * wide,))],
        compiler_params=pltpu.CompilerParams(vmem_limit_bytes=16 << 20),
        name="place_rows",
    )(lane, *halves)


def mixer_product(joined, masked):
    return lax.dot_general(joined, masked, CONTRACT_ROWS, preferred_element_type=F32).astype(BF)


class Plain:
    def __init__(self, outer, inner):
        self.tp, self.wide, self.cores, self.outer = outer, inner, 1, outer
        self.member = lax.axis_index("dp")
        self.token_axes, self.token_groups = "dp", None
        self.weight_axes, self.weight_groups = "fsdp", None

    def gather_tokens(self, block):
        return lax.all_gather(
            block, self.token_axes, axis=0, tiled=True, axis_index_groups=self.token_groups
        )

    def scatter_tokens(self, part):
        return lax.psum_scatter(
            part.astype(BF),
            self.token_axes,
            scatter_dimension=0,
            tiled=True,
            axis_index_groups=self.token_groups,
        ).astype(F32)

    def exchange(self, part):
        return lax.all_to_all(
            part,
            self.token_axes,
            split_axis=0,
            concat_axis=0,
            tiled=True,
            axis_index_groups=self.token_groups,
        )

    def gather_weights(self, block):
        return lax.all_gather(
            block, self.weight_axes, axis=0, tiled=True, axis_index_groups=self.weight_groups
        )

    def scatter_weights(self, part):
        return lax.psum_scatter(
            part,
            self.weight_axes,
            scatter_dimension=0,
            tiled=True,
            axis_index_groups=self.weight_groups,
        )

    def inputs(self, packed, w_out, w_down, normed, masked, lengths, make_tables):
        mixer = jnp.concatenate([self.gather_weights(w) for w in (w_out, w_down)], axis=0)
        entry = [self.gather_weights(self.exchange(part)) for part in packed]
        tokens = [self.gather_tokens(block) for block in (normed, masked)]
        lengths = lax.all_gather(lengths, "dp", axis=0, tiled=True)
        return entry, mixer, tokens[0], tokens[1], make_tables(lengths)

    def outputs(self, joined, masked, branch, back_call, tail, normed, own, own_ff):
        cols = self.wide * own
        part = mixer_product(joined, masked)
        grads = [self.scatter_weights(p).astype(F32) for p in (part[:cols], part[cols:])]
        grad_qkv, grad_ff, norm, bias_part = back_call(masked)
        parts = []
        for grad in (grad_qkv, grad_ff):
            part = lax.dot_general(normed, grad, CONTRACT_ROWS, preferred_element_type=F32)
            parts.append(self.scatter_weights(part.astype(BF)))
        norm, branch = self.scatter_tokens(norm), self.scatter_tokens(branch)
        part_qkv, part_ff = [self.exchange(part) for part in parts]
        grad_tokens, stats = tail(norm, bias_part)
        stats = self.scatter_stats(stats)
        return grads[0], grads[1], part_qkv, part_ff, branch, grad_tokens, stats

    def relative(self, blocks, axis):
        return blocks

    def scatter_stats(self, stats):
        parts = lax.all_to_all(stats, AXES, split_axis=0, concat_axis=0, tiled=True)
        return jnp.sum(parts, axis=0)


class Linked(Plain):
    def __init__(self, outer, inner):
        self.outer, self.cores, self.wide = outer, 2, inner // 2
        self.tp = outer * 2
        flat = lax.axis_index("fsdp")
        self.lane = flat // 2
        self.member = lax.axis_index("dp") * 2 + lax.rem(flat, 2)
        spots = [
            [[(z * self.wide + k) * 2 + c for c in range(2)] for k in range(self.wide)]
            for z in range(outer)
        ]
        self.token_axes = self.weight_axes = AXES
        self.token_groups = [
            [spots[z][k][c] for z in range(outer) for c in range(2)] for k in range(self.wide)
        ]
        self.weight_groups = [
            [spots[z][k][c] for k in range(self.wide)] for z in range(outer) for c in range(2)
        ]
        self.spots = spots
        self.lane_index = self.lane.astype(jnp.int32).reshape(1)

    def send(self, value, step=0, dz=0, dc=0):
        pairs = [
            (self.spots[z][k][c], self.spots[z ^ dz][k ^ step][c ^ dc])
            for z in range(self.outer)
            for k in range(self.wide)
            for c in range(2)
        ]
        return lax.ppermute(value, AXES, pairs)

    def gather_lengths(self, lengths):
        parts = [lengths] + [self.send(lengths, dz=dz) for dz in range(1, self.outer)]
        return jnp.concatenate(parts, axis=0)

    def order_lengths(self, mine, other):
        both = jnp.stack([mine, other], axis=1).reshape(self.tp, -1)
        spot = lax.bitwise_xor(jnp.arange(self.tp, dtype=jnp.int32), self.member)
        pick = spot[:, None] == jnp.arange(self.tp, dtype=jnp.int32)[None, :]
        return jnp.sum(jnp.where(pick[:, :, None], both[None], 0), axis=1)

    def inputs(self, packed, w_out, w_down, normed, masked, lengths, make_tables):
        own, own_ff = w_out.shape[0], w_down.shape[0]
        cut = own_ff // 32 * 16 + 32
        half = packed[0].shape[0] // 2
        rows, left, right, lengths = tie(join_call([w_down, w_out]), *packed, lengths)
        mix_x, mix_y = self.send(rows, 1), self.send(rows, 2)
        lengths = self.gather_lengths(lengths)
        left = self.exchange(left)
        left, right, mix_x, mix_y = tie(left, right, mix_x, mix_y)
        left_x, left_y = self.send(left, 1), self.send(left, 2)
        right = self.exchange(right)
        halves = [part for b in (rows, mix_x, mix_y) for part in (b[:cut], b[cut:])]
        right, left_x, left_y, normed, masked, lengths, *halves = tie(
            right, left_x, left_y, normed, masked, lengths, *halves
        )
        normed_all, masked_all = self.gather_tokens(normed), self.gather_tokens(masked)
        right_x, right_y = self.send(right, 1), self.send(right, 2)
        mix_low, mix_high = self.send(halves[2], 2), self.send(halves[5], 1)
        left_low, left_high = self.send(left_x[:half], 2), self.send(left_y[half:], 1)
        tables = make_tables(self.order_lengths(lengths, self.send(lengths, dc=1)))
        halves += [mix_low, mix_high]
        mixer = place_call(self.lane_index, halves, self.wide, own, own_ff, cut)
        right_x, right_y, left_low, left_high, mixer, *tables = tie(
            right_x, right_y, left_low, left_high, *kept(mixer, *tables)
        )
        right_low, right_high = self.send(right_x[:half], 2), self.send(right_y[half:], 1)
        entry = [left, left_x, left_y, left_low, left_high]
        entry += [right, right_x, right_y, right_low, right_high]
        return entry, mixer, normed_all, masked_all, tables

    def first_sends(self, to_x, to_y):
        return self.send(to_x, 1), self.send(to_y, 2)

    def last_sends(self, got, x_high, y_low):
        from_x, from_y = got
        low, high = from_x[: y_low.shape[0]], from_y[: x_high.shape[0]]
        return (
            self.send((x_high.astype(F32) + high.astype(F32)).astype(BF), 1),
            self.send((y_low.astype(F32) + low.astype(F32)).astype(BF), 2),
        )

    def lane_sum(self, own_low, own_high, first, last):
        low = own_low.astype(F32) + first[0][own_low.shape[0] :].astype(F32)
        high = own_high.astype(F32) + first[1][own_high.shape[0] :].astype(F32)
        return low + last[1].astype(F32), high + last[0].astype(F32)

    def outputs(self, joined, masked, branch, back_call, tail, normed, own, own_ff):
        cut = own_ff // 32 * 16 + 32
        rest = own_ff - cut
        size = normed.shape[1] // self.wide // 2
        first, last = ((6, 2), (7, 5)), ((3,), (4,), (0,), (1,))

        branch = self.scatter_tokens(branch)
        mix = mixer_grad_call(self.lane_index, joined, masked, self.wide, own, own_ff, cut)
        *mix, masked = tie(*mix, masked)
        mix_first = self.first_sends(mix[0], mix[1])
        grad_qkv, grad_ff, norm, bias_part = back_call(masked)
        *mix_first, norm, grad_ff, grad_qkv = tie(*mix_first, norm, grad_ff, grad_qkv)
        norm = self.scatter_tokens(norm)
        to_x, to_y = product_call(normed, grad_ff, first, size)
        to_x, to_y, grad_ff = tie(to_x, to_y, grad_ff)
        ff_first = self.first_sends(to_x, to_y)
        x_high, y_low, ff_low, ff_high = product_call(normed, grad_ff, last, size)
        ff_low, grad_qkv = tie(ff_low, grad_qkv)
        to_x, to_y = product_call(normed, grad_qkv, first, size)
        to_x, grad_qkv = tie(to_x, grad_qkv)
        qkv_x, qkv_y, qkv_low, qkv_high = product_call(normed, grad_qkv, last, size)
        branch, to_x, to_y, x_high, y_low, qkv_low, *ff_first = tie(
            branch, to_x, to_y, x_high, y_low, qkv_low, *ff_first
        )
        ff_last = self.last_sends(ff_first, x_high, y_low)
        part_ff = self.joined_sum((x_high, y_low, ff_low, ff_high), ff_first, ff_last)
        part_ff, to_x, to_y = tie(part_ff, to_x, to_y)
        qkv_first = self.first_sends(to_x, to_y)
        part_ff = self.exchange(part_ff)
        results = tail(norm, bias_part)
        *qkv_first, grad_tokens, stats = tie(*qkv_first, *results)
        qkv_last = self.last_sends(qkv_first, qkv_x, qkv_y)
        part_qkv = self.joined_sum((qkv_x, qkv_y, qkv_low, qkv_high), qkv_first, qkv_last)
        stats = self.keep(self.chip_stats(stats), 1, self.lane, self.wide, "step")
        part_ff, part_qkv, stats, *mix = tie(part_ff, part_qkv, stats, *mix_first, *mix[2:])
        part_qkv = self.exchange(part_qkv)
        mix_first, mix = mix[:2], mix[2:]
        mix_x, mix_y = add_call(mix_first, mix[0], mix[1])
        mix_last = self.send(mix_x, 1), self.send(mix_y, 2)
        stats = self.scatter_stats(stats)
        grad_w_out, grad_w_down = mixer_sum_call(mix[2], mix[3], mix_first, mix_last, own)
        return grad_w_out, grad_w_down, part_qkv, part_ff, branch, grad_tokens, stats

    def joined_sum(self, late, first, last):
        return sum_call(late[2], late[3], first, last)

    def keep(self, values, axis, place, count, name):
        pick = lambda spot: lax.dynamic_index_in_dim(values, spot, axis, keepdims=False)
        got = [self.send(pick(lax.bitwise_xor(place, j)), **{name: j}) for j in range(1, count)]
        return pick(place) + sum(got)

    def chip_stats(self, stats):
        split = stats.reshape(self.outer, self.wide, 2, -1)
        return self.keep(split, 2, lax.rem(self.member, 2), 2, "dc")

    def scatter_stats(self, split):
        return self.keep(split, 0, self.member // 2, self.outer, "dz")

    def relative(self, blocks, axis):
        shape = blocks.shape
        split = blocks.reshape(shape[:axis] + (2, 2) + shape[axis + 1 :])
        split = jnp.where(self.lane >= 2, jnp.flip(split, axis), split)
        split = jnp.where(lax.rem(self.lane, 2) == 1, jnp.flip(split, axis + 1), split)
        return split.reshape(shape)


def on_device(
    tokens, ln_gain, ln_shift, w_qkv, b_qkv, w_out, w_gate, w_up, w_down, grad_out, seq_lengths
):
    outer, inner = lax.axis_size("dp"), lax.axis_size("fsdp")
    linked = outer == 4 and inner == 8
    net = Linked(outer, inner) if linked else Plain(outer, inner)
    tp, wide, cores = net.tp, net.wide, net.cores
    rows_tok, width = tokens.shape
    own = w_qkv.shape[0]
    own_ff = w_down.shape[0]
    cols, cols_ff = wide * own, wide * own_ff
    main = cols_ff // TILE * TILE
    rest = cols_ff - main
    widths = (3 * cols, 2 * cols_ff)
    plan = lambda member: column_plan(
        member, outer, wide, cores, own, own_ff, cols, main, rest
    )

    _, valid, _ = block_terms(seq_lengths[0], rows_tok)
    keep_row = valid.astype(F32)[:, None]
    widened = tokens.astype(F32)
    centered = widened - jnp.mean(widened, axis=1, keepdims=True)
    inv_std = lax.rsqrt(jnp.mean(centered * centered, axis=1, keepdims=True) + EPS)
    scaled = centered * inv_std
    normed = (scaled * ln_gain + ln_shift).astype(BF)
    masked = (grad_out.astype(F32) * keep_row).astype(BF)

    def lanes_first(x):
        split = x.reshape(rows_tok, outer, wide, cores * own)
        return net.relative(jnp.swapaxes(split, 1, 2), 1).reshape(rows_tok, width)

    def lanes_back(x):
        split = net.relative(x.reshape(rows_tok, wide, outer, cores * own), 1)
        return jnp.swapaxes(split, 1, 2).reshape(rows_tok, width)

    lengths = seq_lengths
    arrays = [w_qkv, w_gate, w_up]

    bias = lax.dynamic_index_in_dim(
        jnp.transpose(b_qkv.reshape(3, outer, wide, cores, own), (1, 3, 0, 2, 4)).reshape(tp, -1),
        net.member,
        0,
    )
    bias = jnp.broadcast_to(bias, (8, 3 * cols))

    def make_tables(lengths):
        position, _, allowed = jax.vmap(lambda row: block_terms(row, rows_tok))(lengths)
        return [*turn_tables(position), jnp.where(allowed, 0.0, NEG), bias]

    entry, mixer, normed_all, masked_all, (cos_t, sin_t, mask, bias) = net.inputs(
        pack_call(arrays, plan, tp, widths),
        w_out,
        w_down,
        lanes_first(normed),
        masked,
        lengths,
        make_tables,
    )
    sizes = (cols, main, rest)
    joined, qkv, proj_ff, branch = forward_call(
        normed_all, bias, cos_t, sin_t, mask, entry, mixer, sizes
    )
    back_call = lambda masked: backward_call(
        masked, proj_ff, qkv, cos_t, sin_t, mask, mixer, entry, sizes
    )

    def tail(grad_norm, bias_part):
        grad_norm = lanes_back(grad_norm)
        lifted_grad = grad_norm * ln_gain
        grad_in = inv_std * (
            lifted_grad
            - jnp.mean(lifted_grad, axis=1, keepdims=True)
            - scaled * jnp.mean(lifted_grad * scaled, axis=1, keepdims=True)
        )
        grad_tokens = (grad_out.astype(F32) + grad_in).astype(BF)
        shards = outer * inner
        gain_part = jnp.sum(grad_norm * scaled, axis=0)
        shift_part = jnp.sum(grad_norm, axis=0)
        bias_full = lax.dynamic_update_index_in_dim(
            jnp.zeros((tp, 3 * cols), F32), bias_part[0], net.member, 0
        )
        bias_full = jnp.transpose(bias_full.reshape(outer, cores, 3, wide, own), (2, 0, 3, 1, 4))
        stats = jnp.concatenate(
            [
                gain_part.reshape(shards, own),
                shift_part.reshape(shards, own),
                bias_full.reshape(shards, 3 * own),
            ],
            axis=1,
        )
        return grad_tokens, stats

    grad_w_out, grad_w_down, part_qkv, part_ff, branch, grad_tokens, stats = net.outputs(
        joined, masked_all, branch, back_call, tail, normed_all, own, own_ff
    )
    output = (widened + keep_row * branch).astype(BF)
    grad_w_gate, grad_w_up = unpack_call(
        part_ff, 1, plan, tp, [w_gate.shape[1], w_up.shape[1]]
    )
    part_qkv, stats, grad_w_gate, grad_w_up = tie(part_qkv, stats, grad_w_gate, grad_w_up)
    (grad_w_qkv,) = unpack_call(part_qkv, 0, plan, tp, [w_qkv.shape[1]])
    return (
        output,
        grad_tokens,
        grad_w_qkv,
        grad_w_out,
        grad_w_gate,
        grad_w_up,
        grad_w_down,
        stats[:own],
        stats[own : 2 * own],
        stats[2 * own :],
    )


def solution(mesh):
    rows = P(AXES, None)
    return jax.shard_map(
        on_device,
        mesh=mesh,
        in_specs=(rows, P(), P(), rows, P(), rows, rows, rows, rows, rows, rows),
        out_specs=(rows,) * 7 + (P(AXES),) * 3,
        check_vma=False,
    )
```

```python
import functools
import math

import jax
import jax.numpy as jnp
from jax import lax
from jax.experimental import pallas as pl
from jax.experimental.pallas import tpu as pltpu
from jax.sharding import PartitionSpec as P

HD = 64
ROT = 16
EPS = 1e-05
NEG = -1e30
TILE = 128
AXES = ("dp", "fsdp")
BF = jnp.bfloat16
F32 = jnp.float32
CONTRACT_ROWS = (((0,), (0,)), ((), ()))
CONTRACT_COLS = (((1,), (1,)), ((), ()))


def block_terms(lengths_row, rows_tok):
    ends = jnp.cumsum(lengths_row)
    place = jnp.arange(rows_tok, dtype=jnp.int32)
    segment = jnp.sum((place[:, None] >= ends[None, :]).astype(jnp.int32), axis=1)
    starts = jnp.concatenate([ends - lengths_row, ends[-1:]])
    labels = jnp.arange(starts.shape[0], dtype=jnp.int32)
    begin = jnp.sum(jnp.where(segment[:, None] == labels[None, :], starts[None, :], 0), axis=1)
    position = (place - begin).astype(F32)
    valid = segment < lengths_row.shape[0]
    label_tok = jnp.where(valid, segment, lengths_row.shape[0] + place)
    allowed = (label_tok[:, None] == label_tok[None, :]) & (place[None, :] <= place[:, None])
    return (position, valid, allowed)


def turn_tables(position):
    half = ROT // 2
    freq = jnp.exp(jnp.arange(half, dtype=F32) * (-2.0 * math.log(10000.0) / ROT))
    turn = position.reshape(-1)[:, None] * freq[None, :]
    cosine, sine = jnp.cos(turn), jnp.sin(turn)
    rest = (turn.shape[0], HD - ROT)
    cos_t = jnp.concatenate([cosine, cosine, jnp.ones(rest, F32)], axis=1)
    sin_t = jnp.concatenate([-sine, sine, jnp.zeros(rest, F32)], axis=1)
    return (jnp.tile(cos_t, (1, 2)), jnp.tile(sin_t, (1, 2)))


def tie(*values):
    return lax.optimization_barrier(values)


def turned(v, cos_t, sin_t, low_half):
    partner = jnp.where(low_half, pltpu.roll(v, TILE - ROT // 2, 1), pltpu.roll(v, ROT // 2, 1))
    return v * cos_t + partner * sin_t

def stacked(v, first):
    zero = jnp.zeros_like(v)
    return jnp.concatenate([jnp.where(first, v, zero), jnp.where(first, zero, v)], axis=0)

def softmax_of(query2, keys, bias2):
    scores = lax.dot_general(query2, keys, (((1,), (1,)), ((), ())), preferred_element_type=F32)
    scores = scores * 0.125 + bias2
    lifted = jnp.exp(scores - jnp.max(scores, axis=1, keepdims=True))
    return lifted / jnp.sum(lifted, axis=1, keepdims=True)

def attend_rows(cols, main, rest, at, pq_ref, pf_ref, bias_ref, tables, joined_ref, qkv_ref):
    cos_t, sin_t, bias2, first, low_half = tables
    size = cos_t.shape[0]
    rows = slice(at, at + size)
    for pair in range(cols // TILE):
        places = [g * cols + pair * TILE for g in range(3)]
        query, keys, values = (
            pq_ref[rows, p : p + TILE] + bias_ref[0:1, p : p + TILE] for p in places
        )
        query = turned(query, cos_t, sin_t, low_half).astype(BF)
        keys = turned(keys, cos_t, sin_t, low_half).astype(BF)
        values = values.astype(BF)
        for p, v in zip(places, (query, keys, values)):
            qkv_ref[rows, p : p + TILE] = v
        probs = softmax_of(stacked(query, first), keys, bias2).astype(BF)
        mixed = jnp.dot(probs, values, preferred_element_type=F32)
        joined_ref[rows, pair * TILE : (pair + 1) * TILE] = jnp.where(
            first, mixed[:size], mixed[size:]
        ).astype(BF)
    for j in range(main // TILE):
        gate = pf_ref[rows, j * TILE : (j + 1) * TILE]
        up = pf_ref[rows, main + j * TILE : main + (j + 1) * TILE]
        hid = gate * jax.nn.sigmoid(gate) * up
        joined_ref[rows, cols + j * TILE : cols + (j + 1) * TILE] = hid.astype(BF)
    if rest:
        tail = pf_ref[rows, 2 * main :]
        up = pltpu.roll(tail, rest, 1)
        hid = tail * jax.nn.sigmoid(tail) * up
        joined_ref[rows, cols + main :] = hid[:, :rest].astype(BF)


def attend_back_rows(cols, main, rest, at, pf_ref, back_ref, qkv_ref, tables, gq_ref, gf_ref, sum_ref):
    cos_t, sin_t, bias2, first, low_half = tables
    size = cos_t.shape[0]
    rows = slice(at, at + size)
    across = (((0,), (0,)), ((), ()))
    for pair in range(cols // TILE):
        places = [g * cols + pair * TILE for g in range(3)]
        query, keys, values = (qkv_ref[rows, p : p + TILE] for p in places)
        query2 = stacked(query, first)
        mixed2 = stacked(back_ref[rows, pair * TILE : (pair + 1) * TILE].astype(BF), first)
        probs = softmax_of(query2, keys, bias2)
        grad_probs = lax.dot_general(
            mixed2, values, (((1,), (1,)), ((), ())), preferred_element_type=F32
        )
        inner = jnp.sum(probs * grad_probs, axis=1, keepdims=True)
        grad_scores = (probs * (grad_probs - inner)).astype(BF)
        gq = jnp.dot(grad_scores, keys, preferred_element_type=F32)
        gq = jnp.where(first, gq[:size], gq[size:]) * 0.125
        gk = lax.dot_general(grad_scores, query2, across, preferred_element_type=F32) * 0.125
        gv = lax.dot_general(probs.astype(BF), mixed2, across, preferred_element_type=F32)
        gq = turned(gq, cos_t, -sin_t, low_half)
        gk = turned(gk, cos_t, -sin_t, low_half)
        for p, v in zip(places, (gq, gk, gv)):
            low = v.astype(BF)
            gq_ref[rows, p : p + TILE] = low
            sum_ref[0:1, p : p + TILE] += jnp.sum(low.astype(F32), axis=0, keepdims=True)

    def gates(gate, up, grad_hid):
        sigma = jax.nn.sigmoid(gate)
        slope = sigma * (1.0 + gate * (1.0 - sigma))
        return (grad_hid * up * slope, grad_hid * (gate * sigma))

    for j in range(main // TILE):
        p, q = j * TILE, main + j * TILE
        grad_hid = back_ref[rows, cols + j * TILE : cols + (j + 1) * TILE]
        gg, gu = gates(pf_ref[rows, p : p + TILE], pf_ref[rows, q : q + TILE], grad_hid)
        gf_ref[rows, p : p + TILE] = gg.astype(BF)
        gf_ref[rows, q : q + TILE] = gu.astype(BF)
    if rest:
        tail = pf_ref[rows, 2 * main :]
        short = back_ref[rows, cols + main :]
        grad_hid = jnp.concatenate([short, jnp.zeros_like(short)], axis=1)
        gg, gu = gates(tail, pltpu.roll(tail, rest, 1), grad_hid)
        lane = lax.broadcasted_iota(jnp.int32, (size, TILE), 1)
        both = jnp.where(lane < rest, gg, pltpu.roll(gu, rest, 1))
        gf_ref[rows, 2 * main :] = both.astype(BF)


def block_tables(cos_ref, sin_ref, mask_ref, block, size):
    lane = lax.broadcasted_iota(jnp.int32, (size, TILE), 1)
    rows = slice(block * size, (block + 1) * size)
    mask = mask_ref[block]
    return (
        cos_ref[rows, :],
        sin_ref[rows, :],
        jnp.concatenate([mask, mask], axis=0),
        lane < HD,
        lane % HD < ROT // 2,
    )


def stack_copies(pieces, whole, sem, start):
    copies, count = [], len(pieces) // 2
    edge = pieces[0].shape[1]
    for group, columns in enumerate((pl.ds(0, edge), pl.ds(edge, whole.shape[1] - edge))):
        at = 0
        for i in range(group * count, (group + 1) * count):
            size = pieces[i].shape[0]
            dst = whole.at[pl.ds(at, size), columns]
            copies.append(pltpu.make_async_copy(pieces[i], dst, sem.at[start + i]))
            at += size
    return copies


def forward_kernel(sizes, count, block, *refs):
    cols, main, rest = sizes
    normed_ref, bias_ref, cos_ref, sin_ref, mask_ref = refs[:5]
    pieces, mixer_any = refs[5 : 5 + count], refs[5 + count]
    joined_ref, qkv_ref, pf_ref, branch_ref = refs[6 + count : 10 + count]
    entry, wm, pq, sem = refs[10 + count :]
    groups = [
        stack_copies(pieces, entry, sem, 0),
        [pltpu.make_async_copy(mixer_any, wm, sem.at[count])],
    ]
    opening = pl.program_id(0) == 0

    @pl.when(opening)
    def _():
        for group in groups:
            for copy in group:
                copy.start()

    def arrive(group):
        @pl.when(opening)
        def _():
            for copy in groups[group]:
                copy.wait()

    normed = normed_ref[...]
    arrive(0)
    pq[...] = jnp.dot(normed, entry[:, : 3 * cols], preferred_element_type=F32)
    pf_ref[...] = jnp.dot(normed, entry[:, 3 * cols :], preferred_element_type=F32)
    for i in range(normed.shape[0] // block):
        tables = block_tables(cos_ref, sin_ref, mask_ref, i, block)
        attend_rows(
            cols, main, rest, i * block, pq, pf_ref, bias_ref, tables, joined_ref, qkv_ref
        )
    arrive(1)
    branch = jnp.dot(joined_ref[...], wm[...], preferred_element_type=F32)
    branch_ref[...] = branch.astype(BF)


def backward_kernel(sizes, count, block, *refs):
    cols, main, rest = sizes
    masked_ref, pf_ref, qkv_ref, cos_ref, sin_ref, mask_ref, mixer_any = refs[:7]
    pieces = refs[7 : 7 + count]
    gq_ref, gf_ref, norm_ref, sum_ref = refs[7 + count : 11 + count]
    wm, entry, back, sem = refs[11 + count :]
    mixer_copy = pltpu.make_async_copy(mixer_any, wm, sem.at[count])
    copies = stack_copies(pieces, entry, sem, 0)
    opening = pl.program_id(0) == 0

    @pl.when(opening)
    def _():
        mixer_copy.start()
        for copy in copies:
            copy.start()
        sum_ref[...] = jnp.zeros_like(sum_ref)
        mixer_copy.wait()

    back[...] = lax.dot_general(
        masked_ref[...], wm[...], CONTRACT_COLS, preferred_element_type=F32
    )
    for i in range(masked_ref.shape[0] // block):
        tables = block_tables(cos_ref, sin_ref, mask_ref, i, block)
        attend_back_rows(
            cols, main, rest, i * block, pf_ref, back, qkv_ref, tables, gq_ref, gf_ref, sum_ref
        )

    @pl.when(opening)
    def _():
        for copy in copies:
            copy.wait()

    cut = 3 * cols
    total = lax.dot_general(
        gq_ref[...], entry[:, :cut], CONTRACT_COLS, preferred_element_type=F32
    )
    total += lax.dot_general(
        gf_ref[...], entry[:, cut:], CONTRACT_COLS, preferred_element_type=F32
    )
    norm_ref[...] = total.astype(BF)


STEP = 256
HIDDEN_COST = pl.CostEstimate(flops=1, bytes_accessed=1, transcendentals=0)


def row_spec(width, rows=STEP):
    return pl.BlockSpec((rows, width), lambda i: (i, 0))


ANYWHERE = pl.BlockSpec(memory_space=pl.ANY)
HELD = pl.BlockSpec(memory_space=pltpu.VMEM)


def kept(*arrays):
    return [pltpu.with_memory_space_constraint(array, pltpu.HBM) for array in arrays]


def stepping(limit):
    return pltpu.CompilerParams(
        dimension_semantics=("arbitrary",), vmem_limit_bytes=limit << 20
    )


def forward_call(normed, bias, cos_t, sin_t, mask, pieces, mixer, sizes):
    cols, main, rest = sizes
    everyone, width = normed.shape
    block = mask.shape[1]
    count = len(pieces)
    joint = cols + main + rest
    return pl.pallas_call(
        functools.partial(forward_kernel, sizes, count, block),
        grid=(everyone // STEP,),
        in_specs=[
            row_spec(width),
            pl.BlockSpec((8, 3 * cols), lambda i: (0, 0)),
            row_spec(TILE),
            row_spec(TILE),
            pl.BlockSpec((STEP // block, block, block), lambda i: (i, 0, 0)),
        ]
        + [ANYWHERE] * (count + 1),
        out_specs=[
            row_spec(joint),
            row_spec(3 * cols),
            row_spec(2 * (main + rest)),
            row_spec(width),
        ],
        out_shape=[
            pltpu.HBM((everyone, joint), BF),
            pltpu.HBM((everyone, 3 * cols), BF),
            pltpu.HBM((everyone, 2 * (main + rest)), F32),
            pltpu.HBM((everyone, width), BF),
        ],
        scratch_shapes=[
            pltpu.VMEM((width, 3 * cols + 2 * (main + rest)), BF),
            pltpu.VMEM((joint, width), BF),
            pltpu.VMEM((STEP, 3 * cols), F32),
            pltpu.SemaphoreType.DMA((count + 1,)),
        ],
        compiler_params=stepping(36),
        cost_estimate=HIDDEN_COST,
        name="forward",
    )(*kept(normed, bias, cos_t, sin_t, mask, *pieces, mixer))


def backward_call(masked, pf, qkv, cos_t, sin_t, mask, mixer, pieces, sizes):
    cols, main, rest = sizes
    everyone, width = masked.shape
    block = mask.shape[1]
    count = len(pieces)
    joint = cols + main + rest
    total = 3 * cols + 2 * (main + rest)
    return pl.pallas_call(
        functools.partial(backward_kernel, sizes, count, block),
        grid=(everyone // STEP,),
        in_specs=[
            row_spec(width),
            row_spec(2 * (main + rest)),
            row_spec(3 * cols),
            row_spec(TILE),
            row_spec(TILE),
            pl.BlockSpec((STEP // block, block, block), lambda i: (i, 0, 0)),
        ]
        + [ANYWHERE] * (count + 1),
        out_specs=[
            row_spec(3 * cols),
            row_spec(2 * (main + rest)),
            row_spec(width),
            pl.BlockSpec((8, 3 * cols), lambda i: (0, 0)),
        ],
        out_shape=[
            pltpu.HBM((everyone, 3 * cols), BF),
            pltpu.HBM((everyone, 2 * (main + rest)), BF),
            pltpu.HBM((everyone, width), BF),
            pltpu.HBM((8, 3 * cols), F32),
        ],
        scratch_shapes=[
            pltpu.VMEM((joint, width), BF),
            pltpu.VMEM((width, total), BF),
            pltpu.VMEM((STEP, joint), F32),
            pltpu.SemaphoreType.DMA((count + 1,)),
        ],
        compiler_params=stepping(36),
        cost_estimate=HIDDEN_COST,
        name="backward",
    )(*kept(masked, pf, qkv, cos_t, sin_t, mask, mixer, *pieces))


def product_call(normed, grad, groups, size):
    low, width = 0, grad.shape[1]
    slabs = [slab for group in groups for slab in group]
    places = [(g, at) for g, group in enumerate(groups) for at in range(len(group))]
    count = len(slabs)

    def kernel(table_ref, lhs_any, grad_any, *refs):
        outs, (lhs, grad, held, sem) = refs[: len(groups)], refs[len(groups) :]
        loads = [pltpu.make_async_copy(grad_any.at[:, pl.ds(low, width)], grad, sem.at[2 * count])]
        copies = []
        for i, (g, at) in enumerate(places):
            slab = pl.multiple_of(table_ref[i] * size, size)
            src = lhs_any.at[:, pl.ds(slab, size)]
            loads.append(pltpu.make_async_copy(src, lhs.at[i], sem.at[count + i]))
            dst = outs[g].at[pl.ds(at * size, size), :]
            copies.append(pltpu.make_async_copy(held.at[i], dst, sem.at[i]))
        for load in loads:
            load.start()
        loads[0].wait()

        def step(i, _):
            for j in range(count):
                pl.when(i == j)(loads[1 + j].wait)
            held[i] = lax.dot_general(
                lhs[i], grad[...], CONTRACT_ROWS, preferred_element_type=F32
            ).astype(BF)
            for j, copy in enumerate(copies):
                pl.when(i == j)(copy.start)

        lax.fori_loop(0, count, step, None)
        for copy in copies:
            copy.wait()

    everyone = normed.shape[0]
    return pl.pallas_call(
        kernel,
        in_specs=[pl.BlockSpec(memory_space=pltpu.SMEM), ANYWHERE, ANYWHERE],
        out_specs=[pl.BlockSpec(memory_space=pltpu.HBM)] * len(groups),
        out_shape=[pltpu.HBM((len(group) * size, width), BF) for group in groups],
        scratch_shapes=[
            pltpu.VMEM((count, everyone, size), BF),
            pltpu.VMEM((everyone, width), BF),
            pltpu.VMEM((count, size, width), BF),
            pltpu.SemaphoreType.DMA((2 * count + 1,)),
        ],
        compiler_params=pltpu.CompilerParams(vmem_limit_bytes=24 << 20),
        cost_estimate=HIDDEN_COST,
        name="weight_grad",
    )(jnp.array(slabs, jnp.int32), *kept(normed, grad))


def sum_kernel(own_low, own_high, from_x, from_y, last_x, last_y, out_ref):
    def total(*refs):
        return sum(ref[...].astype(F32) for ref in refs).astype(BF)

    out_ref[0] = total(own_low, from_x, last_y)
    out_ref[1] = total(own_high, from_y, last_x)


def sum_call(own_low, own_high, first, last):
    half, width = own_low.shape
    rows = half // 2
    near = pl.BlockSpec((rows, width), lambda i: (i, 0))
    second = pl.BlockSpec((rows, width), lambda i: (i + 2, 0))
    out = pl.pallas_call(
        sum_kernel,
        grid=(2,),
        in_specs=[near, near, second, second, near, near],
        out_specs=pl.BlockSpec((2, rows, width), lambda i: (0, i, 0)),
        out_shape=pltpu.HBM((2, half, width), BF),
        compiler_params=stepping(24),
        cost_estimate=HIDDEN_COST,
        name="sum_lanes",
    )(*kept(own_low, own_high, *first), *last)
    return out.reshape(2 * half, width)


def add_kernel(from_x, from_y, x_high, y_low, to_x, to_y):
    to_x[...] = (x_high[...].astype(F32) + from_y[...].astype(F32)).astype(BF)
    to_y[...] = (y_low[...].astype(F32) + from_x[...].astype(F32)).astype(BF)


def add_call(got, x_high, y_low):
    high, low = x_high.shape, y_low.shape
    block = lambda shape: pl.BlockSpec(shape, lambda i: (0, 0))
    return pl.pallas_call(
        add_kernel,
        grid=(1,),
        in_specs=[block(low), block(high), block(high), block(low)],
        out_specs=[block(high), block(low)],
        out_shape=[pltpu.HBM(high, BF), pltpu.HBM(low, BF)],
        compiler_params=stepping(24),
        cost_estimate=HIDDEN_COST,
        name="add_halves",
    )(*kept(*got, x_high, y_low))


def mixer_sum_call(own_low, own_high, first, last, own):
    (low, width), high = own_low.shape, own_high.shape[0]
    rest = high - own

    def kernel(low_ref, high_ref, x_ref, y_ref, last_x, last_y, out_ref, down_ref):
        low_sum = low_ref[...].astype(F32) + x_ref[...].astype(F32) + last_y[...].astype(F32)
        high_sum = high_ref[...].astype(F32) + y_ref[...].astype(F32) + last_x[...].astype(F32)
        down_ref[:low, :] = low_sum
        down_ref[low:, :] = high_sum[:rest]
        out_ref[...] = high_sum[rest:]

    block = lambda rows, at=0: pl.BlockSpec((rows, width), lambda i: (at, 0))
    return pl.pallas_call(
        kernel,
        grid=(1,),
        in_specs=[block(low), block(high), block(low, 1), block(high, 1), block(high), block(low)],
        out_specs=[block(own), block(low + rest)],
        out_shape=[pltpu.HBM((own, width), F32), pltpu.HBM((low + rest, width), F32)],
        compiler_params=stepping(24),
        cost_estimate=HIDDEN_COST,
        name="sum_mixer",
    )(*kept(own_low, own_high, *first), *last)


def mixer_grad_call(lane, joined, masked, wide, own, own_ff, cut):
    everyone, joint = joined.shape
    width = masked.shape[1]
    rest = own + own_ff - cut

    def kernel(lane_ref, joined_any, masked_any, *refs):
        to_x, to_y, x_high, y_low, own_low, own_high, joined_ref, masked_ref, whole, sem = refs
        run_copies([(joined_any, joined_ref), (masked_any, masked_ref)], sem)
        masked = masked_ref[...]

        def product(at, size):
            whole[pl.ds(at, size), :] = lax.dot_general(
                joined_ref[:, pl.ds(at, size)],
                masked,
                CONTRACT_ROWS,
                preferred_element_type=F32,
            ).astype(BF)

        lax.fori_loop(
            0, joint // STEP, lambda i, _: product(pl.multiple_of(i * STEP, STEP), STEP), None
        )
        if joint % STEP:
            product(joint // STEP * STEP, joint % STEP)
        halves = [
            own_low,
            own_high,
            to_x.at[pl.ds(cut, cut), :],
            x_high,
            y_low,
            to_y.at[pl.ds(rest, rest), :],
            to_x.at[pl.ds(0, cut), :],
            to_y.at[pl.ds(0, rest), :],
        ]
        pairs = row_spans(wide, own, own_ff, cut, lane_ref[0], halves, whole)
        run_copies([(there, here) for here, there in pairs], sem)

    shapes = [(size, width) for size in (2 * cut, 2 * rest, rest, cut, cut, rest)]
    return pl.pallas_call(
        kernel,
        in_specs=[pl.BlockSpec(memory_space=pltpu.SMEM), ANYWHERE, ANYWHERE],
        out_specs=[pl.BlockSpec(memory_space=pltpu.HBM)] * len(shapes),
        out_shape=[pltpu.HBM(shape, BF) for shape in shapes],
        scratch_shapes=[
            pltpu.VMEM((everyone, joint), BF),
            pltpu.VMEM((everyone, width), BF),
            pltpu.VMEM((joint, width), BF),
            pltpu.SemaphoreType.DMA((3 * wide,)),
        ],
        compiler_params=pltpu.CompilerParams(vmem_limit_bytes=40 << 20),
        cost_estimate=HIDDEN_COST,
        name="mixer_grad",
    )(lane, *kept(joined, masked))


def column_plan(member, outer, wide, cores, own, own_ff, cols, main, rest):
    z, c = member // cores, member % cores
    out = []
    for g in range(3):
        for k in range(wide):
            src = (((g * outer + z) * wide + k) * cores + c) * own
            out.append((0, src, 0, g * cols + k * own, own))
    for which in range(2):
        for k in range(wide):
            src = ((z * wide + k) * cores + c) * own_ff
            lo, hi = k * own_ff, (k + 1) * own_ff
            cut = min(hi, main)
            if cut > lo:
                out.append((1 + which, src, 1, which * main + lo, cut - lo))
            low = max(lo, main)
            if hi > low:
                at = 2 * main + which * rest + low - main
                out.append((1 + which, src + low - lo, 1, at, hi - low))
    return out


def pack_kernel(plan, tp, bases, *refs):
    arrays, packed = refs[:3], refs[3:]
    rows = arrays[0].shape[0]
    edge = packed[0].shape[1]
    for member in range(tp):
        at = slice(member * rows, (member + 1) * rows)
        for which, src, part, dst, width in plan(member):
            dst += bases[part]
            for ref, low, high in ((packed[0], 0, edge), (packed[1], edge, sum(bases))):
                start, stop = max(dst, low), min(dst + width, high)
                if start < stop:
                    there = slice(src + start - dst, src + stop - dst)
                    ref[at, start - low : stop - low] = arrays[which][:, there]


def pack_call(arrays, plan, tp, widths):
    rows = arrays[0].shape[0]
    total = sum(widths)
    edge = total // 2 // TILE * TILE
    return pl.pallas_call(
        functools.partial(pack_kernel, plan, tp, (0, widths[0], total - widths[0])),
        in_specs=[HELD] * 3,
        out_specs=[HELD] * 2,
        out_shape=[jax.ShapeDtypeStruct((tp * rows, w), BF) for w in (edge, total - edge)],
        compiler_params=pltpu.CompilerParams(vmem_limit_bytes=32 << 20),
        name="pack_columns",
    )(*arrays)


def unpack_kernel(plan, tp, part, *refs):
    packed, outs = refs[0], refs[1:]
    rows = outs[0].shape[0]
    for member in range(tp):
        at = slice(member * rows, (member + 1) * rows)
        for which, src, source, dst, width in plan(member):
            if source == part:
                out = outs[which - part]
                out[:, src : src + width] = packed[at, dst : dst + width].astype(F32)


def unpack_call(packed, part, plan, tp, widths):
    rows = packed.shape[0] // tp
    return pl.pallas_call(
        functools.partial(unpack_kernel, plan, tp, part),
        in_specs=[HELD],
        out_specs=[HELD] * len(widths),
        out_shape=[jax.ShapeDtypeStruct((rows, width), F32) for width in widths],
        compiler_params=pltpu.CompilerParams(vmem_limit_bytes=32 << 20),
        cost_estimate=HIDDEN_COST,
        name="unpack_columns",
    )(packed)


def join_kernel(count, *refs):
    ins, out, sem = refs[:count], refs[count], refs[count + 1]
    copies, at = [], 0
    for i, ref in enumerate(ins):
        size = ref.shape[0]
        copies.append(pltpu.make_async_copy(ref, out.at[pl.ds(at, size), :], sem.at[i]))
        at += size
    for copy in copies:
        copy.start()
    for copy in copies:
        copy.wait()


def join_call(arrays):
    count = len(arrays)
    rows, width = sum(array.shape[0] for array in arrays), arrays[0].shape[1]
    return pl.pallas_call(
        functools.partial(join_kernel, count),
        in_specs=[pl.BlockSpec(memory_space=pl.ANY)] * count,
        out_specs=pl.BlockSpec(memory_space=pltpu.VMEM),
        out_shape=jax.ShapeDtypeStruct((rows, width), BF),
        scratch_shapes=[pltpu.SemaphoreType.DMA((count,))],
        compiler_params=pltpu.CompilerParams(vmem_limit_bytes=16 << 20),
        name="join_rows",
    )(*arrays)


def row_spans(wide, own, own_ff, cut, lane, halves, whole):
    spans = []
    base = wide * own
    for j in range(wide):
        spot = lax.bitwise_xor(lane, j)
        down = pl.multiple_of(base + spot * own_ff, 16)
        down_low = pl.multiple_of(base + spot * own_ff + cut, 16)
        out = pl.multiple_of(spot * own, 16)
        low, high = halves[2 * j : 2 * j + 2]
        rest = own_ff - cut
        spans.append((low, whole.at[pl.ds(down, cut), :]))
        spans.append((high.at[pl.ds(0, rest), :], whole.at[pl.ds(down_low, rest), :]))
        spans.append((high.at[pl.ds(rest, own), :], whole.at[pl.ds(out, own), :]))
    return spans


def run_copies(pairs, sem):
    copies = [pltpu.make_async_copy(src, dst, sem.at[i]) for i, (src, dst) in enumerate(pairs)]
    for copy in copies:
        copy.start()
    for copy in copies:
        copy.wait()


def place_call(lane, halves, wide, own, own_ff, cut):
    width = halves[0].shape[1]

    def kernel(lane_ref, *refs):
        ins, out, sem = refs[:-2], refs[-2], refs[-1]
        run_copies(row_spans(wide, own, own_ff, cut, lane_ref[0], ins, out), sem)

    return pl.pallas_call(
        kernel,
        in_specs=[pl.BlockSpec(memory_space=pltpu.SMEM)]
        + [pl.BlockSpec(memory_space=pl.ANY)] * len(halves),
        out_specs=pl.BlockSpec(memory_space=pltpu.VMEM),
        out_shape=jax.ShapeDtypeStruct((wide * (own + own_ff), width), BF),
        scratch_shapes=[pltpu.SemaphoreType.DMA((3 * wide,))],
        compiler_params=pltpu.CompilerParams(vmem_limit_bytes=16 << 20),
        name="place_rows",
    )(lane, *halves)


def mixer_product(joined, masked):
    return lax.dot_general(joined, masked, CONTRACT_ROWS, preferred_element_type=F32).astype(BF)


class Plain:
    def __init__(self, outer, inner):
        self.tp, self.wide, self.cores, self.outer = outer, inner, 1, outer
        self.member = lax.axis_index("dp")
        self.token_axes, self.token_groups = "dp", None
        self.weight_axes, self.weight_groups = "fsdp", None

    def gather_tokens(self, block):
        return lax.all_gather(
            block, self.token_axes, axis=0, tiled=True, axis_index_groups=self.token_groups
        )

    def scatter_tokens(self, part):
        return lax.psum_scatter(
            part.astype(BF),
            self.token_axes,
            scatter_dimension=0,
            tiled=True,
            axis_index_groups=self.token_groups,
        ).astype(F32)

    def exchange(self, part):
        return lax.all_to_all(
            part,
            self.token_axes,
            split_axis=0,
            concat_axis=0,
            tiled=True,
            axis_index_groups=self.token_groups,
        )

    def gather_weights(self, block):
        return lax.all_gather(
            block, self.weight_axes, axis=0, tiled=True, axis_index_groups=self.weight_groups
        )

    def scatter_weights(self, part):
        return lax.psum_scatter(
            part,
            self.weight_axes,
            scatter_dimension=0,
            tiled=True,
            axis_index_groups=self.weight_groups,
        )

    def inputs(self, packed, w_out, w_down, normed, masked, lengths, make_tables):
        mixer = jnp.concatenate([self.gather_weights(w) for w in (w_out, w_down)], axis=0)
        entry = [self.gather_weights(self.exchange(part)) for part in packed]
        tokens = [self.gather_tokens(block) for block in (normed, masked)]
        lengths = lax.all_gather(lengths, "dp", axis=0, tiled=True)
        return entry, mixer, tokens[0], tokens[1], make_tables(lengths)

    def outputs(self, joined, masked, branch, back_call, tail, normed, own, own_ff):
        cols = self.wide * own
        part = mixer_product(joined, masked)
        grads = [self.scatter_weights(p).astype(F32) for p in (part[:cols], part[cols:])]
        grad_qkv, grad_ff, norm, bias_part = back_call(masked)
        parts = []
        for grad in (grad_qkv, grad_ff):
            part = lax.dot_general(normed, grad, CONTRACT_ROWS, preferred_element_type=F32)
            parts.append(self.scatter_weights(part.astype(BF)))
        norm, branch = self.scatter_tokens(norm), self.scatter_tokens(branch)
        part_qkv, part_ff = [self.exchange(part) for part in parts]
        grad_tokens, stats = tail(norm, bias_part)
        stats = self.scatter_stats(stats)
        return grads[0], grads[1], part_qkv, part_ff, branch, grad_tokens, stats

    def relative(self, blocks, axis):
        return blocks

    def scatter_stats(self, stats):
        parts = lax.all_to_all(stats, AXES, split_axis=0, concat_axis=0, tiled=True)
        return jnp.sum(parts, axis=0)


class Linked(Plain):
    def __init__(self, outer, inner):
        self.outer, self.cores, self.wide = outer, 2, inner // 2
        self.tp = outer * 2
        flat = lax.axis_index("fsdp")
        self.lane = flat // 2
        self.member = lax.axis_index("dp") * 2 + lax.rem(flat, 2)
        spots = [
            [[(z * self.wide + k) * 2 + c for c in range(2)] for k in range(self.wide)]
            for z in range(outer)
        ]
        self.token_axes = self.weight_axes = AXES
        self.token_groups = [
            [spots[z][k][c] for z in range(outer) for c in range(2)] for k in range(self.wide)
        ]
        self.weight_groups = [
            [spots[z][k][c] for k in range(self.wide)] for z in range(outer) for c in range(2)
        ]
        self.spots = spots
        self.lane_index = self.lane.astype(jnp.int32).reshape(1)

    def send(self, value, step=0, dz=0, dc=0):
        pairs = [
            (self.spots[z][k][c], self.spots[z ^ dz][k ^ step][c ^ dc])
            for z in range(self.outer)
            for k in range(self.wide)
            for c in range(2)
        ]
        return lax.ppermute(value, AXES, pairs)

    def gather_lengths(self, lengths):
        parts = [lengths] + [self.send(lengths, dz=dz) for dz in range(1, self.outer)]
        return jnp.concatenate(parts, axis=0)

    def order_lengths(self, mine, other):
        both = jnp.stack([mine, other], axis=1).reshape(self.tp, -1)
        spot = lax.bitwise_xor(jnp.arange(self.tp, dtype=jnp.int32), self.member)
        pick = spot[:, None] == jnp.arange(self.tp, dtype=jnp.int32)[None, :]
        return jnp.sum(jnp.where(pick[:, :, None], both[None], 0), axis=1)

    def inputs(self, packed, w_out, w_down, normed, masked, lengths, make_tables):
        own, own_ff = w_out.shape[0], w_down.shape[0]
        cut = own_ff // 32 * 16 + 32
        half = packed[0].shape[0] // 2
        rows, left, right, lengths = tie(join_call([w_down, w_out]), *packed, lengths)
        mix_x, mix_y = self.send(rows, 1), self.send(rows, 2)
        lengths = self.gather_lengths(lengths)
        left = self.exchange(left)
        left, right, mix_x, mix_y = tie(left, right, mix_x, mix_y)
        left_x, left_y = self.send(left, 1), self.send(left, 2)
        right = self.exchange(right)
        halves = [part for b in (rows, mix_x, mix_y) for part in (b[:cut], b[cut:])]
        right, left_x, left_y, normed, masked, lengths, *halves = tie(
            right, left_x, left_y, normed, masked, lengths, *halves
        )
        normed_all, masked_all = self.gather_tokens(normed), self.gather_tokens(masked)
        right_x, right_y = self.send(right, 1), self.send(right, 2)
        mix_low, mix_high = self.send(halves[2], 2), self.send(halves[5], 1)
        left_low, left_high = self.send(left_x[:half], 2), self.send(left_y[half:], 1)
        tables = make_tables(self.order_lengths(lengths, self.send(lengths, dc=1)))
        halves += [mix_low, mix_high]
        mixer = place_call(self.lane_index, halves, self.wide, own, own_ff, cut)
        right_x, right_y, left_low, left_high, mixer, *tables = tie(
            right_x, right_y, left_low, left_high, *kept(mixer, *tables)
        )
        right_low, right_high = self.send(right_x[:half], 2), self.send(right_y[half:], 1)
        entry = [left, left_x, left_y, left_low, left_high]
        entry += [right, right_x, right_y, right_low, right_high]
        return entry, mixer, normed_all, masked_all, tables

    def first_sends(self, to_x, to_y):
        return self.send(to_x, 1), self.send(to_y, 2)

    def last_sends(self, got, x_high, y_low):
        from_x, from_y = got
        low, high = from_x[: y_low.shape[0]], from_y[: x_high.shape[0]]
        return (
            self.send((x_high.astype(F32) + high.astype(F32)).astype(BF), 1),
            self.send((y_low.astype(F32) + low.astype(F32)).astype(BF), 2),
        )

    def lane_sum(self, own_low, own_high, first, last):
        low = own_low.astype(F32) + first[0][own_low.shape[0] :].astype(F32)
        high = own_high.astype(F32) + first[1][own_high.shape[0] :].astype(F32)
        return low + last[1].astype(F32), high + last[0].astype(F32)

    def outputs(self, joined, masked, branch, back_call, tail, normed, own, own_ff):
        cut = own_ff // 32 * 16 + 32
        rest = own_ff - cut
        size = normed.shape[1] // self.wide // 2
        first, last = ((6, 2), (7, 5)), ((3,), (4,), (0,), (1,))

        branch = self.scatter_tokens(branch)
        mix = mixer_grad_call(self.lane_index, joined, masked, self.wide, own, own_ff, cut)
        *mix, masked = tie(*mix, masked)
        mix_first = self.first_sends(mix[0], mix[1])
        grad_qkv, grad_ff, norm, bias_part = back_call(masked)
        *mix_first, norm, grad_ff, grad_qkv = tie(*mix_first, norm, grad_ff, grad_qkv)
        norm = self.scatter_tokens(norm)
        to_x, to_y = product_call(normed, grad_ff, first, size)
        to_x, to_y, grad_ff = tie(to_x, to_y, grad_ff)
        ff_first = self.first_sends(to_x, to_y)
        x_high, y_low, ff_low, ff_high = product_call(normed, grad_ff, last, size)
        ff_low, grad_qkv = tie(ff_low, grad_qkv)
        to_x, to_y = product_call(normed, grad_qkv, first, size)
        to_x, grad_qkv = tie(to_x, grad_qkv)
        qkv_x, qkv_y, qkv_low, qkv_high = product_call(normed, grad_qkv, last, size)
        branch, to_x, to_y, x_high, y_low, qkv_low, *ff_first = tie(
            branch, to_x, to_y, x_high, y_low, qkv_low, *ff_first
        )
        ff_last = self.last_sends(ff_first, x_high, y_low)
        part_ff = self.joined_sum((x_high, y_low, ff_low, ff_high), ff_first, ff_last)
        part_ff, to_x, to_y = tie(part_ff, to_x, to_y)
        qkv_first = self.first_sends(to_x, to_y)
        part_ff = self.exchange(part_ff)
        results = tail(norm, bias_part)
        *qkv_first, grad_tokens, stats = tie(*qkv_first, *results)
        qkv_last = self.last_sends(qkv_first, qkv_x, qkv_y)
        part_qkv = self.joined_sum((qkv_x, qkv_y, qkv_low, qkv_high), qkv_first, qkv_last)
        stats = self.depth_stats(stats)
        part_ff, part_qkv, stats, *mix = tie(part_ff, part_qkv, stats, *mix_first, *mix[2:])
        part_qkv = self.exchange(part_qkv)
        mix_first, mix = mix[:2], mix[2:]
        mix_x, mix_y = add_call(mix_first, mix[0], mix[1])
        mix_last = self.send(mix_x, 1), self.send(mix_y, 2)
        stats = self.scatter_stats(stats)
        grad_w_out, grad_w_down = mixer_sum_call(mix[2], mix[3], mix_first, mix_last, own)
        return grad_w_out, grad_w_down, part_qkv, part_ff, branch, grad_tokens, stats

    def joined_sum(self, late, first, last):
        return sum_call(late[2], late[3], first, last)

    def keep(self, values, axis, place, count, name):
        pick = lambda spot: lax.dynamic_index_in_dim(values, spot, axis, keepdims=False)
        got = [self.send(pick(lax.bitwise_xor(place, j)), **{name: j}) for j in range(1, count)]
        return pick(place) + sum(got)

    def depth_stats(self, stats):
        split = stats.reshape(self.outer, self.wide, 2, -1)
        return self.keep(split, 0, self.member // 2, self.outer, "dz")

    def scatter_stats(self, split):
        split = self.keep(split, 0, self.lane, self.wide, "step")
        return self.keep(split, 0, lax.rem(self.member, 2), 2, "dc")

    def relative(self, blocks, axis):
        shape = blocks.shape
        split = blocks.reshape(shape[:axis] + (2, 2) + shape[axis + 1 :])
        split = jnp.where(self.lane >= 2, jnp.flip(split, axis), split)
        split = jnp.where(lax.rem(self.lane, 2) == 1, jnp.flip(split, axis + 1), split)
        return split.reshape(shape)


def on_device(
    tokens, ln_gain, ln_shift, w_qkv, b_qkv, w_out, w_gate, w_up, w_down, grad_out, seq_lengths
):
    outer, inner = lax.axis_size("dp"), lax.axis_size("fsdp")
    linked = outer == 4 and inner == 8
    net = Linked(outer, inner) if linked else Plain(outer, inner)
    tp, wide, cores = net.tp, net.wide, net.cores
    rows_tok, width = tokens.shape
    own = w_qkv.shape[0]
    own_ff = w_down.shape[0]
    cols, cols_ff = wide * own, wide * own_ff
    main = cols_ff // TILE * TILE
    rest = cols_ff - main
    widths = (3 * cols, 2 * cols_ff)
    plan = lambda member: column_plan(
        member, outer, wide, cores, own, own_ff, cols, main, rest
    )

    _, valid, _ = block_terms(seq_lengths[0], rows_tok)
    keep_row = valid.astype(F32)[:, None]
    widened = tokens.astype(F32)
    centered = widened - jnp.mean(widened, axis=1, keepdims=True)
    inv_std = lax.rsqrt(jnp.mean(centered * centered, axis=1, keepdims=True) + EPS)
    scaled = centered * inv_std
    normed = (scaled * ln_gain + ln_shift).astype(BF)
    masked = (grad_out.astype(F32) * keep_row).astype(BF)

    def lanes_first(x):
        split = x.reshape(rows_tok, outer, wide, cores * own)
        return net.relative(jnp.swapaxes(split, 1, 2), 1).reshape(rows_tok, width)

    def lanes_back(x):
        split = net.relative(x.reshape(rows_tok, wide, outer, cores * own), 1)
        return jnp.swapaxes(split, 1, 2).reshape(rows_tok, width)

    lengths = seq_lengths
    arrays = [w_qkv, w_gate, w_up]

    bias = lax.dynamic_index_in_dim(
        jnp.transpose(b_qkv.reshape(3, outer, wide, cores, own), (1, 3, 0, 2, 4)).reshape(tp, -1),
        net.member,
        0,
    )
    bias = jnp.broadcast_to(bias, (8, 3 * cols))

    def make_tables(lengths):
        position, _, allowed = jax.vmap(lambda row: block_terms(row, rows_tok))(lengths)
        return [*turn_tables(position), jnp.where(allowed, 0.0, NEG), bias]

    entry, mixer, normed_all, masked_all, (cos_t, sin_t, mask, bias) = net.inputs(
        pack_call(arrays, plan, tp, widths),
        w_out,
        w_down,
        lanes_first(normed),
        masked,
        lengths,
        make_tables,
    )
    sizes = (cols, main, rest)
    joined, qkv, proj_ff, branch = forward_call(
        normed_all, bias, cos_t, sin_t, mask, entry, mixer, sizes
    )
    back_call = lambda masked: backward_call(
        masked, proj_ff, qkv, cos_t, sin_t, mask, mixer, entry, sizes
    )

    def tail(grad_norm, bias_part):
        grad_norm = lanes_back(grad_norm)
        lifted_grad = grad_norm * ln_gain
        grad_in = inv_std * (
            lifted_grad
            - jnp.mean(lifted_grad, axis=1, keepdims=True)
            - scaled * jnp.mean(lifted_grad * scaled, axis=1, keepdims=True)
        )
        grad_tokens = (grad_out.astype(F32) + grad_in).astype(BF)
        shards = outer * inner
        gain_part = jnp.sum(grad_norm * scaled, axis=0)
        shift_part = jnp.sum(grad_norm, axis=0)
        bias_full = lax.dynamic_update_index_in_dim(
            jnp.zeros((tp, 3 * cols), F32), bias_part[0], net.member, 0
        )
        bias_full = jnp.transpose(bias_full.reshape(outer, cores, 3, wide, own), (2, 0, 3, 1, 4))
        stats = jnp.concatenate(
            [
                gain_part.reshape(shards, own),
                shift_part.reshape(shards, own),
                bias_full.reshape(shards, 3 * own),
            ],
            axis=1,
        )
        return grad_tokens, stats

    grad_w_out, grad_w_down, part_qkv, part_ff, branch, grad_tokens, stats = net.outputs(
        joined, masked_all, branch, back_call, tail, normed_all, own, own_ff
    )
    output = (widened + keep_row * branch).astype(BF)
    grad_w_gate, grad_w_up = unpack_call(
        part_ff, 1, plan, tp, [w_gate.shape[1], w_up.shape[1]]
    )
    part_qkv, stats, grad_w_gate, grad_w_up = tie(part_qkv, stats, grad_w_gate, grad_w_up)
    (grad_w_qkv,) = unpack_call(part_qkv, 0, plan, tp, [w_qkv.shape[1]])
    return (
        output,
        grad_tokens,
        grad_w_qkv,
        grad_w_out,
        grad_w_gate,
        grad_w_up,
        grad_w_down,
        stats[:own],
        stats[own : 2 * own],
        stats[2 * own :],
    )


def solution(mesh):
    rows = P(AXES, None)
    return jax.shard_map(
        on_device,
        mesh=mesh,
        in_specs=(rows, P(), P(), rows, P(), rows, rows, rows, rows, rows, rows),
        out_specs=(rows,) * 7 + (P(AXES),) * 3,
        check_vma=False,
    )
```

```python
import functools
import math

import jax
import jax.numpy as jnp
from jax import lax
from jax.experimental import pallas as pl
from jax.experimental.pallas import tpu as pltpu
from jax.sharding import PartitionSpec as P

HD = 64
ROT = 16
EPS = 1e-05
NEG = -1e30
TILE = 128
AXES = ("dp", "fsdp")
BF = jnp.bfloat16
F32 = jnp.float32
CONTRACT_ROWS = (((0,), (0,)), ((), ()))
CONTRACT_COLS = (((1,), (1,)), ((), ()))


def block_terms(lengths_row, rows_tok):
    ends = jnp.cumsum(lengths_row)
    place = jnp.arange(rows_tok, dtype=jnp.int32)
    segment = jnp.sum((place[:, None] >= ends[None, :]).astype(jnp.int32), axis=1)
    starts = jnp.concatenate([ends - lengths_row, ends[-1:]])
    labels = jnp.arange(starts.shape[0], dtype=jnp.int32)
    begin = jnp.sum(jnp.where(segment[:, None] == labels[None, :], starts[None, :], 0), axis=1)
    position = (place - begin).astype(F32)
    valid = segment < lengths_row.shape[0]
    label_tok = jnp.where(valid, segment, lengths_row.shape[0] + place)
    allowed = (label_tok[:, None] == label_tok[None, :]) & (place[None, :] <= place[:, None])
    return (position, valid, allowed)


def turn_tables(position):
    half = ROT // 2
    freq = jnp.exp(jnp.arange(half, dtype=F32) * (-2.0 * math.log(10000.0) / ROT))
    turn = position.reshape(-1)[:, None] * freq[None, :]
    cosine, sine = jnp.cos(turn), jnp.sin(turn)
    rest = (turn.shape[0], HD - ROT)
    cos_t = jnp.concatenate([cosine, cosine, jnp.ones(rest, F32)], axis=1)
    sin_t = jnp.concatenate([-sine, sine, jnp.zeros(rest, F32)], axis=1)
    return (jnp.tile(cos_t, (1, 2)), jnp.tile(sin_t, (1, 2)))


def tie(*values):
    return lax.optimization_barrier(values)


def turned(v, cos_t, sin_t, low_half):
    partner = jnp.where(low_half, pltpu.roll(v, TILE - ROT // 2, 1), pltpu.roll(v, ROT // 2, 1))
    return v * cos_t + partner * sin_t

def stacked(v, first):
    zero = jnp.zeros_like(v)
    return jnp.concatenate([jnp.where(first, v, zero), jnp.where(first, zero, v)], axis=0)

def softmax_of(query2, keys, bias2):
    scores = lax.dot_general(query2, keys, (((1,), (1,)), ((), ())), preferred_element_type=F32)
    scores = scores * 0.125 + bias2
    lifted = jnp.exp(scores - jnp.max(scores, axis=1, keepdims=True))
    return lifted / jnp.sum(lifted, axis=1, keepdims=True)

def attend_rows(cols, main, rest, at, pq_ref, pf_ref, bias_ref, tables, joined_ref, qkv_ref):
    cos_t, sin_t, bias2, first, low_half = tables
    size = cos_t.shape[0]
    rows = slice(at, at + size)
    for pair in range(cols // TILE):
        places = [g * cols + pair * TILE for g in range(3)]
        query, keys, values = (
            pq_ref[rows, p : p + TILE] + bias_ref[0:1, p : p + TILE] for p in places
        )
        query = turned(query, cos_t, sin_t, low_half).astype(BF)
        keys = turned(keys, cos_t, sin_t, low_half).astype(BF)
        values = values.astype(BF)
        for p, v in zip(places, (query, keys, values)):
            qkv_ref[rows, p : p + TILE] = v
        probs = softmax_of(stacked(query, first), keys, bias2).astype(BF)
        mixed = jnp.dot(probs, values, preferred_element_type=F32)
        joined_ref[rows, pair * TILE : (pair + 1) * TILE] = jnp.where(
            first, mixed[:size], mixed[size:]
        ).astype(BF)
    for j in range(main // TILE):
        gate = pf_ref[rows, j * TILE : (j + 1) * TILE]
        up = pf_ref[rows, main + j * TILE : main + (j + 1) * TILE]
        hid = gate * jax.nn.sigmoid(gate) * up
        joined_ref[rows, cols + j * TILE : cols + (j + 1) * TILE] = hid.astype(BF)
    if rest:
        tail = pf_ref[rows, 2 * main :]
        up = pltpu.roll(tail, rest, 1)
        hid = tail * jax.nn.sigmoid(tail) * up
        joined_ref[rows, cols + main :] = hid[:, :rest].astype(BF)


def attend_back_rows(cols, main, rest, at, pf_ref, back_ref, qkv_ref, tables, gq_ref, gf_ref, sum_ref):
    cos_t, sin_t, bias2, first, low_half = tables
    size = cos_t.shape[0]
    rows = slice(at, at + size)
    across = (((0,), (0,)), ((), ()))
    for pair in range(cols // TILE):
        places = [g * cols + pair * TILE for g in range(3)]
        query, keys, values = (qkv_ref[rows, p : p + TILE] for p in places)
        query2 = stacked(query, first)
        mixed2 = stacked(back_ref[rows, pair * TILE : (pair + 1) * TILE].astype(BF), first)
        probs = softmax_of(query2, keys, bias2)
        grad_probs = lax.dot_general(
            mixed2, values, (((1,), (1,)), ((), ())), preferred_element_type=F32
        )
        inner = jnp.sum(probs * grad_probs, axis=1, keepdims=True)
        grad_scores = (probs * (grad_probs - inner)).astype(BF)
        gq = jnp.dot(grad_scores, keys, preferred_element_type=F32)
        gq = jnp.where(first, gq[:size], gq[size:]) * 0.125
        gk = lax.dot_general(grad_scores, query2, across, preferred_element_type=F32) * 0.125
        gv = lax.dot_general(probs.astype(BF), mixed2, across, preferred_element_type=F32)
        gq = turned(gq, cos_t, -sin_t, low_half)
        gk = turned(gk, cos_t, -sin_t, low_half)
        for p, v in zip(places, (gq, gk, gv)):
            low = v.astype(BF)
            gq_ref[rows, p : p + TILE] = low
            sum_ref[0:1, p : p + TILE] += jnp.sum(low.astype(F32), axis=0, keepdims=True)

    def gates(gate, up, grad_hid):
        sigma = jax.nn.sigmoid(gate)
        slope = sigma * (1.0 + gate * (1.0 - sigma))
        return (grad_hid * up * slope, grad_hid * (gate * sigma))

    for j in range(main // TILE):
        p, q = j * TILE, main + j * TILE
        grad_hid = back_ref[rows, cols + j * TILE : cols + (j + 1) * TILE]
        gg, gu = gates(pf_ref[rows, p : p + TILE], pf_ref[rows, q : q + TILE], grad_hid)
        gf_ref[rows, p : p + TILE] = gg.astype(BF)
        gf_ref[rows, q : q + TILE] = gu.astype(BF)
    if rest:
        tail = pf_ref[rows, 2 * main :]
        short = back_ref[rows, cols + main :]
        grad_hid = jnp.concatenate([short, jnp.zeros_like(short)], axis=1)
        gg, gu = gates(tail, pltpu.roll(tail, rest, 1), grad_hid)
        lane = lax.broadcasted_iota(jnp.int32, (size, TILE), 1)
        both = jnp.where(lane < rest, gg, pltpu.roll(gu, rest, 1))
        gf_ref[rows, 2 * main :] = both.astype(BF)


def block_tables(cos_ref, sin_ref, mask_ref, block, size):
    lane = lax.broadcasted_iota(jnp.int32, (size, TILE), 1)
    rows = slice(block * size, (block + 1) * size)
    mask = mask_ref[block]
    return (
        cos_ref[rows, :],
        sin_ref[rows, :],
        jnp.concatenate([mask, mask], axis=0),
        lane < HD,
        lane % HD < ROT // 2,
    )


def stack_copies(pieces, whole, sem, start):
    copies, count = [], len(pieces) // 2
    edge = pieces[0].shape[1]
    for group, columns in enumerate((pl.ds(0, edge), pl.ds(edge, whole.shape[1] - edge))):
        at = 0
        for i in range(group * count, (group + 1) * count):
            size = pieces[i].shape[0]
            dst = whole.at[pl.ds(at, size), columns]
            copies.append(pltpu.make_async_copy(pieces[i], dst, sem.at[start + i]))
            at += size
    return copies


def forward_kernel(sizes, count, block, *refs):
    cols, main, rest = sizes
    normed_ref, bias_ref, cos_ref, sin_ref, mask_ref = refs[:5]
    pieces, mixer_any = refs[5 : 5 + count], refs[5 + count]
    joined_ref, qkv_ref, pf_ref, branch_ref = refs[6 + count : 10 + count]
    entry, wm, pq, sem = refs[10 + count :]
    groups = [
        stack_copies(pieces, entry, sem, 0),
        [pltpu.make_async_copy(mixer_any, wm, sem.at[count])],
    ]
    opening = pl.program_id(0) == 0

    @pl.when(opening)
    def _():
        for group in groups:
            for copy in group:
                copy.start()

    def arrive(group):
        @pl.when(opening)
        def _():
            for copy in groups[group]:
                copy.wait()

    normed = normed_ref[...]
    arrive(0)
    pq[...] = jnp.dot(normed, entry[:, : 3 * cols], preferred_element_type=F32)
    pf_ref[...] = jnp.dot(normed, entry[:, 3 * cols :], preferred_element_type=F32)
    for i in range(normed.shape[0] // block):
        tables = block_tables(cos_ref, sin_ref, mask_ref, i, block)
        attend_rows(
            cols, main, rest, i * block, pq, pf_ref, bias_ref, tables, joined_ref, qkv_ref
        )
    arrive(1)
    branch = jnp.dot(joined_ref[...], wm[...], preferred_element_type=F32)
    branch_ref[...] = branch.astype(BF)


def backward_kernel(sizes, count, block, *refs):
    cols, main, rest = sizes
    masked_ref, pf_ref, qkv_ref, cos_ref, sin_ref, mask_ref, mixer_any = refs[:7]
    pieces = refs[7 : 7 + count]
    gq_ref, gf_ref, norm_ref, sum_ref = refs[7 + count : 11 + count]
    wm, entry, back, sem = refs[11 + count :]
    mixer_copy = pltpu.make_async_copy(mixer_any, wm, sem.at[count])
    copies = stack_copies(pieces, entry, sem, 0)
    opening = pl.program_id(0) == 0

    @pl.when(opening)
    def _():
        mixer_copy.start()
        for copy in copies:
            copy.start()
        sum_ref[...] = jnp.zeros_like(sum_ref)
        mixer_copy.wait()

    back[...] = lax.dot_general(
        masked_ref[...], wm[...], CONTRACT_COLS, preferred_element_type=F32
    )
    for i in range(masked_ref.shape[0] // block):
        tables = block_tables(cos_ref, sin_ref, mask_ref, i, block)
        attend_back_rows(
            cols, main, rest, i * block, pf_ref, back, qkv_ref, tables, gq_ref, gf_ref, sum_ref
        )

    @pl.when(opening)
    def _():
        for copy in copies:
            copy.wait()

    cut = 3 * cols
    total = lax.dot_general(
        gq_ref[...], entry[:, :cut], CONTRACT_COLS, preferred_element_type=F32
    )
    total += lax.dot_general(
        gf_ref[...], entry[:, cut:], CONTRACT_COLS, preferred_element_type=F32
    )
    norm_ref[...] = total.astype(BF)


STEP = 256
HIDDEN_COST = pl.CostEstimate(flops=1, bytes_accessed=1, transcendentals=0)


def row_spec(width, rows=STEP):
    return pl.BlockSpec((rows, width), lambda i: (i, 0))


ANYWHERE = pl.BlockSpec(memory_space=pl.ANY)
HELD = pl.BlockSpec(memory_space=pltpu.VMEM)


def kept(*arrays):
    return [pltpu.with_memory_space_constraint(array, pltpu.HBM) for array in arrays]


def stepping(limit):
    return pltpu.CompilerParams(
        dimension_semantics=("arbitrary",), vmem_limit_bytes=limit << 20
    )


def forward_call(normed, bias, cos_t, sin_t, mask, pieces, mixer, sizes):
    cols, main, rest = sizes
    everyone, width = normed.shape
    block = mask.shape[1]
    count = len(pieces)
    joint = cols + main + rest
    return pl.pallas_call(
        functools.partial(forward_kernel, sizes, count, block),
        grid=(everyone // STEP,),
        in_specs=[
            row_spec(width),
            pl.BlockSpec((8, 3 * cols), lambda i: (0, 0)),
            row_spec(TILE),
            row_spec(TILE),
            pl.BlockSpec((STEP // block, block, block), lambda i: (i, 0, 0)),
        ]
        + [ANYWHERE] * (count + 1),
        out_specs=[
            row_spec(joint),
            row_spec(3 * cols),
            row_spec(2 * (main + rest)),
            row_spec(width),
        ],
        out_shape=[
            pltpu.HBM((everyone, joint), BF),
            pltpu.HBM((everyone, 3 * cols), BF),
            pltpu.HBM((everyone, 2 * (main + rest)), F32),
            pltpu.HBM((everyone, width), BF),
        ],
        scratch_shapes=[
            pltpu.VMEM((width, 3 * cols + 2 * (main + rest)), BF),
            pltpu.VMEM((joint, width), BF),
            pltpu.VMEM((STEP, 3 * cols), F32),
            pltpu.SemaphoreType.DMA((count + 1,)),
        ],
        compiler_params=stepping(36),
        cost_estimate=HIDDEN_COST,
        name="forward",
    )(*kept(normed, bias, cos_t, sin_t, mask, *pieces, mixer))


def backward_call(masked, pf, qkv, cos_t, sin_t, mask, mixer, pieces, sizes):
    cols, main, rest = sizes
    everyone, width = masked.shape
    block = mask.shape[1]
    count = len(pieces)
    joint = cols + main + rest
    total = 3 * cols + 2 * (main + rest)
    return pl.pallas_call(
        functools.partial(backward_kernel, sizes, count, block),
        grid=(everyone // STEP,),
        in_specs=[
            row_spec(width),
            row_spec(2 * (main + rest)),
            row_spec(3 * cols),
            row_spec(TILE),
            row_spec(TILE),
            pl.BlockSpec((STEP // block, block, block), lambda i: (i, 0, 0)),
        ]
        + [ANYWHERE] * (count + 1),
        out_specs=[
            row_spec(3 * cols),
            row_spec(2 * (main + rest)),
            row_spec(width),
            pl.BlockSpec((8, 3 * cols), lambda i: (0, 0)),
        ],
        out_shape=[
            pltpu.HBM((everyone, 3 * cols), BF),
            pltpu.HBM((everyone, 2 * (main + rest)), BF),
            pltpu.HBM((everyone, width), BF),
            pltpu.HBM((8, 3 * cols), F32),
        ],
        scratch_shapes=[
            pltpu.VMEM((joint, width), BF),
            pltpu.VMEM((width, total), BF),
            pltpu.VMEM((STEP, joint), F32),
            pltpu.SemaphoreType.DMA((count + 1,)),
        ],
        compiler_params=stepping(36),
        cost_estimate=HIDDEN_COST,
        name="backward",
    )(*kept(masked, pf, qkv, cos_t, sin_t, mask, mixer, *pieces))


def product_call(normed, grad, groups, size):
    low, width = 0, grad.shape[1]
    slabs = [slab for group in groups for slab in group]
    places = [(g, at) for g, group in enumerate(groups) for at in range(len(group))]
    count = len(slabs)

    def kernel(table_ref, lhs_any, grad_any, *refs):
        outs, (lhs, grad, held, sem) = refs[: len(groups)], refs[len(groups) :]
        loads = [pltpu.make_async_copy(grad_any.at[:, pl.ds(low, width)], grad, sem.at[2 * count])]
        copies = []
        for i, (g, at) in enumerate(places):
            slab = pl.multiple_of(table_ref[i] * size, size)
            src = lhs_any.at[:, pl.ds(slab, size)]
            loads.append(pltpu.make_async_copy(src, lhs.at[i], sem.at[count + i]))
            dst = outs[g].at[pl.ds(at * size, size), :]
            copies.append(pltpu.make_async_copy(held.at[i], dst, sem.at[i]))
        for load in loads:
            load.start()
        loads[0].wait()

        def step(i, _):
            for j in range(count):
                pl.when(i == j)(loads[1 + j].wait)
            held[i] = lax.dot_general(
                lhs[i], grad[...], CONTRACT_ROWS, preferred_element_type=F32
            ).astype(BF)
            for j, copy in enumerate(copies):
                pl.when(i == j)(copy.start)

        lax.fori_loop(0, count, step, None)
        for copy in copies:
            copy.wait()

    everyone = normed.shape[0]
    return pl.pallas_call(
        kernel,
        in_specs=[pl.BlockSpec(memory_space=pltpu.SMEM), ANYWHERE, ANYWHERE],
        out_specs=[pl.BlockSpec(memory_space=pltpu.HBM)] * len(groups),
        out_shape=[pltpu.HBM((len(group) * size, width), BF) for group in groups],
        scratch_shapes=[
            pltpu.VMEM((count, everyone, size), BF),
            pltpu.VMEM((everyone, width), BF),
            pltpu.VMEM((count, size, width), BF),
            pltpu.SemaphoreType.DMA((2 * count + 1,)),
        ],
        compiler_params=pltpu.CompilerParams(vmem_limit_bytes=24 << 20),
        cost_estimate=HIDDEN_COST,
        name="weight_grad",
    )(jnp.array(slabs, jnp.int32), *kept(normed, grad))


def sum_kernel(own_low, own_high, from_x, from_y, last_x, last_y, out_ref):
    def total(*refs):
        return sum(ref[...].astype(F32) for ref in refs).astype(BF)

    out_ref[0] = total(own_low, from_x, last_y)
    out_ref[1] = total(own_high, from_y, last_x)


def sum_call(own_low, own_high, first, last):
    half, width = own_low.shape
    rows = half // 2
    near = pl.BlockSpec((rows, width), lambda i: (i, 0))
    second = pl.BlockSpec((rows, width), lambda i: (i + 2, 0))
    out = pl.pallas_call(
        sum_kernel,
        grid=(2,),
        in_specs=[near, near, second, second, near, near],
        out_specs=pl.BlockSpec((2, rows, width), lambda i: (0, i, 0)),
        out_shape=pltpu.HBM((2, half, width), BF),
        compiler_params=stepping(24),
        cost_estimate=HIDDEN_COST,
        name="sum_lanes",
    )(*kept(own_low, own_high, *first), *last)
    return out.reshape(2 * half, width)


def add_kernel(from_x, from_y, x_high, y_low, to_x, to_y):
    to_x[...] = (x_high[...].astype(F32) + from_y[...].astype(F32)).astype(BF)
    to_y[...] = (y_low[...].astype(F32) + from_x[...].astype(F32)).astype(BF)


def add_call(got, x_high, y_low):
    high, low = x_high.shape, y_low.shape
    block = lambda shape: pl.BlockSpec(shape, lambda i: (0, 0))
    return pl.pallas_call(
        add_kernel,
        grid=(1,),
        in_specs=[block(low), block(high), block(high), block(low)],
        out_specs=[block(high), block(low)],
        out_shape=[pltpu.HBM(high, BF), pltpu.HBM(low, BF)],
        compiler_params=stepping(24),
        cost_estimate=HIDDEN_COST,
        name="add_halves",
    )(*kept(*got, x_high, y_low))


def mixer_sum_call(own_low, own_high, first, last, own):
    (low, width), high = own_low.shape, own_high.shape[0]
    rest = high - own

    def kernel(low_ref, high_ref, x_ref, y_ref, last_x, last_y, out_ref, down_ref):
        low_sum = low_ref[...].astype(F32) + x_ref[...].astype(F32) + last_y[...].astype(F32)
        high_sum = high_ref[...].astype(F32) + y_ref[...].astype(F32) + last_x[...].astype(F32)
        down_ref[:low, :] = low_sum
        down_ref[low:, :] = high_sum[:rest]
        out_ref[...] = high_sum[rest:]

    block = lambda rows, at=0: pl.BlockSpec((rows, width), lambda i: (at, 0))
    return pl.pallas_call(
        kernel,
        grid=(1,),
        in_specs=[block(low), block(high), block(low, 1), block(high, 1), block(high), block(low)],
        out_specs=[block(own), block(low + rest)],
        out_shape=[pltpu.HBM((own, width), F32), pltpu.HBM((low + rest, width), F32)],
        compiler_params=stepping(24),
        cost_estimate=HIDDEN_COST,
        name="sum_mixer",
    )(*kept(own_low, own_high, *first), *last)


def mixer_grad_call(lane, joined, masked, wide, own, own_ff, cut):
    everyone, joint = joined.shape
    width = masked.shape[1]
    rest = own + own_ff - cut

    def kernel(lane_ref, joined_any, masked_any, *refs):
        to_x, to_y, x_high, y_low, own_low, own_high, joined_ref, masked_ref, whole, sem = refs
        run_copies([(joined_any, joined_ref), (masked_any, masked_ref)], sem)
        masked = masked_ref[...]

        def product(at, size):
            whole[pl.ds(at, size), :] = lax.dot_general(
                joined_ref[:, pl.ds(at, size)],
                masked,
                CONTRACT_ROWS,
                preferred_element_type=F32,
            ).astype(BF)

        lax.fori_loop(
            0, joint // STEP, lambda i, _: product(pl.multiple_of(i * STEP, STEP), STEP), None
        )
        if joint % STEP:
            product(joint // STEP * STEP, joint % STEP)
        halves = [
            own_low,
            own_high,
            to_x.at[pl.ds(cut, cut), :],
            x_high,
            y_low,
            to_y.at[pl.ds(rest, rest), :],
            to_x.at[pl.ds(0, cut), :],
            to_y.at[pl.ds(0, rest), :],
        ]
        pairs = row_spans(wide, own, own_ff, cut, lane_ref[0], halves, whole)
        run_copies([(there, here) for here, there in pairs], sem)

    shapes = [(size, width) for size in (2 * cut, 2 * rest, rest, cut, cut, rest)]
    return pl.pallas_call(
        kernel,
        in_specs=[pl.BlockSpec(memory_space=pltpu.SMEM), ANYWHERE, ANYWHERE],
        out_specs=[pl.BlockSpec(memory_space=pltpu.HBM)] * len(shapes),
        out_shape=[pltpu.HBM(shape, BF) for shape in shapes],
        scratch_shapes=[
            pltpu.VMEM((everyone, joint), BF),
            pltpu.VMEM((everyone, width), BF),
            pltpu.VMEM((joint, width), BF),
            pltpu.SemaphoreType.DMA((3 * wide,)),
        ],
        compiler_params=pltpu.CompilerParams(vmem_limit_bytes=40 << 20),
        cost_estimate=HIDDEN_COST,
        name="mixer_grad",
    )(lane, *kept(joined, masked))


def column_plan(member, outer, wide, cores, own, own_ff, cols, main, rest):
    z, c = member // cores, member % cores
    out = []
    for g in range(3):
        for k in range(wide):
            src = (((g * outer + z) * wide + k) * cores + c) * own
            out.append((0, src, 0, g * cols + k * own, own))
    for which in range(2):
        for k in range(wide):
            src = ((z * wide + k) * cores + c) * own_ff
            lo, hi = k * own_ff, (k + 1) * own_ff
            cut = min(hi, main)
            if cut > lo:
                out.append((1 + which, src, 1, which * main + lo, cut - lo))
            low = max(lo, main)
            if hi > low:
                at = 2 * main + which * rest + low - main
                out.append((1 + which, src + low - lo, 1, at, hi - low))
    return out


def pack_kernel(plan, tp, bases, *refs):
    packed, arrays, sem = refs[3:5], refs[5:8], refs[8]
    run_copies(list(zip(refs[:3], arrays)), sem)
    rows = arrays[0].shape[0]
    edge = packed[0].shape[1]
    for member in range(tp):
        at = slice(member * rows, (member + 1) * rows)
        for which, src, part, dst, width in plan(member):
            dst += bases[part]
            for ref, low, high in ((packed[0], 0, edge), (packed[1], edge, sum(bases))):
                start, stop = max(dst, low), min(dst + width, high)
                if start < stop:
                    there = slice(src + start - dst, src + stop - dst)
                    ref[at, start - low : stop - low] = arrays[which][:, there]


def pack_call(arrays, plan, tp, widths):
    rows = arrays[0].shape[0]
    total = sum(widths)
    edge = total // 2 // TILE * TILE
    return pl.pallas_call(
        functools.partial(pack_kernel, plan, tp, (0, widths[0], total - widths[0])),
        in_specs=[ANYWHERE] * 3,
        out_specs=[HELD] * 2,
        out_shape=[jax.ShapeDtypeStruct((tp * rows, w), BF) for w in (edge, total - edge)],
        scratch_shapes=[pltpu.VMEM(array.shape, BF) for array in arrays]
        + [pltpu.SemaphoreType.DMA((3,))],
        compiler_params=pltpu.CompilerParams(vmem_limit_bytes=32 << 20),
        name="pack_columns",
    )(*kept(*arrays))


def unpack_kernel(plan, tp, part, *refs):
    packed, outs = refs[0], refs[1:]
    rows = outs[0].shape[0]
    for member in range(tp):
        at = slice(member * rows, (member + 1) * rows)
        for which, src, source, dst, width in plan(member):
            if source == part:
                out = outs[which - part]
                out[:, src : src + width] = packed[at, dst : dst + width].astype(F32)


def unpack_call(packed, part, plan, tp, widths):
    rows = packed.shape[0] // tp
    return pl.pallas_call(
        functools.partial(unpack_kernel, plan, tp, part),
        in_specs=[HELD],
        out_specs=[HELD] * len(widths),
        out_shape=[jax.ShapeDtypeStruct((rows, width), F32) for width in widths],
        compiler_params=pltpu.CompilerParams(vmem_limit_bytes=32 << 20),
        cost_estimate=HIDDEN_COST,
        name="unpack_columns",
    )(packed)


def join_kernel(count, *refs):
    ins, out, sem = refs[:count], refs[count], refs[count + 1]
    copies, at = [], 0
    for i, ref in enumerate(ins):
        size = ref.shape[0]
        copies.append(pltpu.make_async_copy(ref, out.at[pl.ds(at, size), :], sem.at[i]))
        at += size
    for copy in copies:
        copy.start()
    for copy in copies:
        copy.wait()


def join_call(arrays):
    count = len(arrays)
    rows, width = sum(array.shape[0] for array in arrays), arrays[0].shape[1]
    return pl.pallas_call(
        functools.partial(join_kernel, count),
        in_specs=[pl.BlockSpec(memory_space=pl.ANY)] * count,
        out_specs=pl.BlockSpec(memory_space=pltpu.VMEM),
        out_shape=jax.ShapeDtypeStruct((rows, width), BF),
        scratch_shapes=[pltpu.SemaphoreType.DMA((count,))],
        compiler_params=pltpu.CompilerParams(vmem_limit_bytes=16 << 20),
        name="join_rows",
    )(*arrays)


def row_spans(wide, own, own_ff, cut, lane, halves, whole):
    spans = []
    base = wide * own
    for j in range(wide):
        spot = lax.bitwise_xor(lane, j)
        down = pl.multiple_of(base + spot * own_ff, 16)
        down_low = pl.multiple_of(base + spot * own_ff + cut, 16)
        out = pl.multiple_of(spot * own, 16)
        low, high = halves[2 * j : 2 * j + 2]
        rest = own_ff - cut
        spans.append((low, whole.at[pl.ds(down, cut), :]))
        spans.append((high.at[pl.ds(0, rest), :], whole.at[pl.ds(down_low, rest), :]))
        spans.append((high.at[pl.ds(rest, own), :], whole.at[pl.ds(out, own), :]))
    return spans


def run_copies(pairs, sem):
    copies = [pltpu.make_async_copy(src, dst, sem.at[i]) for i, (src, dst) in enumerate(pairs)]
    for copy in copies:
        copy.start()
    for copy in copies:
        copy.wait()


def place_call(lane, halves, wide, own, own_ff, cut):
    width = halves[0].shape[1]

    def kernel(lane_ref, *refs):
        ins, out, sem = refs[:-2], refs[-2], refs[-1]
        run_copies(row_spans(wide, own, own_ff, cut, lane_ref[0], ins, out), sem)

    return pl.pallas_call(
        kernel,
        in_specs=[pl.BlockSpec(memory_space=pltpu.SMEM)]
        + [pl.BlockSpec(memory_space=pl.ANY)] * len(halves),
        out_specs=pl.BlockSpec(memory_space=pltpu.VMEM),
        out_shape=jax.ShapeDtypeStruct((wide * (own + own_ff), width), BF),
        scratch_shapes=[pltpu.SemaphoreType.DMA((3 * wide,))],
        compiler_params=pltpu.CompilerParams(vmem_limit_bytes=16 << 20),
        name="place_rows",
    )(lane, *halves)


def mixer_product(joined, masked):
    return lax.dot_general(joined, masked, CONTRACT_ROWS, preferred_element_type=F32).astype(BF)


class Plain:
    def __init__(self, outer, inner):
        self.tp, self.wide, self.cores, self.outer = outer, inner, 1, outer
        self.member = lax.axis_index("dp")
        self.token_axes, self.token_groups = "dp", None
        self.weight_axes, self.weight_groups = "fsdp", None

    def gather_tokens(self, block):
        return lax.all_gather(
            block, self.token_axes, axis=0, tiled=True, axis_index_groups=self.token_groups
        )

    def scatter_tokens(self, part):
        return lax.psum_scatter(
            part.astype(BF),
            self.token_axes,
            scatter_dimension=0,
            tiled=True,
            axis_index_groups=self.token_groups,
        ).astype(F32)

    def exchange(self, part):
        return lax.all_to_all(
            part,
            self.token_axes,
            split_axis=0,
            concat_axis=0,
            tiled=True,
            axis_index_groups=self.token_groups,
        )

    def gather_weights(self, block):
        return lax.all_gather(
            block, self.weight_axes, axis=0, tiled=True, axis_index_groups=self.weight_groups
        )

    def scatter_weights(self, part):
        return lax.psum_scatter(
            part,
            self.weight_axes,
            scatter_dimension=0,
            tiled=True,
            axis_index_groups=self.weight_groups,
        )

    def inputs(self, packed, w_out, w_down, normed, masked, lengths, make_tables):
        mixer = jnp.concatenate([self.gather_weights(w) for w in (w_out, w_down)], axis=0)
        entry = [self.gather_weights(self.exchange(part)) for part in packed]
        tokens = [self.gather_tokens(block) for block in (normed, masked)]
        lengths = lax.all_gather(lengths, "dp", axis=0, tiled=True)
        return entry, mixer, tokens[0], tokens[1], make_tables(lengths)

    def outputs(self, joined, masked, branch, back_call, tail, normed, own, own_ff):
        cols = self.wide * own
        part = mixer_product(joined, masked)
        grads = [self.scatter_weights(p).astype(F32) for p in (part[:cols], part[cols:])]
        grad_qkv, grad_ff, norm, bias_part = back_call(masked)
        parts = []
        for grad in (grad_qkv, grad_ff):
            part = lax.dot_general(normed, grad, CONTRACT_ROWS, preferred_element_type=F32)
            parts.append(self.scatter_weights(part.astype(BF)))
        norm, branch = self.scatter_tokens(norm), self.scatter_tokens(branch)
        part_qkv, part_ff = [self.exchange(part) for part in parts]
        grad_tokens, stats = tail(norm, bias_part)
        stats = self.scatter_stats(stats)
        return grads[0], grads[1], part_qkv, part_ff, branch, grad_tokens, stats

    def relative(self, blocks, axis):
        return blocks

    def scatter_stats(self, stats):
        parts = lax.all_to_all(stats, AXES, split_axis=0, concat_axis=0, tiled=True)
        return jnp.sum(parts, axis=0)


class Linked(Plain):
    def __init__(self, outer, inner):
        self.outer, self.cores, self.wide = outer, 2, inner // 2
        self.tp = outer * 2
        flat = lax.axis_index("fsdp")
        self.lane = flat // 2
        self.member = lax.axis_index("dp") * 2 + lax.rem(flat, 2)
        spots = [
            [[(z * self.wide + k) * 2 + c for c in range(2)] for k in range(self.wide)]
            for z in range(outer)
        ]
        self.token_axes = self.weight_axes = AXES
        self.token_groups = [
            [spots[z][k][c] for z in range(outer) for c in range(2)] for k in range(self.wide)
        ]
        self.weight_groups = [
            [spots[z][k][c] for k in range(self.wide)] for z in range(outer) for c in range(2)
        ]
        self.spots = spots
        self.lane_index = self.lane.astype(jnp.int32).reshape(1)

    def send(self, value, step=0, dz=0, dc=0):
        pairs = [
            (self.spots[z][k][c], self.spots[z ^ dz][k ^ step][c ^ dc])
            for z in range(self.outer)
            for k in range(self.wide)
            for c in range(2)
        ]
        return lax.ppermute(value, AXES, pairs)

    def gather_lengths(self, lengths):
        parts = [lengths] + [self.send(lengths, dz=dz) for dz in range(1, self.outer)]
        return jnp.concatenate(parts, axis=0)

    def order_lengths(self, mine, other):
        both = jnp.stack([mine, other], axis=1).reshape(self.tp, -1)
        spot = lax.bitwise_xor(jnp.arange(self.tp, dtype=jnp.int32), self.member)
        pick = spot[:, None] == jnp.arange(self.tp, dtype=jnp.int32)[None, :]
        return jnp.sum(jnp.where(pick[:, :, None], both[None], 0), axis=1)

    def inputs(self, packed, w_out, w_down, normed, masked, lengths, make_tables):
        own, own_ff = w_out.shape[0], w_down.shape[0]
        cut = own_ff // 32 * 16 + 32
        half = packed[0].shape[0] // 2
        rows, left, right, lengths = tie(join_call([w_down, w_out]), *packed, lengths)
        mix_x, mix_y = self.send(rows, 1), self.send(rows, 2)
        lengths = self.gather_lengths(lengths)
        left = self.exchange(left)
        left, right, mix_x, mix_y = tie(left, right, mix_x, mix_y)
        left_x, left_y = self.send(left, 1), self.send(left, 2)
        right = self.exchange(right)
        halves = [part for b in (rows, mix_x, mix_y) for part in (b[:cut], b[cut:])]
        right, left_x, left_y, normed, masked, lengths, *halves = tie(
            right, left_x, left_y, normed, masked, lengths, *halves
        )
        normed_all, masked_all = self.gather_tokens(normed), self.gather_tokens(masked)
        right_x, right_y = self.send(right, 1), self.send(right, 2)
        mix_low, mix_high = self.send(halves[2], 2), self.send(halves[5], 1)
        left_low, left_high = self.send(left_x[:half], 2), self.send(left_y[half:], 1)
        tables = make_tables(self.order_lengths(lengths, self.send(lengths, dc=1)))
        halves += [mix_low, mix_high]
        mixer = place_call(self.lane_index, halves, self.wide, own, own_ff, cut)
        right_x, right_y, left_low, left_high, mixer, *tables = tie(
            right_x, right_y, left_low, left_high, *kept(mixer, *tables)
        )
        right_low, right_high = self.send(right_x[:half], 2), self.send(right_y[half:], 1)
        entry = [left, left_x, left_y, left_low, left_high]
        entry += [right, right_x, right_y, right_low, right_high]
        return entry, mixer, normed_all, masked_all, tables

    def first_sends(self, to_x, to_y):
        return self.send(to_x, 1), self.send(to_y, 2)

    def last_sends(self, got, x_high, y_low):
        from_x, from_y = got
        low, high = from_x[: y_low.shape[0]], from_y[: x_high.shape[0]]
        return (
            self.send((x_high.astype(F32) + high.astype(F32)).astype(BF), 1),
            self.send((y_low.astype(F32) + low.astype(F32)).astype(BF), 2),
        )

    def lane_sum(self, own_low, own_high, first, last):
        low = own_low.astype(F32) + first[0][own_low.shape[0] :].astype(F32)
        high = own_high.astype(F32) + first[1][own_high.shape[0] :].astype(F32)
        return low + last[1].astype(F32), high + last[0].astype(F32)

    def outputs(self, joined, masked, branch, back_call, tail, normed, own, own_ff):
        cut = own_ff // 32 * 16 + 32
        rest = own_ff - cut
        size = normed.shape[1] // self.wide // 2
        first, last = ((6, 2), (7, 5)), ((3,), (4,), (0,), (1,))

        branch = self.scatter_tokens(branch)
        mix = mixer_grad_call(self.lane_index, joined, masked, self.wide, own, own_ff, cut)
        *mix, masked = tie(*mix, masked)
        mix_first = self.first_sends(mix[0], mix[1])
        grad_qkv, grad_ff, norm, bias_part = back_call(masked)
        *mix_first, norm, grad_ff, grad_qkv = tie(*mix_first, norm, grad_ff, grad_qkv)
        norm = self.scatter_tokens(norm)
        to_x, to_y = product_call(normed, grad_ff, first, size)
        to_x, to_y, grad_ff = tie(to_x, to_y, grad_ff)
        ff_first = self.first_sends(to_x, to_y)
        x_high, y_low, ff_low, ff_high = product_call(normed, grad_ff, last, size)
        ff_low, grad_qkv = tie(ff_low, grad_qkv)
        to_x, to_y = product_call(normed, grad_qkv, first, size)
        to_x, grad_qkv = tie(to_x, grad_qkv)
        qkv_x, qkv_y, qkv_low, qkv_high = product_call(normed, grad_qkv, last, size)
        branch, to_x, to_y, x_high, y_low, qkv_low, *ff_first = tie(
            branch, to_x, to_y, x_high, y_low, qkv_low, *ff_first
        )
        ff_last = self.last_sends(ff_first, x_high, y_low)
        part_ff = self.joined_sum((x_high, y_low, ff_low, ff_high), ff_first, ff_last)
        part_ff, to_x, to_y = tie(part_ff, to_x, to_y)
        qkv_first = self.first_sends(to_x, to_y)
        part_ff = self.exchange(part_ff)
        results = tail(norm, bias_part)
        *qkv_first, grad_tokens, stats = tie(*qkv_first, *results)
        qkv_last = self.last_sends(qkv_first, qkv_x, qkv_y)
        part_qkv = self.joined_sum((qkv_x, qkv_y, qkv_low, qkv_high), qkv_first, qkv_last)
        stats = self.depth_stats(stats)
        part_ff, part_qkv, stats, *mix = tie(part_ff, part_qkv, stats, *mix_first, *mix[2:])
        part_qkv = self.exchange(part_qkv)
        mix_first, mix = mix[:2], mix[2:]
        mix_x, mix_y = add_call(mix_first, mix[0], mix[1])
        mix_last = self.send(mix_x, 1), self.send(mix_y, 2)
        stats = self.scatter_stats(stats)
        grad_w_out, grad_w_down = mixer_sum_call(mix[2], mix[3], mix_first, mix_last, own)
        return grad_w_out, grad_w_down, part_qkv, part_ff, branch, grad_tokens, stats

    def joined_sum(self, late, first, last):
        return sum_call(late[2], late[3], first, last)

    def keep(self, values, axis, place, count, name):
        pick = lambda spot: lax.dynamic_index_in_dim(values, spot, axis, keepdims=False)
        got = [self.send(pick(lax.bitwise_xor(place, j)), **{name: j}) for j in range(1, count)]
        return pick(place) + sum(got)

    def depth_stats(self, stats):
        split = stats.reshape(self.outer, self.wide, 2, -1)
        return self.keep(split, 0, self.member // 2, self.outer, "dz")

    def scatter_stats(self, split):
        split = self.keep(split, 0, self.lane, self.wide, "step")
        return self.keep(split, 0, lax.rem(self.member, 2), 2, "dc")

    def relative(self, blocks, axis):
        shape = blocks.shape
        split = blocks.reshape(shape[:axis] + (2, 2) + shape[axis + 1 :])
        split = jnp.where(self.lane >= 2, jnp.flip(split, axis), split)
        split = jnp.where(lax.rem(self.lane, 2) == 1, jnp.flip(split, axis + 1), split)
        return split.reshape(shape)


def on_device(
    tokens, ln_gain, ln_shift, w_qkv, b_qkv, w_out, w_gate, w_up, w_down, grad_out, seq_lengths
):
    outer, inner = lax.axis_size("dp"), lax.axis_size("fsdp")
    linked = outer == 4 and inner == 8
    net = Linked(outer, inner) if linked else Plain(outer, inner)
    tp, wide, cores = net.tp, net.wide, net.cores
    rows_tok, width = tokens.shape
    own = w_qkv.shape[0]
    own_ff = w_down.shape[0]
    cols, cols_ff = wide * own, wide * own_ff
    main = cols_ff // TILE * TILE
    rest = cols_ff - main
    widths = (3 * cols, 2 * cols_ff)
    plan = lambda member: column_plan(
        member, outer, wide, cores, own, own_ff, cols, main, rest
    )

    _, valid, _ = block_terms(seq_lengths[0], rows_tok)
    keep_row = valid.astype(F32)[:, None]
    widened = tokens.astype(F32)
    centered = widened - jnp.mean(widened, axis=1, keepdims=True)
    inv_std = lax.rsqrt(jnp.mean(centered * centered, axis=1, keepdims=True) + EPS)
    scaled = centered * inv_std
    normed = (scaled * ln_gain + ln_shift).astype(BF)
    masked = (grad_out.astype(F32) * keep_row).astype(BF)

    def lanes_first(x):
        split = x.reshape(rows_tok, outer, wide, cores * own)
        return net.relative(jnp.swapaxes(split, 1, 2), 1).reshape(rows_tok, width)

    def lanes_back(x):
        split = net.relative(x.reshape(rows_tok, wide, outer, cores * own), 1)
        return jnp.swapaxes(split, 1, 2).reshape(rows_tok, width)

    lengths = seq_lengths
    arrays = [w_qkv, w_gate, w_up]

    bias = lax.dynamic_index_in_dim(
        jnp.transpose(b_qkv.reshape(3, outer, wide, cores, own), (1, 3, 0, 2, 4)).reshape(tp, -1),
        net.member,
        0,
    )
    bias = jnp.broadcast_to(bias, (8, 3 * cols))

    def make_tables(lengths):
        position, _, allowed = jax.vmap(lambda row: block_terms(row, rows_tok))(lengths)
        return [*turn_tables(position), jnp.where(allowed, 0.0, NEG), bias]

    entry, mixer, normed_all, masked_all, (cos_t, sin_t, mask, bias) = net.inputs(
        pack_call(arrays, plan, tp, widths),
        w_out,
        w_down,
        lanes_first(normed),
        masked,
        lengths,
        make_tables,
    )
    sizes = (cols, main, rest)
    joined, qkv, proj_ff, branch = forward_call(
        normed_all, bias, cos_t, sin_t, mask, entry, mixer, sizes
    )
    back_call = lambda masked: backward_call(
        masked, proj_ff, qkv, cos_t, sin_t, mask, mixer, entry, sizes
    )

    def tail(grad_norm, bias_part):
        grad_norm = lanes_back(grad_norm)
        lifted_grad = grad_norm * ln_gain
        grad_in = inv_std * (
            lifted_grad
            - jnp.mean(lifted_grad, axis=1, keepdims=True)
            - scaled * jnp.mean(lifted_grad * scaled, axis=1, keepdims=True)
        )
        grad_tokens = (grad_out.astype(F32) + grad_in).astype(BF)
        shards = outer * inner
        gain_part = jnp.sum(grad_norm * scaled, axis=0)
        shift_part = jnp.sum(grad_norm, axis=0)
        bias_full = lax.dynamic_update_index_in_dim(
            jnp.zeros((tp, 3 * cols), F32), bias_part[0], net.member, 0
        )
        bias_full = jnp.transpose(bias_full.reshape(outer, cores, 3, wide, own), (2, 0, 3, 1, 4))
        stats = jnp.concatenate(
            [
                gain_part.reshape(shards, own),
                shift_part.reshape(shards, own),
                bias_full.reshape(shards, 3 * own),
            ],
            axis=1,
        )
        return grad_tokens, stats

    grad_w_out, grad_w_down, part_qkv, part_ff, branch, grad_tokens, stats = net.outputs(
        joined, masked_all, branch, back_call, tail, normed_all, own, own_ff
    )
    output = (widened + keep_row * branch).astype(BF)
    grad_w_gate, grad_w_up = unpack_call(
        part_ff, 1, plan, tp, [w_gate.shape[1], w_up.shape[1]]
    )
    part_qkv, stats, grad_w_gate, grad_w_up = tie(part_qkv, stats, grad_w_gate, grad_w_up)
    (grad_w_qkv,) = unpack_call(part_qkv, 0, plan, tp, [w_qkv.shape[1]])
    return (
        output,
        grad_tokens,
        grad_w_qkv,
        grad_w_out,
        grad_w_gate,
        grad_w_up,
        grad_w_down,
        stats[:own],
        stats[own : 2 * own],
        stats[2 * own :],
    )


def solution(mesh):
    rows = P(AXES, None)
    return jax.shard_map(
        on_device,
        mesh=mesh,
        in_specs=(rows, P(), P(), rows, P(), rows, rows, rows, rows, rows, rows),
        out_specs=(rows,) * 7 + (P(AXES),) * 3,
        check_vma=False,
    )
```

```python
import functools
import math

import jax
import jax.numpy as jnp
from jax import lax
from jax.experimental import pallas as pl
from jax.experimental.pallas import tpu as pltpu
from jax.sharding import PartitionSpec as P

HD = 64
ROT = 16
EPS = 1e-05
NEG = -1e30
TILE = 128
AXES = ("dp", "fsdp")
BF = jnp.bfloat16
F32 = jnp.float32
CONTRACT_ROWS = (((0,), (0,)), ((), ()))
CONTRACT_COLS = (((1,), (1,)), ((), ()))


def block_terms(lengths_row, rows_tok):
    ends = jnp.cumsum(lengths_row)
    place = jnp.arange(rows_tok, dtype=jnp.int32)
    segment = jnp.sum((place[:, None] >= ends[None, :]).astype(jnp.int32), axis=1)
    starts = jnp.concatenate([ends - lengths_row, ends[-1:]])
    labels = jnp.arange(starts.shape[0], dtype=jnp.int32)
    begin = jnp.sum(jnp.where(segment[:, None] == labels[None, :], starts[None, :], 0), axis=1)
    position = (place - begin).astype(F32)
    valid = segment < lengths_row.shape[0]
    label_tok = jnp.where(valid, segment, lengths_row.shape[0] + place)
    allowed = (label_tok[:, None] == label_tok[None, :]) & (place[None, :] <= place[:, None])
    return (position, valid, allowed)


def turn_tables(position):
    half = ROT // 2
    freq = jnp.exp(jnp.arange(half, dtype=F32) * (-2.0 * math.log(10000.0) / ROT))
    turn = position.reshape(-1)[:, None] * freq[None, :]
    cosine, sine = jnp.cos(turn), jnp.sin(turn)
    rest = (turn.shape[0], HD - ROT)
    cos_t = jnp.concatenate([cosine, cosine, jnp.ones(rest, F32)], axis=1)
    sin_t = jnp.concatenate([-sine, sine, jnp.zeros(rest, F32)], axis=1)
    return (jnp.tile(cos_t, (1, 2)), jnp.tile(sin_t, (1, 2)))


def tie(*values):
    return lax.optimization_barrier(values)


def turned(v, cos_t, sin_t, low_half):
    partner = jnp.where(low_half, pltpu.roll(v, TILE - ROT // 2, 1), pltpu.roll(v, ROT // 2, 1))
    return v * cos_t + partner * sin_t

def stacked(v, first):
    zero = jnp.zeros_like(v)
    return jnp.concatenate([jnp.where(first, v, zero), jnp.where(first, zero, v)], axis=0)

def softmax_of(query2, keys, bias2):
    scores = lax.dot_general(query2, keys, (((1,), (1,)), ((), ())), preferred_element_type=F32)
    scores = scores * 0.125 + bias2
    lifted = jnp.exp(scores - jnp.max(scores, axis=1, keepdims=True))
    return lifted / jnp.sum(lifted, axis=1, keepdims=True)

def attend_rows(cols, main, rest, at, pq_ref, pf_ref, bias_ref, tables, joined_ref, qkv_ref):
    cos_t, sin_t, bias2, first, low_half = tables
    size = cos_t.shape[0]
    rows = slice(at, at + size)
    for pair in range(cols // TILE):
        places = [g * cols + pair * TILE for g in range(3)]
        query, keys, values = (
            pq_ref[rows, p : p + TILE] + bias_ref[0:1, p : p + TILE] for p in places
        )
        query = turned(query, cos_t, sin_t, low_half).astype(BF)
        keys = turned(keys, cos_t, sin_t, low_half).astype(BF)
        values = values.astype(BF)
        for p, v in zip(places, (query, keys, values)):
            qkv_ref[rows, p : p + TILE] = v
        probs = softmax_of(stacked(query, first), keys, bias2).astype(BF)
        mixed = jnp.dot(probs, values, preferred_element_type=F32)
        joined_ref[rows, pair * TILE : (pair + 1) * TILE] = jnp.where(
            first, mixed[:size], mixed[size:]
        ).astype(BF)
    for j in range(main // TILE):
        gate = pf_ref[rows, j * TILE : (j + 1) * TILE]
        up = pf_ref[rows, main + j * TILE : main + (j + 1) * TILE]
        hid = gate * jax.nn.sigmoid(gate) * up
        joined_ref[rows, cols + j * TILE : cols + (j + 1) * TILE] = hid.astype(BF)
    if rest:
        tail = pf_ref[rows, 2 * main :]
        up = pltpu.roll(tail, rest, 1)
        hid = tail * jax.nn.sigmoid(tail) * up
        joined_ref[rows, cols + main :] = hid[:, :rest].astype(BF)


def attend_back_rows(cols, main, rest, at, pf_ref, back_ref, qkv_ref, tables, gq_ref, gf_ref, sum_ref):
    cos_t, sin_t, bias2, first, low_half = tables
    size = cos_t.shape[0]
    rows = slice(at, at + size)
    across = (((0,), (0,)), ((), ()))
    for pair in range(cols // TILE):
        places = [g * cols + pair * TILE for g in range(3)]
        query, keys, values = (qkv_ref[rows, p : p + TILE] for p in places)
        query2 = stacked(query, first)
        mixed2 = stacked(back_ref[rows, pair * TILE : (pair + 1) * TILE].astype(BF), first)
        probs = softmax_of(query2, keys, bias2)
        grad_probs = lax.dot_general(
            mixed2, values, (((1,), (1,)), ((), ())), preferred_element_type=F32
        )
        inner = jnp.sum(probs * grad_probs, axis=1, keepdims=True)
        grad_scores = (probs * (grad_probs - inner)).astype(BF)
        gq = jnp.dot(grad_scores, keys, preferred_element_type=F32)
        gq = jnp.where(first, gq[:size], gq[size:]) * 0.125
        gk = lax.dot_general(grad_scores, query2, across, preferred_element_type=F32) * 0.125
        gv = lax.dot_general(probs.astype(BF), mixed2, across, preferred_element_type=F32)
        gq = turned(gq, cos_t, -sin_t, low_half)
        gk = turned(gk, cos_t, -sin_t, low_half)
        for p, v in zip(places, (gq, gk, gv)):
            low = v.astype(BF)
            gq_ref[rows, p : p + TILE] = low
            sum_ref[0:1, p : p + TILE] += jnp.sum(low.astype(F32), axis=0, keepdims=True)

    def gates(gate, up, grad_hid):
        sigma = jax.nn.sigmoid(gate)
        slope = sigma * (1.0 + gate * (1.0 - sigma))
        return (grad_hid * up * slope, grad_hid * (gate * sigma))

    for j in range(main // TILE):
        p, q = j * TILE, main + j * TILE
        grad_hid = back_ref[rows, cols + j * TILE : cols + (j + 1) * TILE]
        gg, gu = gates(pf_ref[rows, p : p + TILE], pf_ref[rows, q : q + TILE], grad_hid)
        gf_ref[rows, p : p + TILE] = gg.astype(BF)
        gf_ref[rows, q : q + TILE] = gu.astype(BF)
    if rest:
        tail = pf_ref[rows, 2 * main :]
        short = back_ref[rows, cols + main :]
        grad_hid = jnp.concatenate([short, jnp.zeros_like(short)], axis=1)
        gg, gu = gates(tail, pltpu.roll(tail, rest, 1), grad_hid)
        lane = lax.broadcasted_iota(jnp.int32, (size, TILE), 1)
        both = jnp.where(lane < rest, gg, pltpu.roll(gu, rest, 1))
        gf_ref[rows, 2 * main :] = both.astype(BF)


def block_tables(cos_ref, sin_ref, mask_ref, block, size):
    lane = lax.broadcasted_iota(jnp.int32, (size, TILE), 1)
    rows = slice(block * size, (block + 1) * size)
    mask = mask_ref[block]
    return (
        cos_ref[rows, :],
        sin_ref[rows, :],
        jnp.concatenate([mask, mask], axis=0),
        lane < HD,
        lane % HD < ROT // 2,
    )


def stack_copies(pieces, whole, sem, start):
    copies, count = [], len(pieces) // 2
    edge = pieces[0].shape[1]
    for group, columns in enumerate((pl.ds(0, edge), pl.ds(edge, whole.shape[1] - edge))):
        at = 0
        for i in range(group * count, (group + 1) * count):
            size = pieces[i].shape[0]
            dst = whole.at[pl.ds(at, size), columns]
            copies.append(pltpu.make_async_copy(pieces[i], dst, sem.at[start + i]))
            at += size
    return copies


def forward_kernel(sizes, count, block, *refs):
    cols, main, rest = sizes
    normed_ref, bias_ref, cos_ref, sin_ref, mask_ref = refs[:5]
    pieces, mixer_any = refs[5 : 5 + count], refs[5 + count]
    joined_ref, qkv_ref, pf_ref, branch_ref = refs[6 + count : 10 + count]
    entry, wm, pq, sem = refs[10 + count :]
    groups = [
        stack_copies(pieces, entry, sem, 0),
        [pltpu.make_async_copy(mixer_any, wm, sem.at[count])],
    ]
    opening = pl.program_id(0) == 0

    @pl.when(opening)
    def _():
        for group in groups:
            for copy in group:
                copy.start()

    def arrive(group):
        @pl.when(opening)
        def _():
            for copy in groups[group]:
                copy.wait()

    normed = normed_ref[...]
    arrive(0)
    pq[...] = jnp.dot(normed, entry[:, : 3 * cols], preferred_element_type=F32)
    pf_ref[...] = jnp.dot(normed, entry[:, 3 * cols :], preferred_element_type=F32)
    for i in range(normed.shape[0] // block):
        tables = block_tables(cos_ref, sin_ref, mask_ref, i, block)
        attend_rows(
            cols, main, rest, i * block, pq, pf_ref, bias_ref, tables, joined_ref, qkv_ref
        )
    arrive(1)
    branch = jnp.dot(joined_ref[...], wm[...], preferred_element_type=F32)
    branch_ref[...] = branch.astype(BF)


def backward_kernel(sizes, count, block, *refs):
    cols, main, rest = sizes
    masked_ref, pf_ref, qkv_ref, cos_ref, sin_ref, mask_ref, mixer_any = refs[:7]
    pieces = refs[7 : 7 + count]
    gq_ref, gf_ref, norm_ref, sum_ref = refs[7 + count : 11 + count]
    wm, entry, back, sem = refs[11 + count :]
    mixer_copy = pltpu.make_async_copy(mixer_any, wm, sem.at[count])
    copies = stack_copies(pieces, entry, sem, 0)
    opening = pl.program_id(0) == 0

    @pl.when(opening)
    def _():
        mixer_copy.start()
        for copy in copies:
            copy.start()
        sum_ref[...] = jnp.zeros_like(sum_ref)
        mixer_copy.wait()

    back[...] = lax.dot_general(
        masked_ref[...], wm[...], CONTRACT_COLS, preferred_element_type=F32
    )
    for i in range(masked_ref.shape[0] // block):
        tables = block_tables(cos_ref, sin_ref, mask_ref, i, block)
        attend_back_rows(
            cols, main, rest, i * block, pf_ref, back, qkv_ref, tables, gq_ref, gf_ref, sum_ref
        )

    @pl.when(opening)
    def _():
        for copy in copies:
            copy.wait()

    cut = 3 * cols
    total = lax.dot_general(
        gq_ref[...], entry[:, :cut], CONTRACT_COLS, preferred_element_type=F32
    )
    total += lax.dot_general(
        gf_ref[...], entry[:, cut:], CONTRACT_COLS, preferred_element_type=F32
    )
    norm_ref[...] = total.astype(BF)


STEP = 256
HIDDEN_COST = pl.CostEstimate(flops=1, bytes_accessed=1, transcendentals=0)


def row_spec(width, rows=STEP):
    return pl.BlockSpec((rows, width), lambda i: (i, 0))


ANYWHERE = pl.BlockSpec(memory_space=pl.ANY)
HELD = pl.BlockSpec(memory_space=pltpu.VMEM)


def kept(*arrays):
    return [pltpu.with_memory_space_constraint(array, pltpu.HBM) for array in arrays]


def stepping(limit):
    return pltpu.CompilerParams(
        dimension_semantics=("arbitrary",), vmem_limit_bytes=limit << 20
    )


def forward_call(normed, bias, cos_t, sin_t, mask, pieces, mixer, sizes):
    cols, main, rest = sizes
    everyone, width = normed.shape
    block = mask.shape[1]
    count = len(pieces)
    joint = cols + main + rest
    return pl.pallas_call(
        functools.partial(forward_kernel, sizes, count, block),
        grid=(everyone // STEP,),
        in_specs=[
            row_spec(width),
            pl.BlockSpec((8, 3 * cols), lambda i: (0, 0)),
            row_spec(TILE),
            row_spec(TILE),
            pl.BlockSpec((STEP // block, block, block), lambda i: (i, 0, 0)),
        ]
        + [ANYWHERE] * (count + 1),
        out_specs=[
            row_spec(joint),
            row_spec(3 * cols),
            row_spec(2 * (main + rest)),
            row_spec(width),
        ],
        out_shape=[
            pltpu.HBM((everyone, joint), BF),
            pltpu.HBM((everyone, 3 * cols), BF),
            pltpu.HBM((everyone, 2 * (main + rest)), F32),
            pltpu.HBM((everyone, width), BF),
        ],
        scratch_shapes=[
            pltpu.VMEM((width, 3 * cols + 2 * (main + rest)), BF),
            pltpu.VMEM((joint, width), BF),
            pltpu.VMEM((STEP, 3 * cols), F32),
            pltpu.SemaphoreType.DMA((count + 1,)),
        ],
        compiler_params=stepping(36),
        cost_estimate=HIDDEN_COST,
        name="forward",
    )(*kept(normed, bias, cos_t, sin_t, mask, *pieces, mixer))


def backward_call(masked, pf, qkv, cos_t, sin_t, mask, mixer, pieces, sizes):
    cols, main, rest = sizes
    everyone, width = masked.shape
    block = mask.shape[1]
    count = len(pieces)
    joint = cols + main + rest
    total = 3 * cols + 2 * (main + rest)
    return pl.pallas_call(
        functools.partial(backward_kernel, sizes, count, block),
        grid=(everyone // STEP,),
        in_specs=[
            row_spec(width),
            row_spec(2 * (main + rest)),
            row_spec(3 * cols),
            row_spec(TILE),
            row_spec(TILE),
            pl.BlockSpec((STEP // block, block, block), lambda i: (i, 0, 0)),
        ]
        + [ANYWHERE] * (count + 1),
        out_specs=[
            row_spec(3 * cols),
            row_spec(2 * (main + rest)),
            row_spec(width),
            pl.BlockSpec((8, 3 * cols), lambda i: (0, 0)),
        ],
        out_shape=[
            pltpu.HBM((everyone, 3 * cols), BF),
            pltpu.HBM((everyone, 2 * (main + rest)), BF),
            pltpu.HBM((everyone, width), BF),
            pltpu.HBM((8, 3 * cols), F32),
        ],
        scratch_shapes=[
            pltpu.VMEM((joint, width), BF),
            pltpu.VMEM((width, total), BF),
            pltpu.VMEM((STEP, joint), F32),
            pltpu.SemaphoreType.DMA((count + 1,)),
        ],
        compiler_params=stepping(36),
        cost_estimate=HIDDEN_COST,
        name="backward",
    )(*kept(masked, pf, qkv, cos_t, sin_t, mask, mixer, *pieces))


def product_call(normed, grad, groups, size):
    low, width = 0, grad.shape[1]
    slabs = [slab for group in groups for slab in group]
    places = [(g, at) for g, group in enumerate(groups) for at in range(len(group))]
    count = len(slabs)

    def kernel(table_ref, lhs_any, grad_any, *refs):
        outs, (lhs, grad, held, sem) = refs[: len(groups)], refs[len(groups) :]
        loads = [pltpu.make_async_copy(grad_any.at[:, pl.ds(low, width)], grad, sem.at[2 * count])]
        copies = []
        for i, (g, at) in enumerate(places):
            slab = pl.multiple_of(table_ref[i] * size, size)
            src = lhs_any.at[:, pl.ds(slab, size)]
            loads.append(pltpu.make_async_copy(src, lhs.at[i], sem.at[count + i]))
            dst = outs[g].at[pl.ds(at * size, size), :]
            copies.append(pltpu.make_async_copy(held.at[i], dst, sem.at[i]))
        for load in loads:
            load.start()
        loads[0].wait()

        def step(i, _):
            for j in range(count):
                pl.when(i == j)(loads[1 + j].wait)
            held[i] = lax.dot_general(
                lhs[i], grad[...], CONTRACT_ROWS, preferred_element_type=F32
            ).astype(BF)
            for j, copy in enumerate(copies):
                pl.when(i == j)(copy.start)

        lax.fori_loop(0, count, step, None)
        for copy in copies:
            copy.wait()

    everyone = normed.shape[0]
    return pl.pallas_call(
        kernel,
        in_specs=[pl.BlockSpec(memory_space=pltpu.SMEM), ANYWHERE, ANYWHERE],
        out_specs=[pl.BlockSpec(memory_space=pltpu.HBM)] * len(groups),
        out_shape=[pltpu.HBM((len(group) * size, width), BF) for group in groups],
        scratch_shapes=[
            pltpu.VMEM((count, everyone, size), BF),
            pltpu.VMEM((everyone, width), BF),
            pltpu.VMEM((count, size, width), BF),
            pltpu.SemaphoreType.DMA((2 * count + 1,)),
        ],
        compiler_params=pltpu.CompilerParams(vmem_limit_bytes=24 << 20),
        cost_estimate=HIDDEN_COST,
        name="weight_grad",
    )(jnp.array(slabs, jnp.int32), *kept(normed, grad))


def sum_kernel(own_low, own_high, from_x, from_y, last_x, last_y, out_ref):
    def total(*refs):
        return sum(ref[...].astype(F32) for ref in refs).astype(BF)

    out_ref[0] = total(own_low, from_x, last_y)
    out_ref[1] = total(own_high, from_y, last_x)


def sum_call(own_low, own_high, first, last):
    half, width = own_low.shape
    rows = half // 2
    near = pl.BlockSpec((rows, width), lambda i: (i, 0))
    second = pl.BlockSpec((rows, width), lambda i: (i + 2, 0))
    out = pl.pallas_call(
        sum_kernel,
        grid=(2,),
        in_specs=[near, near, second, second, near, near],
        out_specs=pl.BlockSpec((2, rows, width), lambda i: (0, i, 0)),
        out_shape=pltpu.HBM((2, half, width), BF),
        compiler_params=stepping(24),
        cost_estimate=HIDDEN_COST,
        name="sum_lanes",
    )(*kept(own_low, own_high, *first), *last)
    return out.reshape(2 * half, width)


def add_kernel(from_x, from_y, x_high, y_low, to_x, to_y):
    to_x[...] = (x_high[...].astype(F32) + from_y[...].astype(F32)).astype(BF)
    to_y[...] = (y_low[...].astype(F32) + from_x[...].astype(F32)).astype(BF)


def add_call(got, x_high, y_low):
    high, low = x_high.shape, y_low.shape
    block = lambda shape: pl.BlockSpec(shape, lambda i: (0, 0))
    return pl.pallas_call(
        add_kernel,
        grid=(1,),
        in_specs=[block(low), block(high), block(high), block(low)],
        out_specs=[block(high), block(low)],
        out_shape=[pltpu.HBM(high, BF), pltpu.HBM(low, BF)],
        compiler_params=stepping(24),
        cost_estimate=HIDDEN_COST,
        name="add_halves",
    )(*kept(*got, x_high, y_low))


def mixer_sum_call(own_low, own_high, first, last, own):
    (low, width), high = own_low.shape, own_high.shape[0]
    rest = high - own

    def kernel(low_ref, high_ref, x_ref, y_ref, last_x, last_y, out_ref, down_ref):
        low_sum = low_ref[...].astype(F32) + x_ref[...].astype(F32) + last_y[...].astype(F32)
        high_sum = high_ref[...].astype(F32) + y_ref[...].astype(F32) + last_x[...].astype(F32)
        down_ref[:low, :] = low_sum
        down_ref[low:, :] = high_sum[:rest]
        out_ref[...] = high_sum[rest:]

    block = lambda rows, at=0: pl.BlockSpec((rows, width), lambda i: (at, 0))
    return pl.pallas_call(
        kernel,
        grid=(1,),
        in_specs=[block(low), block(high), block(low, 1), block(high, 1), block(high), block(low)],
        out_specs=[block(own), block(low + rest)],
        out_shape=[pltpu.HBM((own, width), F32), pltpu.HBM((low + rest, width), F32)],
        compiler_params=stepping(24),
        cost_estimate=HIDDEN_COST,
        name="sum_mixer",
    )(*kept(own_low, own_high, *first), *last)


def mixer_grad_call(lane, joined, masked, wide, own, own_ff, cut):
    everyone, joint = joined.shape
    width = masked.shape[1]
    rest = own + own_ff - cut

    def kernel(lane_ref, joined_any, masked_any, *refs):
        to_x, to_y, x_high, y_low, own_low, own_high, joined_ref, masked_ref, whole, sem = refs
        run_copies([(joined_any, joined_ref), (masked_any, masked_ref)], sem)
        masked = masked_ref[...]

        def product(at, size):
            whole[pl.ds(at, size), :] = lax.dot_general(
                joined_ref[:, pl.ds(at, size)],
                masked,
                CONTRACT_ROWS,
                preferred_element_type=F32,
            ).astype(BF)

        lax.fori_loop(
            0, joint // STEP, lambda i, _: product(pl.multiple_of(i * STEP, STEP), STEP), None
        )
        if joint % STEP:
            product(joint // STEP * STEP, joint % STEP)
        halves = [
            own_low,
            own_high,
            to_x.at[pl.ds(cut, cut), :],
            x_high,
            y_low,
            to_y.at[pl.ds(rest, rest), :],
            to_x.at[pl.ds(0, cut), :],
            to_y.at[pl.ds(0, rest), :],
        ]
        pairs = row_spans(wide, own, own_ff, cut, lane_ref[0], halves, whole)
        run_copies([(there, here) for here, there in pairs], sem)

    shapes = [(size, width) for size in (2 * cut, 2 * rest, rest, cut, cut, rest)]
    return pl.pallas_call(
        kernel,
        in_specs=[pl.BlockSpec(memory_space=pltpu.SMEM), ANYWHERE, ANYWHERE],
        out_specs=[pl.BlockSpec(memory_space=pltpu.HBM)] * len(shapes),
        out_shape=[pltpu.HBM(shape, BF) for shape in shapes],
        scratch_shapes=[
            pltpu.VMEM((everyone, joint), BF),
            pltpu.VMEM((everyone, width), BF),
            pltpu.VMEM((joint, width), BF),
            pltpu.SemaphoreType.DMA((3 * wide,)),
        ],
        compiler_params=pltpu.CompilerParams(vmem_limit_bytes=40 << 20),
        cost_estimate=HIDDEN_COST,
        name="mixer_grad",
    )(lane, *kept(joined, masked))


def column_plan(member, outer, wide, cores, own, own_ff, cols, main, rest):
    z, c = member // cores, member % cores
    out = []
    for g in range(3):
        for k in range(wide):
            src = (((g * outer + z) * wide + k) * cores + c) * own
            out.append((0, src, 0, g * cols + k * own, own))
    for which in range(2):
        for k in range(wide):
            src = ((z * wide + k) * cores + c) * own_ff
            lo, hi = k * own_ff, (k + 1) * own_ff
            cut = min(hi, main)
            if cut > lo:
                out.append((1 + which, src, 1, which * main + lo, cut - lo))
            low = max(lo, main)
            if hi > low:
                at = 2 * main + which * rest + low - main
                out.append((1 + which, src + low - lo, 1, at, hi - low))
    return out


def pack_kernel(plan, tp, bases, *refs):
    arrays, packed = refs[:3], refs[3:]
    rows = arrays[0].shape[0]
    edge = packed[0].shape[1]
    for member in range(tp):
        at = slice(member * rows, (member + 1) * rows)
        for which, src, part, dst, width in plan(member):
            dst += bases[part]
            for ref, low, high in ((packed[0], 0, edge), (packed[1], edge, sum(bases))):
                start, stop = max(dst, low), min(dst + width, high)
                if start < stop:
                    there = slice(src + start - dst, src + stop - dst)
                    ref[at, start - low : stop - low] = arrays[which][:, there]


def pack_call(arrays, plan, tp, widths):
    rows = arrays[0].shape[0]
    total = sum(widths)
    edge = total // 2 // TILE * TILE
    return pl.pallas_call(
        functools.partial(pack_kernel, plan, tp, (0, widths[0], total - widths[0])),
        in_specs=[HELD] * 3,
        out_specs=[HELD] * 2,
        out_shape=[jax.ShapeDtypeStruct((tp * rows, w), BF) for w in (edge, total - edge)],
        compiler_params=pltpu.CompilerParams(vmem_limit_bytes=32 << 20),
        name="pack_columns",
    )(*arrays)


def unpack_kernel(plan, tp, part, *refs):
    packed, outs = refs[0], refs[1:]
    rows = outs[0].shape[0]
    for member in range(tp):
        at = slice(member * rows, (member + 1) * rows)
        for which, src, source, dst, width in plan(member):
            if source == part:
                out = outs[which - part]
                out[:, src : src + width] = packed[at, dst : dst + width].astype(F32)


def unpack_call(packed, part, plan, tp, widths):
    rows = packed.shape[0] // tp
    return pl.pallas_call(
        functools.partial(unpack_kernel, plan, tp, part),
        in_specs=[HELD],
        out_specs=[HELD] * len(widths),
        out_shape=[jax.ShapeDtypeStruct((rows, width), F32) for width in widths],
        compiler_params=pltpu.CompilerParams(vmem_limit_bytes=32 << 20),
        cost_estimate=HIDDEN_COST,
        name="unpack_columns",
    )(packed)


def join_kernel(count, *refs):
    ins, out, sem = refs[:count], refs[count], refs[count + 1]
    copies, at = [], 0
    for i, ref in enumerate(ins):
        size = ref.shape[0]
        copies.append(pltpu.make_async_copy(ref, out.at[pl.ds(at, size), :], sem.at[i]))
        at += size
    for copy in copies:
        copy.start()
    for copy in copies:
        copy.wait()


def join_call(arrays):
    count = len(arrays)
    rows, width = sum(array.shape[0] for array in arrays), arrays[0].shape[1]
    return pl.pallas_call(
        functools.partial(join_kernel, count),
        in_specs=[pl.BlockSpec(memory_space=pl.ANY)] * count,
        out_specs=pl.BlockSpec(memory_space=pltpu.VMEM),
        out_shape=jax.ShapeDtypeStruct((rows, width), BF),
        scratch_shapes=[pltpu.SemaphoreType.DMA((count,))],
        compiler_params=pltpu.CompilerParams(vmem_limit_bytes=16 << 20),
        name="join_rows",
    )(*arrays)


def row_spans(wide, own, own_ff, cut, lane, halves, whole):
    spans = []
    base = wide * own
    for j in range(wide):
        spot = lax.bitwise_xor(lane, j)
        down = pl.multiple_of(base + spot * own_ff, 16)
        down_low = pl.multiple_of(base + spot * own_ff + cut, 16)
        out = pl.multiple_of(spot * own, 16)
        low, high = halves[2 * j : 2 * j + 2]
        rest = own_ff - cut
        spans.append((low, whole.at[pl.ds(down, cut), :]))
        spans.append((high.at[pl.ds(0, rest), :], whole.at[pl.ds(down_low, rest), :]))
        spans.append((high.at[pl.ds(rest, own), :], whole.at[pl.ds(out, own), :]))
    return spans


def run_copies(pairs, sem):
    copies = [pltpu.make_async_copy(src, dst, sem.at[i]) for i, (src, dst) in enumerate(pairs)]
    for copy in copies:
        copy.start()
    for copy in copies:
        copy.wait()


def place_call(lane, halves, wide, own, own_ff, cut):
    width = halves[0].shape[1]

    def kernel(lane_ref, *refs):
        ins, out, sem = refs[:-2], refs[-2], refs[-1]
        run_copies(row_spans(wide, own, own_ff, cut, lane_ref[0], ins, out), sem)

    return pl.pallas_call(
        kernel,
        in_specs=[pl.BlockSpec(memory_space=pltpu.SMEM)]
        + [pl.BlockSpec(memory_space=pl.ANY)] * len(halves),
        out_specs=pl.BlockSpec(memory_space=pltpu.VMEM),
        out_shape=jax.ShapeDtypeStruct((wide * (own + own_ff), width), BF),
        scratch_shapes=[pltpu.SemaphoreType.DMA((3 * wide,))],
        compiler_params=pltpu.CompilerParams(vmem_limit_bytes=16 << 20),
        name="place_rows",
    )(lane, *halves)


def mixer_product(joined, masked):
    return lax.dot_general(joined, masked, CONTRACT_ROWS, preferred_element_type=F32).astype(BF)


class Plain:
    def __init__(self, outer, inner):
        self.tp, self.wide, self.cores, self.outer = outer, inner, 1, outer
        self.member = lax.axis_index("dp")
        self.token_axes, self.token_groups = "dp", None
        self.weight_axes, self.weight_groups = "fsdp", None

    def gather_tokens(self, block):
        return lax.all_gather(
            block, self.token_axes, axis=0, tiled=True, axis_index_groups=self.token_groups
        )

    def scatter_tokens(self, part):
        return lax.psum_scatter(
            part.astype(BF),
            self.token_axes,
            scatter_dimension=0,
            tiled=True,
            axis_index_groups=self.token_groups,
        ).astype(F32)

    def exchange(self, part):
        return lax.all_to_all(
            part,
            self.token_axes,
            split_axis=0,
            concat_axis=0,
            tiled=True,
            axis_index_groups=self.token_groups,
        )

    def gather_weights(self, block):
        return lax.all_gather(
            block, self.weight_axes, axis=0, tiled=True, axis_index_groups=self.weight_groups
        )

    def scatter_weights(self, part):
        return lax.psum_scatter(
            part,
            self.weight_axes,
            scatter_dimension=0,
            tiled=True,
            axis_index_groups=self.weight_groups,
        )

    def inputs(self, packed, w_out, w_down, normed, masked, lengths, make_tables):
        mixer = jnp.concatenate([self.gather_weights(w) for w in (w_out, w_down)], axis=0)
        entry = [self.gather_weights(self.exchange(part)) for part in packed]
        tokens = [self.gather_tokens(block) for block in (normed, masked)]
        lengths = lax.all_gather(lengths, "dp", axis=0, tiled=True)
        return entry, mixer, tokens[0], tokens[1], make_tables(lengths)

    def outputs(self, joined, masked, branch, back_call, tail, normed, own, own_ff):
        cols = self.wide * own
        part = mixer_product(joined, masked)
        grads = [self.scatter_weights(p).astype(F32) for p in (part[:cols], part[cols:])]
        grad_qkv, grad_ff, norm, bias_part = back_call(masked)
        parts = []
        for grad in (grad_qkv, grad_ff):
            part = lax.dot_general(normed, grad, CONTRACT_ROWS, preferred_element_type=F32)
            parts.append(self.scatter_weights(part.astype(BF)))
        norm, branch = self.scatter_tokens(norm), self.scatter_tokens(branch)
        part_qkv, part_ff = [self.exchange(part) for part in parts]
        grad_tokens, stats = tail(norm, bias_part)
        return grads[0], grads[1], part_qkv, part_ff, branch, grad_tokens, stats

    def relative(self, blocks, axis):
        return blocks

    def scatter_stats(self, stats):
        parts = lax.all_to_all(stats, AXES, split_axis=0, concat_axis=0, tiled=True)
        return jnp.sum(parts, axis=0)


class Linked(Plain):
    def __init__(self, outer, inner):
        self.outer, self.cores, self.wide = outer, 2, inner // 2
        self.tp = outer * 2
        flat = lax.axis_index("fsdp")
        self.lane = flat // 2
        self.member = lax.axis_index("dp") * 2 + lax.rem(flat, 2)
        spots = [
            [[(z * self.wide + k) * 2 + c for c in range(2)] for k in range(self.wide)]
            for z in range(outer)
        ]
        self.token_axes = self.weight_axes = AXES
        self.token_groups = [
            [spots[z][k][c] for z in range(outer) for c in range(2)] for k in range(self.wide)
        ]
        self.weight_groups = [
            [spots[z][k][c] for k in range(self.wide)] for z in range(outer) for c in range(2)
        ]
        self.spots = spots
        self.lane_index = self.lane.astype(jnp.int32).reshape(1)

    def send(self, value, step=0, dz=0, dc=0):
        pairs = [
            (self.spots[z][k][c], self.spots[z ^ dz][k ^ step][c ^ dc])
            for z in range(self.outer)
            for k in range(self.wide)
            for c in range(2)
        ]
        return lax.ppermute(value, AXES, pairs)

    def gather_lengths(self, lengths):
        parts = [lengths] + [self.send(lengths, dz=dz) for dz in range(1, self.outer)]
        return jnp.concatenate(parts, axis=0)

    def order_lengths(self, mine, other):
        both = jnp.stack([mine, other], axis=1).reshape(self.tp, -1)
        spot = lax.bitwise_xor(jnp.arange(self.tp, dtype=jnp.int32), self.member)
        pick = spot[:, None] == jnp.arange(self.tp, dtype=jnp.int32)[None, :]
        return jnp.sum(jnp.where(pick[:, :, None], both[None], 0), axis=1)

    def inputs(self, packed, w_out, w_down, normed, masked, lengths, make_tables):
        own, own_ff = w_out.shape[0], w_down.shape[0]
        cut = own_ff // 32 * 16 + 32
        half = packed[0].shape[0] // 2
        rows, left, right, lengths = tie(join_call([w_down, w_out]), *packed, lengths)
        mix_x, mix_y = self.send(rows, 1), self.send(rows, 2)
        lengths = self.gather_lengths(lengths)
        left = self.exchange(left)
        left, right, mix_x, mix_y = tie(left, right, mix_x, mix_y)
        left_x, left_y = self.send(left, 1), self.send(left, 2)
        right = self.exchange(right)
        halves = [part for b in (rows, mix_x, mix_y) for part in (b[:cut], b[cut:])]
        right, left_x, left_y, normed, masked, lengths, *halves = tie(
            right, left_x, left_y, normed, masked, lengths, *halves
        )
        normed_all, masked_all = self.gather_tokens(normed), self.gather_tokens(masked)
        right_x, right_y = self.send(right, 1), self.send(right, 2)
        mix_low, mix_high = self.send(halves[2], 2), self.send(halves[5], 1)
        left_low, left_high = self.send(left_x[:half], 2), self.send(left_y[half:], 1)
        tables = make_tables(self.order_lengths(lengths, self.send(lengths, dc=1)))
        halves += [mix_low, mix_high]
        mixer = place_call(self.lane_index, halves, self.wide, own, own_ff, cut)
        right_x, right_y, left_low, left_high, mixer, *tables = tie(
            right_x, right_y, left_low, left_high, *kept(mixer, *tables)
        )
        right_low, right_high = self.send(right_x[:half], 2), self.send(right_y[half:], 1)
        entry = [left, left_x, left_y, left_low, left_high]
        entry += [right, right_x, right_y, right_low, right_high]
        return entry, mixer, normed_all, masked_all, tables

    def first_sends(self, to_x, to_y):
        return self.send(to_x, 1), self.send(to_y, 2)

    def last_sends(self, got, x_high, y_low):
        from_x, from_y = got
        low, high = from_x[: y_low.shape[0]], from_y[: x_high.shape[0]]
        return (
            self.send((x_high.astype(F32) + high.astype(F32)).astype(BF), 1),
            self.send((y_low.astype(F32) + low.astype(F32)).astype(BF), 2),
        )

    def lane_sum(self, own_low, own_high, first, last):
        low = own_low.astype(F32) + first[0][own_low.shape[0] :].astype(F32)
        high = own_high.astype(F32) + first[1][own_high.shape[0] :].astype(F32)
        return low + last[1].astype(F32), high + last[0].astype(F32)

    def outputs(self, joined, masked, branch, back_call, tail, normed, own, own_ff):
        cut = own_ff // 32 * 16 + 32
        rest = own_ff - cut
        size = normed.shape[1] // self.wide // 2
        first, last = ((6, 2), (7, 5)), ((3,), (4,), (0,), (1,))

        branch = self.scatter_tokens(branch)
        mix = mixer_grad_call(self.lane_index, joined, masked, self.wide, own, own_ff, cut)
        *mix, masked = tie(*mix, masked)
        mix_first = self.first_sends(mix[0], mix[1])
        grad_qkv, grad_ff, norm, bias_part = back_call(masked)
        *mix_first, norm, grad_ff, grad_qkv = tie(*mix_first, norm, grad_ff, grad_qkv)
        norm = self.scatter_tokens(norm)
        to_x, to_y = product_call(normed, grad_ff, first, size)
        to_x, to_y, grad_ff = tie(to_x, to_y, grad_ff)
        ff_first = self.first_sends(to_x, to_y)
        x_high, y_low, ff_low, ff_high = product_call(normed, grad_ff, last, size)
        ff_low, grad_qkv = tie(ff_low, grad_qkv)
        to_x, to_y = product_call(normed, grad_qkv, first, size)
        to_x, grad_qkv = tie(to_x, grad_qkv)
        qkv_x, qkv_y, qkv_low, qkv_high = product_call(normed, grad_qkv, last, size)
        branch, to_x, to_y, x_high, y_low, qkv_low, *ff_first = tie(
            branch, to_x, to_y, x_high, y_low, qkv_low, *ff_first
        )
        ff_last = self.last_sends(ff_first, x_high, y_low)
        part_ff = self.joined_sum((x_high, y_low, ff_low, ff_high), ff_first, ff_last)
        part_ff, to_x, to_y = tie(part_ff, to_x, to_y)
        qkv_first = self.first_sends(to_x, to_y)
        part_ff = self.exchange(part_ff)
        results = tail(norm, bias_part)
        *qkv_first, grad_tokens, stats = tie(*qkv_first, *results)
        qkv_last = self.last_sends(qkv_first, qkv_x, qkv_y)
        part_qkv = self.joined_sum((qkv_x, qkv_y, qkv_low, qkv_high), qkv_first, qkv_last)
        stats = self.depth_stats(stats)
        part_ff, part_qkv, stats, *mix = tie(part_ff, part_qkv, stats, *mix_first, *mix[2:])
        part_qkv = self.exchange(part_qkv)
        mix_first, mix = mix[:2], mix[2:]
        mix_x, mix_y = add_call(mix_first, mix[0], mix[1])
        mix_last = self.send(mix_x, 1), self.send(mix_y, 2)
        grad_w_out, grad_w_down = mixer_sum_call(mix[2], mix[3], mix_first, mix_last, own)
        return grad_w_out, grad_w_down, part_qkv, part_ff, branch, grad_tokens, stats

    def joined_sum(self, late, first, last):
        return sum_call(late[2], late[3], first, last)

    def keep(self, values, axis, place, count, name):
        pick = lambda spot: lax.dynamic_index_in_dim(values, spot, axis, keepdims=False)
        got = [self.send(pick(lax.bitwise_xor(place, j)), **{name: j}) for j in range(1, count)]
        return pick(place) + sum(got)

    def depth_stats(self, stats):
        split = stats.reshape(self.outer, self.wide, 2, -1)
        return self.keep(split, 0, self.member // 2, self.outer, "dz")

    def scatter_stats(self, split):
        split = self.keep(split, 0, self.lane, self.wide, "step")
        return self.keep(split, 0, lax.rem(self.member, 2), 2, "dc")

    def relative(self, blocks, axis):
        shape = blocks.shape
        split = blocks.reshape(shape[:axis] + (2, 2) + shape[axis + 1 :])
        split = jnp.where(self.lane >= 2, jnp.flip(split, axis), split)
        split = jnp.where(lax.rem(self.lane, 2) == 1, jnp.flip(split, axis + 1), split)
        return split.reshape(shape)


def on_device(
    tokens, ln_gain, ln_shift, w_qkv, b_qkv, w_out, w_gate, w_up, w_down, grad_out, seq_lengths
):
    outer, inner = lax.axis_size("dp"), lax.axis_size("fsdp")
    linked = outer == 4 and inner == 8
    net = Linked(outer, inner) if linked else Plain(outer, inner)
    tp, wide, cores = net.tp, net.wide, net.cores
    rows_tok, width = tokens.shape
    own = w_qkv.shape[0]
    own_ff = w_down.shape[0]
    cols, cols_ff = wide * own, wide * own_ff
    main = cols_ff // TILE * TILE
    rest = cols_ff - main
    widths = (3 * cols, 2 * cols_ff)
    plan = lambda member: column_plan(
        member, outer, wide, cores, own, own_ff, cols, main, rest
    )

    _, valid, _ = block_terms(seq_lengths[0], rows_tok)
    keep_row = valid.astype(F32)[:, None]
    widened = tokens.astype(F32)
    centered = widened - jnp.mean(widened, axis=1, keepdims=True)
    inv_std = lax.rsqrt(jnp.mean(centered * centered, axis=1, keepdims=True) + EPS)
    scaled = centered * inv_std
    normed = (scaled * ln_gain + ln_shift).astype(BF)
    masked = (grad_out.astype(F32) * keep_row).astype(BF)

    def lanes_first(x):
        split = x.reshape(rows_tok, outer, wide, cores * own)
        return net.relative(jnp.swapaxes(split, 1, 2), 1).reshape(rows_tok, width)

    def lanes_back(x):
        split = net.relative(x.reshape(rows_tok, wide, outer, cores * own), 1)
        return jnp.swapaxes(split, 1, 2).reshape(rows_tok, width)

    lengths = seq_lengths
    arrays = [w_qkv, w_gate, w_up]

    bias = lax.dynamic_index_in_dim(
        jnp.transpose(b_qkv.reshape(3, outer, wide, cores, own), (1, 3, 0, 2, 4)).reshape(tp, -1),
        net.member,
        0,
    )
    bias = jnp.broadcast_to(bias, (8, 3 * cols))

    def make_tables(lengths):
        position, _, allowed = jax.vmap(lambda row: block_terms(row, rows_tok))(lengths)
        return [*turn_tables(position), jnp.where(allowed, 0.0, NEG), bias]

    entry, mixer, normed_all, masked_all, (cos_t, sin_t, mask, bias) = net.inputs(
        pack_call(arrays, plan, tp, widths),
        w_out,
        w_down,
        lanes_first(normed),
        masked,
        lengths,
        make_tables,
    )
    sizes = (cols, main, rest)
    joined, qkv, proj_ff, branch = forward_call(
        normed_all, bias, cos_t, sin_t, mask, entry, mixer, sizes
    )
    back_call = lambda masked: backward_call(
        masked, proj_ff, qkv, cos_t, sin_t, mask, mixer, entry, sizes
    )

    def tail(grad_norm, bias_part):
        grad_norm = lanes_back(grad_norm)
        lifted_grad = grad_norm * ln_gain
        grad_in = inv_std * (
            lifted_grad
            - jnp.mean(lifted_grad, axis=1, keepdims=True)
            - scaled * jnp.mean(lifted_grad * scaled, axis=1, keepdims=True)
        )
        grad_tokens = (grad_out.astype(F32) + grad_in).astype(BF)
        shards = outer * inner
        gain_part = jnp.sum(grad_norm * scaled, axis=0)
        shift_part = jnp.sum(grad_norm, axis=0)
        bias_full = lax.dynamic_update_index_in_dim(
            jnp.zeros((tp, 3 * cols), F32), bias_part[0], net.member, 0
        )
        bias_full = jnp.transpose(bias_full.reshape(outer, cores, 3, wide, own), (2, 0, 3, 1, 4))
        stats = jnp.concatenate(
            [
                gain_part.reshape(shards, own),
                shift_part.reshape(shards, own),
                bias_full.reshape(shards, 3 * own),
            ],
            axis=1,
        )
        return grad_tokens, stats

    grad_w_out, grad_w_down, part_qkv, part_ff, branch, grad_tokens, stats = net.outputs(
        joined, masked_all, branch, back_call, tail, normed_all, own, own_ff
    )
    output = (widened + keep_row * branch).astype(BF)
    grad_w_gate, grad_w_up = unpack_call(
        part_ff, 1, plan, tp, [w_gate.shape[1], w_up.shape[1]]
    )
    stats, grad_w_gate, grad_w_up = tie(stats, grad_w_gate, grad_w_up)
    stats = net.scatter_stats(stats)
    part_qkv, stats, grad_w_gate, grad_w_up = tie(part_qkv, stats, grad_w_gate, grad_w_up)
    (grad_w_qkv,) = unpack_call(part_qkv, 0, plan, tp, [w_qkv.shape[1]])
    return (
        output,
        grad_tokens,
        grad_w_qkv,
        grad_w_out,
        grad_w_gate,
        grad_w_up,
        grad_w_down,
        stats[:own],
        stats[own : 2 * own],
        stats[2 * own :],
    )


def solution(mesh):
    rows = P(AXES, None)
    return jax.shard_map(
        on_device,
        mesh=mesh,
        in_specs=(rows, P(), P(), rows, P(), rows, rows, rows, rows, rows, rows),
        out_specs=(rows,) * 7 + (P(AXES),) * 3,
        check_vma=False,
    )
```

```python
import functools
import math

import jax
import jax.numpy as jnp
from jax import lax
from jax.experimental import pallas as pl
from jax.experimental.pallas import tpu as pltpu
from jax.sharding import PartitionSpec as P

HD = 64
ROT = 16
EPS = 1e-05
NEG = -1e30
TILE = 128
AXES = ("dp", "fsdp")
BF = jnp.bfloat16
F32 = jnp.float32
CONTRACT_ROWS = (((0,), (0,)), ((), ()))
CONTRACT_COLS = (((1,), (1,)), ((), ()))


def block_terms(lengths_row, rows_tok):
    ends = jnp.cumsum(lengths_row)
    place = jnp.arange(rows_tok, dtype=jnp.int32)
    segment = jnp.sum((place[:, None] >= ends[None, :]).astype(jnp.int32), axis=1)
    starts = jnp.concatenate([ends - lengths_row, ends[-1:]])
    labels = jnp.arange(starts.shape[0], dtype=jnp.int32)
    begin = jnp.sum(jnp.where(segment[:, None] == labels[None, :], starts[None, :], 0), axis=1)
    position = (place - begin).astype(F32)
    valid = segment < lengths_row.shape[0]
    label_tok = jnp.where(valid, segment, lengths_row.shape[0] + place)
    allowed = (label_tok[:, None] == label_tok[None, :]) & (place[None, :] <= place[:, None])
    return (position, valid, allowed)


def turn_tables(position):
    half = ROT // 2
    freq = jnp.exp(jnp.arange(half, dtype=F32) * (-2.0 * math.log(10000.0) / ROT))
    turn = position.reshape(-1)[:, None] * freq[None, :]
    cosine, sine = jnp.cos(turn), jnp.sin(turn)
    rest = (turn.shape[0], HD - ROT)
    cos_t = jnp.concatenate([cosine, cosine, jnp.ones(rest, F32)], axis=1)
    sin_t = jnp.concatenate([-sine, sine, jnp.zeros(rest, F32)], axis=1)
    return (jnp.tile(cos_t, (1, 2)), jnp.tile(sin_t, (1, 2)))


def tie(*values):
    return lax.optimization_barrier(values)


def turned(v, cos_t, sin_t, low_half):
    partner = jnp.where(low_half, pltpu.roll(v, TILE - ROT // 2, 1), pltpu.roll(v, ROT // 2, 1))
    return v * cos_t + partner * sin_t

def stacked(v, first):
    zero = jnp.zeros_like(v)
    return jnp.concatenate([jnp.where(first, v, zero), jnp.where(first, zero, v)], axis=0)

def softmax_of(query2, keys, bias2):
    scores = lax.dot_general(query2, keys, (((1,), (1,)), ((), ())), preferred_element_type=F32)
    scores = scores * 0.125 + bias2
    lifted = jnp.exp(scores - jnp.max(scores, axis=1, keepdims=True))
    return lifted / jnp.sum(lifted, axis=1, keepdims=True)

def attend_rows(cols, main, rest, at, pq_ref, pf_ref, bias_ref, tables, joined_ref, qkv_ref):
    cos_t, sin_t, bias2, first, low_half = tables
    size = cos_t.shape[0]
    rows = slice(at, at + size)
    for pair in range(cols // TILE):
        places = [g * cols + pair * TILE for g in range(3)]
        query, keys, values = (
            pq_ref[rows, p : p + TILE] + bias_ref[0:1, p : p + TILE] for p in places
        )
        query = turned(query, cos_t, sin_t, low_half).astype(BF)
        keys = turned(keys, cos_t, sin_t, low_half).astype(BF)
        values = values.astype(BF)
        for p, v in zip(places, (query, keys, values)):
            qkv_ref[rows, p : p + TILE] = v
        probs = softmax_of(stacked(query, first), keys, bias2).astype(BF)
        mixed = jnp.dot(probs, values, preferred_element_type=F32)
        joined_ref[rows, pair * TILE : (pair + 1) * TILE] = jnp.where(
            first, mixed[:size], mixed[size:]
        ).astype(BF)
    for j in range(main // TILE):
        gate = pf_ref[rows, j * TILE : (j + 1) * TILE]
        up = pf_ref[rows, main + j * TILE : main + (j + 1) * TILE]
        hid = gate * jax.nn.sigmoid(gate) * up
        joined_ref[rows, cols + j * TILE : cols + (j + 1) * TILE] = hid.astype(BF)
    if rest:
        tail = pf_ref[rows, 2 * main :]
        up = pltpu.roll(tail, rest, 1)
        hid = tail * jax.nn.sigmoid(tail) * up
        joined_ref[rows, cols + main :] = hid[:, :rest].astype(BF)


def attend_back_rows(cols, main, rest, at, pf_ref, back_ref, qkv_ref, tables, gq_ref, gf_ref, sum_ref):
    cos_t, sin_t, bias2, first, low_half = tables
    size = cos_t.shape[0]
    rows = slice(at, at + size)
    across = (((0,), (0,)), ((), ()))
    for pair in range(cols // TILE):
        places = [g * cols + pair * TILE for g in range(3)]
        query, keys, values = (qkv_ref[rows, p : p + TILE] for p in places)
        query2 = stacked(query, first)
        mixed2 = stacked(back_ref[rows, pair * TILE : (pair + 1) * TILE].astype(BF), first)
        probs = softmax_of(query2, keys, bias2)
        grad_probs = lax.dot_general(
            mixed2, values, (((1,), (1,)), ((), ())), preferred_element_type=F32
        )
        inner = jnp.sum(probs * grad_probs, axis=1, keepdims=True)
        grad_scores = (probs * (grad_probs - inner)).astype(BF)
        gq = jnp.dot(grad_scores, keys, preferred_element_type=F32)
        gq = jnp.where(first, gq[:size], gq[size:]) * 0.125
        gk = lax.dot_general(grad_scores, query2, across, preferred_element_type=F32) * 0.125
        gv = lax.dot_general(probs.astype(BF), mixed2, across, preferred_element_type=F32)
        gq = turned(gq, cos_t, -sin_t, low_half)
        gk = turned(gk, cos_t, -sin_t, low_half)
        for p, v in zip(places, (gq, gk, gv)):
            low = v.astype(BF)
            gq_ref[rows, p : p + TILE] = low
            sum_ref[0:1, p : p + TILE] += jnp.sum(low.astype(F32), axis=0, keepdims=True)

    def gates(gate, up, grad_hid):
        sigma = jax.nn.sigmoid(gate)
        slope = sigma * (1.0 + gate * (1.0 - sigma))
        return (grad_hid * up * slope, grad_hid * (gate * sigma))

    for j in range(main // TILE):
        p, q = j * TILE, main + j * TILE
        grad_hid = back_ref[rows, cols + j * TILE : cols + (j + 1) * TILE]
        gg, gu = gates(pf_ref[rows, p : p + TILE], pf_ref[rows, q : q + TILE], grad_hid)
        gf_ref[rows, p : p + TILE] = gg.astype(BF)
        gf_ref[rows, q : q + TILE] = gu.astype(BF)
    if rest:
        tail = pf_ref[rows, 2 * main :]
        short = back_ref[rows, cols + main :]
        grad_hid = jnp.concatenate([short, jnp.zeros_like(short)], axis=1)
        gg, gu = gates(tail, pltpu.roll(tail, rest, 1), grad_hid)
        lane = lax.broadcasted_iota(jnp.int32, (size, TILE), 1)
        both = jnp.where(lane < rest, gg, pltpu.roll(gu, rest, 1))
        gf_ref[rows, 2 * main :] = both.astype(BF)


def block_tables(cos_ref, sin_ref, mask_ref, block, size):
    lane = lax.broadcasted_iota(jnp.int32, (size, TILE), 1)
    rows = slice(block * size, (block + 1) * size)
    mask = mask_ref[block]
    return (
        cos_ref[rows, :],
        sin_ref[rows, :],
        jnp.concatenate([mask, mask], axis=0),
        lane < HD,
        lane % HD < ROT // 2,
    )


def stack_copies(pieces, whole, sem, start):
    copies, count = [], len(pieces) // 2
    edge = pieces[0].shape[1]
    for group, columns in enumerate((pl.ds(0, edge), pl.ds(edge, whole.shape[1] - edge))):
        at = 0
        for i in range(group * count, (group + 1) * count):
            size = pieces[i].shape[0]
            dst = whole.at[pl.ds(at, size), columns]
            copies.append(pltpu.make_async_copy(pieces[i], dst, sem.at[start + i]))
            at += size
    return copies


def forward_kernel(sizes, count, block, *refs):
    cols, main, rest = sizes
    normed_ref, bias_ref, cos_ref, sin_ref, mask_ref = refs[:5]
    pieces, mixer_any = refs[5 : 5 + count], refs[5 + count]
    joined_ref, qkv_ref, pf_ref, branch_ref = refs[6 + count : 10 + count]
    entry, wm, pq, sem = refs[10 + count :]
    groups = [
        stack_copies(pieces, entry, sem, 0),
        [pltpu.make_async_copy(mixer_any, wm, sem.at[count])],
    ]
    opening = pl.program_id(0) == 0

    @pl.when(opening)
    def _():
        for group in groups:
            for copy in group:
                copy.start()

    def arrive(group):
        @pl.when(opening)
        def _():
            for copy in groups[group]:
                copy.wait()

    normed = normed_ref[...]
    arrive(0)
    pq[...] = jnp.dot(normed, entry[:, : 3 * cols], preferred_element_type=F32)
    pf_ref[...] = jnp.dot(normed, entry[:, 3 * cols :], preferred_element_type=F32)
    for i in range(normed.shape[0] // block):
        tables = block_tables(cos_ref, sin_ref, mask_ref, i, block)
        attend_rows(
            cols, main, rest, i * block, pq, pf_ref, bias_ref, tables, joined_ref, qkv_ref
        )
    arrive(1)
    branch = jnp.dot(joined_ref[...], wm[...], preferred_element_type=F32)
    branch_ref[...] = branch.astype(BF)


def backward_kernel(sizes, count, block, *refs):
    cols, main, rest = sizes
    masked_ref, pf_ref, qkv_ref, cos_ref, sin_ref, mask_ref, mixer_any = refs[:7]
    pieces = refs[7 : 7 + count]
    gq_ref, gf_ref, norm_ref, sum_ref = refs[7 + count : 11 + count]
    wm, entry, back, sem = refs[11 + count :]
    mixer_copy = pltpu.make_async_copy(mixer_any, wm, sem.at[count])
    copies = stack_copies(pieces, entry, sem, 0)
    opening = pl.program_id(0) == 0

    @pl.when(opening)
    def _():
        mixer_copy.start()
        for copy in copies:
            copy.start()
        sum_ref[...] = jnp.zeros_like(sum_ref)
        mixer_copy.wait()

    back[...] = lax.dot_general(
        masked_ref[...], wm[...], CONTRACT_COLS, preferred_element_type=F32
    )
    for i in range(masked_ref.shape[0] // block):
        tables = block_tables(cos_ref, sin_ref, mask_ref, i, block)
        attend_back_rows(
            cols, main, rest, i * block, pf_ref, back, qkv_ref, tables, gq_ref, gf_ref, sum_ref
        )

    @pl.when(opening)
    def _():
        for copy in copies:
            copy.wait()

    cut = 3 * cols
    total = lax.dot_general(
        gq_ref[...], entry[:, :cut], CONTRACT_COLS, preferred_element_type=F32
    )
    total += lax.dot_general(
        gf_ref[...], entry[:, cut:], CONTRACT_COLS, preferred_element_type=F32
    )
    norm_ref[...] = total.astype(BF)


STEP = 256
HIDDEN_COST = pl.CostEstimate(flops=1, bytes_accessed=1, transcendentals=0)


def row_spec(width, rows=STEP):
    return pl.BlockSpec((rows, width), lambda i: (i, 0))


ANYWHERE = pl.BlockSpec(memory_space=pl.ANY)
HELD = pl.BlockSpec(memory_space=pltpu.VMEM)


def kept(*arrays):
    return [pltpu.with_memory_space_constraint(array, pltpu.HBM) for array in arrays]


def stepping(limit):
    return pltpu.CompilerParams(
        dimension_semantics=("arbitrary",), vmem_limit_bytes=limit << 20
    )


def forward_call(normed, bias, cos_t, sin_t, mask, pieces, mixer, sizes):
    cols, main, rest = sizes
    everyone, width = normed.shape
    block = mask.shape[1]
    count = len(pieces)
    joint = cols + main + rest
    return pl.pallas_call(
        functools.partial(forward_kernel, sizes, count, block),
        grid=(everyone // STEP,),
        in_specs=[
            row_spec(width),
            pl.BlockSpec((8, 3 * cols), lambda i: (0, 0)),
            row_spec(TILE),
            row_spec(TILE),
            pl.BlockSpec((STEP // block, block, block), lambda i: (i, 0, 0)),
        ]
        + [ANYWHERE] * (count + 1),
        out_specs=[
            row_spec(joint),
            row_spec(3 * cols),
            row_spec(2 * (main + rest)),
            row_spec(width),
        ],
        out_shape=[
            pltpu.HBM((everyone, joint), BF),
            pltpu.HBM((everyone, 3 * cols), BF),
            pltpu.HBM((everyone, 2 * (main + rest)), F32),
            pltpu.HBM((everyone, width), BF),
        ],
        scratch_shapes=[
            pltpu.VMEM((width, 3 * cols + 2 * (main + rest)), BF),
            pltpu.VMEM((joint, width), BF),
            pltpu.VMEM((STEP, 3 * cols), F32),
            pltpu.SemaphoreType.DMA((count + 1,)),
        ],
        compiler_params=stepping(36),
        cost_estimate=HIDDEN_COST,
        name="forward",
    )(*kept(normed, bias, cos_t, sin_t, mask, *pieces, mixer))


def backward_call(masked, pf, qkv, cos_t, sin_t, mask, mixer, pieces, sizes):
    cols, main, rest = sizes
    everyone, width = masked.shape
    block = mask.shape[1]
    count = len(pieces)
    joint = cols + main + rest
    total = 3 * cols + 2 * (main + rest)
    return pl.pallas_call(
        functools.partial(backward_kernel, sizes, count, block),
        grid=(everyone // STEP,),
        in_specs=[
            row_spec(width),
            row_spec(2 * (main + rest)),
            row_spec(3 * cols),
            row_spec(TILE),
            row_spec(TILE),
            pl.BlockSpec((STEP // block, block, block), lambda i: (i, 0, 0)),
        ]
        + [ANYWHERE] * (count + 1),
        out_specs=[
            row_spec(3 * cols),
            row_spec(2 * (main + rest)),
            row_spec(width),
            pl.BlockSpec((8, 3 * cols), lambda i: (0, 0)),
        ],
        out_shape=[
            pltpu.HBM((everyone, 3 * cols), BF),
            pltpu.HBM((everyone, 2 * (main + rest)), BF),
            pltpu.HBM((everyone, width), BF),
            pltpu.HBM((8, 3 * cols), F32),
        ],
        scratch_shapes=[
            pltpu.VMEM((joint, width), BF),
            pltpu.VMEM((width, total), BF),
            pltpu.VMEM((STEP, joint), F32),
            pltpu.SemaphoreType.DMA((count + 1,)),
        ],
        compiler_params=stepping(36),
        cost_estimate=HIDDEN_COST,
        name="backward",
    )(*kept(masked, pf, qkv, cos_t, sin_t, mask, mixer, *pieces))


def product_call(normed, grad, groups, size):
    low, width = 0, grad.shape[1]
    slabs = [slab for group in groups for slab in group]
    places = [(g, at) for g, group in enumerate(groups) for at in range(len(group))]
    count = len(slabs)

    def kernel(table_ref, lhs_any, grad_any, *refs):
        outs, (lhs, grad, held, sem) = refs[: len(groups)], refs[len(groups) :]
        loads = [pltpu.make_async_copy(grad_any.at[:, pl.ds(low, width)], grad, sem.at[2 * count])]
        copies = []
        for i, (g, at) in enumerate(places):
            slab = pl.multiple_of(table_ref[i] * size, size)
            src = lhs_any.at[:, pl.ds(slab, size)]
            loads.append(pltpu.make_async_copy(src, lhs.at[i], sem.at[count + i]))
            dst = outs[g].at[pl.ds(at * size, size), :]
            copies.append(pltpu.make_async_copy(held.at[i], dst, sem.at[i]))
        for load in loads:
            load.start()
        loads[0].wait()

        def step(i, _):
            for j in range(count):
                pl.when(i == j)(loads[1 + j].wait)
            held[i] = lax.dot_general(
                lhs[i], grad[...], CONTRACT_ROWS, preferred_element_type=F32
            ).astype(BF)
            for j, copy in enumerate(copies):
                pl.when(i == j)(copy.start)

        lax.fori_loop(0, count, step, None)
        for copy in copies:
            copy.wait()

    everyone = normed.shape[0]
    return pl.pallas_call(
        kernel,
        in_specs=[pl.BlockSpec(memory_space=pltpu.SMEM), ANYWHERE, ANYWHERE],
        out_specs=[pl.BlockSpec(memory_space=pltpu.HBM)] * len(groups),
        out_shape=[pltpu.HBM((len(group) * size, width), BF) for group in groups],
        scratch_shapes=[
            pltpu.VMEM((count, everyone, size), BF),
            pltpu.VMEM((everyone, width), BF),
            pltpu.VMEM((count, size, width), BF),
            pltpu.SemaphoreType.DMA((2 * count + 1,)),
        ],
        compiler_params=pltpu.CompilerParams(vmem_limit_bytes=24 << 20),
        cost_estimate=HIDDEN_COST,
        name="weight_grad",
    )(jnp.array(slabs, jnp.int32), *kept(normed, grad))


def sum_kernel(own_low, own_high, from_x, from_y, last_x, last_y, out_ref):
    def total(*refs):
        return sum(ref[...].astype(F32) for ref in refs).astype(BF)

    out_ref[0] = total(own_low, from_x, last_y)
    out_ref[1] = total(own_high, from_y, last_x)


def sum_call(own_low, own_high, first, last):
    half, width = own_low.shape
    rows = half // 2
    near = pl.BlockSpec((rows, width), lambda i: (i, 0))
    second = pl.BlockSpec((rows, width), lambda i: (i + 2, 0))
    out = pl.pallas_call(
        sum_kernel,
        grid=(2,),
        in_specs=[near, near, second, second, near, near],
        out_specs=pl.BlockSpec((2, rows, width), lambda i: (0, i, 0)),
        out_shape=pltpu.HBM((2, half, width), BF),
        compiler_params=stepping(24),
        cost_estimate=HIDDEN_COST,
        name="sum_lanes",
    )(*kept(own_low, own_high, *first), *last)
    return out.reshape(2 * half, width)


def add_kernel(from_x, from_y, x_high, y_low, to_x, to_y):
    to_x[...] = (x_high[...].astype(F32) + from_y[...].astype(F32)).astype(BF)
    to_y[...] = (y_low[...].astype(F32) + from_x[...].astype(F32)).astype(BF)


def add_call(got, x_high, y_low):
    high, low = x_high.shape, y_low.shape
    block = lambda shape: pl.BlockSpec(shape, lambda i: (0, 0))
    return pl.pallas_call(
        add_kernel,
        grid=(1,),
        in_specs=[block(low), block(high), block(high), block(low)],
        out_specs=[block(high), block(low)],
        out_shape=[pltpu.HBM(high, BF), pltpu.HBM(low, BF)],
        compiler_params=stepping(24),
        cost_estimate=HIDDEN_COST,
        name="add_halves",
    )(*kept(*got, x_high, y_low))


def mixer_sum_call(own_low, own_high, first, last, own):
    (low, width), high = own_low.shape, own_high.shape[0]
    rest = high - own

    def kernel(low_ref, high_ref, x_ref, y_ref, last_x, last_y, out_ref, down_ref):
        low_sum = low_ref[...].astype(F32) + x_ref[...].astype(F32) + last_y[...].astype(F32)
        high_sum = high_ref[...].astype(F32) + y_ref[...].astype(F32) + last_x[...].astype(F32)
        down_ref[:low, :] = low_sum
        down_ref[low:, :] = high_sum[:rest]
        out_ref[...] = high_sum[rest:]

    block = lambda rows, at=0: pl.BlockSpec((rows, width), lambda i: (at, 0))
    return pl.pallas_call(
        kernel,
        grid=(1,),
        in_specs=[block(low), block(high), block(low, 1), block(high, 1), block(high), block(low)],
        out_specs=[block(own), block(low + rest)],
        out_shape=[pltpu.HBM((own, width), F32), pltpu.HBM((low + rest, width), F32)],
        compiler_params=stepping(24),
        cost_estimate=HIDDEN_COST,
        name="sum_mixer",
    )(*kept(own_low, own_high, *first), *last)


def mixer_grad_call(lane, joined, masked, wide, own, own_ff, cut):
    everyone, joint = joined.shape
    width = masked.shape[1]
    rest = own + own_ff - cut

    def kernel(lane_ref, joined_any, masked_any, *refs):
        to_x, to_y, x_high, y_low, own_low, own_high, joined_ref, masked_ref, whole, sem = refs
        run_copies([(joined_any, joined_ref), (masked_any, masked_ref)], sem)
        masked = masked_ref[...]

        def product(at, size):
            whole[pl.ds(at, size), :] = lax.dot_general(
                joined_ref[:, pl.ds(at, size)],
                masked,
                CONTRACT_ROWS,
                preferred_element_type=F32,
            ).astype(BF)

        lax.fori_loop(
            0, joint // STEP, lambda i, _: product(pl.multiple_of(i * STEP, STEP), STEP), None
        )
        if joint % STEP:
            product(joint // STEP * STEP, joint % STEP)
        halves = [
            own_low,
            own_high,
            to_x.at[pl.ds(cut, cut), :],
            x_high,
            y_low,
            to_y.at[pl.ds(rest, rest), :],
            to_x.at[pl.ds(0, cut), :],
            to_y.at[pl.ds(0, rest), :],
        ]
        pairs = row_spans(wide, own, own_ff, cut, lane_ref[0], halves, whole)
        run_copies([(there, here) for here, there in pairs], sem)

    shapes = [(size, width) for size in (2 * cut, 2 * rest, rest, cut, cut, rest)]
    return pl.pallas_call(
        kernel,
        in_specs=[pl.BlockSpec(memory_space=pltpu.SMEM), ANYWHERE, ANYWHERE],
        out_specs=[pl.BlockSpec(memory_space=pltpu.HBM)] * len(shapes),
        out_shape=[pltpu.HBM(shape, BF) for shape in shapes],
        scratch_shapes=[
            pltpu.VMEM((everyone, joint), BF),
            pltpu.VMEM((everyone, width), BF),
            pltpu.VMEM((joint, width), BF),
            pltpu.SemaphoreType.DMA((3 * wide,)),
        ],
        compiler_params=pltpu.CompilerParams(vmem_limit_bytes=40 << 20),
        cost_estimate=HIDDEN_COST,
        name="mixer_grad",
    )(lane, *kept(joined, masked))


def column_plan(member, outer, wide, cores, own, own_ff, cols, main, rest):
    z, c = member // cores, member % cores
    out = []
    for g in range(3):
        for k in range(wide):
            src = (((g * outer + z) * wide + k) * cores + c) * own
            out.append((0, src, 0, g * cols + k * own, own))
    for which in range(2):
        for k in range(wide):
            src = ((z * wide + k) * cores + c) * own_ff
            lo, hi = k * own_ff, (k + 1) * own_ff
            cut = min(hi, main)
            if cut > lo:
                out.append((1 + which, src, 1, which * main + lo, cut - lo))
            low = max(lo, main)
            if hi > low:
                at = 2 * main + which * rest + low - main
                out.append((1 + which, src + low - lo, 1, at, hi - low))
    return out


def pack_kernel(plan, tp, bases, *refs):
    packed, arrays, sem = refs[3:5], refs[5:8], refs[8]
    run_copies(list(zip(refs[:3], arrays)), sem)
    rows = arrays[0].shape[0]
    edge = packed[0].shape[1]
    for member in range(tp):
        at = slice(member * rows, (member + 1) * rows)
        for which, src, part, dst, width in plan(member):
            dst += bases[part]
            for ref, low, high in ((packed[0], 0, edge), (packed[1], edge, sum(bases))):
                start, stop = max(dst, low), min(dst + width, high)
                if start < stop:
                    there = slice(src + start - dst, src + stop - dst)
                    ref[at, start - low : stop - low] = arrays[which][:, there]


def pack_call(arrays, plan, tp, widths):
    rows = arrays[0].shape[0]
    total = sum(widths)
    edge = total // 2 // TILE * TILE
    return pl.pallas_call(
        functools.partial(pack_kernel, plan, tp, (0, widths[0], total - widths[0])),
        in_specs=[ANYWHERE] * 3,
        out_specs=[HELD] * 2,
        out_shape=[jax.ShapeDtypeStruct((tp * rows, w), BF) for w in (edge, total - edge)],
        scratch_shapes=[pltpu.VMEM(array.shape, BF) for array in arrays]
        + [pltpu.SemaphoreType.DMA((3,))],
        compiler_params=pltpu.CompilerParams(vmem_limit_bytes=32 << 20),
        name="pack_columns",
    )(*kept(*arrays))


def unpack_kernel(plan, tp, part, *refs):
    packed, outs = refs[0], refs[1:]
    rows = outs[0].shape[0]
    for member in range(tp):
        at = slice(member * rows, (member + 1) * rows)
        for which, src, source, dst, width in plan(member):
            if source == part:
                out = outs[which - part]
                out[:, src : src + width] = packed[at, dst : dst + width].astype(F32)


def unpack_call(packed, part, plan, tp, widths):
    rows = packed.shape[0] // tp
    return pl.pallas_call(
        functools.partial(unpack_kernel, plan, tp, part),
        in_specs=[HELD],
        out_specs=[HELD] * len(widths),
        out_shape=[jax.ShapeDtypeStruct((rows, width), F32) for width in widths],
        compiler_params=pltpu.CompilerParams(vmem_limit_bytes=32 << 20),
        cost_estimate=HIDDEN_COST,
        name="unpack_columns",
    )(packed)


def join_kernel(count, *refs):
    ins, out, sem = refs[:count], refs[count], refs[count + 1]
    copies, at = [], 0
    for i, ref in enumerate(ins):
        size = ref.shape[0]
        copies.append(pltpu.make_async_copy(ref, out.at[pl.ds(at, size), :], sem.at[i]))
        at += size
    for copy in copies:
        copy.start()
    for copy in copies:
        copy.wait()


def join_call(arrays):
    count = len(arrays)
    rows, width = sum(array.shape[0] for array in arrays), arrays[0].shape[1]
    return pl.pallas_call(
        functools.partial(join_kernel, count),
        in_specs=[pl.BlockSpec(memory_space=pl.ANY)] * count,
        out_specs=pl.BlockSpec(memory_space=pltpu.VMEM),
        out_shape=jax.ShapeDtypeStruct((rows, width), BF),
        scratch_shapes=[pltpu.SemaphoreType.DMA((count,))],
        compiler_params=pltpu.CompilerParams(vmem_limit_bytes=16 << 20),
        name="join_rows",
    )(*arrays)


def row_spans(wide, own, own_ff, cut, lane, halves, whole):
    spans = []
    base = wide * own
    for j in range(wide):
        spot = lax.bitwise_xor(lane, j)
        down = pl.multiple_of(base + spot * own_ff, 16)
        down_low = pl.multiple_of(base + spot * own_ff + cut, 16)
        out = pl.multiple_of(spot * own, 16)
        low, high = halves[2 * j : 2 * j + 2]
        rest = own_ff - cut
        spans.append((low, whole.at[pl.ds(down, cut), :]))
        spans.append((high.at[pl.ds(0, rest), :], whole.at[pl.ds(down_low, rest), :]))
        spans.append((high.at[pl.ds(rest, own), :], whole.at[pl.ds(out, own), :]))
    return spans


def run_copies(pairs, sem):
    copies = [pltpu.make_async_copy(src, dst, sem.at[i]) for i, (src, dst) in enumerate(pairs)]
    for copy in copies:
        copy.start()
    for copy in copies:
        copy.wait()


def place_call(lane, halves, wide, own, own_ff, cut):
    width = halves[0].shape[1]

    def kernel(lane_ref, *refs):
        ins, out, sem = refs[:-2], refs[-2], refs[-1]
        run_copies(row_spans(wide, own, own_ff, cut, lane_ref[0], ins, out), sem)

    return pl.pallas_call(
        kernel,
        in_specs=[pl.BlockSpec(memory_space=pltpu.SMEM)]
        + [pl.BlockSpec(memory_space=pl.ANY)] * len(halves),
        out_specs=pl.BlockSpec(memory_space=pltpu.VMEM),
        out_shape=jax.ShapeDtypeStruct((wide * (own + own_ff), width), BF),
        scratch_shapes=[pltpu.SemaphoreType.DMA((3 * wide,))],
        compiler_params=pltpu.CompilerParams(vmem_limit_bytes=16 << 20),
        name="place_rows",
    )(lane, *halves)


def mixer_product(joined, masked):
    return lax.dot_general(joined, masked, CONTRACT_ROWS, preferred_element_type=F32).astype(BF)


class Plain:
    def __init__(self, outer, inner):
        self.tp, self.wide, self.cores, self.outer = outer, inner, 1, outer
        self.member = lax.axis_index("dp")
        self.token_axes, self.token_groups = "dp", None
        self.weight_axes, self.weight_groups = "fsdp", None

    def gather_tokens(self, block):
        return lax.all_gather(
            block, self.token_axes, axis=0, tiled=True, axis_index_groups=self.token_groups
        )

    def scatter_tokens(self, part):
        return lax.psum_scatter(
            part.astype(BF),
            self.token_axes,
            scatter_dimension=0,
            tiled=True,
            axis_index_groups=self.token_groups,
        ).astype(F32)

    def exchange(self, part):
        return lax.all_to_all(
            part,
            self.token_axes,
            split_axis=0,
            concat_axis=0,
            tiled=True,
            axis_index_groups=self.token_groups,
        )

    def gather_weights(self, block):
        return lax.all_gather(
            block, self.weight_axes, axis=0, tiled=True, axis_index_groups=self.weight_groups
        )

    def scatter_weights(self, part):
        return lax.psum_scatter(
            part,
            self.weight_axes,
            scatter_dimension=0,
            tiled=True,
            axis_index_groups=self.weight_groups,
        )

    def inputs(self, packed, w_out, w_down, normed, masked, lengths, make_tables):
        mixer = jnp.concatenate([self.gather_weights(w) for w in (w_out, w_down)], axis=0)
        entry = [self.gather_weights(self.exchange(part)) for part in packed]
        tokens = [self.gather_tokens(block) for block in (normed, masked)]
        lengths = lax.all_gather(lengths, "dp", axis=0, tiled=True)
        return entry, mixer, tokens[0], tokens[1], make_tables(lengths)

    def outputs(self, joined, masked, branch, back_call, tail, normed, own, own_ff):
        cols = self.wide * own
        part = mixer_product(joined, masked)
        grads = [self.scatter_weights(p).astype(F32) for p in (part[:cols], part[cols:])]
        grad_qkv, grad_ff, norm, bias_part = back_call(masked)
        parts = []
        for grad in (grad_qkv, grad_ff):
            part = lax.dot_general(normed, grad, CONTRACT_ROWS, preferred_element_type=F32)
            parts.append(self.scatter_weights(part.astype(BF)))
        norm, branch = self.scatter_tokens(norm), self.scatter_tokens(branch)
        part_qkv, part_ff = [self.exchange(part) for part in parts]
        grad_tokens, stats = tail(norm, bias_part)
        return grads[0], grads[1], part_qkv, part_ff, branch, grad_tokens, stats

    def relative(self, blocks, axis):
        return blocks

    def scatter_stats(self, stats):
        parts = lax.all_to_all(stats, AXES, split_axis=0, concat_axis=0, tiled=True)
        return jnp.sum(parts, axis=0)


class Linked(Plain):
    def __init__(self, outer, inner):
        self.outer, self.cores, self.wide = outer, 2, inner // 2
        self.tp = outer * 2
        flat = lax.axis_index("fsdp")
        self.lane = flat // 2
        self.member = lax.axis_index("dp") * 2 + lax.rem(flat, 2)
        spots = [
            [[(z * self.wide + k) * 2 + c for c in range(2)] for k in range(self.wide)]
            for z in range(outer)
        ]
        self.token_axes = self.weight_axes = AXES
        self.token_groups = [
            [spots[z][k][c] for z in range(outer) for c in range(2)] for k in range(self.wide)
        ]
        self.weight_groups = [
            [spots[z][k][c] for k in range(self.wide)] for z in range(outer) for c in range(2)
        ]
        self.spots = spots
        self.lane_index = self.lane.astype(jnp.int32).reshape(1)

    def send(self, value, step=0, dz=0, dc=0):
        pairs = [
            (self.spots[z][k][c], self.spots[z ^ dz][k ^ step][c ^ dc])
            for z in range(self.outer)
            for k in range(self.wide)
            for c in range(2)
        ]
        return lax.ppermute(value, AXES, pairs)

    def gather_lengths(self, lengths):
        parts = [lengths] + [self.send(lengths, dz=dz) for dz in range(1, self.outer)]
        return jnp.concatenate(parts, axis=0)

    def order_lengths(self, mine, other):
        both = jnp.stack([mine, other], axis=1).reshape(self.tp, -1)
        spot = lax.bitwise_xor(jnp.arange(self.tp, dtype=jnp.int32), self.member)
        pick = spot[:, None] == jnp.arange(self.tp, dtype=jnp.int32)[None, :]
        return jnp.sum(jnp.where(pick[:, :, None], both[None], 0), axis=1)

    def inputs(self, packed, w_out, w_down, normed, masked, lengths, make_tables):
        own, own_ff = w_out.shape[0], w_down.shape[0]
        cut = own_ff // 32 * 16 + 32
        half = packed[0].shape[0] // 2
        rows, left, right, lengths = tie(join_call([w_down, w_out]), *packed, lengths)
        mix_x, mix_y = self.send(rows, 1), self.send(rows, 2)
        lengths = self.gather_lengths(lengths)
        left = self.exchange(left)
        left, right, mix_x, mix_y = tie(left, right, mix_x, mix_y)
        left_x, left_y = self.send(left, 1), self.send(left, 2)
        right = self.exchange(right)
        halves = [part for b in (rows, mix_x, mix_y) for part in (b[:cut], b[cut:])]
        right, left_x, left_y, normed, masked, lengths, *halves = tie(
            right, left_x, left_y, normed, masked, lengths, *halves
        )
        normed_all, masked_all = self.gather_tokens(normed), self.gather_tokens(masked)
        right_x, right_y = self.send(right, 1), self.send(right, 2)
        mix_low, mix_high = self.send(halves[2], 2), self.send(halves[5], 1)
        left_low, left_high = self.send(left_x[:half], 2), self.send(left_y[half:], 1)
        tables = make_tables(self.order_lengths(lengths, self.send(lengths, dc=1)))
        halves += [mix_low, mix_high]
        mixer = place_call(self.lane_index, halves, self.wide, own, own_ff, cut)
        right_x, right_y, left_low, left_high, mixer, *tables = tie(
            right_x, right_y, left_low, left_high, *kept(mixer, *tables)
        )
        right_low, right_high = self.send(right_x[:half], 2), self.send(right_y[half:], 1)
        entry = [left, left_x, left_y, left_low, left_high]
        entry += [right, right_x, right_y, right_low, right_high]
        return entry, mixer, normed_all, masked_all, tables

    def first_sends(self, to_x, to_y):
        return self.send(to_x, 1), self.send(to_y, 2)

    def last_sends(self, got, x_high, y_low):
        from_x, from_y = got
        low, high = from_x[: y_low.shape[0]], from_y[: x_high.shape[0]]
        return (
            self.send((x_high.astype(F32) + high.astype(F32)).astype(BF), 1),
            self.send((y_low.astype(F32) + low.astype(F32)).astype(BF), 2),
        )

    def lane_sum(self, own_low, own_high, first, last):
        low = own_low.astype(F32) + first[0][own_low.shape[0] :].astype(F32)
        high = own_high.astype(F32) + first[1][own_high.shape[0] :].astype(F32)
        return low + last[1].astype(F32), high + last[0].astype(F32)

    def outputs(self, joined, masked, branch, back_call, tail, normed, own, own_ff):
        cut = own_ff // 32 * 16 + 32
        rest = own_ff - cut
        size = normed.shape[1] // self.wide // 2
        first, last = ((6, 2), (7, 5)), ((3,), (4,), (0,), (1,))

        branch = self.scatter_tokens(branch)
        mix = mixer_grad_call(self.lane_index, joined, masked, self.wide, own, own_ff, cut)
        *mix, masked = tie(*mix, masked)
        mix_first = self.first_sends(mix[0], mix[1])
        grad_qkv, grad_ff, norm, bias_part = back_call(masked)
        *mix_first, norm, grad_ff, grad_qkv = tie(*mix_first, norm, grad_ff, grad_qkv)
        norm = self.scatter_tokens(norm)
        to_x, to_y = product_call(normed, grad_ff, first, size)
        to_x, to_y, grad_ff = tie(to_x, to_y, grad_ff)
        ff_first = self.first_sends(to_x, to_y)
        x_high, y_low, ff_low, ff_high = product_call(normed, grad_ff, last, size)
        ff_low, grad_qkv = tie(ff_low, grad_qkv)
        to_x, to_y = product_call(normed, grad_qkv, first, size)
        to_x, grad_qkv = tie(to_x, grad_qkv)
        qkv_x, qkv_y, qkv_low, qkv_high = product_call(normed, grad_qkv, last, size)
        branch, to_x, to_y, x_high, y_low, qkv_low, *ff_first = tie(
            branch, to_x, to_y, x_high, y_low, qkv_low, *ff_first
        )
        ff_last = self.last_sends(ff_first, x_high, y_low)
        part_ff = self.joined_sum((x_high, y_low, ff_low, ff_high), ff_first, ff_last)
        part_ff, to_x, to_y = tie(part_ff, to_x, to_y)
        qkv_first = self.first_sends(to_x, to_y)
        part_ff = self.exchange(part_ff)
        results = tail(norm, bias_part)
        *qkv_first, grad_tokens, stats = tie(*qkv_first, *results)
        qkv_last = self.last_sends(qkv_first, qkv_x, qkv_y)
        part_qkv = self.joined_sum((qkv_x, qkv_y, qkv_low, qkv_high), qkv_first, qkv_last)
        stats = self.depth_stats(stats)
        part_ff, part_qkv, stats, *mix = tie(part_ff, part_qkv, stats, *mix_first, *mix[2:])
        part_qkv = self.exchange(part_qkv)
        mix_first, mix = mix[:2], mix[2:]
        mix_x, mix_y = add_call(mix_first, mix[0], mix[1])
        mix_last = self.send(mix_x, 1), self.send(mix_y, 2)
        grad_w_out, grad_w_down = mixer_sum_call(mix[2], mix[3], mix_first, mix_last, own)
        return grad_w_out, grad_w_down, part_qkv, part_ff, branch, grad_tokens, stats

    def joined_sum(self, late, first, last):
        return sum_call(late[2], late[3], first, last)

    def keep(self, values, axis, place, count, name):
        pick = lambda spot: lax.dynamic_index_in_dim(values, spot, axis, keepdims=False)
        got = [self.send(pick(lax.bitwise_xor(place, j)), **{name: j}) for j in range(1, count)]
        return pick(place) + sum(got)

    def depth_stats(self, stats):
        split = stats.reshape(self.outer, self.wide, 2, -1)
        return self.keep(split, 0, self.member // 2, self.outer, "dz")

    def scatter_stats(self, split):
        split = self.keep(split, 0, self.lane, self.wide, "step")
        return self.keep(split, 0, lax.rem(self.member, 2), 2, "dc")

    def relative(self, blocks, axis):
        shape = blocks.shape
        split = blocks.reshape(shape[:axis] + (2, 2) + shape[axis + 1 :])
        split = jnp.where(self.lane >= 2, jnp.flip(split, axis), split)
        split = jnp.where(lax.rem(self.lane, 2) == 1, jnp.flip(split, axis + 1), split)
        return split.reshape(shape)


def on_device(
    tokens, ln_gain, ln_shift, w_qkv, b_qkv, w_out, w_gate, w_up, w_down, grad_out, seq_lengths
):
    outer, inner = lax.axis_size("dp"), lax.axis_size("fsdp")
    linked = outer == 4 and inner == 8
    net = Linked(outer, inner) if linked else Plain(outer, inner)
    tp, wide, cores = net.tp, net.wide, net.cores
    rows_tok, width = tokens.shape
    own = w_qkv.shape[0]
    own_ff = w_down.shape[0]
    cols, cols_ff = wide * own, wide * own_ff
    main = cols_ff // TILE * TILE
    rest = cols_ff - main
    widths = (3 * cols, 2 * cols_ff)
    plan = lambda member: column_plan(
        member, outer, wide, cores, own, own_ff, cols, main, rest
    )

    _, valid, _ = block_terms(seq_lengths[0], rows_tok)
    keep_row = valid.astype(F32)[:, None]
    widened = tokens.astype(F32)
    centered = widened - jnp.mean(widened, axis=1, keepdims=True)
    inv_std = lax.rsqrt(jnp.mean(centered * centered, axis=1, keepdims=True) + EPS)
    scaled = centered * inv_std
    normed = (scaled * ln_gain + ln_shift).astype(BF)
    masked = (grad_out.astype(F32) * keep_row).astype(BF)

    def lanes_first(x):
        split = x.reshape(rows_tok, outer, wide, cores * own)
        return net.relative(jnp.swapaxes(split, 1, 2), 1).reshape(rows_tok, width)

    def lanes_back(x):
        split = net.relative(x.reshape(rows_tok, wide, outer, cores * own), 1)
        return jnp.swapaxes(split, 1, 2).reshape(rows_tok, width)

    lengths = seq_lengths
    arrays = [w_qkv, w_gate, w_up]

    bias = lax.dynamic_index_in_dim(
        jnp.transpose(b_qkv.reshape(3, outer, wide, cores, own), (1, 3, 0, 2, 4)).reshape(tp, -1),
        net.member,
        0,
    )
    bias = jnp.broadcast_to(bias, (8, 3 * cols))

    def make_tables(lengths):
        position, _, allowed = jax.vmap(lambda row: block_terms(row, rows_tok))(lengths)
        return [*turn_tables(position), jnp.where(allowed, 0.0, NEG), bias]

    entry, mixer, normed_all, masked_all, (cos_t, sin_t, mask, bias) = net.inputs(
        pack_call(arrays, plan, tp, widths),
        w_out,
        w_down,
        lanes_first(normed),
        masked,
        lengths,
        make_tables,
    )
    sizes = (cols, main, rest)
    joined, qkv, proj_ff, branch = forward_call(
        normed_all, bias, cos_t, sin_t, mask, entry, mixer, sizes
    )
    back_call = lambda masked: backward_call(
        masked, proj_ff, qkv, cos_t, sin_t, mask, mixer, entry, sizes
    )

    def tail(grad_norm, bias_part):
        grad_norm = lanes_back(grad_norm)
        lifted_grad = grad_norm * ln_gain
        grad_in = inv_std * (
            lifted_grad
            - jnp.mean(lifted_grad, axis=1, keepdims=True)
            - scaled * jnp.mean(lifted_grad * scaled, axis=1, keepdims=True)
        )
        grad_tokens = (grad_out.astype(F32) + grad_in).astype(BF)
        shards = outer * inner
        gain_part = jnp.sum(grad_norm * scaled, axis=0)
        shift_part = jnp.sum(grad_norm, axis=0)
        bias_full = lax.dynamic_update_index_in_dim(
            jnp.zeros((tp, 3 * cols), F32), bias_part[0], net.member, 0
        )
        bias_full = jnp.transpose(bias_full.reshape(outer, cores, 3, wide, own), (2, 0, 3, 1, 4))
        stats = jnp.concatenate(
            [
                gain_part.reshape(shards, own),
                shift_part.reshape(shards, own),
                bias_full.reshape(shards, 3 * own),
            ],
            axis=1,
        )
        return grad_tokens, stats

    grad_w_out, grad_w_down, part_qkv, part_ff, branch, grad_tokens, stats = net.outputs(
        joined, masked_all, branch, back_call, tail, normed_all, own, own_ff
    )
    output = (widened + keep_row * branch).astype(BF)
    grad_w_gate, grad_w_up = unpack_call(
        part_ff, 1, plan, tp, [w_gate.shape[1], w_up.shape[1]]
    )
    stats, grad_w_gate, grad_w_up = tie(stats, grad_w_gate, grad_w_up)
    stats = net.scatter_stats(stats)
    part_qkv, stats, grad_w_gate, grad_w_up = tie(part_qkv, stats, grad_w_gate, grad_w_up)
    (grad_w_qkv,) = unpack_call(part_qkv, 0, plan, tp, [w_qkv.shape[1]])
    return (
        output,
        grad_tokens,
        grad_w_qkv,
        grad_w_out,
        grad_w_gate,
        grad_w_up,
        grad_w_down,
        stats[:own],
        stats[own : 2 * own],
        stats[2 * own :],
    )


def solution(mesh):
    rows = P(AXES, None)
    return jax.shard_map(
        on_device,
        mesh=mesh,
        in_specs=(rows, P(), P(), rows, P(), rows, rows, rows, rows, rows, rows),
        out_specs=(rows,) * 7 + (P(AXES),) * 3,
        check_vma=False,
    )
```
